32 devices in a mesh: fsdp: 2 (over x), ctx: 4 (over y, core), tp: 4 (over z).
Axes of the slice: x: 2, y: 2, z: 4, core: 2. Of those that a mesh axis runs over, the one named last changes fastest.
Arguments:
- hidden_in: bfloat16 [2048, 2048], P(('fsdp', 'ctx'), 'tp'), may hold values from -6 to 6
- out_grad: bfloat16 [2048, 2048], P(('fsdp', 'ctx'), 'tp'), may hold values from -6 to 6
- attn_gain: bfloat16 [2048], P('fsdp'), may hold values from 0.5 to 1.5
- w_query: bfloat16 [2048, 2048], P('fsdp', 'tp'), may hold values from -0.1875 to 0.1875
- w_key: bfloat16 [2048, 2048], P('fsdp', 'tp'), may hold values from -0.1875 to 0.1875
- w_value: bfloat16 [2048, 2048], P('fsdp', 'tp'), may hold values from -0.125 to 0.125
- w_output: bfloat16 [2048, 2048], P('fsdp', 'tp'), may hold values from -0.75 to 0.75
- ffn_gain: bfloat16 [2048], P('fsdp'), may hold values from 0.5 to 1.5
- w_router: bfloat16 [2048, 4], P('fsdp'), may hold values from -0.09375 to 0.09375
- w_gate: bfloat16 [4, 2048, 5632], P(None, 'fsdp', 'tp'), may hold values from -0.125 to 0.125
- w_up: bfloat16 [4, 2048, 5632], P(None, 'fsdp', 'tp'), may hold values from -0.125 to 0.125
- w_down: bfloat16 [4, 2048, 5632], P(None, 'fsdp', 'tp'), may hold values from -0.15625 to 0.15625
- routes: int32 [2048, 2], P(('fsdp', 'ctx')), may hold values from 0 to 3, all different within a row; in each aligned block of 256 rows (0 to 255, 256 to 511, ...) at most 160 rows name the same one
Outputs:
- block_out: bfloat16 [2048, 2048], P(('fsdp', 'ctx'), 'tp')
- in_grad: float32 [2048, 2048], P(('fsdp', 'ctx'), 'tp')
- grad_attn_gain: float32 [2048], P(('fsdp', 'ctx'))
- grad_query: float32 [2048, 2048], P(('fsdp', 'ctx'), 'tp')
- grad_key: float32 [2048, 2048], P(('fsdp', 'ctx'), 'tp')
- grad_value: float32 [2048, 2048], P(('fsdp', 'ctx'), 'tp')
- grad_output: float32 [2048, 2048], P(('fsdp', 'ctx'), 'tp')
- grad_ffn_gain: float32 [2048], P(('fsdp', 'ctx'))
- grad_router: float32 [2048, 4], P(('fsdp', 'ctx'))
- grad_gate: float32 [4, 2048, 5632], P(None, ('fsdp', 'ctx'), 'tp')
- grad_up: float32 [4, 2048, 5632], P(None, ('fsdp', 'ctx'), 'tp')
- grad_down: float32 [4, 2048, 5632], P(None, ('fsdp', 'ctx'), 'tp')
The draws below stay inside these ranges and needn't reach their ends.
Inputs may be any that keep to these rules, and one draw needn't show every extreme that they name: `routes`: each row names 2 different experts. Among the 256 rows of one device no expert is named by more than 160 rows, and in every draw some device has an expert named by exactly 160 rows.
All inputs are finite; a program needn't handle non-finite values.
Results may differ from the reference program's by a relative error of at most 0.02.
Values may be sent and summed in bfloat16 or wider, within the bound.
A program may use at most 320 MiB of HBM per device.

```python
import math
import jax
import jax.numpy as jnp
import numpy as np
from jax import lax

D = 2048
HEADS = 16
HD = 128
FF = 5632
EXPERTS = 4
TOPK = 2
TOK_DEV = 256
CAP = 160
SEQ = 1024
TOKENS = 2048
N_FSDP = 2


def steps_of(key, extent, shards, low, largest):
    def one(dim, blocks):
        heights = jax.random.uniform(jax.random.fold_in(jax.random.fold_in(key, 6), dim), (blocks,), jnp.float32, low / len(shards), largest / len(shards))
        return jnp.repeat(jnp.exp(heights), extent[dim] // blocks).reshape((-1,) + (1,) * (len(extent) - dim - 1))

    loudness = one(*shards[0])
    for cut in shards[1:]:
        loudness = loudness * one(*cut)
    return loudness


def routed_block(own_key, own, number, rows, amount, top, bound, lean):
    order = jax.random.permutation(own_key, amount)
    crowded, ordinary = portions_of(amount, rows * top, bound, lean, True), portions_of(amount, rows * top, bound, lean, False)
    places = jnp.arange(amount)

    def named(lengths, rotation):
        used = int((lengths > 0).sum())
        fixed = max(1, used // 4)
        shifted = fixed + (places - fixed + rotation * (used - fixed)) % max(1, amount - fixed)
        return jnp.zeros((amount,), jnp.int32).at[order[jnp.where(places < fixed, places, shifted)]].set(jnp.asarray(lengths, jnp.int32))

    lengths = jnp.where(number % 4 == 0, named(crowded, number // 4), named(ordinary, number - number // 4 - 1))
    mixed = jax.random.permutation(jax.random.fold_in(own, 3), amount)
    source_of, receiver = mixed[0:amount // 2 * 2:2], mixed[1:amount // 2 * 2:2]
    margin = jnp.minimum(lengths[source_of] - 1, bound - lengths[receiver]) // 2
    margin = jnp.where((source_of == order[0]) | (receiver == order[0]) | (lengths[receiver] == 0), 0, jnp.maximum(margin, 0))
    shifted = jax.random.randint(jax.random.fold_in(own, 4), (amount // 2,), 0, 1 << 20) % (margin + 1)
    lengths = lengths.at[source_of].add(-shifted).at[receiver].add(shifted)
    labels = jnp.searchsorted(jnp.cumsum(lengths), jnp.arange(rows * top), side="right").astype(jnp.int32)
    table = labels.reshape(top, rows).T
    table = table[jax.random.permutation(jax.random.fold_in(own, 1), rows)]
    rotation = jax.random.randint(jax.random.fold_in(own, 2), (rows, 1), 0, top)
    return jnp.take_along_axis(table, (jnp.arange(top)[None, :] + rotation) % top, axis=1)


def portions_of(amount, total, limit, lean, full):
    weights = [(1 << 20) // math.isqrt(standing ** lean) + 1 for standing in range(1, amount + 1)]
    largest = limit if full else min(limit, max(-(-total // amount), total * weights[0] // sum(weights)))
    least = 1 if total - largest >= amount - 1 else 0
    given, surplus = [largest] + [least] * (amount - 1), total - largest - least * (amount - 1)
    while surplus > 0:
        candidates = [i for i in range(1, amount) if given[i] < largest] or [i for i in range(1, amount) if given[i] < limit]
        pool, budget = sum([weights[i] for i in candidates]), surplus
        for i in candidates:
            more = min(limit - given[i], max(1, budget * weights[i] // pool), surplus)
            given[i] = given[i] + more
            surplus = surplus - more
    return np.array(given)


def noise(own_key, shape, width, most, cuts=(), held_as=jnp.bfloat16):
    array = width * jax.random.normal(own_key, shape, jnp.float32)
    if cuts:
        array = array * steps_of(own_key, shape, cuts, -0.22, 0.18)
    return jnp.clip(array, -most, most).astype(held_as)


def setup_inputs(seed: int = 0) -> dict:
    seeds = jax.random.split(jax.random.key(seed), 14)
    hidden_in = noise(seeds[0], (TOKENS, D), 1.0, 6.0, ((0, 8), (1, 4)))
    out_grad = noise(seeds[1], (TOKENS, D), 1.0, 6.0, ((0, 8), (1, 4)))
    attn_gain = jnp.clip(1.0 + 0.1 * jax.random.normal(seeds[2], (D,), jnp.float32), 0.5, 1.5).astype(jnp.bfloat16)
    w_query = noise(seeds[3], (D, D), (D // 2) ** -0.5, 0.1875, ((0, 2), (1, 4)))
    w_key = noise(seeds[4], (D, D), (D // 2) ** -0.5, 0.1875, ((0, 2), (1, 4)))
    w_value = noise(seeds[5], (D, D), D ** -0.5, 0.125, ((0, 2), (1, 4)))
    w_output = noise(seeds[6], (D, D), (D // 32) ** -0.5, 0.75, ((0, 2), (1, 4)))
    ffn_gain = jnp.clip(1.0 + 0.1 * jax.random.normal(seeds[7], (D,), jnp.float32), 0.5, 1.5).astype(jnp.bfloat16)
    w_router = noise(seeds[8], (D, EXPERTS), (2 * D) ** -0.5, 0.09375, ((0, 2),))
    w_gate = noise(seeds[9], (EXPERTS, D, FF), D ** -0.5, 0.125, ((1, 2), (2, 4)))
    w_up = noise(seeds[10], (EXPERTS, D, FF), D ** -0.5, 0.125, ((1, 2), (2, 4)))
    w_down = noise(seeds[11], (EXPERTS, D, FF), (FF // 4) ** -0.5, 0.15625, ((1, 2), (2, 4)))
    routes_keys = jax.random.split(jax.random.fold_in(seeds[12], 1), TOKENS // TOK_DEV)
    routes_turns = jax.random.permutation(jax.random.fold_in(seeds[12], 3), TOKENS // TOK_DEV)
    routes = jax.vmap(lambda own, number: routed_block(jax.random.fold_in(seeds[12], 2), own, number, TOK_DEV, EXPERTS, TOPK, CAP, 2))(routes_keys, routes_turns).reshape((TOKENS, TOPK))
    return dict(hidden_in=hidden_in, out_grad=out_grad, attn_gain=attn_gain, w_query=w_query, w_key=w_key, w_value=w_value, w_output=w_output, ffn_gain=ffn_gain, w_router=w_router, w_gate=w_gate, w_up=w_up, w_down=w_down, routes=routes)


EPS = 1e-05
THETA = 10000.0
NEG = -1e+30
HIGH = lax.Precision.HIGHEST

@jax.custom_vjp
def low(v):
    return lax.optimization_barrier(v.astype(jnp.bfloat16)).astype(jnp.float32)

@jax.custom_vjp
def low_back(v):
    return v

def low_keep(v):
    return (low(v), None)

def low_pass(kept, grad):
    return (grad,)

def back_keep(v):
    return (v, None)

def back_low(kept, grad):
    return (low(grad),)
low.defvjp(low_keep, low_pass)
low_back.defvjp(back_keep, back_low)

def matmul(left, right):
    return jnp.dot(left, right, precision=HIGH, preferred_element_type=jnp.float32)

def rms_scale(values):
    return lax.rsqrt(lax.optimization_barrier(jnp.mean(values * values, axis=-1, keepdims=True)) + EPS)

def rotary_tables(positions):
    half_size = HD // 2
    frequency = THETA ** (-(jnp.arange(half_size, dtype=jnp.float32) * 2.0 / HD))
    angles = positions.astype(jnp.float32)[:, None] * frequency[None, :]
    return (jnp.cos(angles)[:, None, :], jnp.sin(angles)[:, None, :])

def rotate(values, cosine, sine_table):
    half_size = values.shape[-1] // 2
    first_half = values[..., :half_size]
    second_half = values[..., half_size:]
    return jnp.concatenate([first_half * cosine - second_half * sine_table, second_half * cosine + first_half * sine_table], axis=-1)

def rope_tokens(values, cosine, sine_table):
    shaped = values.reshape(N_FSDP, SEQ, HEADS, HD)
    return rotate(shaped, cosine, sine_table).reshape(N_FSDP * SEQ, HEADS, HD)

def route_table(routes, expert_count):
    return (routes[:, :, None] == jnp.arange(expert_count, dtype=jnp.int32)[None, None, :]).astype(jnp.float32)

def gate_values(logits, route_onehot):
    picked = lax.optimization_barrier(jnp.sum(route_onehot * logits[:, None, :], axis=-1))
    weights = jax.nn.softmax(picked, axis=-1)
    return (lax.optimization_barrier(jnp.sum(weights[:, :, None] * route_onehot, axis=1)), weights)

def dispatch(routes, expert, capacity):
    count_rows = routes.shape[0]
    chosen = lax.optimization_barrier(jnp.sum((routes == expert).astype(jnp.int32), axis=1)).astype(jnp.int32)
    slot_of = (jnp.cumsum(chosen) - 1).astype(jnp.int32)
    target = jnp.where(chosen > 0, slot_of, capacity).astype(jnp.int32)
    row_index = jnp.zeros((capacity,), jnp.int32).at[target].set(jnp.arange(count_rows, dtype=jnp.int32), mode='drop')
    slot_live = (jnp.arange(capacity, dtype=jnp.int32) < jnp.sum(chosen).astype(jnp.int32)).astype(jnp.float32)
    return (row_index, slot_live, jnp.maximum(slot_of, 0).astype(jnp.int32), chosen.astype(jnp.float32))

def expert_rows(normed_rows, route_rows, mix_rows, gate_w, up_w, down_w):
    total_rows = jnp.zeros(normed_rows.shape, jnp.float32)
    for expert in range(EXPERTS):
        row_index, slot_live, slot_of, chosen = dispatch(route_rows, expert, CAP)
        picked = normed_rows[row_index]
        gate_act = low_back(matmul(picked, gate_w[expert]))
        up_act = low_back(matmul(picked, up_w[expert]))
        hidden_act = low(jax.nn.silu(gate_act) * up_act)
        result = low_back(matmul(hidden_act, down_w[expert].T))
        total_rows = total_rows + (mix_rows[:, expert] * chosen)[:, None] * result[slot_of]
    return total_rows

def attention(query_rows, key_rows, value_rows):
    seq_shape = (N_FSDP, SEQ, HEADS, HD)
    query_seq = query_rows.reshape(seq_shape)
    key_seq = key_rows.reshape(seq_shape)
    value_seq = value_rows.reshape(seq_shape)
    blocks = SEQ // TOK_DEV
    score_scale = 1.0 / math.sqrt(HD)

    def one_block(position):
        seq_index = position // blocks
        block_index = position % blocks
        query_here = lax.dynamic_index_in_dim(query_seq, seq_index, 0, False)
        query_block = lax.dynamic_slice_in_dim(query_here, block_index * TOK_DEV, TOK_DEV, 0)
        keys_here = lax.dynamic_index_in_dim(key_seq, seq_index, 0, False)
        values_here = lax.dynamic_index_in_dim(value_seq, seq_index, 0, False)
        scores = low_back(jnp.einsum('qhd,khd->hqk', query_block, keys_here, precision=HIGH) * score_scale)
        query_pos = block_index * TOK_DEV + jnp.arange(TOK_DEV, dtype=jnp.int32)
        key_pos = jnp.arange(SEQ, dtype=jnp.int32)
        scores = jnp.where(key_pos[None, None, :] <= query_pos[None, :, None], scores, NEG)
        prob_rows = jax.nn.softmax(scores, axis=-1)
        mixed = jnp.einsum('hqk,khd->qhd', low(prob_rows), values_here, precision=HIGH)
        return low(low_back(mixed))
    outputs = lax.map(jax.checkpoint(one_block), jnp.arange(N_FSDP * blocks, dtype=jnp.int32))
    return outputs.reshape(N_FSDP * SEQ, HEADS * HD)

def reference(hidden_in, out_grad, attn_gain, w_query, w_key, w_value, w_output, ffn_gain, w_router, w_gate, w_up, w_down, routes):
    weights_in = tuple((array_in.astype(jnp.float32) for array_in in (attn_gain, w_query, w_key, w_value, w_output, ffn_gain, w_router, w_gate, w_up, w_down)))
    inputs_wide = hidden_in.astype(jnp.float32)
    route_onehot = route_table(routes, EXPERTS)
    cosine, sine_table = rotary_tables(jnp.arange(SEQ, dtype=jnp.int32))

    def forward(inputs, weights):
        gain_one, query_w, key_w, value_w, output_w, gain_two, router_w, gate_w, up_w, down_w = weights
        normed_one = low(inputs * rms_scale(inputs) * gain_one)
        query_pre = low_back(matmul(normed_one, query_w))
        key_pre = low_back(matmul(normed_one, key_w))
        value_rows = low(low_back(matmul(normed_one, value_w)))
        query_rows = low(rope_tokens(query_pre, cosine, sine_table))
        key_rows = low(rope_tokens(key_pre, cosine, sine_table))
        attended = attention(query_rows, key_rows, value_rows.reshape(TOKENS, HEADS, HD))
        resid = inputs + low_back(matmul(attended, output_w.T))
        normed_two = low(resid * rms_scale(resid) * gain_two)
        logits = low_back(matmul(normed_two, router_w))
        mix_gates, gate_pair = gate_values(logits, route_onehot)
        blocks_in = (normed_two.reshape(-1, TOK_DEV, D), routes.reshape(-1, TOK_DEV, TOPK), mix_gates.reshape(-1, TOK_DEV, EXPERTS))
        moe_rows = lax.map(jax.checkpoint(lambda packed: expert_rows(packed[0], packed[1], packed[2], gate_w, up_w, down_w)), blocks_in)
        return resid + moe_rows.reshape(TOKENS, D)
    out_value, pull_back = jax.vjp(forward, inputs_wide, weights_in)
    input_grad, weight_grads = pull_back(out_grad.astype(jnp.float32))
    g_gain_one, g_query, g_key, g_value, g_output, g_gain_two, g_router, g_gate, g_up, g_down = weight_grads
    return (out_value.astype(jnp.bfloat16), input_grad, g_gain_one, g_query, g_key, g_value, g_output, g_gain_two, g_router, g_gate, g_up, g_down)
```

```python
from functools import partial
import math

import jax
import jax.numpy as jnp
from jax import lax
from jax.experimental import pallas as pl
from jax.experimental.pallas import tpu as pltpu
from jax.sharding import PartitionSpec as P

HD = 128
CAP = 160


EPS = 1e-05
THETA = 10000.0
NEG = -1e30
BF = jnp.bfloat16
F32 = jnp.float32


def mm(left, right):
    return jnp.dot(left, right, preferred_element_type=F32)


def mm_t(left, right):
    return lax.dot_general(left, right, (((1,), (1,)), ((), ())), preferred_element_type=F32)


def t_mm(left, right):
    return lax.dot_general(left, right, (((0,), (0,)), ((), ())), preferred_element_type=F32)


def rotary_tables(positions):
    half_size = HD // 2
    frequency = THETA ** (-(jnp.arange(half_size, dtype=F32) * 2.0 / HD))
    angles = positions.astype(F32)[:, None] * frequency[None, :]
    return (jnp.cos(angles)[:, None, :], jnp.sin(angles)[:, None, :])


def rotate(values, cosine, sine_table):
    half_size = values.shape[-1] // 2
    first_half = values[..., :half_size]
    second_half = values[..., half_size:]
    return jnp.concatenate(
        [
            first_half * cosine - second_half * sine_table,
            second_half * cosine + first_half * sine_table,
        ],
        axis=-1,
    )


def softmax_rows(query, key, first_row):
    scores = mm_t(query, key) * (1.0 / math.sqrt(HD))
    rows = first_row + lax.broadcasted_iota(jnp.int32, scores.shape, 0)
    cols = lax.broadcasted_iota(jnp.int32, scores.shape, 1)
    scores = jnp.where(cols <= rows, scores, NEG)
    top = jnp.max(scores, axis=-1, keepdims=True)
    weights = jnp.exp(scores - top)
    return weights / jnp.sum(weights, axis=-1, keepdims=True)


def attention_forward_kernel(query_ref, key_ref, value_ref, out_ref):
    first_row = lax.axis_index("ctx") * query_ref.shape[0]
    probs = softmax_rows(query_ref[...], key_ref[...], first_row)
    out_ref[...] = mm(probs.astype(BF), value_ref[...]).astype(BF)


def attention_forward(query, kv):
    rows, width = query.shape
    keys = kv.shape[0]
    heads = width // HD
    return pl.pallas_call(
        attention_forward_kernel,
        grid=(heads,),
        out_shape=jax.ShapeDtypeStruct((rows, width), BF),
        in_specs=[
            pl.BlockSpec((rows, HD), lambda h: (0, h)),
            pl.BlockSpec((keys, HD), lambda h: (0, h)),
            pl.BlockSpec((keys, HD), lambda h: (0, h + heads)),
        ],
        out_specs=pl.BlockSpec((rows, HD), lambda h: (0, h)),
        cost_estimate=pl.CostEstimate(
            flops=4 * rows * keys * width,
            bytes_accessed=2 * (2 * rows * width + 2 * keys * width),
            transcendentals=rows * keys * heads,
        ),
        name="attention_forward",
    )(query, kv, kv)


def attention_backward_kernel(query_ref, key_ref, value_ref, dout_ref, dq_ref, dk_ref, dv_ref):
    first_row = lax.axis_index("ctx") * query_ref.shape[0]
    scale = 1.0 / math.sqrt(HD)
    probs = softmax_rows(query_ref[...], key_ref[...], first_row)
    d_probs = mm_t(dout_ref[...], value_ref[...])
    delta = jnp.sum(probs * d_probs, axis=-1, keepdims=True)
    d_scores = (probs * (d_probs - delta)).astype(BF)
    dq_ref[...] = mm(d_scores, key_ref[...]) * scale
    dk_ref[...] = (t_mm(d_scores, query_ref[...]) * scale).astype(BF)
    dv_ref[...] = t_mm(probs.astype(BF), dout_ref[...]).astype(BF)


def attention_backward(query, kv, dout):
    rows, width = query.shape
    keys = kv.shape[0]
    heads = width // HD
    return pl.pallas_call(
        attention_backward_kernel,
        grid=(heads,),
        out_shape=(
            jax.ShapeDtypeStruct((rows, width), F32),
            jax.ShapeDtypeStruct((keys, width), BF),
            jax.ShapeDtypeStruct((keys, width), BF),
        ),
        in_specs=[
            pl.BlockSpec((rows, HD), lambda h: (0, h)),
            pl.BlockSpec((keys, HD), lambda h: (0, h)),
            pl.BlockSpec((keys, HD), lambda h: (0, h + heads)),
            pl.BlockSpec((rows, HD), lambda h: (0, h)),
        ],
        out_specs=(
            pl.BlockSpec((rows, HD), lambda h: (0, h)),
            pl.BlockSpec((keys, HD), lambda h: (0, h)),
            pl.BlockSpec((keys, HD), lambda h: (0, h)),
        ),
        cost_estimate=pl.CostEstimate(
            flops=10 * rows * keys * width,
            bytes_accessed=2 * (4 * rows * width + 4 * keys * width),
            transcendentals=rows * keys * heads,
        ),
        name="attention_backward",
    )(query, kv, kv, dout)


def shards(
    hidden_in,
    out_grad,
    attn_gain,
    w_query,
    w_key,
    w_value,
    w_output,
    ffn_gain,
    w_router,
    w_gate,
    w_up,
    w_down,
    routes,
):
    rows_here, width_tp = hidden_in.shape
    here_tp = lax.axis_index("tp")
    here_ctx = lax.axis_index("ctx")
    here_fsdp = lax.axis_index("fsdp")
    n_fsdp = lax.axis_size("fsdp")
    n_ctx = lax.axis_size("ctx")
    n_tp = lax.axis_size("tp")
    experts = w_gate.shape[0]
    assert experts == n_ctx
    width = width_tp * n_tp
    part = width // n_fsdp
    pair = n_fsdp == 2
    heads_width = w_query.shape[1]

    def shift_ctx(value, k):
        return lax.ppermute(value, "ctx", [(i, (i + k) % n_ctx) for i in range(n_ctx)])

    def swap_fsdp(value):
        return lax.ppermute(value, "fsdp", [(0, 1), (1, 0)])

    def other_parts(weight):
        if pair:
            return [weight, swap_fsdp(weight)]
        return [lax.all_gather(weight, "fsdp", axis=0, tiled=True)]

    def split(values):
        if pair:
            return [
                lax.dynamic_slice_in_dim(values, here_fsdp * part, part, 1),
                lax.dynamic_slice_in_dim(values, (1 - here_fsdp) * part, part, 1),
            ]
        return [values]

    def join(pieces):
        if pair:
            first = here_fsdp == 0
            return jnp.concatenate(
                [jnp.where(first, pieces[0], pieces[1]), jnp.where(first, pieces[1], pieces[0])],
                axis=1,
            )
        return pieces[0]

    def into(values, weights):
        return sum(mm(x, w) for x, w in zip(split(values), weights))

    def back(values, weights):
        return join([mm_t(values, w) for w in weights])

    def my_features(values):
        return lax.dynamic_slice_in_dim(values, here_tp * width_tp, width_tp, values.ndim - 1)

    inputs_full = lax.all_gather(hidden_in, "tp", axis=1, tiled=True)
    attn_w = jnp.concatenate([w_query, w_key, w_value, w_output], axis=1)
    if pair:
        quarter = part // n_ctx
        own_quarter = lax.dynamic_slice_in_dim(attn_w, here_ctx * quarter, quarter, 0)
        other_quarter = swap_fsdp(own_quarter)
        attn_other = lax.all_gather(other_quarter, "ctx", axis=0, tiled=True)
        attn_parts = [attn_w, attn_other]
    else:
        attn_parts = [lax.all_gather(attn_w, "fsdp", axis=0, tiled=True)]
    qkv_parts = [w[:, : 3 * heads_width] for w in attn_parts]
    out_parts = [w[:, 3 * heads_width :] for w in attn_parts]
    small = jnp.concatenate([attn_gain[:, None], ffn_gain[:, None], w_router], axis=1)
    small = lax.all_gather(small, "fsdp", axis=0, tiled=True)
    gain_one = small[:, 0].astype(F32)
    gain_two = small[:, 1].astype(F32)
    router_w = small[:, 2:]

    inputs_wide = inputs_full.astype(F32)
    scale_one = lax.rsqrt(jnp.mean(inputs_wide * inputs_wide, axis=-1, keepdims=True) + EPS)
    normed_one = (inputs_wide * scale_one * gain_one).astype(BF)
    heads_here = heads_width // HD
    head_shape = (rows_here, heads_here, HD)
    flat_shape = (rows_here, heads_width)
    positions = here_ctx * rows_here + jnp.arange(rows_here, dtype=jnp.int32)
    cosine, sine_table = rotary_tables(positions)
    qkv = into(normed_one, qkv_parts)
    query_pre = qkv[:, :heads_width].reshape(head_shape)
    key_pre = qkv[:, heads_width : 2 * heads_width].reshape(head_shape)
    query = rotate(query_pre, cosine, sine_table).astype(BF).reshape(flat_shape)
    key = rotate(key_pre, cosine, sine_table).astype(BF).reshape(flat_shape)
    value = qkv[:, 2 * heads_width :].astype(BF)
    kv = lax.all_gather(jnp.concatenate([key, value], axis=1), "ctx", axis=0, tiled=True)
    attended = attention_forward(query, kv)
    attn_share = lax.psum_scatter(
        back(attended, out_parts).astype(BF), "tp", scatter_dimension=1, tiled=True
    )
    resid = hidden_in.astype(F32) + attn_share.astype(F32)
    square = lax.psum(jnp.sum(resid * resid, axis=-1, keepdims=True), "tp")
    scale_two = lax.rsqrt(square / width + EPS)
    unit_two = resid * scale_two
    gain_two_here = my_features(gain_two)
    normed_two = lax.all_gather(
        (unit_two * gain_two_here).astype(BF), "tp", axis=1, tiled=True
    )

    logits = mm(normed_two, router_w)
    route_onehot = (routes[:, :, None] == jnp.arange(experts, dtype=jnp.int32)).astype(F32)
    picked_logits = jnp.sum(route_onehot * logits[:, None, :], axis=-1)
    gate_pair = jax.nn.softmax(picked_logits, axis=-1)
    relative = (jnp.arange(experts, dtype=jnp.int32) + here_ctx) % experts
    names = (routes[:, :, None] == relative).astype(F32)
    mix_gates = jnp.sum(gate_pair[:, :, None] * names, axis=1)
    chosen = jnp.sum(names, axis=1)
    before = jnp.tril(jnp.ones((rows_here, rows_here), BF), -1)
    slot_of = mm(before, chosen.astype(BF)).astype(jnp.int32)
    slots = jnp.arange(CAP, dtype=jnp.int32)
    pick = (slot_of.T[:, None, :] == slots[None, :, None]) & (chosen.T[:, None, :] > 0)
    pick_low = pick.astype(BF)
    pick_flat = pick_low.reshape(experts * CAP, rows_here)

    def dispatch(slabs):
        return jnp.concatenate(
            [slabs[0]] + [shift_ctx(slabs[k], k) for k in range(1, experts)], axis=0
        )

    def give_back(values):
        slabs = values.reshape(experts, CAP, values.shape[-1])
        return [slabs[0]] + [shift_ctx(slabs[k], -k) for k in range(1, experts)]

    grad_full = lax.all_gather(out_grad, "tp", axis=1, tiled=True)
    grad_rows = dispatch(mm(pick_flat, grad_full).astype(BF).reshape(experts, CAP, width))
    token_rows = dispatch(mm(pick_flat, normed_two).astype(BF).reshape(experts, CAP, width))
    gate_slots = jnp.sum(jnp.where(pick, mix_gates.T[:, None, :], 0.0), axis=-1)
    gate_rows = dispatch(gate_slots[:, :, None])

    gate_w = other_parts(lax.dynamic_index_in_dim(w_gate, here_ctx, 0, False))
    up_w = other_parts(lax.dynamic_index_in_dim(w_up, here_ctx, 0, False))
    down_w = other_parts(lax.dynamic_index_in_dim(w_down, here_ctx, 0, False))
    gate_act = into(token_rows, gate_w)
    up_act = into(token_rows, up_w)
    sigma_act = jax.nn.sigmoid(gate_act)
    hidden_act = (gate_act * sigma_act * up_act).astype(BF)
    result = back(hidden_act, down_w)
    d_result = (gate_rows * grad_rows.astype(F32)).astype(BF)
    gate_dot = jnp.sum(result * grad_rows.astype(F32), axis=-1, keepdims=True)
    returned = give_back(result.astype(BF))
    returned_dot = give_back(gate_dot)
    moe_part = sum(
        mix_gates[:, k][:, None] * t_mm(pick_low[k], returned[k]) for k in range(experts)
    )
    moe_share = lax.psum_scatter(moe_part.astype(BF), "tp", scatter_dimension=1, tiled=True)
    block_out = (resid + moe_share.astype(F32)).astype(BF)

    d_hidden = into(d_result, down_w)
    d_gate_act = (d_hidden * up_act * sigma_act * (1.0 + gate_act * (1.0 - sigma_act))).astype(BF)
    d_up_act = (d_hidden * gate_act * sigma_act).astype(BF)
    d_rows = join(
        [mm_t(d_gate_act, wg) + mm_t(d_up_act, wu) for wg, wu in zip(gate_w, up_w)]
    )
    returned_grad = give_back(d_rows.astype(BF))
    d_normed_part = sum(t_mm(pick_low[k], returned_grad[k]) for k in range(experts))
    d_gate_slots = jnp.stack([jnp.sum(
        jnp.where(pick[k], returned_dot[k], 0.0), axis=0
    ) for k in range(experts)], axis=1)

    def expert_grad(left, right):
        halves = split(left)
        if pair:
            other = swap_fsdp(t_mm(halves[1], right).astype(BF))
            mine = t_mm(halves[0], right) + other.astype(F32)
            mine = mine.astype(BF)
        else:
            mine = lax.psum_scatter(
                t_mm(halves[0], right).astype(BF), "fsdp", scatter_dimension=0, tiled=True
            )
        cut = part // n_ctx
        out = jnp.zeros((experts, cut, right.shape[1]), F32)
        for k in range(experts):
            piece = lax.dynamic_slice_in_dim(mine, ((here_ctx + k) % n_ctx) * cut, cut, 0)
            if k:
                piece = shift_ctx(piece, k)
            out = lax.dynamic_update_index_in_dim(
                out, piece.astype(F32), (here_ctx + n_ctx - k) % n_ctx, 0
            )
        return out

    grad_down = expert_grad(d_result, hidden_act)
    grad_gate = expert_grad(token_rows, d_gate_act)
    grad_up = expert_grad(token_rows, d_up_act)

    d_normed = lax.psum_scatter(d_normed_part.astype(BF), "tp", scatter_dimension=1, tiled=True)
    gate_grad = lax.psum(d_gate_slots, "tp")
    pair_grad = jnp.sum(names * gate_grad[:, None, :], axis=-1)
    pick_grad = gate_pair * (pair_grad - jnp.sum(gate_pair * pair_grad, axis=-1, keepdims=True))
    logit_grad = jnp.sum(pick_grad[:, :, None] * route_onehot, axis=1).astype(BF)
    router_here = lax.dynamic_slice_in_dim(router_w, here_tp * width_tp, width_tp, 0)
    d_normed = d_normed.astype(F32) + mm_t(logit_grad, router_here)
    grad_router_part = t_mm(normed_two, logit_grad)
    grad_gain_two_part = jnp.sum(d_normed * unit_two, axis=0)
    gained_two = gain_two_here * d_normed
    dot_two = lax.psum(jnp.sum(unit_two * gained_two, axis=-1, keepdims=True), "tp") / width
    d_resid = out_grad.astype(F32) + scale_two * (gained_two - unit_two * dot_two)
    d_attn = lax.all_gather(d_resid.astype(BF), "tp", axis=1, tiled=True)

    d_attended = into(d_attn, out_parts).astype(BF)
    d_query, key_grad, value_grad = attention_backward(query, kv, d_attended)
    kv_grad = lax.psum_scatter(
        jnp.concatenate([key_grad, value_grad], axis=1), "ctx", scatter_dimension=0, tiled=True
    ).astype(F32)
    d_query_pre = rotate(d_query.reshape(head_shape), cosine, -sine_table)
    d_key_pre = rotate(kv_grad[:, :heads_width].reshape(head_shape), cosine, -sine_table)
    d_qkv = jnp.concatenate(
        [
            d_query_pre.astype(BF).reshape(flat_shape),
            d_key_pre.astype(BF).reshape(flat_shape),
            kv_grad[:, heads_width:].astype(BF),
        ],
        axis=1,
    )
    d_normed_one = lax.psum_scatter(
        back(d_qkv, qkv_parts).astype(BF), "tp", scatter_dimension=1, tiled=True
    ).astype(F32)
    unit_one = hidden_in.astype(F32) * scale_one
    grad_gain_one_part = jnp.sum(d_normed_one * unit_one, axis=0)
    gained_one = my_features(gain_one) * d_normed_one
    dot_one = lax.psum(jnp.sum(unit_one * gained_one, axis=-1, keepdims=True), "tp") / width
    in_grad = d_resid + scale_one * (gained_one - unit_one * dot_one)

    grad_qkv_part = t_mm(normed_one, d_qkv)
    grad_output_part = t_mm(d_attn, attended)
    grad_attn = lax.psum_scatter(
        jnp.concatenate([grad_qkv_part, grad_output_part], axis=1).astype(BF),
        ("fsdp", "ctx"),
        scatter_dimension=0,
        tiled=True,
    ).astype(F32)
    gains = jnp.stack([grad_gain_one_part, grad_gain_two_part], axis=1)
    gains = lax.dynamic_update_slice_in_dim(
        jnp.zeros((width, 2), F32), gains, here_tp * width_tp, 0
    )
    small_part = jnp.concatenate([gains, grad_router_part / n_tp], axis=1)
    small_grad = lax.psum(
        lax.psum_scatter(small_part, ("fsdp", "ctx"), scatter_dimension=0, tiled=True), "tp"
    )
    return (
        block_out,
        in_grad,
        small_grad[:, 0],
        grad_attn[:, :heads_width],
        grad_attn[:, heads_width : 2 * heads_width],
        grad_attn[:, 2 * heads_width : 3 * heads_width],
        grad_attn[:, 3 * heads_width :],
        small_grad[:, 1],
        small_grad[:, 2:],
        grad_gate,
        grad_up,
        grad_down,
    )


def solution(mesh):
    rows = ("fsdp", "ctx")
    placed = (
        P(rows, "tp"),
        P(rows, "tp"),
        P("fsdp"),
        P("fsdp", "tp"),
        P("fsdp", "tp"),
        P("fsdp", "tp"),
        P("fsdp", "tp"),
        P("fsdp"),
        P("fsdp", None),
        P(None, "fsdp", "tp"),
        P(None, "fsdp", "tp"),
        P(None, "fsdp", "tp"),
        P(rows, None),
    )
    return jax.shard_map(
        shards,
        mesh=mesh,
        in_specs=placed,
        out_specs=(
            P(rows, "tp"),
            P(rows, "tp"),
            P(rows),
            P(rows, "tp"),
            P(rows, "tp"),
            P(rows, "tp"),
            P(rows, "tp"),
            P(rows),
            P(rows, None),
            P(None, rows, "tp"),
            P(None, rows, "tp"),
            P(None, rows, "tp"),
        ),
        check_vma=False,
    )
```

```python
from functools import partial
import math

import jax
import jax.numpy as jnp
from jax import lax
from jax.experimental import pallas as pl
from jax.experimental.pallas import tpu as pltpu
from jax.sharding import PartitionSpec as P

HD = 128
CAP = 160


EPS = 1e-05
THETA = 10000.0
NEG = -1e30
BF = jnp.bfloat16
F32 = jnp.float32


def mm(left, right):
    return jnp.dot(left, right, preferred_element_type=F32)


def mm_t(left, right):
    return lax.dot_general(left, right, (((1,), (1,)), ((), ())), preferred_element_type=F32)


def t_mm(left, right):
    return lax.dot_general(left, right, (((0,), (0,)), ((), ())), preferred_element_type=F32)


def rotary_tables(positions):
    half_size = HD // 2
    frequency = THETA ** (-(jnp.arange(half_size, dtype=F32) * 2.0 / HD))
    angles = positions.astype(F32)[:, None] * frequency[None, :]
    return (jnp.cos(angles)[:, None, :], jnp.sin(angles)[:, None, :])


def rotate(values, cosine, sine_table):
    half_size = values.shape[-1] // 2
    first_half = values[..., :half_size]
    second_half = values[..., half_size:]
    return jnp.concatenate(
        [
            first_half * cosine - second_half * sine_table,
            second_half * cosine + first_half * sine_table,
        ],
        axis=-1,
    )


MESH = pl.DeviceIdType.MESH
VM = pl.BlockSpec(memory_space=pltpu.VMEM)
DMA = pltpu.SemaphoreType.DMA


def peer(axis, n, k):
    return lax.rem(lax.axis_index(axis) + k, n)


def greet(groups):
    barrier = pltpu.get_barrier_semaphore()
    for axis, n in groups:
        for k in range(1, n):
            pl.semaphore_signal(
                barrier, inc=1, device_id={axis: peer(axis, n, k)}, device_id_type=MESH
            )
    pl.semaphore_wait(barrier, sum(n - 1 for _, n in groups))


def send(source, target, axis, n, k, sems):
    copy = pltpu.make_async_remote_copy(
        src_ref=source,
        dst_ref=target,
        send_sem=sems[0].at[k - 1],
        recv_sem=sems[1].at[k - 1],
        device_id={axis: peer(axis, n, k)},
        device_id_type=MESH,
    )
    copy.start()
    return copy


def columns(n, size):
    return pl.ds(pl.multiple_of(n * size, 128), size)


def gather_columns(own, full, axis, n, sems):
    size = own.shape[1]
    place = full.at[:, columns(lax.axis_index(axis), size)]
    copies = [send(own, place, axis, n, k, sems) for k in range(1, n)]
    place[...] = own[...]
    return copies


def scatter_columns(part, slots, axis, n, sems):
    size = slots.shape[2]
    return [
        send(part.at[:, columns(peer(axis, n, k), size)], slots.at[k - 1], axis, n, k, sems)
        for k in range(1, n)
    ]


def finish(copies):
    for copy in copies:
        copy.wait()


def row_sums(values):
    ones = jnp.ones((8, values.shape[1]), F32)
    return lax.dot_general(
        ones,
        values,
        (((1,), (1,)), ((), ())),
        precision=lax.Precision.HIGHEST,
        preferred_element_type=F32,
    )


def as_column(sums):
    eighth = jnp.full((8, 128), 0.125, F32)
    return lax.dot_general(
        sums,
        eighth,
        (((0,), (0,)), ((), ())),
        precision=lax.Precision.HIGHEST,
        preferred_element_type=F32,
    )


def total_over(sums, mine, slots, axis, n, sems):
    mine[...] = sums
    copies = [send(mine, slots.at[k - 1], axis, n, k, sems) for k in range(1, n)]
    finish(copies)
    total = sums
    for k in range(1, n):
        total = total + slots[k - 1]
    return total


def call(kernel, out_shape, inputs, scratch, collective, name):
    return pl.pallas_call(
        kernel,
        out_shape=out_shape,
        in_specs=[VM] * len(inputs),
        out_specs=jax.tree.map(lambda _: VM, out_shape),
        scratch_shapes=scratch,
        compiler_params=pltpu.CompilerParams(collective_id=collective, has_side_effects=True),
        cost_estimate=pl.CostEstimate(flops=0, bytes_accessed=0, transcendentals=0),
        name=name,
    )(*inputs)


def shape(dims, dtype):
    return jax.ShapeDtypeStruct(dims, dtype)


def pair_of_sems(n):
    return [DMA((n - 1,)), DMA((n - 1,))]


def first_norm(hidden, grad, small, n_tp, n_fsdp):
    rows, size = hidden.shape
    width = size * n_tp

    def kernel(hid, grd, sml, out, scale, grd_full, sml_full, hid_full, *sems):
        greet([("tp", n_tp), ("fsdp", n_fsdp)])
        gains = gather_columns(sml, sml_full, "fsdp", n_fsdp, sems[0:2])
        hids = gather_columns(hid, hid_full, "tp", n_tp, sems[2:4])
        grads = gather_columns(grd, grd_full, "tp", n_tp, sems[4:6])
        finish(gains)
        finish(hids)
        values = hid_full[...].astype(F32)
        mean = jnp.sum(values * values, axis=-1, keepdims=True) * (1.0 / width)
        factor = lax.rsqrt(mean + EPS)
        scale[...] = jnp.broadcast_to(factor, scale.shape)
        out[...] = (values * factor * sml_full[0:1, :]).astype(BF)
        finish(grads)

    return call(
        kernel,
        (
            shape((rows, width), BF),
            shape((rows, 128), F32),
            shape((rows, width), BF),
            shape((8, width), F32),
        ),
        (hidden, grad, small),
        [pltpu.VMEM((rows, width), BF)] + pair_of_sems(n_fsdp) + pair_of_sems(n_tp) * 2,
        1,
        "first_norm",
    )


def gather_rows(value, axis, n, collective):
    rows = value.shape[0]

    def kernel(own, full, *sems):
        greet([(axis, n)])
        place = full.at[pl.ds(pl.multiple_of(lax.axis_index(axis) * rows, 16), rows), :]
        copies = [send(own, place, axis, n, k, sems) for k in range(1, n)]
        place[...] = own[...]
        finish(copies)

    return call(
        kernel,
        shape((rows * n, value.shape[1]), value.dtype),
        (value,),
        pair_of_sems(n),
        collective,
        "gather_" + axis,
    )


def softmax_rows(query, key, first_row):
    scores = mm_t(query, key) * (1.0 / math.sqrt(HD))
    rows = first_row + lax.broadcasted_iota(jnp.int32, scores.shape, 0)
    cols = lax.broadcasted_iota(jnp.int32, scores.shape, 1)
    scores = jnp.where(cols <= rows, scores, NEG)
    top = jnp.max(scores, axis=-1, keepdims=True)
    weights = jnp.exp(scores - top)
    return weights / jnp.sum(weights, axis=-1, keepdims=True)


def attention_forward(query, kv, n_ctx):
    rows, width = query.shape
    heads = width // HD

    def kernel(qry, own, out, full, *sems):
        greet([("ctx", n_ctx)])
        here = lax.axis_index("ctx")
        place = full.at[pl.ds(pl.multiple_of(here * rows, 16), rows), :]
        copies = [send(own, place, "ctx", n_ctx, k, sems) for k in range(1, n_ctx)]
        place[...] = own[...]
        finish(copies)

        @pl.loop(0, heads)
        def _(h):
            probs = softmax_rows(qry[:, columns(h, HD)], full[:, columns(h, HD)], here * rows)
            out[:, columns(h, HD)] = mm(
                probs.astype(BF), full[:, columns(h + heads, HD)]
            ).astype(BF)

    return call(
        kernel,
        (shape((rows, width), BF), shape((rows * n_ctx, 2 * width), BF)),
        (query, kv),
        pair_of_sems(n_ctx),
        2,
        "attention_forward",
    )


def second_norm(part, hidden, gain, n_tp):
    rows, size = hidden.shape
    width = size * n_tp

    def kernel(prt, hid, gn, resid, scale, out, slots, mine, sums, low, *sems):
        greet([("tp", n_tp)])
        here = lax.axis_index("tp")
        copies = scatter_columns(prt, slots, "tp", n_tp, sems[0:2])
        total = prt[:, columns(here, size)].astype(F32)
        finish(copies)
        for k in range(1, n_tp):
            total = total + slots[k - 1].astype(F32)
        total = hid[...].astype(F32) + total
        resid[...] = total
        square = total_over(row_sums(total * total), mine, sums, "tp", n_tp, sems[2:4])
        factor = lax.rsqrt(as_column(square) * (1.0 / width) + EPS)
        scale[...] = factor
        low[...] = (resid[...] * factor[:, 0:1] * gn[0:1, :]).astype(BF)
        finish(gather_columns(low, out, "tp", n_tp, sems[4:6]))

    return call(
        kernel,
        (shape((rows, size), F32), shape((rows, 128), F32), shape((rows, width), BF)),
        (part, hidden, gain),
        [
            pltpu.VMEM((n_tp - 1, rows, size), BF),
            pltpu.VMEM((8, rows), F32),
            pltpu.VMEM((n_tp - 1, 8, rows), F32),
            pltpu.VMEM((rows, size), BF),
        ]
        + pair_of_sems(n_tp) * 3,
        3,
        "second_norm",
    )


def second_norm_back(part, dots, gates, onehot, names, router, resid, scale, gain, grad, n_tp):
    rows, size = resid.shape
    width = size * n_tp

    def kernel(
        prt, dts, gts, one, nms, rtr, rsd, scl, gn, grd,
        d_resid, d_attn, d_gain, d_logits, slots, mine, sums, mine_two, sums_two, low, *sems
    ):
        greet([("tp", n_tp)])
        here = lax.axis_index("tp")
        copies = scatter_columns(prt, slots, "tp", n_tp, sems[0:2])
        gate_grad = total_over(dts[...], mine, sums, "tp", n_tp, sems[2:4])
        both = [jnp.sum(nms[j] * gate_grad, axis=0, keepdims=True) for j in range(2)]
        gate = [gts[j : j + 1, :] for j in range(2)]
        mean = gate[0] * both[0] + gate[1] * both[1]
        logits = sum(gate[j] * (both[j] - mean) * one[j] for j in range(2))
        d_logits[...] = logits
        total = prt[:, columns(here, size)].astype(F32) + lax.dot_general(
            logits.astype(BF),
            rtr[...].astype(BF),
            (((0,), (0,)), ((), ())),
            preferred_element_type=F32,
        )
        finish(copies)
        for k in range(1, n_tp):
            total = total + slots[k - 1].astype(F32)
        factor = scl[:, 0:1]
        unit = rsd[...] * factor
        d_gain[...] = jnp.broadcast_to(jnp.sum(total * unit, axis=0, keepdims=True), d_gain.shape)
        gained = total * gn[0:1, :]
        d_resid[...] = gained
        dot = total_over(row_sums(unit * gained), mine_two, sums_two, "tp", n_tp, sems[4:6])
        dot = as_column(dot)[:, 0:1] * (1.0 / width)
        result = grd[...].astype(F32) + factor * (d_resid[...] - rsd[...] * factor * dot)
        d_resid[...] = result
        low[...] = result.astype(BF)
        finish(gather_columns(low, d_attn, "tp", n_tp, sems[6:8]))

    return call(
        kernel,
        (
            shape((rows, size), F32),
            shape((rows, width), BF),
            shape((8, size), F32),
            shape((8, rows), F32),
        ),
        (part, dots, gates, onehot, names, router, resid, scale, gain, grad),
        [
            pltpu.VMEM((n_tp - 1, rows, size), BF),
            pltpu.VMEM((8, rows), F32),
            pltpu.VMEM((n_tp - 1, 8, rows), F32),
            pltpu.VMEM((8, rows), F32),
            pltpu.VMEM((n_tp - 1, 8, rows), F32),
            pltpu.VMEM((rows, size), BF),
        ]
        + pair_of_sems(n_tp) * 4,
        4,
        "second_norm_back",
    )


def attention_backward(query, kv, dout, n_ctx):
    rows, width = query.shape
    heads = width // HD
    scale = 1.0 / math.sqrt(HD)

    def kernel(qry, full, dot, dq, dkv, low, slots, *sems):
        greet([("ctx", n_ctx)])
        here = lax.axis_index("ctx")

        @pl.loop(0, heads)
        def _(h):
            at, at_v = columns(h, HD), columns(h + heads, HD)
            probs = softmax_rows(qry[:, at], full[:, at], here * rows)
            d_probs = mm_t(dot[:, at], full[:, at_v])
            delta = jnp.sum(probs * d_probs, axis=-1, keepdims=True)
            d_scores = (probs * (d_probs - delta)).astype(BF)
            dq[:, at] = mm(d_scores, full[:, at]) * scale
            low[:, at] = (t_mm(d_scores, qry[:, at]) * scale).astype(BF)
            low[:, at_v] = t_mm(probs.astype(BF), dot[:, at]).astype(BF)

        copies = []
        for k in range(1, n_ctx):
            to = peer("ctx", n_ctx, k) * rows
            copies.append(
                send(
                    low.at[pl.ds(pl.multiple_of(to, 16), rows), :],
                    slots.at[k - 1],
                    "ctx",
                    n_ctx,
                    k,
                    sems,
                )
            )
        total = low[pl.ds(pl.multiple_of(here * rows, 16), rows), :].astype(F32)
        finish(copies)
        for k in range(1, n_ctx):
            total = total + slots[k - 1].astype(F32)
        dkv[...] = total

    return call(
        kernel,
        (shape((rows, width), F32), shape((rows, 2 * width), F32)),
        (query, kv, dout),
        [
            pltpu.VMEM((rows * n_ctx, 2 * width), BF),
            pltpu.VMEM((n_ctx - 1, rows, 2 * width), BF),
        ]
        + pair_of_sems(n_ctx),
        5,
        "attention_backward",
    )


def first_norm_back(part, hidden, scale, gain, d_resid, n_tp):
    rows, size = hidden.shape
    width = size * n_tp

    def kernel(prt, hid, scl, gn, dr, out, d_gain, slots, mine, sums, *sems):
        greet([("tp", n_tp)])
        here = lax.axis_index("tp")
        copies = scatter_columns(prt, slots, "tp", n_tp, sems[0:2])
        total = prt[:, columns(here, size)].astype(F32)
        finish(copies)
        for k in range(1, n_tp):
            total = total + slots[k - 1].astype(F32)
        factor = scl[:, 0:1]
        unit = hid[...].astype(F32) * factor
        d_gain[...] = jnp.broadcast_to(jnp.sum(total * unit, axis=0, keepdims=True), d_gain.shape)
        gained = total * gn[0:1, :]
        out[...] = gained
        dot = total_over(row_sums(unit * gained), mine, sums, "tp", n_tp, sems[2:4])
        dot = as_column(dot)[:, 0:1] * (1.0 / width)
        unit = hid[...].astype(F32) * factor
        out[...] = dr[...] + factor * (out[...] - unit * dot)

    return call(
        kernel,
        (shape((rows, size), F32), shape((8, size), F32)),
        (part, hidden, scale, gain, d_resid),
        [
            pltpu.VMEM((n_tp - 1, rows, size), BF),
            pltpu.VMEM((8, rows), F32),
            pltpu.VMEM((n_tp - 1, 8, rows), F32),
        ]
        + pair_of_sems(n_tp) * 2,
        6,
        "first_norm_back",
    )


def after(value, *needed):
    held = lax.optimization_barrier((value, *needed))
    return held[0]


def shards(
    hidden_in,
    out_grad,
    attn_gain,
    w_query,
    w_key,
    w_value,
    w_output,
    ffn_gain,
    w_router,
    w_gate,
    w_up,
    w_down,
    routes,
):
    rows_here, width_tp = hidden_in.shape
    here_tp = lax.axis_index("tp")
    here_ctx = lax.axis_index("ctx")
    here_fsdp = lax.axis_index("fsdp")
    n_fsdp = lax.axis_size("fsdp")
    n_ctx = lax.axis_size("ctx")
    n_tp = lax.axis_size("tp")
    experts = w_gate.shape[0]
    assert experts == n_ctx
    width = width_tp * n_tp
    part = width // n_fsdp
    pair = n_fsdp == 2
    heads_width = w_query.shape[1]

    def shift_ctx(value, k):
        return lax.ppermute(value, "ctx", [(i, (i + k) % n_ctx) for i in range(n_ctx)])

    def swap_fsdp(value):
        return lax.ppermute(value, "fsdp", [(0, 1), (1, 0)])

    def other_parts(weight):
        if pair:
            return [weight, swap_fsdp(weight)]
        return [lax.all_gather(weight, "fsdp", axis=0, tiled=True)]

    def split(values):
        if pair:
            return [
                lax.dynamic_slice_in_dim(values, here_fsdp * part, part, 1),
                lax.dynamic_slice_in_dim(values, (1 - here_fsdp) * part, part, 1),
            ]
        return [values]

    def join(pieces):
        if pair:
            first = here_fsdp == 0
            return jnp.concatenate(
                [jnp.where(first, pieces[0], pieces[1]), jnp.where(first, pieces[1], pieces[0])],
                axis=1,
            )
        return pieces[0]

    def into(values, weights):
        return sum(mm(x, w) for x, w in zip(split(values), weights))

    def back(values, weights):
        return join([mm_t(values, w) for w in weights])

    def my_features(values):
        return lax.dynamic_slice_in_dim(values, here_tp * width_tp, width_tp, values.ndim - 1)

    attn_w = jnp.concatenate([w_query, w_key, w_value, w_output], axis=1)
    if pair:
        quarter = part // n_ctx
        own_quarter = lax.dynamic_slice_in_dim(attn_w, here_ctx * quarter, quarter, 0)
        other_quarter = swap_fsdp(own_quarter)
    gate_w = other_parts(lax.dynamic_index_in_dim(w_gate, here_ctx, 0, False))
    up_w = other_parts(lax.dynamic_index_in_dim(w_up, here_ctx, 0, False))
    down_w = other_parts(lax.dynamic_index_in_dim(w_down, here_ctx, 0, False))
    small = jnp.concatenate(
        [attn_gain[None], ffn_gain[None], w_router.T, jnp.zeros((2, part), BF)], axis=0
    ).astype(F32)
    normed_one, scale_one, grad_full, small_full = first_norm(
        hidden_in, out_grad, small, n_tp, n_fsdp
    )
    scale_one = scale_one[:, :1]
    if pair:
        attn_parts = [attn_w, gather_rows(other_quarter, "ctx", n_ctx, 7)]
    else:
        attn_parts = [lax.all_gather(attn_w, "fsdp", axis=0, tiled=True)]
    qkv_parts = [w[:, : 3 * heads_width] for w in attn_parts]
    out_parts = [w[:, 3 * heads_width :] for w in attn_parts]
    small_here = my_features(small_full)
    gain_one_here = jnp.broadcast_to(small_here[0:1], small_here.shape)
    gain_two_here = jnp.broadcast_to(small_here[1:2], small_here.shape)
    router_w = small_full[2 : 2 + experts].astype(BF)
    router_here = jnp.concatenate(
        [small_here[2 : 2 + experts], jnp.zeros((8 - experts, width_tp), F32)], axis=0
    )

    heads_here = heads_width // HD
    head_shape = (rows_here, heads_here, HD)
    flat_shape = (rows_here, heads_width)
    positions = here_ctx * rows_here + jnp.arange(rows_here, dtype=jnp.int32)
    cosine, sine_table = rotary_tables(positions)
    qkv = into(normed_one, qkv_parts)
    query_pre = qkv[:, :heads_width].reshape(head_shape)
    key_pre = qkv[:, heads_width : 2 * heads_width].reshape(head_shape)
    query = rotate(query_pre, cosine, sine_table).astype(BF).reshape(flat_shape)
    key = rotate(key_pre, cosine, sine_table).astype(BF).reshape(flat_shape)
    value = qkv[:, 2 * heads_width :].astype(BF)
    attended, kv = attention_forward(query, jnp.concatenate([key, value], axis=1), n_ctx)
    resid, scale_two, normed_two = second_norm(
        back(attended, out_parts).astype(BF), hidden_in, gain_two_here, n_tp
    )

    logits = mm_t(normed_two, router_w)
    route_onehot = (routes[:, :, None] == jnp.arange(experts, dtype=jnp.int32)).astype(F32)
    picked_logits = jnp.sum(route_onehot * logits[:, None, :], axis=-1)
    gate_pair = jax.nn.softmax(picked_logits, axis=-1)
    relative = (jnp.arange(experts, dtype=jnp.int32) + here_ctx) % experts
    names = (routes[:, :, None] == relative).astype(F32)
    mix_gates = jnp.sum(gate_pair[:, :, None] * names, axis=1)
    chosen = jnp.sum(names, axis=1)
    before = jnp.tril(jnp.ones((rows_here, rows_here), BF), -1)
    slot_of = mm(before, chosen.astype(BF)).astype(jnp.int32)
    slots = jnp.arange(CAP, dtype=jnp.int32)
    pick = (slot_of.T[:, None, :] == slots[None, :, None]) & (chosen.T[:, None, :] > 0)
    pick_low = pick.astype(BF)
    pick_flat = pick_low.reshape(experts * CAP, rows_here)

    def dispatch(slabs):
        return jnp.concatenate(
            [slabs[0]] + [shift_ctx(slabs[k], k) for k in range(1, experts)], axis=0
        )

    def give_back(values):
        slabs = values.reshape(experts, CAP, values.shape[-1])
        return [slabs[0]] + [shift_ctx(slabs[k], -k) for k in range(1, experts)]

    grad_rows = dispatch(mm(pick_flat, grad_full).astype(BF).reshape(experts, CAP, width))
    token_rows = dispatch(mm(pick_flat, normed_two).astype(BF).reshape(experts, CAP, width))
    gate_slots = jnp.sum(jnp.where(pick, mix_gates.T[:, None, :], 0.0), axis=-1)
    gate_rows = dispatch(gate_slots[:, :, None])

    gate_act = into(token_rows, gate_w)
    up_act = into(token_rows, up_w)
    sigma_act = jax.nn.sigmoid(gate_act)
    hidden_act = (gate_act * sigma_act * up_act).astype(BF)
    d_result = (gate_rows * grad_rows.astype(F32)).astype(BF)

    def grad_send(left, right):
        halves = split(left)
        if pair:
            away = t_mm(halves[1], right).astype(BF)
            return halves[0], right, away, swap_fsdp(away)
        return halves[0], right, None, None

    def grad_sum(mine, right, away, other):
        if pair:
            return (t_mm(mine, right) + other.astype(F32)).astype(BF)
        return lax.psum_scatter(t_mm(mine, right).astype(BF), "fsdp", scatter_dimension=0, tiled=True)

    def grad_spread(mine):
        cut = part // n_ctx
        out = jnp.zeros((experts, cut, mine.shape[1]), F32)
        for k in range(experts):
            piece = lax.dynamic_slice_in_dim(mine, ((here_ctx + k) % n_ctx) * cut, cut, 0)
            if k:
                piece = shift_ctx(piece, k)
            out = lax.dynamic_update_index_in_dim(
                out, piece.astype(F32), (here_ctx + n_ctx - k) % n_ctx, 0
            )
        return out

    down_sent = grad_send(d_result, hidden_act)
    if pair:
        hidden_act = after(hidden_act, down_sent[2])
    result = back(hidden_act, down_w)
    gate_dot = jnp.sum(result * grad_rows.astype(F32), axis=-1, keepdims=True)
    returned = give_back(result.astype(BF))
    returned_dot = give_back(gate_dot)
    moe_part = sum(
        mix_gates[:, k][:, None] * t_mm(pick_low[k], returned[k]) for k in range(experts)
    )
    moe_share = lax.psum_scatter(moe_part.astype(BF), "tp", scatter_dimension=1, tiled=True)
    block_out = (resid + moe_share.astype(F32)).astype(BF)

    d_hidden = into(d_result, down_w)
    d_gate_act = (d_hidden * up_act * sigma_act * (1.0 + gate_act * (1.0 - sigma_act))).astype(BF)
    d_up_act = (d_hidden * gate_act * sigma_act).astype(BF)
    d_rows = join(
        [mm_t(d_gate_act, wg) + mm_t(d_up_act, wu) for wg, wu in zip(gate_w, up_w)]
    )
    returned_grad = give_back(d_rows.astype(BF))
    gate_sent = grad_send(token_rows, d_gate_act)
    up_sent = grad_send(token_rows, d_up_act)
    d_normed_part = sum(t_mm(pick_low[k], returned_grad[k]) for k in range(experts))
    d_gate_slots = jnp.stack(
        [jnp.sum(jnp.where(pick[k], returned_dot[k], 0.0), axis=0) for k in range(experts)]
    )
    up_rows = [(0, 8 - experts), (0, 0)]
    d_gate_slots = jnp.pad(d_gate_slots, up_rows)

    if pair:
        d_normed_part = after(d_normed_part, gate_sent[2], up_sent[2])
    d_resid, d_attn, gain_two_part, d_logits = second_norm_back(
        d_normed_part.astype(BF),
        d_gate_slots,
        jnp.pad(gate_pair.T, [(0, 6), (0, 0)]),
        jnp.pad(jnp.transpose(route_onehot, (1, 2, 0)), [(0, 0)] + up_rows),
        jnp.pad(jnp.transpose(names, (1, 2, 0)), [(0, 0)] + up_rows),
        router_here,
        resid,
        scale_two,
        gain_two_here,
        out_grad,
        n_tp,
    )
    grad_router_part = mm(d_logits[:experts].astype(BF), normed_two)

    d_attended = into(d_attn, out_parts).astype(BF)
    d_query, kv_grad = attention_backward(query, kv, d_attended, n_ctx)
    grad_down = grad_spread(grad_sum(*down_sent))
    grad_gate = grad_spread(grad_sum(*gate_sent))
    grad_up = grad_spread(grad_sum(*up_sent))
    d_query_pre = rotate(d_query.reshape(head_shape), cosine, -sine_table)
    d_key_pre = rotate(kv_grad[:, :heads_width].reshape(head_shape), cosine, -sine_table)
    d_qkv = jnp.concatenate(
        [
            d_query_pre.astype(BF).reshape(flat_shape),
            d_key_pre.astype(BF).reshape(flat_shape),
            kv_grad[:, heads_width:].astype(BF),
        ],
        axis=1,
    )
    in_grad, gain_one_part = first_norm_back(
        back(d_qkv, qkv_parts).astype(BF), hidden_in, scale_one, gain_one_here, d_resid, n_tp
    )

    grad_qkv_part = t_mm(normed_one, d_qkv)
    grad_output_part = t_mm(d_attn, attended)
    grad_attn = lax.psum_scatter(
        jnp.concatenate([grad_qkv_part, grad_output_part], axis=1).astype(BF),
        ("fsdp", "ctx"),
        scatter_dimension=0,
        tiled=True,
    ).astype(F32)
    gains = jnp.stack([gain_one_part[0], gain_two_part[0]], axis=1)
    gains = lax.dynamic_update_slice_in_dim(
        jnp.zeros((width, 2), F32), gains, here_tp * width_tp, 0
    )
    small_part = jnp.concatenate([gains, grad_router_part.T / n_tp], axis=1)
    small_grad = lax.psum(
        lax.psum_scatter(small_part, ("fsdp", "ctx"), scatter_dimension=0, tiled=True), "tp"
    )
    return (
        block_out,
        in_grad,
        small_grad[:, 0],
        grad_attn[:, :heads_width],
        grad_attn[:, heads_width : 2 * heads_width],
        grad_attn[:, 2 * heads_width : 3 * heads_width],
        grad_attn[:, 3 * heads_width :],
        small_grad[:, 1],
        small_grad[:, 2:],
        grad_gate,
        grad_up,
        grad_down,
    )


def solution(mesh):
    rows = ("fsdp", "ctx")
    placed = (
        P(rows, "tp"),
        P(rows, "tp"),
        P("fsdp"),
        P("fsdp", "tp"),
        P("fsdp", "tp"),
        P("fsdp", "tp"),
        P("fsdp", "tp"),
        P("fsdp"),
        P("fsdp", None),
        P(None, "fsdp", "tp"),
        P(None, "fsdp", "tp"),
        P(None, "fsdp", "tp"),
        P(rows, None),
    )
    return jax.shard_map(
        shards,
        mesh=mesh,
        in_specs=placed,
        out_specs=(
            P(rows, "tp"),
            P(rows, "tp"),
            P(rows),
            P(rows, "tp"),
            P(rows, "tp"),
            P(rows, "tp"),
            P(rows, "tp"),
            P(rows),
            P(rows, None),
            P(None, rows, "tp"),
            P(None, rows, "tp"),
            P(None, rows, "tp"),
        ),
        check_vma=False,
    )
```

```python
from functools import partial
import math

import jax
import jax.numpy as jnp
from jax import lax
from jax.experimental import pallas as pl
from jax.experimental.pallas import tpu as pltpu
from jax.sharding import PartitionSpec as P

HD = 128
CAP = 160


EPS = 1e-05
THETA = 10000.0
NEG = -1e30
BF = jnp.bfloat16
F32 = jnp.float32


def mm(left, right):
    return jnp.dot(left, right, preferred_element_type=F32)


def mm_t(left, right):
    return lax.dot_general(left, right, (((1,), (1,)), ((), ())), preferred_element_type=F32)


def t_mm(left, right):
    return lax.dot_general(left, right, (((0,), (0,)), ((), ())), preferred_element_type=F32)


def rotary_tables(positions):
    half_size = HD // 2
    frequency = THETA ** (-(jnp.arange(half_size, dtype=F32) * 2.0 / HD))
    angles = positions.astype(F32)[:, None] * frequency[None, :]
    return (jnp.cos(angles)[:, None, :], jnp.sin(angles)[:, None, :])


def rotate(values, cosine, sine_table):
    half_size = values.shape[-1] // 2
    first_half = values[..., :half_size]
    second_half = values[..., half_size:]
    return jnp.concatenate(
        [
            first_half * cosine - second_half * sine_table,
            second_half * cosine + first_half * sine_table,
        ],
        axis=-1,
    )


MESH = pl.DeviceIdType.MESH
VM = pl.BlockSpec(memory_space=pltpu.VMEM)
DMA = pltpu.SemaphoreType.DMA


def peer(axis, n, k):
    return lax.rem(lax.axis_index(axis) + k, n)


def greet(groups):
    barrier = pltpu.get_barrier_semaphore()
    for axis, n in groups:
        for k in range(1, n):
            pl.semaphore_signal(
                barrier, inc=1, device_id={axis: peer(axis, n, k)}, device_id_type=MESH
            )
    pl.semaphore_wait(barrier, sum(n - 1 for _, n in groups))


def remote(source, target, sems, i, to):
    copy = pltpu.make_async_remote_copy(
        src_ref=source,
        dst_ref=target,
        send_sem=sems[0].at[i],
        recv_sem=sems[1].at[i],
        device_id=to,
        device_id_type=MESH,
    )
    copy.start()
    return copy


def send(source, target, axis, n, k, sems):
    return remote(source, target, sems, k - 1, {axis: peer(axis, n, k)})


def columns(n, size):
    return pl.ds(pl.multiple_of(n * size, 128), size)


def stretch(n, size):
    return pl.ds(pl.multiple_of(n * size, 16), size)


def gather_columns(own, full, axis, n, sems):
    size = own.shape[1]
    place = full.at[:, columns(lax.axis_index(axis), size)]
    copies = [send(own, place, axis, n, k, sems) for k in range(1, n)]
    place[...] = own[...]
    return copies


def scatter_columns(part, slots, axis, n, sems):
    size = slots.shape[2]
    return [
        send(part.at[:, columns(peer(axis, n, k), size)], slots.at[k - 1], axis, n, k, sems)
        for k in range(1, n)
    ]


def finish(copies):
    for copy in copies:
        copy.wait()


def quad():
    here = lax.axis_index("ctx")
    return here, here + 1 - 2 * lax.rem(here, 2), lax.rem(here + 2, 4)


def gather_square(own, full, sems, between):
    rows = own.shape[0]
    here, beside, across = quad()
    place = full.at[stretch(here, rows), :]
    first = remote(own, place, sems, 0, {"ctx": across})
    second = remote(own, place, sems, 1, {"ctx": beside})
    place[...] = own[...]
    between()
    first.wait()
    come = full.at[stretch(across, rows), :]
    third = remote(come, come, sems, 2, {"ctx": beside})
    second.wait()
    third.wait()


def row_sums(values):
    ones = jnp.ones((8, values.shape[1]), F32)
    return lax.dot_general(
        ones,
        values,
        (((1,), (1,)), ((), ())),
        precision=lax.Precision.HIGHEST,
        preferred_element_type=F32,
    )


def as_column(rows, weight):
    return lax.dot_general(
        rows,
        weight,
        (((0,), (0,)), ((), ())),
        precision=lax.Precision.HIGHEST,
        preferred_element_type=F32,
    )


def eighth():
    return jnp.full((8, 128), 0.125, F32)


def total_over(sums, mine, slots, axis, n, sems):
    mine[...] = sums
    copies = [send(mine, slots.at[k - 1], axis, n, k, sems) for k in range(1, n)]
    finish(copies)
    total = sums
    for k in range(1, n):
        total = total + slots[k - 1]
    return total


def call(kernel, out_shape, inputs, scratch, collective, name):
    return pl.pallas_call(
        kernel,
        out_shape=out_shape,
        in_specs=[VM] * len(inputs),
        out_specs=jax.tree.map(lambda _: VM, out_shape),
        scratch_shapes=scratch,
        compiler_params=pltpu.CompilerParams(collective_id=collective, has_side_effects=True),
        cost_estimate=pl.CostEstimate(flops=0, bytes_accessed=0, transcendentals=0),
        name=name,
    )(*inputs)


def shape(dims, dtype):
    return jax.ShapeDtypeStruct(dims, dtype)


def pair_of_sems(n):
    return [DMA((n,)), DMA((n,))]


def gather_tp(value, n_tp):
    rows, size = value.shape

    def kernel(own, full, *sems):
        greet([("tp", n_tp)])
        finish(gather_columns(own, full, "tp", n_tp, sems))

    return call(
        kernel, shape((rows, size * n_tp), value.dtype), (value,), pair_of_sems(n_tp), 1, "gather_tp"
    )


def first_norm(full, grad, gain, quarter, n_tp, n_ctx):
    rows, width = full.shape
    with_quarter = quarter is not None

    def kernel(*refs):
        hid, grd, gn = refs[:3]
        refs = refs[3:]
        if with_quarter:
            qrt, out, scale, grd_full, qrt_full = refs[:5]
            sems = refs[5:]
            greet([("tp", n_tp), ("ctx", n_ctx)])
        else:
            out, scale, grd_full = refs[:3]
            sems = refs[3:]
            greet([("tp", n_tp)])
        grads = gather_columns(grd, grd_full, "tp", n_tp, sems[0:2])

        def norm():
            values = hid[...].astype(F32)
            mean = jnp.sum(values * values, axis=-1, keepdims=True) * (1.0 / width)
            factor = lax.rsqrt(mean + EPS)
            scale[...] = jnp.broadcast_to(factor, scale.shape)
            out[...] = (values * factor * gn[0:1, :]).astype(BF)

        if with_quarter:
            gather_square(qrt, qrt_full, sems[2:4], norm)
        else:
            norm()
        finish(grads)

    outs = [shape((rows, width), BF), shape((rows, 128), F32), shape((rows, width), BF)]
    inputs = [full, grad, gain]
    if with_quarter:
        outs.append(shape((quarter.shape[0] * n_ctx, quarter.shape[1]), BF))
        inputs.append(quarter)
    return call(
        kernel, tuple(outs), inputs, pair_of_sems(n_tp) + pair_of_sems(3), 7, "first_norm"
    )


def softmax_rows(query, key, first_row):
    scores = mm_t(query, key) * (1.0 / math.sqrt(HD))
    rows = first_row + lax.broadcasted_iota(jnp.int32, scores.shape, 0)
    cols = lax.broadcasted_iota(jnp.int32, scores.shape, 1)
    scores = jnp.where(cols <= rows, scores, NEG)
    top = jnp.max(scores, axis=-1, keepdims=True)
    weights = jnp.exp(scores - top)
    return weights / jnp.sum(weights, axis=-1, keepdims=True)


def attention_forward(query, kv, n_ctx):
    rows, width = query.shape
    heads = width // HD

    def kernel(qry, own, out, full, *sems):
        greet([("ctx", n_ctx)])
        here = lax.axis_index("ctx")
        gather_square(own, full, sems, lambda: None)

        @pl.loop(0, heads)
        def _(h):
            probs = softmax_rows(qry[:, columns(h, HD)], full[:, columns(h, HD)], here * rows)
            out[:, columns(h, HD)] = mm(
                probs.astype(BF), full[:, columns(h + heads, HD)]
            ).astype(BF)

    return call(
        kernel,
        (shape((rows, width), BF), shape((rows * n_ctx, 2 * width), BF)),
        (query, kv),
        pair_of_sems(3),
        2,
        "attention_forward",
    )


def second_norm(part, hidden, gain, slabs, n_tp, n_ctx):
    rows, size = hidden.shape
    width = size * n_tp

    def kernel(prt, hid, gn, slb, resid, scale, out, rowsout, slots, mine, sums, low, *sems):
        greet([("tp", n_tp), ("ctx", n_ctx)])
        here = lax.axis_index("tp")
        copies = scatter_columns(prt, slots, "tp", n_tp, sems[0:2])
        moved = [
            send(
                slb.at[pl.ds(k * CAP, CAP)], rowsout.at[pl.ds(k * CAP, CAP)],
                "ctx", n_ctx, k, sems[6:8],
            )
            for k in range(1, n_ctx)
        ]
        rowsout[0:CAP] = slb[0:CAP]
        total = prt[:, columns(here, size)].astype(F32)
        finish(copies)
        for k in range(1, n_tp):
            total = total + slots[k - 1].astype(F32)
        total = hid[...].astype(F32) + total
        resid[...] = total
        square = total_over(row_sums(total * total), mine, sums, "tp", n_tp, sems[2:4])
        factor = lax.rsqrt(as_column(square, eighth()) * (1.0 / width) + EPS)
        scale[...] = factor
        low[...] = (resid[...] * factor[:, 0:1] * gn[0:1, :]).astype(BF)
        finish(gather_columns(low, out, "tp", n_tp, sems[4:6]))
        finish(moved)

    return call(
        kernel,
        (
            shape((rows, size), F32),
            shape((rows, 128), F32),
            shape((rows, width), BF),
            shape(slabs.shape, BF),
        ),
        (part, hidden, gain, slabs),
        [
            pltpu.VMEM((n_tp - 1, rows, size), BF),
            pltpu.VMEM((8, rows), F32),
            pltpu.VMEM((n_tp - 1, 8, rows), F32),
            pltpu.VMEM((rows, size), BF),
        ]
        + pair_of_sems(n_tp) * 3
        + pair_of_sems(n_ctx),
        3,
        "second_norm",
    )


def dispatch_rows(normed, picks, router, onehot, names, n_ctx):
    rows, width = normed.shape
    experts = n_ctx

    def kernel(
        nrm, pck, rtr, one, nms, tokens, slot_gates, gates, mix, slabs, own_gates, *sems
    ):
        greet([("ctx", n_ctx)])
        copies = []
        for k in (2, 3, 1, 0):
            slab = mm(pck[k * CAP : (k + 1) * CAP], nrm[...]).astype(BF)
            if k == 0:
                tokens[0:CAP] = slab
            else:
                slabs[k - 1] = slab
                copies.append(
                    send(
                        slabs.at[k - 1], tokens.at[pl.ds(k * CAP, CAP)],
                        "ctx", n_ctx, k, sems[0:2],
                    )
                )
        logits = mm_t(rtr[...].astype(BF), nrm[...])
        named = [jnp.sum(one[j] * logits, axis=0, keepdims=True) for j in range(2)]
        top = jnp.maximum(named[0], named[1])
        powers = [jnp.exp(value - top) for value in named]
        both = powers[0] + powers[1]
        gate = [value / both for value in powers]
        mixed = gate[0] * nms[0] + gate[1] * nms[1]
        mix[...] = mixed
        order = lax.broadcasted_iota(jnp.int32, (8, rows), 0)
        gates[...] = jnp.where(order == 0, gate[0], jnp.where(order == 1, gate[1], 0.0))
        own_gates[...] = jnp.zeros(own_gates.shape, F32)
        for k in range(experts):
            own_gates[k, :, 0:CAP] = lax.dot_general(
                jnp.broadcast_to(mixed[k : k + 1], (8, rows)),
                pck[k * CAP : (k + 1) * CAP].astype(F32),
                (((1,), (1,)), ((), ())),
                precision=lax.Precision.HIGHEST,
                preferred_element_type=F32,
            )
        slot_gates[0] = own_gates[0]
        for k in range(1, n_ctx):
            copies.append(
                send(own_gates.at[k], slot_gates.at[k], "ctx", n_ctx, k, sems[2:4])
            )
        finish(copies)

    return call(
        kernel,
        (
            shape((experts * CAP, width), BF),
            shape((experts, 8, rows), F32),
            shape((8, rows), F32),
            shape((8, rows), F32),
        ),
        (normed, picks, router, onehot, names),
        [pltpu.VMEM((n_ctx - 1, CAP, width), BF), pltpu.VMEM((experts, 8, rows), F32)]
        + pair_of_sems(n_ctx) * 2,
        8,
        "dispatch_rows",
    )


def second_norm_back(
    d_rows, dots, picks, gates, onehot, names, router, resid, scale, gain, grad, n_tp, n_ctx
):
    rows, size = resid.shape
    width = size * n_tp
    experts = n_ctx

    def kernel(
        drw, dts, pck, gts, one, nms, rtr, rsd, scl, gn, grd,
        d_resid, d_attn, d_gain, d_logits,
        back, back_dots, part, slots, mine, sums, mine_two, sums_two, low, *sems
    ):
        greet([("tp", n_tp), ("ctx", n_ctx)])
        here = lax.axis_index("tp")
        small = []
        large = []
        for k in range(1, n_ctx):
            small.append(
                send(dts.at[k], back_dots.at[k - 1], "ctx", n_ctx, n_ctx - k, sems[0:2])
            )
        for k in range(1, n_ctx):
            large.append(
                send(
                    drw.at[pl.ds(k * CAP, CAP)], back.at[k - 1],
                    "ctx", n_ctx, n_ctx - k, sems[2:4],
                )
            )
        finish(small)
        order = lax.broadcasted_iota(jnp.int32, (8, rows), 0)
        own = jnp.zeros((8, rows), F32)
        for k in range(experts):
            by_slot = dts[0] if k == 0 else back_dots[k - 1]
            by_row = lax.dot_general(
                by_slot[:, 0:CAP],
                pck[k * CAP : (k + 1) * CAP].astype(F32),
                (((1,), (0,)), ((), ())),
                precision=lax.Precision.HIGHEST,
                preferred_element_type=F32,
            )
            own = own + jnp.where(order == k, by_row, 0.0)
        gate_grad = total_over(own, mine, sums, "tp", n_tp, sems[4:6])
        both = [jnp.sum(nms[j] * gate_grad, axis=0, keepdims=True) for j in range(2)]
        gate = [gts[j : j + 1, :] for j in range(2)]
        mean = gate[0] * both[0] + gate[1] * both[1]
        logits = sum(gate[j] * (both[j] - mean) * one[j] for j in range(2))
        d_logits[...] = logits
        finish(large)
        copies = []
        for step in range(1, n_tp + 1):
            at = columns(peer("tp", n_tp, step), size)
            block = t_mm(pck[0:CAP], drw[0:CAP, at])
            for k in range(1, experts):
                block = block + t_mm(pck[k * CAP : (k + 1) * CAP], back[k - 1, :, at])
            if step < n_tp:
                part[step - 1] = block.astype(BF)
                copies.append(
                    send(part.at[step - 1], slots.at[step - 1], "tp", n_tp, step, sems[6:8])
                )
            else:
                total = block
        total = total + lax.dot_general(
            logits.astype(BF),
            rtr[...].astype(BF),
            (((0,), (0,)), ((), ())),
            preferred_element_type=F32,
        )
        finish(copies)
        for k in range(1, n_tp):
            total = total + slots[k - 1].astype(F32)
        factor = scl[:, 0:1]
        unit = rsd[...] * factor
        d_gain[...] = jnp.broadcast_to(jnp.sum(total * unit, axis=0, keepdims=True), d_gain.shape)
        gained = total * gn[0:1, :]
        d_resid[...] = gained
        dot = total_over(row_sums(unit * gained), mine_two, sums_two, "tp", n_tp, sems[8:10])
        dot = as_column(dot, eighth())[:, 0:1] * (1.0 / width)
        result = grd[...].astype(F32) + factor * (d_resid[...] - rsd[...] * factor * dot)
        d_resid[...] = result
        low[...] = result.astype(BF)
        finish(gather_columns(low, d_attn, "tp", n_tp, sems[10:12]))

    return call(
        kernel,
        (
            shape((rows, size), F32),
            shape((rows, width), BF),
            shape((8, size), F32),
            shape((8, rows), F32),
        ),
        (d_rows, dots, picks, gates, onehot, names, router, resid, scale, gain, grad),
        [
            pltpu.VMEM((n_ctx - 1, CAP, width), BF),
            pltpu.VMEM((n_ctx - 1, 8, rows), F32),
            pltpu.VMEM((n_tp - 1, rows, size), BF),
            pltpu.VMEM((n_tp - 1, rows, size), BF),
            pltpu.VMEM((8, rows), F32),
            pltpu.VMEM((n_tp - 1, 8, rows), F32),
            pltpu.VMEM((8, rows), F32),
            pltpu.VMEM((n_tp - 1, 8, rows), F32),
            pltpu.VMEM((rows, size), BF),
        ]
        + pair_of_sems(n_ctx) * 2
        + pair_of_sems(n_tp) * 4,
        4,
        "second_norm_back",
    )


def attention_backward(query, kv, dout, n_ctx):
    rows, width = query.shape
    heads = width // HD
    scale = 1.0 / math.sqrt(HD)

    def kernel(qry, full, dot, dq, dkv, low, slots, last, both, *sems):
        greet([("ctx", n_ctx)])
        here, beside, across = quad()
        beyond = lax.rem(beside + 2, 4)

        @pl.loop(0, heads)
        def _(h):
            at, at_v = columns(h, HD), columns(h + heads, HD)
            probs = softmax_rows(qry[:, at], full[:, at], here * rows)
            d_probs = mm_t(dot[:, at], full[:, at_v])
            delta = jnp.sum(probs * d_probs, axis=-1, keepdims=True)
            d_scores = (probs * (d_probs - delta)).astype(BF)
            dq[:, at] = mm(d_scores, full[:, at]) * scale
            low[:, at] = (t_mm(d_scores, qry[:, at]) * scale).astype(BF)
            low[:, at_v] = t_mm(probs.astype(BF), dot[:, at]).astype(BF)

        first = remote(low.at[stretch(beyond, rows), :], slots.at[0], sems, 0, {"ctx": beside})
        second = remote(low.at[stretch(beside, rows), :], slots.at[1], sems, 1, {"ctx": beside})
        first.wait()
        both[...] = (
            low[stretch(across, rows), :].astype(F32) + slots[0].astype(F32)
        ).astype(BF)
        third = remote(both, last, sems, 2, {"ctx": across})
        second.wait()
        dkv[...] = low[stretch(here, rows), :].astype(F32) + slots[1].astype(F32)
        third.wait()
        dkv[...] = dkv[...] + last[...].astype(F32)

    return call(
        kernel,
        (shape((rows, width), F32), shape((rows, 2 * width), F32)),
        (query, kv, dout),
        [
            pltpu.VMEM((rows * n_ctx, 2 * width), BF),
            pltpu.VMEM((2, rows, 2 * width), BF),
            pltpu.VMEM((rows, 2 * width), BF),
            pltpu.VMEM((rows, 2 * width), BF),
        ]
        + pair_of_sems(3),
        5,
        "attention_backward",
    )


def first_norm_back(part, hidden, scale, gain, d_resid, result, n_tp, n_ctx):
    rows, size = hidden.shape
    width = size * n_tp

    def kernel(prt, hid, scl, gn, dr, rst, out, d_gain, back, slots, mine, sums, *sems):
        greet([("tp", n_tp), ("ctx", n_ctx)])
        here = lax.axis_index("tp")
        copies = scatter_columns(prt, slots, "tp", n_tp, sems[0:2])
        moved = [
            send(
                rst.at[pl.ds(k * CAP, CAP)], back.at[pl.ds(k * CAP, CAP)],
                "ctx", n_ctx, n_ctx - k, sems[4:6],
            )
            for k in range(1, n_ctx)
        ]
        back[0:CAP] = rst[0:CAP]
        total = prt[:, columns(here, size)].astype(F32)
        finish(copies)
        for k in range(1, n_tp):
            total = total + slots[k - 1].astype(F32)
        factor = scl[:, 0:1]
        unit = hid[...].astype(F32) * factor
        d_gain[...] = jnp.broadcast_to(jnp.sum(total * unit, axis=0, keepdims=True), d_gain.shape)
        gained = total * gn[0:1, :]
        out[...] = gained
        dot = total_over(row_sums(unit * gained), mine, sums, "tp", n_tp, sems[2:4])
        dot = as_column(dot, eighth())[:, 0:1] * (1.0 / width)
        unit = hid[...].astype(F32) * factor
        out[...] = dr[...] + factor * (out[...] - unit * dot)
        finish(moved)

    return call(
        kernel,
        (shape((rows, size), F32), shape((8, size), F32), shape(result.shape, BF)),
        (part, hidden, scale, gain, d_resid, result),
        [
            pltpu.VMEM((n_tp - 1, rows, size), BF),
            pltpu.VMEM((8, rows), F32),
            pltpu.VMEM((n_tp - 1, 8, rows), F32),
        ]
        + pair_of_sems(n_tp) * 2
        + pair_of_sems(n_ctx),
        6,
        "first_norm_back",
    )


def experts_out(back, picks, mix, resid, n_tp):
    rows, size = resid.shape
    experts = back.shape[0] // CAP

    def kernel(bck, pck, mx, rsd, out, part, slots, gate, *sems):
        greet([("tp", n_tp)])
        order = lax.broadcasted_iota(jnp.int32, (8, 128), 0)
        for k in range(experts):
            gate[k] = as_column(mx[...], jnp.where(order == k, 1.0, 0.0))
        copies = []
        for step in range(1, n_tp + 1):
            at = columns(peer("tp", n_tp, step), size)
            block = jnp.zeros((rows, size), F32)
            for k in range(experts):
                block = block + gate[k][:, 0:1] * t_mm(
                    pck[k * CAP : (k + 1) * CAP], bck[k * CAP : (k + 1) * CAP, at]
                )
            if step < n_tp:
                part[step - 1] = block.astype(BF)
                copies.append(
                    send(part.at[step - 1], slots.at[step - 1], "tp", n_tp, step, sems)
                )
            else:
                total = block
        finish(copies)
        for k in range(1, n_tp):
            total = total + slots[k - 1].astype(F32)
        out[...] = (rsd[...] + total).astype(BF)

    return call(
        kernel,
        shape((rows, size), BF),
        (back, picks, mix, resid),
        [
            pltpu.VMEM((n_tp - 1, rows, size), BF),
            pltpu.VMEM((n_tp - 1, rows, size), BF),
            pltpu.VMEM((experts, rows, 128), F32),
        ]
        + pair_of_sems(n_tp),
        9,
        "experts_out",
    )


def weight_grads(part, n_ctx):
    rows, size = part.shape[2:]

    def kernel(prt, out, near, two, far, one, last, *sems):
        greet([("fsdp", 2), ("ctx", n_ctx)])
        here, beside, across = quad()
        beyond = lax.rem(beside + 2, 4)
        mine = lax.axis_index("fsdp")
        other = 1 - mine
        steps = []
        for i, (half, column) in enumerate(
            [(other, beyond), (mine, beyond), (other, beside), (mine, beside)]
        ):
            steps.append(
                remote(prt.at[half, column], near.at[i], sems[0:2], i, {"ctx": beside})
            )
        cross = []
        for i, half in enumerate((other, mine)):
            steps[i].wait()
            two[i] = (prt[half, across].astype(F32) + near[i].astype(F32)).astype(BF)
            cross.append(remote(two.at[i], far.at[i], sems[2:4], i, {"ctx": across}))
        steps[2].wait()
        cross[0].wait()
        one[...] = (
            prt[other, here].astype(F32) + near[2].astype(F32) + far[0].astype(F32)
        ).astype(BF)
        final = remote(one, last, sems[4:6], 0, {"fsdp": other})
        steps[3].wait()
        cross[1].wait()
        out[...] = prt[mine, here].astype(F32) + near[3].astype(F32) + far[1].astype(F32)
        final.wait()
        out[...] = out[...] + last[...].astype(F32)

    return call(
        kernel,
        shape((rows, size), F32),
        (part,),
        [
            pltpu.VMEM((4, rows, size), BF),
            pltpu.VMEM((2, rows, size), BF),
            pltpu.VMEM((2, rows, size), BF),
            pltpu.VMEM((rows, size), BF),
            pltpu.VMEM((rows, size), BF),
        ]
        + pair_of_sems(4)
        + pair_of_sems(2)
        + pair_of_sems(1),
        10,
        "weight_grads",
    )


def small_grads(part, n_tp, n_ctx):
    size = part.shape[1]
    width = size * n_tp
    places = 2 * n_ctx
    cut = width // places

    def kernel(prt, out, full, slots, *sems):
        barrier = pltpu.get_barrier_semaphore()
        place = lax.axis_index("fsdp") * n_ctx + lax.axis_index("ctx")
        others = []
        for i in range(1, places):
            to = lax.rem(place + i, places)
            others.append((to, {"fsdp": to // n_ctx, "ctx": lax.rem(to, n_ctx)}))
        ahead = [{"tp": peer("tp", n_tp, k)} for k in range(1, n_tp)]
        for device in ahead + [device for _, device in others]:
            pl.semaphore_signal(barrier, inc=1, device_id=device, device_id_type=MESH)
        pl.semaphore_wait(barrier, n_tp - 1 + places - 1)
        finish(gather_columns(prt, full, "tp", n_tp, sems[0:2]))
        copies = [
            remote(full.at[:, columns(to, cut)], slots.at[i], sems[2:4], i, device)
            for i, (to, device) in enumerate(others)
        ]
        total = full[:, columns(place, cut)]
        finish(copies)
        for i in range(places - 1):
            total = total + slots[i]
        out[...] = total

    return call(
        kernel,
        shape((8, cut), F32),
        (part,),
        [pltpu.VMEM((8, width), F32), pltpu.VMEM((places - 1, 8, cut), F32)]
        + pair_of_sems(n_tp)
        + pair_of_sems(places),
        11,
        "small_grads",
    )


def after(value, *needed):
    return lax.optimization_barrier((value, *needed))[0]


def shards(
    hidden_in,
    out_grad,
    attn_gain,
    w_query,
    w_key,
    w_value,
    w_output,
    ffn_gain,
    w_router,
    w_gate,
    w_up,
    w_down,
    routes,
):
    rows_here, width_tp = hidden_in.shape
    here_tp = lax.axis_index("tp")
    here_ctx = lax.axis_index("ctx")
    here_fsdp = lax.axis_index("fsdp")
    n_fsdp = lax.axis_size("fsdp")
    n_ctx = lax.axis_size("ctx")
    n_tp = lax.axis_size("tp")
    experts = w_gate.shape[0]
    assert experts == n_ctx == 4
    width = width_tp * n_tp
    part = width // n_fsdp
    pair = n_fsdp == 2
    heads_width = w_query.shape[1]

    def shift_ctx(value, k):
        return lax.ppermute(value, "ctx", [(i, (i + k) % n_ctx) for i in range(n_ctx)])

    def swap_fsdp(value):
        return lax.ppermute(value, "fsdp", [(0, 1), (1, 0)])

    def other_parts(weight):
        if pair:
            return [weight, swap_fsdp(weight)]
        return [lax.all_gather(weight, "fsdp", axis=0, tiled=True)]

    def split(values):
        if pair:
            return [
                lax.dynamic_slice_in_dim(values, here_fsdp * part, part, 1),
                lax.dynamic_slice_in_dim(values, (1 - here_fsdp) * part, part, 1),
            ]
        return [values]

    def join(pieces):
        if pair:
            first = here_fsdp == 0
            return jnp.concatenate(
                [jnp.where(first, pieces[0], pieces[1]), jnp.where(first, pieces[1], pieces[0])],
                axis=1,
            )
        return pieces[0]

    def into(values, weights):
        return sum(mm(x, w) for x, w in zip(split(values), weights))

    def back(values, weights):
        return join([mm_t(values, w) for w in weights])

    def my_features(values):
        return lax.dynamic_slice_in_dim(values, here_tp * width_tp, width_tp, values.ndim - 1)

    attn_w = jnp.concatenate([w_query, w_key, w_value, w_output], axis=1)
    small = jnp.concatenate(
        [attn_gain[None], ffn_gain[None], w_router.T, jnp.zeros((2, part), BF)], axis=0
    )
    if pair:
        quarter = part // n_ctx
        own_quarter = lax.dynamic_slice_in_dim(attn_w, here_ctx * quarter, quarter, 0)
        other_quarter = swap_fsdp(own_quarter)
        other_small = swap_fsdp(small)
        small_full = join([small, other_small]).astype(F32)
    else:
        other_quarter = None
        small_full = lax.all_gather(small, "fsdp", axis=1, tiled=True).astype(F32)
    gate_w = other_parts(lax.dynamic_index_in_dim(w_gate, here_ctx, 0, False))
    up_w = other_parts(lax.dynamic_index_in_dim(w_up, here_ctx, 0, False))
    down_w = other_parts(lax.dynamic_index_in_dim(w_down, here_ctx, 0, False))
    small_here = my_features(small_full)
    gain_one_here = jnp.broadcast_to(small_here[0:1], small_here.shape)
    gain_two_here = jnp.broadcast_to(small_here[1:2], small_here.shape)
    nothing = [(0, 8 - experts), (0, 0)]
    router_full = jnp.pad(small_full[2 : 2 + experts], nothing)
    router_here = jnp.pad(small_here[2 : 2 + experts], nothing)

    relative = (jnp.arange(experts, dtype=jnp.int32) + here_ctx) % experts
    numbers = jnp.arange(8, dtype=jnp.int32)
    onehot = (routes.T[:, None, :] == numbers[None, :, None]).astype(F32)
    named = (routes.T[:, None, :] == relative[None, :, None]).astype(F32)
    names = jnp.pad(named, [(0, 0)] + nothing)
    chosen = jnp.sum(named, axis=0)
    earlier = jnp.triu(jnp.ones((rows_here, rows_here), BF), 1)
    slot_of = mm(chosen.astype(BF), earlier).astype(jnp.int32)
    slots = jnp.arange(CAP, dtype=jnp.int32)
    picks = (slot_of[:, None, :] == slots[None, :, None]) & (chosen[:, None, :] > 0)
    picks = picks.astype(BF).reshape(experts * CAP, rows_here)

    inputs_full = gather_tp(hidden_in, n_tp)
    gathered = first_norm(inputs_full, out_grad, small_full, other_quarter, n_tp, n_ctx)
    normed_one, scale_one, grad_full = gathered[:3]
    if pair:
        attn_parts = [attn_w, gathered[3]]
    else:
        attn_parts = [lax.all_gather(attn_w, "fsdp", axis=0, tiled=True)]
    qkv_parts = [w[:, : 3 * heads_width] for w in attn_parts]
    out_parts = [w[:, 3 * heads_width :] for w in attn_parts]
    heads_here = heads_width // HD
    head_shape = (rows_here, heads_here, HD)
    flat_shape = (rows_here, heads_width)
    positions = here_ctx * rows_here + jnp.arange(rows_here, dtype=jnp.int32)
    cosine, sine_table = rotary_tables(positions)
    qkv = into(normed_one, qkv_parts)
    query_pre = qkv[:, :heads_width].reshape(head_shape)
    key_pre = qkv[:, heads_width : 2 * heads_width].reshape(head_shape)
    query = rotate(query_pre, cosine, sine_table).astype(BF).reshape(flat_shape)
    key = rotate(key_pre, cosine, sine_table).astype(BF).reshape(flat_shape)
    value = qkv[:, 2 * heads_width :].astype(BF)
    attended, kv = attention_forward(query, jnp.concatenate([key, value], axis=1), n_ctx)
    resid, scale_two, normed_two, grad_rows = second_norm(
        back(attended, out_parts).astype(BF),
        hidden_in,
        gain_two_here,
        mm(picks, grad_full).astype(BF),
        n_tp,
        n_ctx,
    )
    token_rows, slot_gates, gates, mix = dispatch_rows(
        normed_two, picks, router_full, onehot, names, n_ctx
    )
    gate_rows = slot_gates[:, 0, :CAP].reshape(experts * CAP, 1)

    gate_act = into(token_rows, gate_w)
    up_act = into(token_rows, up_w)
    sigma_act = jax.nn.sigmoid(gate_act)
    hidden_act = (gate_act * sigma_act * up_act).astype(BF)
    d_result = (gate_rows * grad_rows.astype(F32)).astype(BF)

    def grad_send(left, right):
        halves = split(left)
        if pair:
            away = t_mm(halves[1], right).astype(BF)
            return halves[0], right, away, swap_fsdp(away)
        return halves[0], right, None, None

    def grad_sum(mine, right, away, other):
        if pair:
            return (t_mm(mine, right) + other.astype(F32)).astype(BF)
        return lax.psum_scatter(
            t_mm(mine, right).astype(BF), "fsdp", scatter_dimension=0, tiled=True
        )

    def grad_spread(mine):
        cut = part // n_ctx
        out = jnp.zeros((experts, cut, mine.shape[1]), F32)
        for k in range(experts):
            piece = lax.dynamic_slice_in_dim(mine, ((here_ctx + k) % n_ctx) * cut, cut, 0)
            if k:
                piece = shift_ctx(piece, k)
            out = lax.dynamic_update_index_in_dim(
                out, piece.astype(F32), (here_ctx + n_ctx - k) % n_ctx, 0
            )
        return out

    down_sent = grad_send(d_result, hidden_act)
    if pair:
        hidden_act = after(hidden_act, down_sent[2])
    result = back(hidden_act, down_w)
    gate_dot = jnp.sum(result * grad_rows.astype(F32), axis=-1).reshape(experts, CAP)
    gate_dot = jnp.broadcast_to(
        jnp.pad(gate_dot, [(0, 0), (0, rows_here - CAP)])[:, None, :], (experts, 8, rows_here)
    )
    d_hidden = into(d_result, down_w)
    d_gate_act = (d_hidden * up_act * sigma_act * (1.0 + gate_act * (1.0 - sigma_act))).astype(BF)
    d_up_act = (d_hidden * gate_act * sigma_act).astype(BF)
    gate_sent = grad_send(token_rows, d_gate_act)
    up_sent = grad_send(token_rows, d_up_act)
    d_rows = join(
        [mm_t(d_gate_act, wg) + mm_t(d_up_act, wu) for wg, wu in zip(gate_w, up_w)]
    ).astype(BF)
    if pair:
        d_rows = after(d_rows, gate_sent[2], up_sent[2])

    d_resid, d_attn, gain_two_part, d_logits = second_norm_back(
        d_rows,
        gate_dot,
        picks,
        gates,
        onehot,
        names,
        router_here,
        resid,
        scale_two,
        gain_two_here,
        out_grad,
        n_tp,
        n_ctx,
    )
    if pair:
        d_attn = after(d_attn, down_sent[3])
    grad_down = grad_spread(grad_sum(*down_sent))

    d_attended = into(d_attn, out_parts).astype(BF)
    d_query, kv_grad = attention_backward(query, kv, d_attended, n_ctx)
    if pair:
        kv_grad = after(kv_grad, gate_sent[3], grad_down)
    grad_gate = grad_spread(grad_sum(*gate_sent))
    d_query_pre = rotate(d_query.reshape(head_shape), cosine, -sine_table)
    d_key_pre = rotate(kv_grad[:, :heads_width].reshape(head_shape), cosine, -sine_table)
    d_qkv = jnp.concatenate(
        [
            d_query_pre.astype(BF).reshape(flat_shape),
            d_key_pre.astype(BF).reshape(flat_shape),
            kv_grad[:, heads_width:].astype(BF),
        ],
        axis=1,
    )
    in_grad, gain_one_part, returned = first_norm_back(
        back(d_qkv, qkv_parts).astype(BF),
        hidden_in,
        scale_one,
        gain_one_here,
        d_resid,
        result.astype(BF),
        n_tp,
        n_ctx,
    )
    if pair:
        in_grad, up_sent_there, grad_gate = lax.optimization_barrier(
            (in_grad, up_sent[3], grad_gate)
        )
        up_sent = (*up_sent[:3], up_sent_there)
    grad_up = grad_spread(grad_sum(*up_sent))
    block_out = experts_out(returned, picks, mix, resid, n_tp)

    grad_attn = jnp.concatenate([t_mm(normed_one, d_qkv), t_mm(d_attn, attended)], axis=1).astype(
        BF
    )
    small_part = jnp.concatenate(
        [
            gain_one_part[:1],
            gain_two_part[:1],
            mm(d_logits[:experts].astype(BF), my_features(normed_two)),
            jnp.zeros((6 - experts, width_tp), F32),
        ],
        axis=0,
    )
    if pair:
        grad_attn = weight_grads(grad_attn.reshape(n_fsdp, n_ctx, quarter, -1), n_ctx)
        small_grad = small_grads(small_part, n_tp, n_ctx)
    else:
        scatter = partial(
            lax.psum_scatter, axis_name=("fsdp", "ctx"), scatter_dimension=0, tiled=True
        )
        grad_attn = scatter(grad_attn).astype(F32)
        small_grad = lax.all_gather(small_part, "tp", axis=1, tiled=True)
        small_grad = scatter(small_grad.T).T
    return (
        block_out,
        in_grad,
        small_grad[0],
        grad_attn[:, :heads_width],
        grad_attn[:, heads_width : 2 * heads_width],
        grad_attn[:, 2 * heads_width : 3 * heads_width],
        grad_attn[:, 3 * heads_width :],
        small_grad[1],
        small_grad[2 : 2 + experts].T,
        grad_gate,
        grad_up,
        grad_down,
    )


def solution(mesh):
    rows = ("fsdp", "ctx")
    placed = (
        P(rows, "tp"),
        P(rows, "tp"),
        P("fsdp"),
        P("fsdp", "tp"),
        P("fsdp", "tp"),
        P("fsdp", "tp"),
        P("fsdp", "tp"),
        P("fsdp"),
        P("fsdp", None),
        P(None, "fsdp", "tp"),
        P(None, "fsdp", "tp"),
        P(None, "fsdp", "tp"),
        P(rows, None),
    )
    return jax.shard_map(
        shards,
        mesh=mesh,
        in_specs=placed,
        out_specs=(
            P(rows, "tp"),
            P(rows, "tp"),
            P(rows),
            P(rows, "tp"),
            P(rows, "tp"),
            P(rows, "tp"),
            P(rows, "tp"),
            P(rows),
            P(rows, None),
            P(None, rows, "tp"),
            P(None, rows, "tp"),
            P(None, rows, "tp"),
        ),
        check_vma=False,
    )
```

```python
from functools import partial
import math

import jax
import jax.numpy as jnp
from jax import lax
from jax.experimental import pallas as pl
from jax.experimental.pallas import tpu as pltpu
from jax.sharding import PartitionSpec as P

HD = 128
CAP = 160


EPS = 1e-05
THETA = 10000.0
NEG = -1e30
BF = jnp.bfloat16
F32 = jnp.float32


def mm(left, right):
    return jnp.dot(left, right, preferred_element_type=F32)


def mm_t(left, right):
    return lax.dot_general(left, right, (((1,), (1,)), ((), ())), preferred_element_type=F32)


def t_mm(left, right):
    return lax.dot_general(left, right, (((0,), (0,)), ((), ())), preferred_element_type=F32)


def rotary_tables(positions):
    half_size = HD // 2
    frequency = THETA ** (-(jnp.arange(half_size, dtype=F32) * 2.0 / HD))
    angles = positions.astype(F32)[:, None] * frequency[None, :]
    cosine, sine = jnp.cos(angles), jnp.sin(angles)
    return jnp.concatenate([cosine, cosine], axis=1), jnp.concatenate([-sine, sine], axis=1)


MESH = pl.DeviceIdType.MESH
VM = pl.BlockSpec(memory_space=pltpu.VMEM)
DMA = pltpu.SemaphoreType.DMA


def peer(axis, n, k):
    return lax.rem(lax.axis_index(axis) + k, n)


def greet(groups):
    barrier = pltpu.get_barrier_semaphore()
    for axis, n in groups:
        for k in range(1, n):
            pl.semaphore_signal(
                barrier, inc=1, device_id={axis: peer(axis, n, k)}, device_id_type=MESH
            )
    pl.semaphore_wait(barrier, sum(n - 1 for _, n in groups))


def remote(source, target, sems, i, to):
    copy = pltpu.make_async_remote_copy(
        src_ref=source,
        dst_ref=target,
        send_sem=sems[0].at[i],
        recv_sem=sems[1].at[i],
        device_id=to,
        device_id_type=MESH,
    )
    copy.start()
    return copy


def send(source, target, axis, n, k, sems):
    return remote(source, target, sems, k - 1, {axis: peer(axis, n, k)})


def columns(n, size):
    return pl.ds(pl.multiple_of(n * size, 128), size)


def stretch(n, size):
    return pl.ds(pl.multiple_of(n * size, 16), size)


def gather_columns(own, full, axis, n, sems):
    size = own.shape[1]
    place = full.at[:, columns(lax.axis_index(axis), size)]
    copies = [send(own, place, axis, n, k, sems) for k in range(1, n)]
    place[...] = own[...]
    return copies


def scatter_columns(part, slots, axis, n, sems):
    size = slots.shape[2]
    return [
        send(part.at[:, columns(peer(axis, n, k), size)], slots.at[k - 1], axis, n, k, sems)
        for k in range(1, n)
    ]


def finish(copies):
    for copy in copies:
        copy.wait()


def quad():
    here = lax.axis_index("ctx")
    return here, here + 1 - 2 * lax.rem(here, 2), lax.rem(here + 2, 4)


def gather_square(own, full, first_row, sems, between):
    rows = own.shape[0]
    here, beside, across = quad()

    def place(rank):
        return full.at[pl.ds(pl.multiple_of(first_row + rank * rows, 16), rows), :]

    first = remote(own, place(here), sems, 0, {"ctx": across})
    second = remote(own, place(here), sems, 1, {"ctx": beside})
    full[pl.ds(pl.multiple_of(first_row + here * rows, 16), rows), :] = own[...]
    between()
    first.wait()
    third = remote(place(across), place(across), sems, 2, {"ctx": beside})
    second.wait()
    third.wait()


def row_sums(values):
    ones = jnp.ones((8, values.shape[1]), F32)
    return lax.dot_general(
        ones,
        values,
        (((1,), (1,)), ((), ())),
        precision=lax.Precision.HIGHEST,
        preferred_element_type=F32,
    )


def as_column(rows, weight):
    return lax.dot_general(
        rows,
        weight,
        (((0,), (0,)), ((), ())),
        precision=lax.Precision.HIGHEST,
        preferred_element_type=F32,
    )


def eighth():
    return jnp.full((8, 128), 0.125, F32)


def total_over(sums, mine, slots, axis, n, sems):
    mine[...] = sums
    copies = [send(mine, slots.at[k - 1], axis, n, k, sems) for k in range(1, n)]
    finish(copies)
    total = sums
    for k in range(1, n):
        total = total + slots[k - 1]
    return total


def call(kernel, out_shape, inputs, scratch, collective, name):
    return pl.pallas_call(
        kernel,
        out_shape=out_shape,
        in_specs=[VM] * len(inputs),
        out_specs=jax.tree.map(lambda _: VM, out_shape),
        scratch_shapes=scratch,
        compiler_params=pltpu.CompilerParams(collective_id=collective, has_side_effects=True),
        cost_estimate=pl.CostEstimate(flops=0, bytes_accessed=0, transcendentals=0),
        name=name,
    )(*inputs)


def shape(dims, dtype):
    return jax.ShapeDtypeStruct(dims, dtype)


def pair_of_sems(n):
    return [DMA((n,)), DMA((n,))]


def gather_tp(value, n_tp):
    rows, size = value.shape

    def kernel(own, full, *sems):
        greet([("tp", n_tp)])
        finish(gather_columns(own, full, "tp", n_tp, sems))

    return call(
        kernel, shape((rows, size * n_tp), value.dtype), (value,), pair_of_sems(n_tp), 1, "gather_tp"
    )


def first_norm(full, grad, gain, weights, quarter, n_tp, n_ctx):
    rows, width = full.shape
    with_quarter = quarter is not None

    def kernel(*refs):
        hid, grd, gn = refs[:3]
        refs = refs[3:]
        if with_quarter:
            wgt, qrt, out, scale, grd_full, wgt_full = refs[:6]
            sems = refs[6:]
            greet([("tp", n_tp), ("ctx", n_ctx)])
        else:
            out, scale, grd_full = refs[:3]
            sems = refs[3:]
            greet([("tp", n_tp)])
        grads = gather_columns(grd, grd_full, "tp", n_tp, sems[0:2])

        def norm():
            values = hid[...].astype(F32)
            mean = jnp.sum(values * values, axis=-1, keepdims=True) * (1.0 / width)
            factor = lax.rsqrt(mean + EPS)
            scale[...] = jnp.broadcast_to(factor, scale.shape)
            out[...] = (values * factor * gn[0:1, :]).astype(BF)

        if with_quarter:
            half = wgt.shape[0]
            mine = lax.axis_index("fsdp")

            def work():
                norm()
                wgt_full[pl.ds(pl.multiple_of(mine * half, 16), half), :] = wgt[...]

            gather_square(qrt, wgt_full, (1 - mine) * half, sems[2:4], work)
        else:
            norm()
        finish(grads)

    outs = [shape((rows, width), BF), shape((rows, 128), F32), shape((rows, width), BF)]
    inputs = [full, grad, gain]
    if with_quarter:
        outs.append(shape((2 * weights.shape[0], weights.shape[1]), BF))
        inputs += [weights, quarter]
    return call(
        kernel, tuple(outs), inputs, pair_of_sems(n_tp) + pair_of_sems(3), 7, "first_norm"
    )


def turn(values, cosine, sine):
    return values * cosine + pltpu.roll(values, HD // 2, axis=1) * sine


def softmax_rows(query, key, first_row):
    scores = mm_t(query, key) * (1.0 / math.sqrt(HD))
    rows = first_row + lax.broadcasted_iota(jnp.int32, scores.shape, 0)
    cols = lax.broadcasted_iota(jnp.int32, scores.shape, 1)
    scores = jnp.where(cols <= rows, scores, NEG)
    top = jnp.max(scores, axis=-1, keepdims=True)
    weights = jnp.exp(scores - top)
    return weights / jnp.sum(weights, axis=-1, keepdims=True)


def attention_forward(qkv, cosine, sine, n_ctx):
    rows = qkv.shape[0]
    width = qkv.shape[1] // 3
    heads = width // HD

    def kernel(prj, cs, sn, out, qry, full, own, *sems):
        greet([("ctx", n_ctx)])
        here = lax.axis_index("ctx")

        @pl.loop(0, heads)
        def _(h):
            own[:, columns(h, HD)] = turn(
                prj[:, columns(h + heads, HD)], cs[...], sn[...]
            ).astype(BF)
            own[:, columns(h + heads, HD)] = prj[:, columns(h + 2 * heads, HD)].astype(BF)

        def queries():
            @pl.loop(0, heads)
            def _(h):
                qry[:, columns(h, HD)] = turn(prj[:, columns(h, HD)], cs[...], sn[...]).astype(BF)

        gather_square(own, full, 0, sems, queries)

        @pl.loop(0, heads)
        def _(h):
            probs = softmax_rows(qry[:, columns(h, HD)], full[:, columns(h, HD)], here * rows)
            out[:, columns(h, HD)] = mm(
                probs.astype(BF), full[:, columns(h + heads, HD)]
            ).astype(BF)

    return call(
        kernel,
        (
            shape((rows, width), BF),
            shape((rows, width), BF),
            shape((rows * n_ctx, 2 * width), BF),
        ),
        (qkv, cosine, sine),
        [pltpu.VMEM((rows, 2 * width), BF)] + pair_of_sems(3),
        2,
        "attention_forward",
    )


def second_norm(part, hidden, gain, slabs, picks, router, onehot, names, n_tp, n_ctx):
    rows, size = hidden.shape
    width = size * n_tp
    experts = n_ctx

    def kernel(
        prt, hid, gn, slb, pck, rtr, one, nms,
        resid, scale, out, moved, tokens, slot_gates, gates, mix,
        slots, mine, sums, low, sent, own_gates, *sems
    ):
        greet([("tp", n_tp), ("ctx", n_ctx)])
        here = lax.axis_index("tp")
        copies = scatter_columns(prt, slots, "tp", n_tp, sems[0:2])
        others = [
            send(
                slb.at[pl.ds(k * CAP, CAP)], moved.at[pl.ds(k * CAP, CAP)],
                "ctx", n_ctx, k, sems[6:8],
            )
            for k in range(1, n_ctx)
        ]
        moved[0:CAP] = slb[0:CAP]
        total = prt[:, columns(here, size)].astype(F32)
        finish(copies)
        for k in range(1, n_tp):
            total = total + slots[k - 1].astype(F32)
        total = hid[...].astype(F32) + total
        resid[...] = total
        square = total_over(row_sums(total * total), mine, sums, "tp", n_tp, sems[2:4])
        factor = lax.rsqrt(as_column(square, eighth()) * (1.0 / width) + EPS)
        scale[...] = factor
        low[...] = (resid[...] * factor[:, 0:1] * gn[0:1, :]).astype(BF)
        copies = gather_columns(low, out, "tp", n_tp, sems[4:6])
        for step in range(n_tp):
            at = columns(peer("tp", n_tp, n_tp - step), size)
            if step:
                copies[step - 1].wait()
                block = out[:, at]
            else:
                block = low[...]
            sent[step] = mm(pck[...], block).astype(BF)
            tokens[0:CAP, at] = sent[step, 0:CAP]
            for k in (2, 3, 1):
                others.append(
                    remote(
                        sent.at[step, pl.ds(k * CAP, CAP)], tokens.at[pl.ds(k * CAP, CAP), at],
                        sems[8:10], step * n_ctx + k, {"ctx": peer("ctx", n_ctx, k)},
                    )
                )
        logits = mm_t(rtr[...].astype(BF), out[...])
        named = [jnp.sum(one[j] * logits, axis=0, keepdims=True) for j in range(2)]
        top = jnp.maximum(named[0], named[1])
        powers = [jnp.exp(value - top) for value in named]
        both = powers[0] + powers[1]
        gate = [value / both for value in powers]
        mixed = gate[0] * nms[0] + gate[1] * nms[1]
        mix[...] = mixed
        order = lax.broadcasted_iota(jnp.int32, (8, rows), 0)
        gates[...] = jnp.where(order == 0, gate[0], jnp.where(order == 1, gate[1], 0.0))
        own_gates[...] = jnp.zeros(own_gates.shape, F32)
        for k in range(experts):
            own_gates[k, :, 0:CAP] = lax.dot_general(
                jnp.broadcast_to(mixed[k : k + 1], (8, rows)),
                pck[k * CAP : (k + 1) * CAP].astype(F32),
                (((1,), (1,)), ((), ())),
                precision=lax.Precision.HIGHEST,
                preferred_element_type=F32,
            )
        slot_gates[0] = own_gates[0]
        for k in range(1, n_ctx):
            others.append(
                send(own_gates.at[k], slot_gates.at[k], "ctx", n_ctx, k, sems[10:12])
            )
        finish(others)

    return call(
        kernel,
        (
            shape((rows, size), F32),
            shape((rows, 128), F32),
            shape((rows, width), BF),
            shape(slabs.shape, BF),
            shape(slabs.shape, BF),
            shape((experts, 8, rows), F32),
            shape((8, rows), F32),
            shape((8, rows), F32),
        ),
        (part, hidden, gain, slabs, picks, router, onehot, names),
        [
            pltpu.VMEM((n_tp - 1, rows, size), BF),
            pltpu.VMEM((8, rows), F32),
            pltpu.VMEM((n_tp - 1, 8, rows), F32),
            pltpu.VMEM((rows, size), BF),
            pltpu.VMEM((n_tp, experts * CAP, size), BF),
            pltpu.VMEM((experts, 8, rows), F32),
        ]
        + pair_of_sems(n_tp) * 3
        + pair_of_sems(n_ctx)
        + pair_of_sems(n_tp * n_ctx)
        + pair_of_sems(n_ctx),
        3,
        "second_norm",
    )


def second_norm_back(
    d_rows, dots, picks, gates, onehot, names, router, resid, scale, gain, grad, n_tp, n_ctx
):
    rows, size = resid.shape
    width = size * n_tp
    experts = n_ctx

    def kernel(
        drw, dts, pck, gts, one, nms, rtr, rsd, scl, gn, grd,
        d_resid, low, d_gain, d_logits,
        back, back_dots, part, slots, mine, sums, mine_two, sums_two, *sems
    ):
        greet([("tp", n_tp), ("ctx", n_ctx)])
        here = lax.axis_index("tp")
        small = []
        large = []
        for k in range(1, n_ctx):
            small.append(
                send(dts.at[k], back_dots.at[k - 1], "ctx", n_ctx, n_ctx - k, sems[0:2])
            )
        for step in range(1, n_tp + 1):
            at = columns(peer("tp", n_tp, step), size)
            for k in (2, 3, 1):
                large.append(
                    remote(
                        drw.at[pl.ds(k * CAP, CAP), at], back.at[k - 1, :, at],
                        sems[2:4], step * n_ctx - k, {"ctx": peer("ctx", n_ctx, n_ctx - k)},
                    )
                )
        finish(small)
        order = lax.broadcasted_iota(jnp.int32, (8, rows), 0)
        own = jnp.zeros((8, rows), F32)
        for k in range(experts):
            by_slot = dts[0] if k == 0 else back_dots[k - 1]
            by_row = lax.dot_general(
                by_slot[:, 0:CAP],
                pck[k * CAP : (k + 1) * CAP].astype(F32),
                (((1,), (0,)), ((), ())),
                precision=lax.Precision.HIGHEST,
                preferred_element_type=F32,
            )
            own = own + jnp.where(order == k, by_row, 0.0)
        gate_grad = total_over(own, mine, sums, "tp", n_tp, sems[4:6])
        both = [jnp.sum(nms[j] * gate_grad, axis=0, keepdims=True) for j in range(2)]
        gate = [gts[j : j + 1, :] for j in range(2)]
        mean = gate[0] * both[0] + gate[1] * both[1]
        logits = sum(gate[j] * (both[j] - mean) * one[j] for j in range(2))
        d_logits[...] = logits
        copies = []
        for step in range(1, n_tp + 1):
            at = columns(peer("tp", n_tp, step), size)
            finish(large[3 * step - 3 : 3 * step])
            block = t_mm(pck[0:CAP], drw[0:CAP, at])
            for k in range(1, experts):
                block = block + t_mm(pck[k * CAP : (k + 1) * CAP], back[k - 1, :, at])
            if step < n_tp:
                part[step - 1] = block.astype(BF)
                copies.append(
                    send(part.at[step - 1], slots.at[step - 1], "tp", n_tp, step, sems[6:8])
                )
            else:
                total = block
        total = total + lax.dot_general(
            logits.astype(BF),
            rtr[...].astype(BF),
            (((0,), (0,)), ((), ())),
            preferred_element_type=F32,
        )
        finish(copies)
        for k in range(1, n_tp):
            total = total + slots[k - 1].astype(F32)
        factor = scl[:, 0:1]
        unit = rsd[...] * factor
        d_gain[...] = jnp.broadcast_to(jnp.sum(total * unit, axis=0, keepdims=True), d_gain.shape)
        gained = total * gn[0:1, :]
        d_resid[...] = gained
        dot = total_over(row_sums(unit * gained), mine_two, sums_two, "tp", n_tp, sems[8:10])
        dot = as_column(dot, eighth())[:, 0:1] * (1.0 / width)
        result = grd[...].astype(F32) + factor * (d_resid[...] - rsd[...] * factor * dot)
        d_resid[...] = result
        low[...] = result.astype(BF)

    return call(
        kernel,
        (
            shape((rows, size), F32),
            shape((rows, size), BF),
            shape((8, size), F32),
            shape((8, rows), F32),
        ),
        (d_rows, dots, picks, gates, onehot, names, router, resid, scale, gain, grad),
        [
            pltpu.VMEM((n_ctx - 1, CAP, width), BF),
            pltpu.VMEM((n_ctx - 1, 8, rows), F32),
            pltpu.VMEM((n_tp - 1, rows, size), BF),
            pltpu.VMEM((n_tp - 1, rows, size), BF),
            pltpu.VMEM((8, rows), F32),
            pltpu.VMEM((n_tp - 1, 8, rows), F32),
            pltpu.VMEM((8, rows), F32),
            pltpu.VMEM((n_tp - 1, 8, rows), F32),
        ]
        + pair_of_sems(n_ctx)
        + pair_of_sems(n_tp * n_ctx)
        + pair_of_sems(n_tp) * 3,
        4,
        "second_norm_back",
    )


def attention_backward(low, output_w, query, kv, cosine, sine, n_tp, n_ctx):
    rows, size = low.shape
    width = size * n_tp
    inner = query.shape[1]
    heads = inner // HD
    scale = 1.0 / math.sqrt(HD)

    def kernel(
        lw, wgt, qry, full, cs, sn, d_attn, d_qkv, dot, dqs, dkv, slots, last, both, total, *sems
    ):
        greet([("tp", n_tp), ("ctx", n_ctx)])
        here, beside, across = quad()
        beyond = lax.rem(beside + 2, 4)
        copies = gather_columns(lw, d_attn, "tp", n_tp, sems[2:4])
        for step in range(n_tp):
            rank = peer("tp", n_tp, n_tp - step)
            weights = wgt[pl.ds(pl.multiple_of(rank * size, 16), size), :]
            if step:
                copies[step - 1].wait()
                total[...] += mm(d_attn[:, columns(rank, size)], weights)
            else:
                total[...] = mm(lw[...], weights)
        dot[...] = total[...].astype(BF)

        @pl.loop(0, heads)
        def _(h):
            at, at_v = columns(h, HD), columns(h + heads, HD)
            probs = softmax_rows(qry[:, at], full[:, at], here * rows)
            d_probs = mm_t(dot[:, at], full[:, at_v])
            delta = jnp.sum(probs * d_probs, axis=-1, keepdims=True)
            d_scores = (probs * (d_probs - delta)).astype(BF)
            dqs[:, at] = mm(d_scores, full[:, at]) * scale
            dkv[:, at] = (t_mm(d_scores, qry[:, at]) * scale).astype(BF)
            dkv[:, at_v] = t_mm(probs.astype(BF), dot[:, at]).astype(BF)

        first = remote(dkv.at[stretch(beyond, rows), :], slots.at[0], sems, 0, {"ctx": beside})
        second = remote(dkv.at[stretch(beside, rows), :], slots.at[1], sems, 1, {"ctx": beside})
        first.wait()
        both[...] = (
            dkv[stretch(across, rows), :].astype(F32) + slots[0].astype(F32)
        ).astype(BF)
        third = remote(both, last, sems, 2, {"ctx": across})

        @pl.loop(0, heads)
        def _(h):
            d_qkv[:, columns(h, HD)] = turn(dqs[:, columns(h, HD)], cs[...], sn[...]).astype(BF)

        second.wait()
        third.wait()

        @pl.loop(0, heads)
        def _(h):
            at, at_v = columns(h, HD), columns(h + heads, HD)
            mine = stretch(here, rows)
            d_key = dkv[mine, at].astype(F32) + slots[1, :, at].astype(F32)
            d_key = d_key + last[:, at].astype(F32)
            d_qkv[:, columns(h + heads, HD)] = turn(d_key, cs[...], sn[...]).astype(BF)
            d_value = dkv[mine, at_v].astype(F32) + slots[1, :, at_v].astype(F32)
            d_value = d_value + last[:, at_v].astype(F32)
            d_qkv[:, columns(h + 2 * heads, HD)] = d_value.astype(BF)

    return call(
        kernel,
        (shape((rows, width), BF), shape((rows, 3 * inner), BF)),
        (low, output_w, query, kv, cosine, sine),
        [
            pltpu.VMEM((rows, inner), BF),
            pltpu.VMEM((rows, inner), F32),
            pltpu.VMEM((rows * n_ctx, 2 * inner), BF),
            pltpu.VMEM((2, rows, 2 * inner), BF),
            pltpu.VMEM((rows, 2 * inner), BF),
            pltpu.VMEM((rows, 2 * inner), BF),
            pltpu.VMEM((rows, inner), F32),
        ]
        + pair_of_sems(3)
        + pair_of_sems(n_tp),
        5,
        "attention_backward",
    )


def first_norm_back(part, hidden, scale, gain, d_resid, n_tp):
    rows, size = hidden.shape
    width = size * n_tp

    def kernel(prt, hid, scl, gn, dr, out, d_gain, slots, mine, sums, *sems):
        greet([("tp", n_tp)])
        here = lax.axis_index("tp")
        copies = scatter_columns(prt, slots, "tp", n_tp, sems[0:2])
        total = prt[:, columns(here, size)].astype(F32)
        finish(copies)
        for k in range(1, n_tp):
            total = total + slots[k - 1].astype(F32)
        factor = scl[:, 0:1]
        unit = hid[...].astype(F32) * factor
        d_gain[...] = jnp.broadcast_to(jnp.sum(total * unit, axis=0, keepdims=True), d_gain.shape)
        gained = total * gn[0:1, :]
        out[...] = gained
        dot = total_over(row_sums(unit * gained), mine, sums, "tp", n_tp, sems[2:4])
        dot = as_column(dot, eighth())[:, 0:1] * (1.0 / width)
        unit = hid[...].astype(F32) * factor
        out[...] = dr[...] + factor * (out[...] - unit * dot)

    return call(
        kernel,
        (shape((rows, size), F32), shape((8, size), F32)),
        (part, hidden, scale, gain, d_resid),
        [
            pltpu.VMEM((n_tp - 1, rows, size), BF),
            pltpu.VMEM((8, rows), F32),
            pltpu.VMEM((n_tp - 1, 8, rows), F32),
        ]
        + pair_of_sems(n_tp) * 2,
        6,
        "first_norm_back",
    )


def weight_grads(part, small, n_tp, n_ctx):
    rows, size = part.shape[2:]
    half = size // 2
    width = small.shape[1] * n_tp
    places = 2 * n_ctx
    cut = width // places

    def kernel(
        prt, sml, out, small_out, near, two, far, one, last, sml_full, sml_slots, *sems
    ):
        barrier = pltpu.get_barrier_semaphore()
        here, beside, across = quad()
        beyond = lax.rem(beside + 2, 4)
        mine = lax.axis_index("fsdp")
        other = 1 - mine
        place = mine * n_ctx + here
        others = []
        for i in range(1, places):
            to = lax.rem(place + i, places)
            others.append((to, {"fsdp": to // n_ctx, "ctx": lax.rem(to, n_ctx)}))
        ahead = [{"tp": peer("tp", n_tp, k)} for k in range(1, n_tp)]
        for device in ahead + [device for _, device in others]:
            pl.semaphore_signal(barrier, inc=1, device_id=device, device_id_type=MESH)
        pl.semaphore_wait(barrier, n_tp - 1 + places - 1)
        gathers = gather_columns(sml, sml_full, "tp", n_tp, sems[6:8])
        left, right = pl.ds(0, half), pl.ds(half, half)
        blocks = [
            (other, beyond, left), (mine, beyond, left), (other, beyond, right),
            (other, beside, right), (other, beside, left), (mine, beside, left),
            (mine, beyond, right), (mine, beside, right),
        ]
        steps = []
        for i, (rank, column, at) in enumerate(blocks):
            steps.append(
                remote(prt.at[rank, column, :, at], near.at[i], sems[0:2], i, {"ctx": beside})
            )
        finish(gathers)
        totals = [
            remote(
                sml_full.at[:, columns(to, cut)], sml_slots.at[i], sems[8:10], i, device
            )
            for i, (to, device) in enumerate(others)
        ]

        def chip(i, rank, column, at):
            steps[i].wait()
            return prt[rank, column, :, at].astype(F32) + near[i].astype(F32)

        first_hop = []
        for slot, (i, rank, column, at, to) in enumerate(
            [
                (0, other, across, left, {"ctx": across}),
                (1, mine, across, left, {"ctx": across}),
                (2, other, across, right, {"fsdp": other}),
                (3, other, here, right, {"fsdp": other}),
            ]
        ):
            two[slot] = chip(i, rank, column, at).astype(BF)
            first_hop.append(remote(two.at[slot], far.at[slot], sems[2:4], slot, to))
        value = chip(4, other, here, left)
        first_hop[0].wait()
        one[0] = (value + far[0].astype(F32)).astype(BF)
        second_hop = [remote(one.at[0], last.at[0], sems[4:6], 0, {"fsdp": other})]
        value = chip(6, mine, across, right)
        first_hop[2].wait()
        one[1] = (value + far[2].astype(F32)).astype(BF)
        second_hop.append(remote(one.at[1], last.at[1], sems[4:6], 1, {"ctx": across}))
        value = chip(5, mine, here, left)
        first_hop[1].wait()
        out[:, left] = value + far[1].astype(F32)
        value = chip(7, mine, here, right)
        first_hop[3].wait()
        out[:, right] = value + far[3].astype(F32)
        finish(totals)
        sums = sml_full[:, columns(place, cut)]
        for i in range(places - 1):
            sums = sums + sml_slots[i]
        small_out[...] = sums
        second_hop[0].wait()
        out[:, left] = out[:, left] + last[0].astype(F32)
        second_hop[1].wait()
        out[:, right] = out[:, right] + last[1].astype(F32)

    return call(
        kernel,
        (shape((rows, size), F32), shape((8, cut), F32)),
        (part, small),
        [
            pltpu.VMEM((8, rows, half), BF),
            pltpu.VMEM((4, rows, half), BF),
            pltpu.VMEM((4, rows, half), BF),
            pltpu.VMEM((2, rows, half), BF),
            pltpu.VMEM((2, rows, half), BF),
            pltpu.VMEM((8, width), F32),
            pltpu.VMEM((places - 1, 8, cut), F32),
        ]
        + pair_of_sems(8)
        + pair_of_sems(4)
        + pair_of_sems(2)
        + pair_of_sems(n_tp)
        + pair_of_sems(places),
        10,
        "weight_grads",
    )


def place_pieces(pieces, n_ctx):
    rows, size = pieces[0].shape
    tile = 64 if rows % 64 == 0 else rows

    def kernel(*refs):
        here = lax.axis_index("ctx")
        for k in range(n_ctx):
            refs[-1][lax.rem(here + n_ctx - k, n_ctx)] = refs[k][...].astype(F32)

    return pl.pallas_call(
        kernel,
        grid=(rows // tile,),
        out_shape=shape((n_ctx, rows, size), F32),
        in_specs=[pl.BlockSpec((tile, size), lambda i: (i, 0))] * n_ctx,
        out_specs=pl.BlockSpec((n_ctx, tile, size), lambda i: (0, i, 0)),
        cost_estimate=pl.CostEstimate(
            flops=0, bytes_accessed=6 * n_ctx * rows * size, transcendentals=0
        ),
        name="place_pieces",
    )(*pieces)


def after(value, *needed):
    return lax.optimization_barrier((value, *needed))[0]


def shards(
    hidden_in,
    out_grad,
    attn_gain,
    w_query,
    w_key,
    w_value,
    w_output,
    ffn_gain,
    w_router,
    w_gate,
    w_up,
    w_down,
    routes,
):
    rows_here, width_tp = hidden_in.shape
    here_tp = lax.axis_index("tp")
    here_ctx = lax.axis_index("ctx")
    here_fsdp = lax.axis_index("fsdp")
    n_fsdp = lax.axis_size("fsdp")
    n_ctx = lax.axis_size("ctx")
    n_tp = lax.axis_size("tp")
    experts = w_gate.shape[0]
    assert experts == n_ctx == 4
    width = width_tp * n_tp
    part = width // n_fsdp
    pair = n_fsdp == 2
    heads_width = w_query.shape[1]

    def shift_ctx(value, k):
        return lax.ppermute(value, "ctx", [(i, (i + k) % n_ctx) for i in range(n_ctx)])

    def swap_fsdp(value):
        return lax.ppermute(value, "fsdp", [(0, 1), (1, 0)])

    def other_parts(weight):
        if pair:
            return [weight, swap_fsdp(weight)]
        return [lax.all_gather(weight, "fsdp", axis=0, tiled=True)]

    def split(values):
        if pair:
            return [
                lax.dynamic_slice_in_dim(values, here_fsdp * part, part, 1),
                lax.dynamic_slice_in_dim(values, (1 - here_fsdp) * part, part, 1),
            ]
        return [values]

    def join(pieces):
        if pair:
            first = here_fsdp == 0
            return jnp.concatenate(
                [jnp.where(first, pieces[0], pieces[1]), jnp.where(first, pieces[1], pieces[0])],
                axis=1,
            )
        return pieces[0]

    def into(values, weights):
        return sum(mm(x, w) for x, w in zip(split(values), weights))

    def back(values, weights):
        return join([mm_t(values, w) for w in weights])

    def my_features(values):
        return lax.dynamic_slice_in_dim(values, here_tp * width_tp, width_tp, values.ndim - 1)

    attn_w = jnp.concatenate([w_query, w_key, w_value, w_output], axis=1)
    small = jnp.concatenate(
        [attn_gain[None], ffn_gain[None], w_router.T, jnp.zeros((2, part), BF)], axis=0
    )
    if pair:
        quarter = part // n_ctx
        own_quarter = lax.dynamic_slice_in_dim(attn_w, here_ctx * quarter, quarter, 0)
        other_quarter = swap_fsdp(own_quarter)
        other_small = swap_fsdp(small)
        small_full = join([small, other_small]).astype(F32)
    else:
        other_quarter = None
        small_full = lax.all_gather(small, "fsdp", axis=1, tiled=True).astype(F32)
    inputs_full = gather_tp(hidden_in, n_tp)

    def expert_parts(weights, ready):
        rank, _ = lax.optimization_barrier((here_ctx, ready))
        return other_parts(lax.dynamic_index_in_dim(weights, rank, 0, False))

    gate_w = expert_parts(w_gate, small)
    up_w = expert_parts(w_up, inputs_full)
    down_w = expert_parts(w_down, inputs_full)
    small_here = my_features(small_full)
    gain_one_here = jnp.broadcast_to(small_here[0:1], small_here.shape)
    gain_two_here = jnp.broadcast_to(small_here[1:2], small_here.shape)
    nothing = [(0, 8 - experts), (0, 0)]
    router_full = jnp.pad(small_full[2 : 2 + experts], nothing)
    router_here = jnp.pad(small_here[2 : 2 + experts], nothing)

    relative = (jnp.arange(experts, dtype=jnp.int32) + here_ctx) % experts
    numbers = jnp.arange(8, dtype=jnp.int32)
    onehot = (routes.T[:, None, :] == numbers[None, :, None]).astype(F32)
    named = (routes.T[:, None, :] == relative[None, :, None]).astype(F32)
    names = jnp.pad(named, [(0, 0)] + nothing)
    chosen = jnp.sum(named, axis=0)
    earlier = jnp.triu(jnp.ones((rows_here, rows_here), BF), 1)
    slot_of = mm(chosen.astype(BF), earlier).astype(jnp.int32)
    slots = jnp.arange(CAP, dtype=jnp.int32)
    picks = (slot_of[:, None, :] == slots[None, :, None]) & (chosen[:, None, :] > 0)
    picks = picks.astype(BF).reshape(experts * CAP, rows_here)

    gathered = first_norm(
        inputs_full, out_grad, small_full, attn_w, other_quarter, n_tp, n_ctx
    )
    normed_one, scale_one, grad_full = gathered[:3]
    if pair:
        attn_full = gathered[3]
    else:
        attn_full = lax.all_gather(attn_w, "fsdp", axis=0, tiled=True)
    qkv_w = attn_full[:, : 3 * heads_width]
    output_w = attn_full[:, 3 * heads_width :]
    positions = here_ctx * rows_here + jnp.arange(rows_here, dtype=jnp.int32)
    cosine, sine = rotary_tables(positions)
    attended, query, kv = attention_forward(mm(normed_one, qkv_w), cosine, sine, n_ctx)
    resid, scale_two, normed_two, grad_rows, token_rows, slot_gates, gates, mix = second_norm(
        mm_t(attended, output_w).astype(BF),
        hidden_in,
        gain_two_here,
        mm(picks, grad_full).astype(BF),
        picks,
        router_full,
        onehot,
        names,
        n_tp,
        n_ctx,
    )
    gate_rows = slot_gates[:, 0, :CAP].reshape(experts * CAP, 1)

    gate_act = into(token_rows, gate_w)
    up_act = into(token_rows, up_w)
    sigma_act = jax.nn.sigmoid(gate_act)
    hidden_act = (gate_act * sigma_act * up_act).astype(BF)
    d_result = (gate_rows * grad_rows.astype(F32)).astype(BF)

    def grad_send(left, right):
        halves = split(left)
        if pair:
            away = t_mm(halves[1], right).astype(BF)
            return halves[0], right, away, swap_fsdp(away)
        return halves[0], right, None, None

    def grad_sum(mine, right, away, other):
        if pair:
            return (t_mm(mine, right) + other.astype(F32)).astype(BF)
        return lax.psum_scatter(
            t_mm(mine, right).astype(BF), "fsdp", scatter_dimension=0, tiled=True
        )

    def grad_spread(mine):
        cut = part // n_ctx
        pieces = []
        for k in range(experts):
            piece = lax.dynamic_slice_in_dim(mine, ((here_ctx + k) % n_ctx) * cut, cut, 0)
            pieces.append(shift_ctx(piece, k) if k else piece)
        return pieces

    down_sent = grad_send(d_result, hidden_act)
    if pair:
        grad_rows = after(grad_rows, down_sent[2])
    d_hidden = into(grad_rows, down_w)
    gate_dot = jnp.sum(hidden_act.astype(F32) * d_hidden, axis=-1).reshape(experts, CAP)
    gate_dot = jnp.broadcast_to(
        jnp.pad(gate_dot, [(0, 0), (0, rows_here - CAP)])[:, None, :], (experts, 8, rows_here)
    )
    d_hidden = gate_rows * d_hidden
    d_gate_act = (d_hidden * up_act * sigma_act * (1.0 + gate_act * (1.0 - sigma_act))).astype(BF)
    d_up_act = (d_hidden * gate_act * sigma_act).astype(BF)
    gate_sent = grad_send(token_rows, d_gate_act)
    up_sent = grad_send(token_rows, d_up_act)
    d_rows = join(
        [mm_t(d_gate_act, wg) + mm_t(d_up_act, wu) for wg, wu in zip(gate_w, up_w)]
    ).astype(BF)
    if pair:
        d_rows = after(d_rows, gate_sent[2], up_sent[2])
    result = back(after(hidden_act, d_rows), down_w)

    d_resid, d_attn_here, gain_two_part, d_logits = second_norm_back(
        d_rows,
        gate_dot,
        picks,
        gates,
        onehot,
        names,
        router_here,
        resid,
        scale_two,
        gain_two_here,
        out_grad,
        n_tp,
        n_ctx,
    )
    if pair:
        d_attn_here = after(d_attn_here, down_sent[3])
    down_pieces = grad_spread(grad_sum(*down_sent))

    if pair:
        d_attn_here = after(d_attn_here, down_pieces[0])
    d_attn, d_qkv = attention_backward(
        d_attn_here, output_w, query, kv, cosine, -sine, n_tp, n_ctx
    )
    if pair:
        d_qkv = after(d_qkv, gate_sent[3], *down_pieces)
    gate_pieces = grad_spread(grad_sum(*gate_sent))
    if pair:
        d_qkv = after(d_qkv, gate_pieces[0])
    in_grad, gain_one_part = first_norm_back(
        mm_t(d_qkv, qkv_w).astype(BF), hidden_in, scale_one, gain_one_here, d_resid, n_tp
    )

    share = my_features(result)
    for k in range(1, n_tp):
        piece = lax.dynamic_slice_in_dim(
            result, ((here_tp + k) % n_tp) * width_tp, width_tp, 1
        ).astype(BF)
        piece = lax.ppermute(piece, "tp", [(i, (i + k) % n_tp) for i in range(n_tp)])
        share = share + piece.astype(F32)
    shares = share.astype(BF).reshape(experts, CAP, width_tp)
    moe_part = jnp.zeros(resid.shape, F32)
    for k in range(experts):
        piece = shift_ctx(shares[k], -k) if k else shares[k]
        pick = picks[k * CAP : (k + 1) * CAP]
        moe_part = moe_part + mix[k][:, None] * t_mm(pick, piece)
    block_out = (resid + moe_part).astype(BF)

    grad_attn = jnp.concatenate([t_mm(normed_one, d_qkv), t_mm(d_attn, attended)], axis=1).astype(
        BF
    )
    small_part = jnp.concatenate(
        [
            gain_one_part[:1],
            gain_two_part[:1],
            mm(d_logits[:experts].astype(BF), my_features(normed_two)),
            jnp.zeros((6 - experts, width_tp), F32),
        ],
        axis=0,
    )
    if pair:
        in_grad, small_part = lax.optimization_barrier((in_grad, small_part))
        grad_attn, small_grad = weight_grads(
            grad_attn.reshape(n_fsdp, n_ctx, quarter, -1), small_part, n_tp, n_ctx
        )
        up_there, grad_attn = lax.optimization_barrier((up_sent[3], grad_attn))
        up_sent = (*up_sent[:3], up_there)
    else:
        scatter = partial(
            lax.psum_scatter, axis_name=("fsdp", "ctx"), scatter_dimension=0, tiled=True
        )
        grad_attn = scatter(grad_attn).astype(F32)
        small_grad = lax.all_gather(small_part, "tp", axis=1, tiled=True)
        small_grad = scatter(small_grad.T).T
    up_pieces = grad_spread(grad_sum(*up_sent))
    grad_gate, grad_up, grad_down = (
        place_pieces(pieces, n_ctx) for pieces in (gate_pieces, up_pieces, down_pieces)
    )
    return (
        block_out,
        in_grad,
        small_grad[0],
        grad_attn[:, :heads_width],
        grad_attn[:, heads_width : 2 * heads_width],
        grad_attn[:, 2 * heads_width : 3 * heads_width],
        grad_attn[:, 3 * heads_width :],
        small_grad[1],
        small_grad[2 : 2 + experts].T,
        grad_gate,
        grad_up,
        grad_down,
    )


def solution(mesh):
    rows = ("fsdp", "ctx")
    placed = (
        P(rows, "tp"),
        P(rows, "tp"),
        P("fsdp"),
        P("fsdp", "tp"),
        P("fsdp", "tp"),
        P("fsdp", "tp"),
        P("fsdp", "tp"),
        P("fsdp"),
        P("fsdp", None),
        P(None, "fsdp", "tp"),
        P(None, "fsdp", "tp"),
        P(None, "fsdp", "tp"),
        P(rows, None),
    )
    return jax.shard_map(
        shards,
        mesh=mesh,
        in_specs=placed,
        out_specs=(
            P(rows, "tp"),
            P(rows, "tp"),
            P(rows),
            P(rows, "tp"),
            P(rows, "tp"),
            P(rows, "tp"),
            P(rows, "tp"),
            P(rows),
            P(rows, None),
            P(None, rows, "tp"),
            P(None, rows, "tp"),
            P(None, rows, "tp"),
        ),
        check_vma=False,
    )
```

```python
from functools import partial
import math

import jax
import jax.numpy as jnp
from jax import lax
from jax.experimental import pallas as pl
from jax.experimental.pallas import tpu as pltpu
from jax.sharding import PartitionSpec as P

HD = 128
CAP = 160


EPS = 1e-05
THETA = 10000.0
NEG = -1e30
BF = jnp.bfloat16
F32 = jnp.float32


def mm(left, right):
    return jnp.dot(left, right, preferred_element_type=F32)


def mm_t(left, right):
    return lax.dot_general(left, right, (((1,), (1,)), ((), ())), preferred_element_type=F32)


def t_mm(left, right):
    return lax.dot_general(left, right, (((0,), (0,)), ((), ())), preferred_element_type=F32)


def rotary_tables(positions):
    half_size = HD // 2
    frequency = THETA ** (-(jnp.arange(half_size, dtype=F32) * 2.0 / HD))
    angles = positions.astype(F32)[:, None] * frequency[None, :]
    cosine, sine = jnp.cos(angles), jnp.sin(angles)
    return jnp.concatenate([cosine, cosine], axis=1), jnp.concatenate([-sine, sine], axis=1)


MESH = pl.DeviceIdType.MESH
VM = pl.BlockSpec(memory_space=pltpu.VMEM)
DMA = pltpu.SemaphoreType.DMA


def peer(axis, n, k):
    return lax.rem(lax.axis_index(axis) + k, n)


def greet(groups):
    barrier = pltpu.get_barrier_semaphore()
    for axis, n in groups:
        for k in range(1, n):
            pl.semaphore_signal(
                barrier, inc=1, device_id={axis: peer(axis, n, k)}, device_id_type=MESH
            )
    pl.semaphore_wait(barrier, sum(n - 1 for _, n in groups))


def described(source, target, sems, i, to):
    return pltpu.make_async_remote_copy(
        src_ref=source,
        dst_ref=target,
        send_sem=sems[0].at[i],
        recv_sem=sems[1].at[i],
        device_id=to,
        device_id_type=MESH,
    )


def remote(source, target, sems, i, to):
    copy = described(source, target, sems, i, to)
    copy.start()
    return copy


def send(source, target, axis, n, k, sems):
    return remote(source, target, sems, k - 1, {axis: peer(axis, n, k)})


def columns(n, size):
    return pl.ds(pl.multiple_of(n * size, 128), size)


def stretch(n, size):
    return pl.ds(pl.multiple_of(n * size, 16), size)


def gather_columns(own, full, axis, n, sems):
    size = own.shape[1]
    place = full.at[:, columns(lax.axis_index(axis), size)]
    copies = [send(own, place, axis, n, k, sems) for k in range(1, n)]
    place[...] = own[...]
    return copies


def scatter_columns(part, slots, axis, n, sems):
    size = slots.shape[2]
    return [
        send(part.at[:, columns(peer(axis, n, k), size)], slots.at[k - 1], axis, n, k, sems)
        for k in range(1, n)
    ]


def finish(copies):
    for copy in copies:
        copy.wait()


def spread(mine, out, n_ctx, sems, order=(2, 1, 3)):
    cut = mine.shape[0] // n_ctx
    return [
        send(mine.at[stretch(peer("ctx", n_ctx, k), cut), :], out.at[k - 1], "ctx", n_ctx, k, sems)
        for k in order
    ]


def quad():
    here = lax.axis_index("ctx")
    return here, here + 1 - 2 * lax.rem(here, 2), lax.rem(here + 2, 4)


def gather_square(own, full, first_row, sems, between):
    rows = own.shape[0]
    cuts = own.shape[1] // 512
    here, beside, across = quad()

    def place(rank, i):
        return full.at[
            pl.ds(pl.multiple_of(first_row + rank * rows, 16), rows), pl.ds(i * 512, 512)
        ]

    first, second, third = [], [], []
    for i in range(cuts):
        piece = own.at[:, pl.ds(i * 512, 512)]
        first.append(remote(piece, place(here, i), sems, 3 * i, {"ctx": across}))
        second.append(remote(piece, place(here, i), sems, 3 * i + 1, {"ctx": beside}))
    full[pl.ds(pl.multiple_of(first_row + here * rows, 16), rows), :] = own[...]
    between()
    for i in range(cuts):
        first[i].wait()
        third.append(
            remote(place(across, i), place(across, i), sems, 3 * i + 2, {"ctx": beside})
        )
    finish(second)
    finish(third)


def row_sums(values):
    ones = jnp.ones((8, values.shape[1]), F32)
    return lax.dot_general(
        ones,
        values,
        (((1,), (1,)), ((), ())),
        precision=lax.Precision.HIGHEST,
        preferred_element_type=F32,
    )


def as_column(rows, weight):
    return lax.dot_general(
        rows,
        weight,
        (((0,), (0,)), ((), ())),
        precision=lax.Precision.HIGHEST,
        preferred_element_type=F32,
    )


def eighth():
    return jnp.full((8, 128), 0.125, F32)


def total_over(sums, mine, slots, axis, n, sems):
    mine[...] = sums
    copies = [send(mine, slots.at[k - 1], axis, n, k, sems) for k in range(1, n)]
    finish(copies)
    total = sums
    for k in range(1, n):
        total = total + slots[k - 1]
    return total


def call(kernel, out_shape, inputs, scratch, collective, name, left=()):
    anywhere = pl.BlockSpec(memory_space=pl.ANY)
    outs = out_shape if isinstance(out_shape, tuple) else (out_shape,)
    specs = [anywhere if i - len(outs) in left else VM for i in range(len(outs))]
    return pl.pallas_call(
        kernel,
        out_shape=out_shape,
        in_specs=[anywhere if i in left else VM for i in range(len(inputs))],
        out_specs=tuple(specs) if isinstance(out_shape, tuple) else specs[0],
        scratch_shapes=scratch,
        compiler_params=pltpu.CompilerParams(collective_id=collective, has_side_effects=True),
        cost_estimate=pl.CostEstimate(flops=0, bytes_accessed=0, transcendentals=0),
        name=name,
    )(*inputs)


def shape(dims, dtype):
    return jax.ShapeDtypeStruct(dims, dtype)


def came_shape(payload, n_ctx):
    return shape((n_ctx - 1, payload.shape[0] // n_ctx, payload.shape[1]), payload.dtype)


def pair_of_sems(n):
    return [DMA((n,)), DMA((n,))]


def gather_tp(value, n_tp):
    rows, size = value.shape

    def kernel(own, full, *sems):
        greet([("tp", n_tp)])
        finish(gather_columns(own, full, "tp", n_tp, sems))

    return call(
        kernel, shape((rows, size * n_tp), value.dtype), (value,), pair_of_sems(n_tp), 1, "gather_tp"
    )


def first_norm(full, grad, gain, weights, quarter, n_tp, n_ctx):
    rows, width = full.shape
    with_quarter = quarter is not None

    def kernel(*refs):
        hid, grd, gn = refs[:3]
        refs = refs[3:]
        if with_quarter:
            wgts, refs = refs[: len(weights)], refs[len(weights) :]
            qrt, out, scale, grd_full, wgt_full = refs[:5]
            sems = refs[5:]
            greet([("tp", n_tp), ("ctx", n_ctx)])
        else:
            out, scale, grd_full = refs[:3]
            sems = refs[3:]
            greet([("tp", n_tp)])
        grads = gather_columns(grd, grd_full, "tp", n_tp, sems[0:2])

        def norm():
            values = hid[...].astype(F32)
            mean = jnp.sum(values * values, axis=-1, keepdims=True) * (1.0 / width)
            factor = lax.rsqrt(mean + EPS)
            scale[...] = jnp.broadcast_to(factor, scale.shape)
            out[...] = (values * factor * gn[0:1, :]).astype(BF)

        if with_quarter:
            half, inner = wgts[0].shape
            mine = lax.axis_index("fsdp")

            def work():
                norm()
                for i, wgt in enumerate(wgts):
                    wgt_full[
                        pl.ds(pl.multiple_of(mine * half, 16), half), pl.ds(i * inner, inner)
                    ] = wgt[...]

            gather_square(qrt, wgt_full, (1 - mine) * half, sems[2:4], work)
        else:
            norm()
        finish(grads)

    outs = [shape((rows, width), BF), shape((rows, 128), F32), shape((rows, width), BF)]
    inputs = [full, grad, gain]
    if with_quarter:
        outs.append(shape((2 * weights[0].shape[0], quarter.shape[1]), BF))
        inputs += [*weights, quarter]
    return call(
        kernel, tuple(outs), inputs, pair_of_sems(n_tp) + pair_of_sems(12), 7, "first_norm"
    )


def turn(values, cosine, sine):
    return values * cosine + pltpu.roll(values, HD // 2, axis=1) * sine


def softmax_rows(query, key, first_row):
    scores = mm_t(query, key) * (1.0 / math.sqrt(HD))
    rows = first_row + lax.broadcasted_iota(jnp.int32, scores.shape, 0)
    cols = lax.broadcasted_iota(jnp.int32, scores.shape, 1)
    scores = jnp.where(cols <= rows, scores, NEG)
    top = jnp.max(scores, axis=-1, keepdims=True)
    weights = jnp.exp(scores - top)
    return weights / jnp.sum(weights, axis=-1, keepdims=True)


def attention_forward(qkv, cosine, sine, n_ctx):
    rows = qkv.shape[0]
    width = qkv.shape[1] // 3
    heads = width // HD

    def kernel(prj, cs, sn, out, qry, full, own, *sems):
        greet([("ctx", n_ctx)])
        here = lax.axis_index("ctx")

        @pl.loop(0, heads)
        def _(h):
            own[:, columns(h, HD)] = turn(
                prj[:, columns(h + heads, HD)], cs[...], sn[...]
            ).astype(BF)
            own[:, columns(h + heads, HD)] = prj[:, columns(h + 2 * heads, HD)].astype(BF)

        def queries():
            @pl.loop(0, heads)
            def _(h):
                qry[:, columns(h, HD)] = turn(prj[:, columns(h, HD)], cs[...], sn[...]).astype(BF)

        gather_square(own, full, 0, sems, queries)

        @pl.loop(0, heads)
        def _(h):
            probs = softmax_rows(qry[:, columns(h, HD)], full[:, columns(h, HD)], here * rows)
            out[:, columns(h, HD)] = mm(
                probs.astype(BF), full[:, columns(h + heads, HD)]
            ).astype(BF)

    return call(
        kernel,
        (
            shape((rows, width), BF),
            shape((rows, width), BF),
            shape((rows * n_ctx, 2 * width), BF),
        ),
        (qkv, cosine, sine),
        [pltpu.VMEM((rows, 2 * width), BF)] + pair_of_sems(6 * width // 512),
        2,
        "attention_forward",
    )


def second_norm(part, hidden, gain, slabs, picks, router, onehot, names, n_tp, n_ctx):
    rows, size = hidden.shape
    width = size * n_tp
    experts = n_ctx

    def kernel(
        prt, hid, gn, slb, pck, rtr, one, nms,
        resid, scale, out, moved, tokens, slot_gates, gates, mix,
        slots, mine, sums, low, sent, own_gates, *sems
    ):
        greet([("tp", n_tp), ("ctx", n_ctx)])
        here = lax.axis_index("tp")
        copies = scatter_columns(prt, slots, "tp", n_tp, sems[0:2])
        others = [
            send(
                slb.at[pl.ds(k * CAP, CAP)], moved.at[pl.ds(k * CAP, CAP)],
                "ctx", n_ctx, k, sems[6:8],
            )
            for k in range(1, n_ctx)
        ]
        moved[0:CAP] = slb[0:CAP]
        total = prt[:, columns(here, size)].astype(F32)
        finish(copies)
        for k in range(1, n_tp):
            total = total + slots[k - 1].astype(F32)
        total = hid[...].astype(F32) + total
        resid[...] = total
        square = total_over(row_sums(total * total), mine, sums, "tp", n_tp, sems[2:4])
        factor = lax.rsqrt(as_column(square, eighth()) * (1.0 / width) + EPS)
        scale[...] = factor
        low[...] = (resid[...] * factor[:, 0:1] * gn[0:1, :]).astype(BF)
        copies = gather_columns(low, out, "tp", n_tp, sems[4:6])
        for step in range(n_tp):
            at = columns(peer("tp", n_tp, n_tp - step), size)
            if step:
                copies[step - 1].wait()
                block = out[:, at]
            else:
                block = low[...]
            sent[step] = mm(pck[...], block).astype(BF)
            tokens[0:CAP, at] = sent[step, 0:CAP]
            for k in (2, 3, 1):
                others.append(
                    remote(
                        sent.at[step, pl.ds(k * CAP, CAP)], tokens.at[pl.ds(k * CAP, CAP), at],
                        sems[8:10], step * n_ctx + k, {"ctx": peer("ctx", n_ctx, k)},
                    )
                )
        logits = mm_t(rtr[...].astype(BF), out[...])
        named = [jnp.sum(one[j] * logits, axis=0, keepdims=True) for j in range(2)]
        top = jnp.maximum(named[0], named[1])
        powers = [jnp.exp(value - top) for value in named]
        both = powers[0] + powers[1]
        gate = [value / both for value in powers]
        mixed = gate[0] * nms[0] + gate[1] * nms[1]
        mix[...] = mixed
        order = lax.broadcasted_iota(jnp.int32, (8, rows), 0)
        gates[...] = jnp.where(order == 0, gate[0], jnp.where(order == 1, gate[1], 0.0))
        own_gates[...] = jnp.zeros(own_gates.shape, F32)
        for k in range(experts):
            own_gates[k, :, 0:CAP] = lax.dot_general(
                jnp.broadcast_to(mixed[k : k + 1], (8, rows)),
                pck[k * CAP : (k + 1) * CAP].astype(F32),
                (((1,), (1,)), ((), ())),
                precision=lax.Precision.HIGHEST,
                preferred_element_type=F32,
            )
        slot_gates[0] = own_gates[0]
        for k in range(1, n_ctx):
            others.append(
                send(own_gates.at[k], slot_gates.at[k], "ctx", n_ctx, k, sems[10:12])
            )
        finish(others)

    return call(
        kernel,
        (
            shape((rows, size), F32),
            shape((rows, 128), F32),
            shape((rows, width), BF),
            shape(slabs.shape, BF),
            shape(slabs.shape, BF),
            shape((experts, 8, rows), F32),
            shape((8, rows), F32),
            shape((8, rows), F32),
        ),
        (part, hidden, gain, slabs, picks, router, onehot, names),
        [
            pltpu.VMEM((n_tp - 1, rows, size), BF),
            pltpu.VMEM((8, rows), F32),
            pltpu.VMEM((n_tp - 1, 8, rows), F32),
            pltpu.VMEM((rows, size), BF),
            pltpu.VMEM((n_tp, experts * CAP, size), BF),
            pltpu.VMEM((experts, 8, rows), F32),
        ]
        + pair_of_sems(n_tp) * 3
        + pair_of_sems(n_ctx)
        + pair_of_sems(n_tp * n_ctx)
        + pair_of_sems(n_ctx),
        3,
        "second_norm",
    )


def second_norm_back(
    acts, weights, dots, picks, gates, onehot, names, router, resid, scale, gain, grad, n_tp, n_ctx
):
    rows, size = resid.shape
    width = size * n_tp
    experts = n_ctx
    hidden = acts[0].shape[1]
    count = len(weights[0])
    part = weights[0][0].shape[0]

    def kernel(*refs):
        dga, dup, hid = refs[:3]
        wgt = [refs[3 + i * count : 3 + (i + 1) * count] for i in range(3)]
        refs = refs[3 + 3 * count :]
        dts, pck, gts, one, nms, rtr, rsd, scl, gn, grd = refs[:10]
        d_resid, low, d_gain, d_logits, out_back = refs[10:15]
        (
            drw, eo, buffer, back, back_dots, parts, slots, mine, sums, mine_two, sums_two, loads,
        ) = refs[15:27]
        sems = refs[27:]
        here = lax.axis_index("tp")
        first = lax.axis_index("fsdp")

        def load(which, rank, slot, lane):
            feature = rank * size
            inside = pl.ds(pl.multiple_of(lax.rem(feature, part), 16), size)
            target = buffer.at[slot, lane]
            if count == 1:
                pltpu.make_async_copy(
                    wgt[which][0].at[inside], target, loads.at[slot, lane]
                ).start()
                return
            own = feature // part == first

            @pl.when(own)
            def _():
                pltpu.make_async_copy(
                    wgt[which][0].at[inside], target, loads.at[slot, lane]
                ).start()

            @pl.when(jnp.logical_not(own))
            def _():
                pltpu.make_async_copy(
                    wgt[which][1].at[inside], target, loads.at[slot, lane]
                ).start()

        def loaded(which, slot, lane):
            pltpu.make_async_copy(
                wgt[which][0].at[pl.ds(0, size)], buffer.at[slot, lane], loads.at[slot, lane]
            ).wait()

        load(0, peer("tp", n_tp, 1), 0, 0)
        load(1, peer("tp", n_tp, 1), 0, 1)
        greet([("tp", n_tp), ("ctx", n_ctx)])
        small = []
        for k in range(1, n_ctx):
            small.append(
                send(dts.at[k], back_dots.at[k - 1], "ctx", n_ctx, n_ctx - k, sems[0:2])
            )

        def slab(k, rank, step):
            at = columns(rank, size)
            return described(
                drw.at[pl.ds(k * CAP, CAP), at], back.at[k - 1, :, at],
                sems[2:4], step * n_ctx + k - 1, {"ctx": peer("ctx", n_ctx, n_ctx - k)},
            )

        @pl.loop(0, n_tp)
        def _(step):
            rank = peer("tp", n_tp, step + 1)
            slot = lax.rem(step, 2)
            loaded(0, slot, 0)
            loaded(1, slot, 1)

            @pl.when(step + 1 < n_tp)
            def _():
                load(0, peer("tp", n_tp, step + 2), 1 - slot, 0)
                load(1, peer("tp", n_tp, step + 2), 1 - slot, 1)

            drw[:, columns(rank, size)] = (
                mm_t(dga[...], buffer[slot, 0]) + mm_t(dup[...], buffer[slot, 1])
            ).astype(BF)
            for k in (2, 3, 1):
                slab(k, rank, step).start()

        load(2, 0, 0, 0)

        @pl.loop(0, n_tp)
        def _(rank):
            slot = lax.rem(rank, 2)
            loaded(2, slot, 0)

            @pl.when(rank + 1 < n_tp)
            def _():
                load(2, rank + 1, 1 - slot, 0)

            eo[:, columns(rank, size)] = mm_t(hid[...], buffer[slot, 0]).astype(BF)

        moved = [
            send(
                eo.at[pl.ds(k * CAP, CAP)], out_back.at[pl.ds(k * CAP, CAP)],
                "ctx", n_ctx, n_ctx - k, sems[10:12],
            )
            for k in range(1, n_ctx)
        ]
        out_back[0:CAP] = eo[0:CAP]
        finish(small)
        order = lax.broadcasted_iota(jnp.int32, (8, rows), 0)
        own = jnp.zeros((8, rows), F32)
        for k in range(experts):
            by_slot = dts[0] if k == 0 else back_dots[k - 1]
            by_row = lax.dot_general(
                by_slot[:, 0:CAP],
                pck[k * CAP : (k + 1) * CAP].astype(F32),
                (((1,), (0,)), ((), ())),
                precision=lax.Precision.HIGHEST,
                preferred_element_type=F32,
            )
            own = own + jnp.where(order == k, by_row, 0.0)
        gate_grad = total_over(own, mine, sums, "tp", n_tp, sems[4:6])
        both = [jnp.sum(nms[j] * gate_grad, axis=0, keepdims=True) for j in range(2)]
        gate = [gts[j : j + 1, :] for j in range(2)]
        mean = gate[0] * both[0] + gate[1] * both[1]
        logits = sum(gate[j] * (both[j] - mean) * one[j] for j in range(2))
        d_logits[...] = logits
        copies = []
        for step in range(1, n_tp + 1):
            rank = peer("tp", n_tp, step)
            at = columns(rank, size)
            for k in (2, 3, 1):
                slab(k, rank, step - 1).wait()
            block = t_mm(pck[0:CAP], drw[0:CAP, at])
            for k in range(1, experts):
                block = block + t_mm(pck[k * CAP : (k + 1) * CAP], back[k - 1, :, at])
            if step < n_tp:
                parts[step - 1] = block.astype(BF)
                copies.append(
                    send(parts.at[step - 1], slots.at[step - 1], "tp", n_tp, step, sems[6:8])
                )
            else:
                total = block
        total = total + lax.dot_general(
            logits.astype(BF),
            rtr[...].astype(BF),
            (((0,), (0,)), ((), ())),
            preferred_element_type=F32,
        )
        finish(copies)
        for k in range(1, n_tp):
            total = total + slots[k - 1].astype(F32)
        factor = scl[:, 0:1]
        unit = rsd[...] * factor
        d_gain[...] = jnp.broadcast_to(jnp.sum(total * unit, axis=0, keepdims=True), d_gain.shape)
        gained = total * gn[0:1, :]
        d_resid[...] = gained
        dot = total_over(row_sums(unit * gained), mine_two, sums_two, "tp", n_tp, sems[8:10])
        dot = as_column(dot, eighth())[:, 0:1] * (1.0 / width)
        result = grd[...].astype(F32) + factor * (d_resid[...] - rsd[...] * factor * dot)
        d_resid[...] = result
        low[...] = result.astype(BF)
        finish(moved)

    flat = [array for group in weights for array in group]
    return call(
        kernel,
        (
            shape((rows, size), F32),
            shape((rows, size), BF),
            shape((8, size), F32),
            shape((8, rows), F32),
            shape((experts * CAP, width), BF),
        ),
        (*acts, *flat, dots, picks, gates, onehot, names, router, resid, scale, gain, grad),
        [
            pltpu.VMEM((experts * CAP, width), BF),
            pltpu.VMEM((experts * CAP, width), BF),
            pltpu.VMEM((2, 2, size, hidden), BF),
            pltpu.VMEM((n_ctx - 1, CAP, width), BF),
            pltpu.VMEM((n_ctx - 1, 8, rows), F32),
            pltpu.VMEM((n_tp - 1, rows, size), BF),
            pltpu.VMEM((n_tp - 1, rows, size), BF),
            pltpu.VMEM((8, rows), F32),
            pltpu.VMEM((n_tp - 1, 8, rows), F32),
            pltpu.VMEM((8, rows), F32),
            pltpu.VMEM((n_tp - 1, 8, rows), F32),
            DMA((2, 2)),
        ]
        + pair_of_sems(n_ctx)
        + pair_of_sems(n_tp * n_ctx)
        + pair_of_sems(n_tp) * 3
        + pair_of_sems(n_ctx),
        4,
        "second_norm_back",
        left=tuple(range(3, 3 + 3 * count)),
    )


def attention_backward(low, output_w, query, kv, cosine, sine, payload, n_tp, n_ctx):
    rows, size = low.shape
    width = size * n_tp
    inner = query.shape[1]
    heads = inner // HD
    scale = 1.0 / math.sqrt(HD)

    def kernel(
        lw, wgt, qry, full, cs, sn, pay, d_attn, d_qkv, came, dot, dqs, dkv, slots, last, both, total, *sems
    ):
        greet([("tp", n_tp), ("ctx", n_ctx)])
        here, beside, across = quad()
        beyond = lax.rem(beside + 2, 4)
        copies = gather_columns(lw, d_attn, "tp", n_tp, sems[2:4])
        moved = spread(pay, came, n_ctx, sems[4:6])
        for step in range(n_tp):
            rank = peer("tp", n_tp, n_tp - step)
            weights = wgt[pl.ds(pl.multiple_of(rank * size, 16), size), :]
            if step:
                copies[step - 1].wait()
                total[...] += mm(d_attn[:, columns(rank, size)], weights)
            else:
                total[...] = mm(lw[...], weights)
        dot[...] = total[...].astype(BF)

        @pl.loop(0, heads)
        def _(h):
            at, at_v = columns(h, HD), columns(h + heads, HD)
            probs = softmax_rows(qry[:, at], full[:, at], here * rows)
            d_probs = mm_t(dot[:, at], full[:, at_v])
            delta = jnp.sum(probs * d_probs, axis=-1, keepdims=True)
            d_scores = (probs * (d_probs - delta)).astype(BF)
            dqs[:, at] = mm(d_scores, full[:, at]) * scale
            dkv[:, at] = (t_mm(d_scores, qry[:, at]) * scale).astype(BF)
            dkv[:, at_v] = t_mm(probs.astype(BF), dot[:, at]).astype(BF)

        first = remote(dkv.at[stretch(beyond, rows), :], slots.at[0], sems, 0, {"ctx": beside})
        second = remote(dkv.at[stretch(beside, rows), :], slots.at[1], sems, 1, {"ctx": beside})
        first.wait()
        both[...] = (
            dkv[stretch(across, rows), :].astype(F32) + slots[0].astype(F32)
        ).astype(BF)
        third = remote(both, last, sems, 2, {"ctx": across})

        @pl.loop(0, heads)
        def _(h):
            d_qkv[:, columns(h, HD)] = turn(dqs[:, columns(h, HD)], cs[...], sn[...]).astype(BF)

        second.wait()
        third.wait()

        @pl.loop(0, heads)
        def _(h):
            at, at_v = columns(h, HD), columns(h + heads, HD)
            mine = stretch(here, rows)
            d_key = dkv[mine, at].astype(F32) + slots[1, :, at].astype(F32)
            d_key = d_key + last[:, at].astype(F32)
            d_qkv[:, columns(h + heads, HD)] = turn(d_key, cs[...], sn[...]).astype(BF)
            d_value = dkv[mine, at_v].astype(F32) + slots[1, :, at_v].astype(F32)
            d_value = d_value + last[:, at_v].astype(F32)
            d_qkv[:, columns(h + 2 * heads, HD)] = d_value.astype(BF)

        finish(moved)

    return call(
        kernel,
        (shape((rows, width), BF), shape((rows, 3 * inner), BF), came_shape(payload, n_ctx)),
        (low, output_w, query, kv, cosine, sine, payload),
        [
            pltpu.VMEM((rows, inner), BF),
            pltpu.VMEM((rows, inner), F32),
            pltpu.VMEM((rows * n_ctx, 2 * inner), BF),
            pltpu.VMEM((2, rows, 2 * inner), BF),
            pltpu.VMEM((rows, 2 * inner), BF),
            pltpu.VMEM((rows, 2 * inner), BF),
            pltpu.VMEM((rows, inner), F32),
        ]
        + pair_of_sems(3)
        + pair_of_sems(n_tp)
        + pair_of_sems(n_ctx),
        5,
        "attention_backward",
        left=(6, -1),
    )


def first_norm_back(part, hidden, scale, gain, d_resid, payload, n_tp, n_ctx):
    rows, size = hidden.shape
    width = size * n_tp

    def kernel(prt, hid, scl, gn, dr, pay, out, d_gain, came, slots, mine, sums, *sems):
        greet([("tp", n_tp), ("ctx", n_ctx)])
        here = lax.axis_index("tp")
        copies = scatter_columns(prt, slots, "tp", n_tp, sems[0:2])
        moved = spread(pay, came, n_ctx, sems[4:6])
        total = prt[:, columns(here, size)].astype(F32)
        finish(copies)
        for k in range(1, n_tp):
            total = total + slots[k - 1].astype(F32)
        factor = scl[:, 0:1]
        unit = hid[...].astype(F32) * factor
        d_gain[...] = jnp.broadcast_to(jnp.sum(total * unit, axis=0, keepdims=True), d_gain.shape)
        gained = total * gn[0:1, :]
        out[...] = gained
        dot = total_over(row_sums(unit * gained), mine, sums, "tp", n_tp, sems[2:4])
        dot = as_column(dot, eighth())[:, 0:1] * (1.0 / width)
        unit = hid[...].astype(F32) * factor
        out[...] = dr[...] + factor * (out[...] - unit * dot)
        finish(moved)

    return call(
        kernel,
        (shape((rows, size), F32), shape((8, size), F32), came_shape(payload, n_ctx)),
        (part, hidden, scale, gain, d_resid, payload),
        [
            pltpu.VMEM((n_tp - 1, rows, size), BF),
            pltpu.VMEM((8, rows), F32),
            pltpu.VMEM((n_tp - 1, 8, rows), F32),
        ]
        + pair_of_sems(n_tp) * 2
        + pair_of_sems(n_ctx),
        6,
        "first_norm_back",
        left=(5, -1),
    )


def weight_grads(parts, groups, small, payload, back, picks, mix, resid, n_tp, n_ctx):
    tokens, block_size = resid.shape
    experts = n_ctx
    rows = parts[0].shape[2]
    width = small.shape[1] * n_tp
    places = 2 * n_ctx
    cut = width // places
    total_columns = sum(size for _, _, size, _ in groups)

    def kernel(*refs):
        prts, refs = refs[: len(parts)], refs[len(parts) :]
        sml, pay, bck, pck, mx, rsd, out, small_out, block_out, came = refs[:10]
        sml_full, sml_slots, mixed, shares, share_slots = refs[10:15]
        refs = refs[15:]
        scratch, sems = refs[: 5 * len(groups)], refs[5 * len(groups) :]
        barrier = pltpu.get_barrier_semaphore()
        here, beside, across = quad()
        beyond = lax.rem(beside + 2, 4)
        mine = lax.axis_index("fsdp")
        other = 1 - mine
        place = mine * n_ctx + here
        others = []
        for i in range(1, places):
            to = lax.rem(place + i, places)
            others.append((to, {"fsdp": to // n_ctx, "ctx": lax.rem(to, n_ctx)}))
        ahead = [{"tp": peer("tp", n_tp, k)} for k in range(1, n_tp)]
        for device in ahead + [device for _, device in others]:
            pl.semaphore_signal(barrier, inc=1, device_id=device, device_id_type=MESH)
        pl.semaphore_wait(barrier, n_tp - 1 + places - 1)
        gathers = gather_columns(sml, sml_full, "tp", n_tp, sems[0:2])
        moved = spread(pay, came, n_ctx, sems[4:6], (2,))
        moves = []
        for g, (which, first, size, ctx_first) in enumerate(groups):
            near = scratch[5 * g]
            at = pl.ds(first, size)
            far_here = (mine, beyond) if ctx_first else (other, beside)
            blocks = [(other, beyond), far_here]
            blocks += [(other, beside) if ctx_first else (mine, beyond), (mine, beside)]
            moves.append(
                [
                    remote(
                        prts[which].at[rank, column, :, at], near.at[i],
                        sems[8 + 6 * g : 10 + 6 * g], i, {"ctx": beside},
                    )
                    for i, (rank, column) in enumerate(blocks)
                ]
            )
        finish(gathers)
        totals = [
            remote(sml_full.at[:, columns(to, cut)], sml_slots.at[i], sems[2:4], i, device)
            for i, (to, device) in enumerate(others)
        ]

        def chip(g, i, rank, column):
            which, first, size, _ = groups[g]
            moves[g][i].wait()
            value = prts[which][rank, column, :, first : first + size].astype(F32)
            return value + scratch[5 * g][i].astype(F32)

        hops = []
        for g, (_, _, _, ctx_first) in enumerate(groups):
            two, far = scratch[5 * g + 1 : 5 * g + 3]
            to = {"ctx": across} if ctx_first else {"fsdp": other}
            pair = [(other, across), (mine, across) if ctx_first else (other, here)]
            sent = []
            for i, (rank, column) in enumerate(pair):
                two[i] = chip(g, i, rank, column).astype(BF)
                sent.append(
                    remote(two.at[i], far.at[i], sems[10 + 6 * g : 12 + 6 * g], i, to)
                )
            hops.append(sent)
        moved += spread(pay, came, n_ctx, sems[4:6], (1, 3))
        order = lax.broadcasted_iota(jnp.int32, (8, 128), 0)
        for k in range(experts):
            mixed[k] = as_column(mx[...], jnp.where(order == k, 1.0, 0.0))
        given = []
        for step in range(1, n_tp + 1):
            at = columns(peer("tp", n_tp, step), block_size)
            block = jnp.zeros((tokens, block_size), F32)
            for k in range(experts):
                block = block + mixed[k][:, 0:1] * t_mm(
                    pck[k * CAP : (k + 1) * CAP], bck[k * CAP : (k + 1) * CAP, at]
                )
            if step < n_tp:
                shares[step - 1] = block.astype(BF)
                given.append(
                    send(shares.at[step - 1], share_slots.at[step - 1], "tp", n_tp, step, sems[6:8])
                )
            else:
                moe = rsd[...] + block
        lasts = []
        for g, (_, _, _, ctx_first) in enumerate(groups):
            far, one, last = scratch[5 * g + 2], scratch[5 * g + 3], scratch[5 * g + 4]
            value = chip(g, 2, *((other, here) if ctx_first else (mine, across)))
            hops[g][0].wait()
            one[...] = (value + far[0].astype(F32)).astype(BF)
            to = {"fsdp": other} if ctx_first else {"ctx": across}
            lasts.append(remote(one, last, sems[12 + 6 * g : 14 + 6 * g], 0, to))
        start = 0
        for g, (_, _, size, _) in enumerate(groups):
            far = scratch[5 * g + 2]
            value = chip(g, 3, mine, here)
            hops[g][1].wait()
            out[:, start : start + size] = value + far[1].astype(F32)
            start += size
        finish(totals)
        sums = sml_full[:, columns(place, cut)]
        for i in range(places - 1):
            sums = sums + sml_slots[i]
        small_out[...] = sums
        finish(given)
        for k in range(1, n_tp):
            moe = moe + share_slots[k - 1].astype(F32)
        block_out[...] = moe.astype(BF)
        start = 0
        for g, (_, _, size, _) in enumerate(groups):
            lasts[g].wait()
            at = pl.ds(start, size)
            out[:, at] = out[:, at] + scratch[5 * g + 4][...].astype(F32)
            start += size
        finish(moved)

    buffers = [
        pltpu.VMEM((8, width), F32),
        pltpu.VMEM((places - 1, 8, cut), F32),
        pltpu.VMEM((experts, tokens, 128), F32),
        pltpu.VMEM((n_tp - 1, tokens, block_size), BF),
        pltpu.VMEM((n_tp - 1, tokens, block_size), BF),
    ]
    sems = pair_of_sems(n_tp) + pair_of_sems(places) + pair_of_sems(n_ctx) + pair_of_sems(n_tp)
    for _, _, size, _ in groups:
        buffers += [
            pltpu.VMEM((4, rows, size), BF),
            pltpu.VMEM((2, rows, size), BF),
            pltpu.VMEM((2, rows, size), BF),
            pltpu.VMEM((rows, size), BF),
            pltpu.VMEM((rows, size), BF),
        ]
        sems += pair_of_sems(4) + pair_of_sems(2) + pair_of_sems(1)
    return call(
        kernel,
        (
            shape((rows, total_columns), F32),
            shape((8, cut), F32),
            shape((tokens, block_size), BF),
            came_shape(payload, n_ctx),
        ),
        (*parts, small, payload, back, picks, mix, resid),
        buffers + sems,
        10,
        "weight_grads",
        left=(len(parts) + 1, -1),
    )


def experts_out(back, picks, mix, resid, payload, n_tp, n_ctx):
    rows, size = resid.shape
    experts = n_ctx

    def kernel(bck, pck, mx, rsd, pay, out, came, part, slots, *sems):
        greet([("tp", n_tp), ("ctx", n_ctx)])
        moved = spread(pay, came, n_ctx, sems[2:4])
        order = lax.broadcasted_iota(jnp.int32, (8, 128), 0)
        gate = [as_column(mx[...], jnp.where(order == k, 1.0, 0.0)) for k in range(experts)]
        copies = []
        for step in range(1, n_tp + 1):
            at = columns(peer("tp", n_tp, step), size)
            block = jnp.zeros((rows, size), F32)
            for k in range(experts):
                block = block + gate[k][:, 0:1] * t_mm(
                    pck[k * CAP : (k + 1) * CAP], bck[k * CAP : (k + 1) * CAP, at]
                )
            if step < n_tp:
                part[step - 1] = block.astype(BF)
                copies.append(
                    send(part.at[step - 1], slots.at[step - 1], "tp", n_tp, step, sems[0:2])
                )
            else:
                total = rsd[...] + block
        finish(copies)
        for k in range(1, n_tp):
            total = total + slots[k - 1].astype(F32)
        out[...] = total.astype(BF)
        finish(moved)

    return call(
        kernel,
        (shape((rows, size), BF), came_shape(payload, n_ctx)),
        (back, picks, mix, resid, payload),
        [
            pltpu.VMEM((n_tp - 1, rows, size), BF),
            pltpu.VMEM((n_tp - 1, rows, size), BF),
        ]
        + pair_of_sems(n_tp)
        + pair_of_sems(n_ctx),
        9,
        "experts_out",
        left=(4, -1),
    )


def place_pieces(own, came, n_ctx):
    rows, size = own.shape
    tile = 64 if rows % 64 == 0 else rows

    def kernel(mine, others, out):
        here = lax.axis_index("ctx")
        out[here] = mine[...].astype(F32)
        for k in range(1, n_ctx):
            out[lax.rem(here + n_ctx - k, n_ctx)] = others[k - 1].astype(F32)

    return pl.pallas_call(
        kernel,
        grid=(rows // tile,),
        out_shape=shape((n_ctx, rows, size), F32),
        in_specs=[
            pl.BlockSpec((tile, size), lambda i: (i, 0)),
            pl.BlockSpec((n_ctx - 1, tile, size), lambda i: (0, i, 0)),
        ],
        out_specs=pl.BlockSpec((n_ctx, tile, size), lambda i: (0, i, 0)),
        cost_estimate=pl.CostEstimate(
            flops=0, bytes_accessed=6 * n_ctx * rows * size, transcendentals=0
        ),
        name="place_pieces",
    )(own, came)


def after(value, *needed):
    return lax.optimization_barrier((value, *needed))[0]


def shards(
    hidden_in,
    out_grad,
    attn_gain,
    w_query,
    w_key,
    w_value,
    w_output,
    ffn_gain,
    w_router,
    w_gate,
    w_up,
    w_down,
    routes,
):
    rows_here, width_tp = hidden_in.shape
    here_tp = lax.axis_index("tp")
    here_ctx = lax.axis_index("ctx")
    here_fsdp = lax.axis_index("fsdp")
    n_fsdp = lax.axis_size("fsdp")
    n_ctx = lax.axis_size("ctx")
    n_tp = lax.axis_size("tp")
    experts = w_gate.shape[0]
    assert experts == n_ctx == 4
    width = width_tp * n_tp
    part = width // n_fsdp
    pair = n_fsdp == 2
    heads_width = w_query.shape[1]

    def swap_fsdp(value):
        return lax.ppermute(value, "fsdp", [(0, 1), (1, 0)])

    def other_parts(weight):
        if pair:
            return [weight, swap_fsdp(weight)]
        return [lax.all_gather(weight, "fsdp", axis=0, tiled=True)]

    def split(values):
        if pair:
            return [
                lax.dynamic_slice_in_dim(values, here_fsdp * part, part, 1),
                lax.dynamic_slice_in_dim(values, (1 - here_fsdp) * part, part, 1),
            ]
        return [values]

    def join(pieces):
        if pair:
            first = here_fsdp == 0
            return jnp.concatenate(
                [jnp.where(first, pieces[0], pieces[1]), jnp.where(first, pieces[1], pieces[0])],
                axis=1,
            )
        return pieces[0]

    def into(values, weights):
        return sum(mm(x, w) for x, w in zip(split(values), weights))

    def back(values, weights):
        return join([mm_t(values, w) for w in weights])

    def my_features(values):
        return lax.dynamic_slice_in_dim(values, here_tp * width_tp, width_tp, values.ndim - 1)

    attn_w = (w_query, w_key, w_value, w_output)
    small = jnp.concatenate(
        [attn_gain[None], ffn_gain[None], w_router.T, jnp.zeros((2, part), BF)], axis=0
    )
    if pair:
        quarter = part // n_ctx
        own_quarter = jnp.concatenate(
            [lax.dynamic_slice_in_dim(w, here_ctx * quarter, quarter, 0) for w in attn_w], axis=1
        )
        other_quarter = swap_fsdp(own_quarter)
        other_small = swap_fsdp(small)
        small_full = join([small, other_small]).astype(F32)
    else:
        other_quarter = None
        small_full = lax.all_gather(small, "fsdp", axis=1, tiled=True).astype(F32)
    inputs_full = gather_tp(hidden_in, n_tp)

    def expert_parts(weights, ready):
        rank, _ = lax.optimization_barrier((here_ctx, ready))
        return other_parts(lax.dynamic_index_in_dim(weights, rank, 0, False))

    gate_w = expert_parts(w_gate, small)
    up_w = expert_parts(w_up, inputs_full)
    down_w = expert_parts(w_down, inputs_full)
    small_here = my_features(small_full)
    gain_one_here = jnp.broadcast_to(small_here[0:1], small_here.shape)
    gain_two_here = jnp.broadcast_to(small_here[1:2], small_here.shape)
    nothing = [(0, 8 - experts), (0, 0)]
    router_full = jnp.pad(small_full[2 : 2 + experts], nothing)
    router_here = jnp.pad(small_here[2 : 2 + experts], nothing)

    relative = (jnp.arange(experts, dtype=jnp.int32) + here_ctx) % experts
    numbers = jnp.arange(8, dtype=jnp.int32)
    onehot = (routes.T[:, None, :] == numbers[None, :, None]).astype(F32)
    named = (routes.T[:, None, :] == relative[None, :, None]).astype(F32)
    names = jnp.pad(named, [(0, 0)] + nothing)
    chosen = jnp.sum(named, axis=0)
    earlier = jnp.triu(jnp.ones((rows_here, rows_here), BF), 1)
    slot_of = mm(chosen.astype(BF), earlier).astype(jnp.int32)
    slots = jnp.arange(CAP, dtype=jnp.int32)
    picks = (slot_of[:, None, :] == slots[None, :, None]) & (chosen[:, None, :] > 0)
    picks = picks.astype(BF).reshape(experts * CAP, rows_here)

    gathered = first_norm(
        inputs_full, out_grad, small_full, attn_w, other_quarter, n_tp, n_ctx
    )
    normed_one, scale_one, grad_full = gathered[:3]
    if pair:
        attn_full = gathered[3]
    else:
        attn_full = lax.all_gather(
            jnp.concatenate(attn_w, axis=1), "fsdp", axis=0, tiled=True
        )
    qkv_w = attn_full[:, : 3 * heads_width]
    output_w = attn_full[:, 3 * heads_width :]
    positions = here_ctx * rows_here + jnp.arange(rows_here, dtype=jnp.int32)
    cosine, sine = rotary_tables(positions)
    attended, query, kv = attention_forward(mm(normed_one, qkv_w), cosine, sine, n_ctx)
    resid, scale_two, normed_two, grad_rows, token_rows, slot_gates, gates, mix = second_norm(
        mm_t(attended, output_w).astype(BF),
        hidden_in,
        gain_two_here,
        mm(picks, grad_full).astype(BF),
        picks,
        router_full,
        onehot,
        names,
        n_tp,
        n_ctx,
    )
    gate_rows = slot_gates[:, 0, :CAP].reshape(experts * CAP, 1)

    gate_act = into(token_rows, gate_w)
    up_act = into(token_rows, up_w)
    sigma_act = jax.nn.sigmoid(gate_act)
    hidden_act = (gate_act * sigma_act * up_act).astype(BF)
    d_result = (gate_rows * grad_rows.astype(F32)).astype(BF)

    def grad_send(left, right):
        halves = split(left)
        if pair:
            away = t_mm(halves[1], right).astype(BF)
            return halves[0], right, away, swap_fsdp(away)
        return halves[0], right, None, None

    def grad_sum(mine, right, away, other):
        if pair:
            return (t_mm(mine, right) + other.astype(F32)).astype(BF)
        return lax.psum_scatter(
            t_mm(mine, right).astype(BF), "fsdp", scatter_dimension=0, tiled=True
        )

    def grad_place(mine, came):
        cut = part // n_ctx
        own = lax.dynamic_slice_in_dim(mine, here_ctx * cut, cut, 0)
        return place_pieces(own, came, n_ctx)

    down_sent = grad_send(d_result, hidden_act)
    if pair:
        grad_rows = after(grad_rows, down_sent[2])
    d_hidden = into(grad_rows, down_w)
    gate_dot = jnp.sum(hidden_act.astype(F32) * d_hidden, axis=-1).reshape(experts, CAP)
    gate_dot = jnp.broadcast_to(
        jnp.pad(gate_dot, [(0, 0), (0, rows_here - CAP)])[:, None, :], (experts, 8, rows_here)
    )
    d_hidden = gate_rows * d_hidden
    d_gate_act = (d_hidden * up_act * sigma_act * (1.0 + gate_act * (1.0 - sigma_act))).astype(BF)
    d_up_act = (d_hidden * gate_act * sigma_act).astype(BF)
    gate_sent = grad_send(token_rows, d_gate_act)

    acts = (d_gate_act, d_up_act, hidden_act)
    if pair:
        acts = lax.optimization_barrier((*acts, gate_sent[2]))[:3]
    d_resid, d_attn_here, gain_two_part, d_logits, returned = second_norm_back(
        acts,
        (gate_w, up_w, down_w),
        gate_dot,
        picks,
        gates,
        onehot,
        names,
        router_here,
        resid,
        scale_two,
        gain_two_here,
        out_grad,
        n_tp,
        n_ctx,
    )
    if pair:
        up_sent = grad_send(token_rows, after(d_up_act, d_resid))
        d_attn_here, *down_sent = lax.optimization_barrier((d_attn_here, *down_sent))
        d_attn_here = after(d_attn_here, up_sent[2])
    else:
        up_sent = grad_send(token_rows, d_up_act)
    grad_down = grad_sum(*down_sent)

    d_attn, d_qkv, down_came = attention_backward(
        d_attn_here, output_w, query, kv, cosine, -sine, grad_down, n_tp, n_ctx
    )
    if pair:
        d_qkv, *gate_sent = lax.optimization_barrier((d_qkv, *gate_sent))
    grad_gate = grad_sum(*gate_sent)
    in_grad, gain_one_part, gate_came = first_norm_back(
        mm_t(d_qkv, qkv_w).astype(BF),
        hidden_in,
        scale_one,
        gain_one_here,
        d_resid,
        grad_gate,
        n_tp,
        n_ctx,
    )
    if pair:
        in_grad, *up_sent = lax.optimization_barrier((in_grad, *up_sent))
    grad_up = grad_sum(*up_sent)

    grad_qkv = t_mm(normed_one, d_qkv).astype(BF)
    grad_output = t_mm(d_attn, attended).astype(BF)
    small_part = jnp.concatenate(
        [
            gain_one_part[:1],
            gain_two_part[:1],
            mm(d_logits[:experts].astype(BF), my_features(normed_two)),
            jnp.zeros((6 - experts, width_tp), F32),
        ],
        axis=0,
    )
    mixing = (returned, picks, mix, resid)
    if pair:
        grad_attn, small_grad, block_out, up_came = weight_grads(
            [value.reshape(n_fsdp, n_ctx, quarter, -1) for value in (grad_qkv, grad_output)],
            [
                (0, 0, 2 * heads_width, True),
                (0, 2 * heads_width, heads_width, False),
                (1, 0, heads_width, False),
            ],
            small_part,
            grad_up,
            *mixing,
            n_tp,
            n_ctx,
        )
    else:
        scatter = partial(
            lax.psum_scatter, axis_name=("fsdp", "ctx"), scatter_dimension=0, tiled=True
        )
        grad_attn = scatter(jnp.concatenate([grad_qkv, grad_output], axis=1)).astype(F32)
        small_grad = lax.all_gather(small_part, "tp", axis=1, tiled=True)
        small_grad = scatter(small_grad.T).T
        block_out, up_came = experts_out(*mixing, grad_up, n_tp, n_ctx)
    grad_down = grad_place(grad_down, down_came)
    grad_gate = grad_place(grad_gate, gate_came)
    grad_up = grad_place(grad_up, up_came)
    return (
        block_out,
        in_grad,
        small_grad[0],
        grad_attn[:, :heads_width],
        grad_attn[:, heads_width : 2 * heads_width],
        grad_attn[:, 2 * heads_width : 3 * heads_width],
        grad_attn[:, 3 * heads_width :],
        small_grad[1],
        small_grad[2 : 2 + experts].T,
        grad_gate,
        grad_up,
        grad_down,
    )


def solution(mesh):
    rows = ("fsdp", "ctx")
    placed = (
        P(rows, "tp"),
        P(rows, "tp"),
        P("fsdp"),
        P("fsdp", "tp"),
        P("fsdp", "tp"),
        P("fsdp", "tp"),
        P("fsdp", "tp"),
        P("fsdp"),
        P("fsdp", None),
        P(None, "fsdp", "tp"),
        P(None, "fsdp", "tp"),
        P(None, "fsdp", "tp"),
        P(rows, None),
    )
    return jax.shard_map(
        shards,
        mesh=mesh,
        in_specs=placed,
        out_specs=(
            P(rows, "tp"),
            P(rows, "tp"),
            P(rows),
            P(rows, "tp"),
            P(rows, "tp"),
            P(rows, "tp"),
            P(rows, "tp"),
            P(rows),
            P(rows, None),
            P(None, rows, "tp"),
            P(None, rows, "tp"),
            P(None, rows, "tp"),
        ),
        check_vma=False,
    )
```

```python
from functools import partial
import math

import jax
import jax.numpy as jnp
from jax import lax
from jax.experimental import pallas as pl
from jax.experimental.pallas import tpu as pltpu
from jax.sharding import PartitionSpec as P

HD = 128
CAP = 160


EPS = 1e-05
THETA = 10000.0
NEG = -1e30
BF = jnp.bfloat16
F32 = jnp.float32


def mm(left, right):
    return jnp.dot(left, right, preferred_element_type=F32)


def mm_t(left, right):
    return lax.dot_general(left, right, (((1,), (1,)), ((), ())), preferred_element_type=F32)


def t_mm(left, right):
    return lax.dot_general(left, right, (((0,), (0,)), ((), ())), preferred_element_type=F32)


def rotary_tables(positions):
    half_size = HD // 2
    frequency = THETA ** (-(jnp.arange(half_size, dtype=F32) * 2.0 / HD))
    angles = positions.astype(F32)[:, None] * frequency[None, :]
    cosine, sine = jnp.cos(angles), jnp.sin(angles)
    return jnp.concatenate([cosine, cosine], axis=1), jnp.concatenate([-sine, sine], axis=1)


MESH = pl.DeviceIdType.MESH
VM = pl.BlockSpec(memory_space=pltpu.VMEM)
DMA = pltpu.SemaphoreType.DMA


def peer(axis, n, k):
    return lax.rem(lax.axis_index(axis) + k, n)


def greet(groups):
    barrier = pltpu.get_barrier_semaphore()
    for axis, n in groups:
        for k in range(1, n):
            pl.semaphore_signal(
                barrier, inc=1, device_id={axis: peer(axis, n, k)}, device_id_type=MESH
            )
    pl.semaphore_wait(barrier, sum(n - 1 for _, n in groups))


def described(source, target, sems, i, to):
    return pltpu.make_async_remote_copy(
        src_ref=source,
        dst_ref=target,
        send_sem=sems[0].at[i],
        recv_sem=sems[1].at[i],
        device_id=to,
        device_id_type=MESH,
    )


def remote(source, target, sems, i, to):
    copy = described(source, target, sems, i, to)
    copy.start()
    return copy


def send(source, target, axis, n, k, sems):
    return remote(source, target, sems, k - 1, {axis: peer(axis, n, k)})


def columns(n, size):
    return pl.ds(pl.multiple_of(n * size, 128), size)


def stretch(n, size):
    return pl.ds(pl.multiple_of(n * size, 16), size)


def gather_columns(own, full, axis, n, sems):
    size = own.shape[1]
    place = full.at[:, columns(lax.axis_index(axis), size)]
    copies = [send(own, place, axis, n, k, sems) for k in range(1, n)]
    place[...] = own[...]
    return copies


def scatter_columns(part, slots, axis, n, sems):
    size = slots.shape[2]
    return [
        send(part.at[:, columns(peer(axis, n, k), size)], slots.at[k - 1], axis, n, k, sems)
        for k in range(1, n)
    ]


def finish(copies):
    for copy in copies:
        copy.wait()


def spread(mine, out, n_ctx, sems, order=(2, 1, 3)):
    cut = mine.shape[0] // n_ctx
    return [
        send(mine.at[stretch(peer("ctx", n_ctx, k), cut), :], out.at[k - 1], "ctx", n_ctx, k, sems)
        for k in order
    ]


def quad():
    here = lax.axis_index("ctx")
    return here, here + 1 - 2 * lax.rem(here, 2), lax.rem(here + 2, 4)


def gather_square(own, places, sems, between, local=None):
    cuts = own.shape[1] // 512
    here, beside, across = quad()
    first, second, third = [], [], []
    for i in range(cuts):
        piece = own.at[:, pl.ds(i * 512, 512)]
        first.append(remote(piece, places(here, i), sems, 3 * i, {"ctx": across}))
        second.append(remote(piece, places(here, i), sems, 3 * i + 1, {"ctx": beside}))
        if local is None:
            places(here, i)[...] = piece[...]
        else:
            pltpu.make_async_copy(piece, places(here, i), local.at[i]).start()
    between()
    for i in range(cuts):
        first[i].wait()
        third.append(
            remote(places(across, i), places(across, i), sems, 3 * i + 2, {"ctx": beside})
        )
    finish(second)
    finish(third)
    if local is not None:
        for i in range(cuts):
            piece = own.at[:, pl.ds(i * 512, 512)]
            pltpu.make_async_copy(piece, places(here, i), local.at[i]).wait()


def row_sums(values):
    ones = jnp.ones((8, values.shape[1]), F32)
    return lax.dot_general(
        ones,
        values,
        (((1,), (1,)), ((), ())),
        precision=lax.Precision.HIGHEST,
        preferred_element_type=F32,
    )


def as_column(rows, weight):
    return lax.dot_general(
        rows,
        weight,
        (((0,), (0,)), ((), ())),
        precision=lax.Precision.HIGHEST,
        preferred_element_type=F32,
    )


def eighth():
    return jnp.full((8, 128), 0.125, F32)


def total_over(sums, mine, slots, axis, n, sems):
    mine[...] = sums
    copies = [send(mine, slots.at[k - 1], axis, n, k, sems) for k in range(1, n)]
    finish(copies)
    total = sums
    for k in range(1, n):
        total = total + slots[k - 1]
    return total


def call(kernel, out_shape, inputs, scratch, collective, name, left=()):
    anywhere = pl.BlockSpec(memory_space=pl.ANY)
    outs = out_shape if isinstance(out_shape, tuple) else (out_shape,)
    specs = [anywhere if i - len(outs) in left else VM for i in range(len(outs))]
    return pl.pallas_call(
        kernel,
        out_shape=out_shape,
        in_specs=[anywhere if i in left else VM for i in range(len(inputs))],
        out_specs=tuple(specs) if isinstance(out_shape, tuple) else specs[0],
        scratch_shapes=scratch,
        compiler_params=pltpu.CompilerParams(collective_id=collective, has_side_effects=True),
        cost_estimate=pl.CostEstimate(flops=0, bytes_accessed=0, transcendentals=0),
        name=name,
    )(*inputs)


def shape(dims, dtype):
    return jax.ShapeDtypeStruct(dims, dtype)


def came_shape(payload, n_ctx):
    return shape((n_ctx - 1, payload.shape[0] // n_ctx, payload.shape[1]), payload.dtype)


def pair_of_sems(n):
    return [DMA((n,)), DMA((n,))]


def gather_tp(value, stacks, n_tp):
    rows, size = value.shape
    many = len(stacks)
    member = stacks[0].shape[1:]

    def kernel(own, *refs):
        stk, full, outs = refs[:many], refs[many], refs[many + 1 : 2 * many + 1]
        held, loads, stores = refs[2 * many + 1 : 2 * many + 4]
        sems = refs[2 * many + 4 :]
        here = lax.axis_index("ctx")
        into = [
            pltpu.make_async_copy(stk[i].at[here], held.at[i], loads.at[i]) for i in range(many)
        ]
        away = [pltpu.make_async_copy(held.at[i], outs[i], stores.at[i]) for i in range(many)]
        for copy in into:
            copy.start()
        greet([("tp", n_tp)])
        copies = gather_columns(own, full, "tp", n_tp, sems)
        for i in range(many):
            into[i].wait()
            away[i].start()
        finish(copies)
        finish(away)

    return call(
        kernel,
        (
            shape((rows, size * n_tp), value.dtype),
            *(shape(member, stack.dtype) for stack in stacks),
        ),
        (value, *stacks),
        [pltpu.VMEM((many, *member), BF), DMA((many,)), DMA((many,))] + pair_of_sems(n_tp),
        1,
        "gather_tp",
        left=tuple(range(1, many + 1)) + tuple(range(-many, 0)),
    )


def first_norm(full, grad, gain, weights, quarter, n_tp, n_ctx):
    rows, width = full.shape
    with_quarter = quarter is not None

    def kernel(*refs):
        hid, grd, gn = refs[:3]
        refs = refs[3:]
        if with_quarter:
            wgts, refs = refs[: len(weights)], refs[len(weights) :]
            qrt, out, scale, grd_full, many_full, last_full, held, local, loads, stores = refs[:10]
            sems = refs[10:]
            half, inner = wgts[0].shape
            last = len(wgts) - 1
            mine = lax.axis_index("fsdp")

            def target(i, first_row, count):
                at = pl.ds(pl.multiple_of(first_row, 16), count)
                if i == last:
                    return last_full.at[at, :]
                return many_full.at[at, pl.ds(i * inner, inner)]

            into = [
                pltpu.make_async_copy(wgts[i], held.at[i], loads.at[i]) for i in range(len(wgts))
            ]
            away = [
                pltpu.make_async_copy(held.at[i], target(i, mine * half, half), stores.at[i])
                for i in range(len(wgts))
            ]
            for copy in into:
                copy.start()
            greet([("tp", n_tp), ("ctx", n_ctx)])
        else:
            out, scale, grd_full = refs[:3]
            sems = refs[3:]
            greet([("tp", n_tp)])
        grads = gather_columns(grd, grd_full, "tp", n_tp, sems[0:2])

        def norm():
            values = hid[...].astype(F32)
            mean = jnp.sum(values * values, axis=-1, keepdims=True) * (1.0 / width)
            factor = lax.rsqrt(mean + EPS)
            scale[...] = jnp.broadcast_to(factor, scale.shape)
            out[...] = (values * factor * gn[0:1, :]).astype(BF)

        if with_quarter:
            count = qrt.shape[0]

            def work():
                for i in range(len(wgts)):
                    into[i].wait()
                    away[i].start()
                norm()

            def places(rank, i):
                return target(i, (1 - mine) * half + rank * count, count)

            gather_square(qrt, places, sems[2:4], work, local)
            finish(away)
        else:
            norm()
        finish(grads)

    outs = [shape((rows, width), BF), shape((rows, 128), F32), shape((rows, width), BF)]
    inputs = [full, grad, gain]
    scratch, left = [], ()
    if with_quarter:
        half, inner = weights[0].shape
        many = len(weights)
        assert inner == 512
        outs.append(shape((2 * half, (many - 1) * inner), BF))
        outs.append(shape((2 * half, inner), BF))
        inputs += [*weights, quarter]
        scratch = [pltpu.VMEM((many, half, inner), BF), DMA((many,)), DMA((many,)), DMA((many,))]
        left = tuple(range(3, 3 + many)) + (-2, -1)
    return call(
        kernel,
        tuple(outs),
        inputs,
        scratch + pair_of_sems(n_tp) + pair_of_sems(12),
        7,
        "first_norm",
        left=left,
    )


def turn(values, cosine, sine):
    return values * cosine + pltpu.roll(values, HD // 2, axis=1) * sine


def softmax_rows(query, key, first_row):
    scores = mm_t(query, key) * (1.0 / math.sqrt(HD))
    rows = first_row + lax.broadcasted_iota(jnp.int32, scores.shape, 0)
    cols = lax.broadcasted_iota(jnp.int32, scores.shape, 1)
    scores = jnp.where(cols <= rows, scores, NEG)
    top = jnp.max(scores, axis=-1, keepdims=True)
    weights = jnp.exp(scores - top)
    return weights / jnp.sum(weights, axis=-1, keepdims=True)


def attention_forward(qkv, cosine, sine, n_ctx):
    rows = qkv.shape[0]
    width = qkv.shape[1] // 3
    heads = width // HD

    def kernel(prj, cs, sn, out, qry, full, own, *sems):
        greet([("ctx", n_ctx)])
        here = lax.axis_index("ctx")

        @pl.loop(0, heads)
        def _(h):
            own[:, columns(h, HD)] = turn(
                prj[:, columns(h + heads, HD)], cs[...], sn[...]
            ).astype(BF)
            own[:, columns(h + heads, HD)] = prj[:, columns(h + 2 * heads, HD)].astype(BF)

        def queries():
            @pl.loop(0, heads)
            def _(h):
                qry[:, columns(h, HD)] = turn(prj[:, columns(h, HD)], cs[...], sn[...]).astype(BF)

        def places(rank, i):
            return full.at[stretch(rank, rows), pl.ds(i * 512, 512)]

        gather_square(own, places, sems, queries)

        @pl.loop(0, heads)
        def _(h):
            probs = softmax_rows(qry[:, columns(h, HD)], full[:, columns(h, HD)], here * rows)
            out[:, columns(h, HD)] = mm(
                probs.astype(BF), full[:, columns(h + heads, HD)]
            ).astype(BF)

    return call(
        kernel,
        (
            shape((rows, width), BF),
            shape((rows, width), BF),
            shape((rows * n_ctx, 2 * width), BF),
        ),
        (qkv, cosine, sine),
        [pltpu.VMEM((rows, 2 * width), BF)] + pair_of_sems(6 * width // 512),
        2,
        "attention_forward",
    )


def second_norm(part, hidden, gain, slabs, picks, router, onehot, names, n_tp, n_ctx):
    rows, size = hidden.shape
    width = size * n_tp
    experts = n_ctx

    def kernel(
        prt, hid, gn, slb, pck, rtr, one, nms,
        resid, scale, out, moved, tokens, slot_gates, gates, mix,
        slots, mine, sums, mine_two, sums_two, low, sent, own_gates, *sems
    ):
        greet([("tp", n_tp), ("ctx", n_ctx)])
        here = lax.axis_index("tp")
        copies = scatter_columns(prt, slots, "tp", n_tp, sems[0:2])
        others = [
            send(
                slb.at[pl.ds(k * CAP, CAP)], moved.at[pl.ds(k * CAP, CAP)],
                "ctx", n_ctx, k, sems[6:8],
            )
            for k in range(1, n_ctx)
        ]
        moved[0:CAP] = slb[0:CAP]
        total = prt[:, columns(here, size)].astype(F32)
        finish(copies)
        for k in range(1, n_tp):
            total = total + slots[k - 1].astype(F32)
        total = hid[...].astype(F32) + total
        resid[...] = total
        square = total_over(row_sums(total * total), mine, sums, "tp", n_tp, sems[2:4])
        factor = lax.rsqrt(as_column(square, eighth()) * (1.0 / width) + EPS)
        scale[...] = factor
        low[...] = (resid[...] * factor[:, 0:1] * gn[0:1, :]).astype(BF)
        partial_logits = mm_t(rtr[...].astype(BF), low[...])
        mine_two[...] = partial_logits
        logit_copies = [
            send(mine_two, sums_two.at[k - 1], "tp", n_tp, k, sems[12:14]) for k in range(1, n_tp)
        ]
        copies = gather_columns(low, out, "tp", n_tp, sems[4:6])

        def route():
            finish(logit_copies)
            logits = partial_logits
            for k in range(1, n_tp):
                logits = logits + sums_two[k - 1]
            named = [jnp.sum(one[j] * logits, axis=0, keepdims=True) for j in range(2)]
            top = jnp.maximum(named[0], named[1])
            powers = [jnp.exp(value - top) for value in named]
            both = powers[0] + powers[1]
            gate = [value / both for value in powers]
            mixed = gate[0] * nms[0] + gate[1] * nms[1]
            mix[...] = mixed
            order = lax.broadcasted_iota(jnp.int32, (8, rows), 0)
            gates[...] = jnp.where(order == 0, gate[0], jnp.where(order == 1, gate[1], 0.0))
            own_gates[...] = jnp.zeros(own_gates.shape, F32)
            for k in range(experts):
                own_gates[k, :, 0:CAP] = lax.dot_general(
                    jnp.broadcast_to(mixed[k : k + 1], (8, rows)),
                    pck[k * CAP : (k + 1) * CAP].astype(F32),
                    (((1,), (1,)), ((), ())),
                    precision=lax.Precision.HIGHEST,
                    preferred_element_type=F32,
                )
            slot_gates[0] = own_gates[0]
            for k in range(1, n_ctx):
                others.append(
                    send(own_gates.at[k], slot_gates.at[k], "ctx", n_ctx, k, sems[10:12])
                )

        for step in range(n_tp):
            at = columns(peer("tp", n_tp, n_tp - step), size)
            if step:
                copies[step - 1].wait()
                block = out[:, at]
            else:
                block = low[...]
            sent[step] = mm(pck[...], block).astype(BF)
            tokens[0:CAP, at] = sent[step, 0:CAP]
            for k in (2, 3, 1):
                others.append(
                    remote(
                        sent.at[step, pl.ds(k * CAP, CAP)], tokens.at[pl.ds(k * CAP, CAP), at],
                        sems[8:10], step * n_ctx + k, {"ctx": peer("ctx", n_ctx, k)},
                    )
                )
            if step == 0:
                route()
        finish(others)

    return call(
        kernel,
        (
            shape((rows, size), F32),
            shape((rows, 128), F32),
            shape((rows, width), BF),
            shape(slabs.shape, BF),
            shape(slabs.shape, BF),
            shape((experts, 8, rows), F32),
            shape((8, rows), F32),
            shape((8, rows), F32),
        ),
        (part, hidden, gain, slabs, picks, router, onehot, names),
        [
            pltpu.VMEM((n_tp - 1, rows, size), BF),
            pltpu.VMEM((8, rows), F32),
            pltpu.VMEM((n_tp - 1, 8, rows), F32),
            pltpu.VMEM((8, rows), F32),
            pltpu.VMEM((n_tp - 1, 8, rows), F32),
            pltpu.VMEM((rows, size), BF),
            pltpu.VMEM((n_tp, experts * CAP, size), BF),
            pltpu.VMEM((experts, 8, rows), F32),
        ]
        + pair_of_sems(n_tp) * 3
        + pair_of_sems(n_ctx)
        + pair_of_sems(n_tp * n_ctx)
        + pair_of_sems(n_ctx)
        + pair_of_sems(n_tp),
        3,
        "second_norm",
    )


def second_norm_back(
    acts, weights, tokens, dots, picks, gates, onehot, names, router, resid, scale, gain, grad,
    n_tp, n_ctx,
):
    rows, size = resid.shape
    width = size * n_tp
    experts = n_ctx
    hidden = acts[0].shape[1]
    count = len(weights[0])
    part = weights[0][0].shape[0]

    def kernel(*refs):
        dga, dup, hid = refs[:3]
        wgt = [refs[3 + i * count : 3 + (i + 1) * count] for i in range(3)]
        refs = refs[3 + 3 * count :]
        tok, dts, pck, gts, one, nms, rtr, rsd, scl, gn, grd = refs[:11]
        d_resid, low, d_gain, d_logits, out_back = refs[11:16]
        refs = refs[16:]
        if count == 2:
            up_away, up_held, up_sem = refs[:1] + refs[1:3]
            refs = refs[3:]
        (
            drw, eo, buffer, back, back_dots, parts, slots, mine, sums, mine_two, sums_two, loads,
        ) = refs[:12]
        sems = refs[12:]
        here = lax.axis_index("tp")
        first = lax.axis_index("fsdp")

        def load(which, rank, slot, lane):
            feature = rank * size
            inside = pl.ds(pl.multiple_of(lax.rem(feature, part), 16), size)
            target = buffer.at[slot, lane]
            if count == 1:
                pltpu.make_async_copy(
                    wgt[which][0].at[inside], target, loads.at[slot, lane]
                ).start()
                return
            own = feature // part == first

            @pl.when(own)
            def _():
                pltpu.make_async_copy(
                    wgt[which][0].at[inside], target, loads.at[slot, lane]
                ).start()

            @pl.when(jnp.logical_not(own))
            def _():
                pltpu.make_async_copy(
                    wgt[which][1].at[inside], target, loads.at[slot, lane]
                ).start()

        def loaded(which, slot, lane):
            pltpu.make_async_copy(
                wgt[which][0].at[pl.ds(0, size)], buffer.at[slot, lane], loads.at[slot, lane]
            ).wait()

        load(0, peer("tp", n_tp, 1), 0, 0)
        load(1, peer("tp", n_tp, 1), 0, 1)
        greet([("tp", n_tp), ("ctx", n_ctx)])
        small = []
        for k in range(1, n_ctx):
            small.append(
                send(dts.at[k], back_dots.at[k - 1], "ctx", n_ctx, n_ctx - k, sems[0:2])
            )

        def slab(k, rank, step):
            at = columns(rank, size)
            return described(
                drw.at[pl.ds(k * CAP, CAP), at], back.at[k - 1, :, at],
                sems[2:4], step * n_ctx + k - 1, {"ctx": peer("ctx", n_ctx, n_ctx - k)},
            )

        @pl.loop(0, n_tp)
        def _(step):
            rank = peer("tp", n_tp, step + 1)
            slot = lax.rem(step, 2)
            loaded(0, slot, 0)
            loaded(1, slot, 1)

            @pl.when(step + 1 < n_tp)
            def _():
                load(0, peer("tp", n_tp, step + 2), 1 - slot, 0)
                load(1, peer("tp", n_tp, step + 2), 1 - slot, 1)

            drw[:, columns(rank, size)] = (
                mm_t(dga[...], buffer[slot, 0]) + mm_t(dup[...], buffer[slot, 1])
            ).astype(BF)
            for k in (2, 3, 1):
                slab(k, rank, step).start()

        load(2, 0, 0, 0)

        @pl.loop(0, n_tp)
        def _(rank):
            slot = lax.rem(rank, 2)
            loaded(2, slot, 0)

            @pl.when(rank + 1 < n_tp)
            def _():
                load(2, rank + 1, 1 - slot, 0)

            eo[:, columns(rank, size)] = mm_t(hid[...], buffer[slot, 0]).astype(BF)

        moved = [
            send(
                eo.at[pl.ds(k * CAP, CAP)], out_back.at[pl.ds(k * CAP, CAP)],
                "ctx", n_ctx, n_ctx - k, sems[10:12],
            )
            for k in range(1, n_ctx)
        ]
        out_back[0:CAP] = eo[0:CAP]
        if count == 2:

            @pl.loop(0, part // 256)
            def _(i):
                at = pl.ds(pl.multiple_of((1 - first) * part + i * 256, 128), 256)
                up_held[stretch(i, 256), :] = t_mm(tok[:, at], dup[...]).astype(BF)

            pltpu.make_async_copy(up_held, up_away, up_sem).start()
        finish(small)
        order = lax.broadcasted_iota(jnp.int32, (8, rows), 0)
        own = jnp.zeros((8, rows), F32)
        for k in range(experts):
            by_slot = dts[0] if k == 0 else back_dots[k - 1]
            by_row = lax.dot_general(
                by_slot[:, 0:CAP],
                pck[k * CAP : (k + 1) * CAP].astype(F32),
                (((1,), (0,)), ((), ())),
                precision=lax.Precision.HIGHEST,
                preferred_element_type=F32,
            )
            own = own + jnp.where(order == k, by_row, 0.0)
        gate_grad = total_over(own, mine, sums, "tp", n_tp, sems[4:6])
        both = [jnp.sum(nms[j] * gate_grad, axis=0, keepdims=True) for j in range(2)]
        gate = [gts[j : j + 1, :] for j in range(2)]
        mean = gate[0] * both[0] + gate[1] * both[1]
        logits = sum(gate[j] * (both[j] - mean) * one[j] for j in range(2))
        d_logits[...] = logits
        copies = []
        for step in range(1, n_tp + 1):
            rank = peer("tp", n_tp, step)
            at = columns(rank, size)
            for k in (2, 3, 1):
                slab(k, rank, step - 1).wait()
            block = t_mm(pck[0:CAP], drw[0:CAP, at])
            for k in range(1, experts):
                block = block + t_mm(pck[k * CAP : (k + 1) * CAP], back[k - 1, :, at])
            if step < n_tp:
                parts[step - 1] = block.astype(BF)
                copies.append(
                    send(parts.at[step - 1], slots.at[step - 1], "tp", n_tp, step, sems[6:8])
                )
            else:
                total = block
        total = total + lax.dot_general(
            logits.astype(BF),
            rtr[...].astype(BF),
            (((0,), (0,)), ((), ())),
            preferred_element_type=F32,
        )
        finish(copies)
        for k in range(1, n_tp):
            total = total + slots[k - 1].astype(F32)
        factor = scl[:, 0:1]
        unit = rsd[...] * factor
        d_gain[...] = jnp.broadcast_to(jnp.sum(total * unit, axis=0, keepdims=True), d_gain.shape)
        gained = total * gn[0:1, :]
        d_resid[...] = gained
        dot = total_over(row_sums(unit * gained), mine_two, sums_two, "tp", n_tp, sems[8:10])
        dot = as_column(dot, eighth())[:, 0:1] * (1.0 / width)
        result = grd[...].astype(F32) + factor * (d_resid[...] - rsd[...] * factor * dot)
        d_resid[...] = result
        low[...] = result.astype(BF)
        finish(moved)
        if count == 2:
            pltpu.make_async_copy(up_held, up_away, up_sem).wait()

    outs = [
        shape((rows, size), F32),
        shape((rows, size), BF),
        shape((8, size), F32),
        shape((8, rows), F32),
        shape((experts * CAP, width), BF),
    ]
    held = []
    if count == 2:
        outs.append(shape((part, hidden), BF))
        held = [pltpu.VMEM((part, hidden), BF), DMA]
    flat = [array for group in weights for array in group]
    return call(
        kernel,
        tuple(outs),
        (*acts, *flat, tokens, dots, picks, gates, onehot, names, router, resid, scale, gain, grad),
        held
        + [
            pltpu.VMEM((experts * CAP, width), BF),
            pltpu.VMEM((experts * CAP, width), BF),
            pltpu.VMEM((2, 2, size, hidden), BF),
            pltpu.VMEM((n_ctx - 1, CAP, width), BF),
            pltpu.VMEM((n_ctx - 1, 8, rows), F32),
            pltpu.VMEM((n_tp - 1, rows, size), BF),
            pltpu.VMEM((n_tp - 1, rows, size), BF),
            pltpu.VMEM((8, rows), F32),
            pltpu.VMEM((n_tp - 1, 8, rows), F32),
            pltpu.VMEM((8, rows), F32),
            pltpu.VMEM((n_tp - 1, 8, rows), F32),
            DMA((2, 2)),
        ]
        + pair_of_sems(n_ctx)
        + pair_of_sems(n_tp * n_ctx)
        + pair_of_sems(n_tp) * 3
        + pair_of_sems(n_ctx),
        4,
        "second_norm_back",
        left=tuple(range(3, 3 + 3 * count)) + ((-1,) if count == 2 else ()),
    )


def attention_backward(low, output_w, query, kv, cosine, sine, payload, n_tp, n_ctx):
    rows, size = low.shape
    width = size * n_tp
    inner = query.shape[1]
    heads = inner // HD
    scale = 1.0 / math.sqrt(HD)

    def kernel(
        lw, wgt, qry, full, cs, sn, pay, d_attn, d_qkv, came, dot, dqs, dkv, slots, last, both, total, kept, *sems
    ):
        greet([("tp", n_tp), ("ctx", n_ctx)])
        here, beside, across = quad()
        beyond = lax.rem(beside + 2, 4)
        copies = gather_columns(lw, d_attn, "tp", n_tp, sems[2:4])
        moved = spread(pay, came, n_ctx, sems[4:6])

        @pl.loop(0, heads)
        def _(h):
            at = columns(h, HD)
            kept[h] = softmax_rows(qry[:, at], full[:, at], here * rows)

        for step in range(n_tp):
            rank = peer("tp", n_tp, n_tp - step)
            weights = wgt[pl.ds(pl.multiple_of(rank * size, 16), size), :]
            if step:
                copies[step - 1].wait()
                total[...] += mm(d_attn[:, columns(rank, size)], weights)
            else:
                total[...] = mm(lw[...], weights)
        dot[...] = total[...].astype(BF)

        @pl.loop(0, heads)
        def _(h):
            at, at_v = columns(h, HD), columns(h + heads, HD)
            probs = kept[h]
            d_probs = mm_t(dot[:, at], full[:, at_v])
            delta = jnp.sum(probs * d_probs, axis=-1, keepdims=True)
            d_scores = (probs * (d_probs - delta)).astype(BF)
            dqs[:, at] = mm(d_scores, full[:, at]) * scale
            dkv[:, at] = (t_mm(d_scores, qry[:, at]) * scale).astype(BF)
            dkv[:, at_v] = t_mm(probs.astype(BF), dot[:, at]).astype(BF)

        first = remote(dkv.at[stretch(beyond, rows), :], slots.at[0], sems, 0, {"ctx": beside})
        second = remote(dkv.at[stretch(beside, rows), :], slots.at[1], sems, 1, {"ctx": beside})
        first.wait()
        both[...] = (
            dkv[stretch(across, rows), :].astype(F32) + slots[0].astype(F32)
        ).astype(BF)
        third = remote(both, last, sems, 2, {"ctx": across})

        @pl.loop(0, heads)
        def _(h):
            d_qkv[:, columns(h, HD)] = turn(dqs[:, columns(h, HD)], cs[...], sn[...]).astype(BF)

        second.wait()
        third.wait()

        @pl.loop(0, heads)
        def _(h):
            at, at_v = columns(h, HD), columns(h + heads, HD)
            mine = stretch(here, rows)
            d_key = dkv[mine, at].astype(F32) + slots[1, :, at].astype(F32)
            d_key = d_key + last[:, at].astype(F32)
            d_qkv[:, columns(h + heads, HD)] = turn(d_key, cs[...], sn[...]).astype(BF)
            d_value = dkv[mine, at_v].astype(F32) + slots[1, :, at_v].astype(F32)
            d_value = d_value + last[:, at_v].astype(F32)
            d_qkv[:, columns(h + 2 * heads, HD)] = d_value.astype(BF)

        finish(moved)

    return call(
        kernel,
        (shape((rows, width), BF), shape((rows, 3 * inner), BF), came_shape(payload, n_ctx)),
        (low, output_w, query, kv, cosine, sine, payload),
        [
            pltpu.VMEM((rows, inner), BF),
            pltpu.VMEM((rows, inner), F32),
            pltpu.VMEM((rows * n_ctx, 2 * inner), BF),
            pltpu.VMEM((2, rows, 2 * inner), BF),
            pltpu.VMEM((rows, 2 * inner), BF),
            pltpu.VMEM((rows, 2 * inner), BF),
            pltpu.VMEM((rows, inner), F32),
            pltpu.VMEM((heads, rows, rows * n_ctx), F32),
        ]
        + pair_of_sems(3)
        + pair_of_sems(n_tp)
        + pair_of_sems(n_ctx),
        5,
        "attention_backward",
        left=(6, -1),
    )


def first_norm_back(part, hidden, scale, gain, d_resid, payload, n_tp, n_ctx):
    rows, size = hidden.shape
    width = size * n_tp

    def kernel(prt, hid, scl, gn, dr, pay, out, d_gain, came, slots, mine, sums, *sems):
        greet([("tp", n_tp), ("ctx", n_ctx)])
        here = lax.axis_index("tp")
        copies = scatter_columns(prt, slots, "tp", n_tp, sems[0:2])
        moved = spread(pay, came, n_ctx, sems[4:6])
        total = prt[:, columns(here, size)].astype(F32)
        finish(copies)
        for k in range(1, n_tp):
            total = total + slots[k - 1].astype(F32)
        factor = scl[:, 0:1]
        unit = hid[...].astype(F32) * factor
        d_gain[...] = jnp.broadcast_to(jnp.sum(total * unit, axis=0, keepdims=True), d_gain.shape)
        gained = total * gn[0:1, :]
        out[...] = gained
        dot = total_over(row_sums(unit * gained), mine, sums, "tp", n_tp, sems[2:4])
        dot = as_column(dot, eighth())[:, 0:1] * (1.0 / width)
        unit = hid[...].astype(F32) * factor
        out[...] = dr[...] + factor * (out[...] - unit * dot)
        finish(moved)

    return call(
        kernel,
        (shape((rows, size), F32), shape((8, size), F32), came_shape(payload, n_ctx)),
        (part, hidden, scale, gain, d_resid, payload),
        [
            pltpu.VMEM((n_tp - 1, rows, size), BF),
            pltpu.VMEM((8, rows), F32),
            pltpu.VMEM((n_tp - 1, 8, rows), F32),
        ]
        + pair_of_sems(n_tp) * 2
        + pair_of_sems(n_ctx),
        6,
        "first_norm_back",
        left=(5, -1),
    )


def weight_grads(parts, groups, small, payload, back, picks, mix, resid, n_tp, n_ctx):
    tokens, block_size = resid.shape
    experts = n_ctx
    rows = parts[0].shape[2]
    width = small.shape[1] * n_tp
    places = 2 * n_ctx
    cut = width // places
    total_columns = sum(size for _, _, size, _ in groups)

    def kernel(*refs):
        prts, refs = refs[: len(parts)], refs[len(parts) :]
        sml, pay, bck, pck, mx, rsd, out, small_out, block_out, came = refs[:10]
        sml_full, sml_slots, mixed, shares, share_slots = refs[10:15]
        refs = refs[15:]
        scratch, sems = refs[: 5 * len(groups)], refs[5 * len(groups) :]
        barrier = pltpu.get_barrier_semaphore()
        here, beside, across = quad()
        beyond = lax.rem(beside + 2, 4)
        mine = lax.axis_index("fsdp")
        other = 1 - mine
        place = mine * n_ctx + here
        others = []
        for i in range(1, places):
            to = lax.rem(place + i, places)
            others.append((to, {"fsdp": to // n_ctx, "ctx": lax.rem(to, n_ctx)}))
        ahead = [{"tp": peer("tp", n_tp, k)} for k in range(1, n_tp)]
        for device in ahead + [device for _, device in others]:
            pl.semaphore_signal(barrier, inc=1, device_id=device, device_id_type=MESH)
        pl.semaphore_wait(barrier, n_tp - 1 + places - 1)
        gathers = gather_columns(sml, sml_full, "tp", n_tp, sems[0:2])
        moved = spread(pay, came, n_ctx, sems[4:6], (2,))
        moves = []
        for g, (which, first, size, ctx_first) in enumerate(groups):
            near = scratch[5 * g]
            at = pl.ds(first, size)
            far_here = (mine, beyond) if ctx_first else (other, beside)
            blocks = [(other, beyond), far_here]
            blocks += [(other, beside) if ctx_first else (mine, beyond), (mine, beside)]
            moves.append(
                [
                    remote(
                        prts[which].at[rank, column, :, at], near.at[i],
                        sems[8 + 6 * g : 10 + 6 * g], i, {"ctx": beside},
                    )
                    for i, (rank, column) in enumerate(blocks)
                ]
            )
        finish(gathers)
        totals = [
            remote(sml_full.at[:, columns(to, cut)], sml_slots.at[i], sems[2:4], i, device)
            for i, (to, device) in enumerate(others)
        ]

        def chip(g, i, rank, column):
            which, first, size, _ = groups[g]
            moves[g][i].wait()
            value = prts[which][rank, column, :, first : first + size].astype(F32)
            return value + scratch[5 * g][i].astype(F32)

        hops = []
        for g, (_, _, _, ctx_first) in enumerate(groups):
            two, far = scratch[5 * g + 1 : 5 * g + 3]
            to = {"ctx": across} if ctx_first else {"fsdp": other}
            pair = [(other, across), (mine, across) if ctx_first else (other, here)]
            sent = []
            for i, (rank, column) in enumerate(pair):
                two[i] = chip(g, i, rank, column).astype(BF)
                sent.append(
                    remote(two.at[i], far.at[i], sems[10 + 6 * g : 12 + 6 * g], i, to)
                )
            hops.append(sent)
        moved += spread(pay, came, n_ctx, sems[4:6], (1, 3))
        order = lax.broadcasted_iota(jnp.int32, (8, 128), 0)
        for k in range(experts):
            mixed[k] = as_column(mx[...], jnp.where(order == k, 1.0, 0.0))
        given = []
        for step in range(1, n_tp + 1):
            at = columns(peer("tp", n_tp, step), block_size)
            block = jnp.zeros((tokens, block_size), F32)
            for k in range(experts):
                block = block + mixed[k][:, 0:1] * t_mm(
                    pck[k * CAP : (k + 1) * CAP], bck[k * CAP : (k + 1) * CAP, at]
                )
            if step < n_tp:
                shares[step - 1] = block.astype(BF)
                given.append(
                    send(shares.at[step - 1], share_slots.at[step - 1], "tp", n_tp, step, sems[6:8])
                )
            else:
                moe = rsd[...] + block
        lasts = []
        for g, (_, _, _, ctx_first) in enumerate(groups):
            far, one, last = scratch[5 * g + 2], scratch[5 * g + 3], scratch[5 * g + 4]
            value = chip(g, 2, *((other, here) if ctx_first else (mine, across)))
            hops[g][0].wait()
            one[...] = (value + far[0].astype(F32)).astype(BF)
            to = {"fsdp": other} if ctx_first else {"ctx": across}
            lasts.append(remote(one, last, sems[12 + 6 * g : 14 + 6 * g], 0, to))
        start = 0
        for g, (_, _, size, _) in enumerate(groups):
            far = scratch[5 * g + 2]
            value = chip(g, 3, mine, here)
            hops[g][1].wait()
            out[:, start : start + size] = value + far[1].astype(F32)
            start += size
        finish(totals)
        sums = sml_full[:, columns(place, cut)]
        for i in range(places - 1):
            sums = sums + sml_slots[i]
        small_out[...] = sums
        finish(given)
        for k in range(1, n_tp):
            moe = moe + share_slots[k - 1].astype(F32)
        block_out[...] = moe.astype(BF)
        start = 0
        for g, (_, _, size, _) in enumerate(groups):
            lasts[g].wait()
            at = pl.ds(start, size)
            out[:, at] = out[:, at] + scratch[5 * g + 4][...].astype(F32)
            start += size
        finish(moved)

    buffers = [
        pltpu.VMEM((8, width), F32),
        pltpu.VMEM((places - 1, 8, cut), F32),
        pltpu.VMEM((experts, tokens, 128), F32),
        pltpu.VMEM((n_tp - 1, tokens, block_size), BF),
        pltpu.VMEM((n_tp - 1, tokens, block_size), BF),
    ]
    sems = pair_of_sems(n_tp) + pair_of_sems(places) + pair_of_sems(n_ctx) + pair_of_sems(n_tp)
    for _, _, size, _ in groups:
        buffers += [
            pltpu.VMEM((4, rows, size), BF),
            pltpu.VMEM((2, rows, size), BF),
            pltpu.VMEM((2, rows, size), BF),
            pltpu.VMEM((rows, size), BF),
            pltpu.VMEM((rows, size), BF),
        ]
        sems += pair_of_sems(4) + pair_of_sems(2) + pair_of_sems(1)
    return call(
        kernel,
        (
            shape((rows, total_columns), F32),
            shape((8, cut), F32),
            shape((tokens, block_size), BF),
            came_shape(payload, n_ctx),
        ),
        (*parts, small, payload, back, picks, mix, resid),
        buffers + sems,
        10,
        "weight_grads",
        left=(len(parts) + 1, -1),
    )


def experts_out(back, picks, mix, resid, payload, n_tp, n_ctx):
    rows, size = resid.shape
    experts = n_ctx

    def kernel(bck, pck, mx, rsd, pay, out, came, part, slots, *sems):
        greet([("tp", n_tp), ("ctx", n_ctx)])
        moved = spread(pay, came, n_ctx, sems[2:4])
        order = lax.broadcasted_iota(jnp.int32, (8, 128), 0)
        gate = [as_column(mx[...], jnp.where(order == k, 1.0, 0.0)) for k in range(experts)]
        copies = []
        for step in range(1, n_tp + 1):
            at = columns(peer("tp", n_tp, step), size)
            block = jnp.zeros((rows, size), F32)
            for k in range(experts):
                block = block + gate[k][:, 0:1] * t_mm(
                    pck[k * CAP : (k + 1) * CAP], bck[k * CAP : (k + 1) * CAP, at]
                )
            if step < n_tp:
                part[step - 1] = block.astype(BF)
                copies.append(
                    send(part.at[step - 1], slots.at[step - 1], "tp", n_tp, step, sems[0:2])
                )
            else:
                total = rsd[...] + block
        finish(copies)
        for k in range(1, n_tp):
            total = total + slots[k - 1].astype(F32)
        out[...] = total.astype(BF)
        finish(moved)

    return call(
        kernel,
        (shape((rows, size), BF), came_shape(payload, n_ctx)),
        (back, picks, mix, resid, payload),
        [
            pltpu.VMEM((n_tp - 1, rows, size), BF),
            pltpu.VMEM((n_tp - 1, rows, size), BF),
        ]
        + pair_of_sems(n_tp)
        + pair_of_sems(n_ctx),
        9,
        "experts_out",
        left=(4, -1),
    )


def write_out(experts_grads, attn_grad, plain, n_ctx):
    _, rows, size = experts_grads[0][1].shape
    steps = max(1, rows // 32)
    tile = rows // steps
    many, block = len(experts_grads), attn_grad.shape[1] // 4

    def kernel(rank, *refs):
        here = rank[0]
        ins, outs = refs[: 2 * many + 1 + len(plain)], refs[2 * many + 1 + len(plain) :]
        for i in range(many):
            mine, came = ins[2 * i : 2 * i + 2]
            outs[i][here] = mine[...].astype(F32)
            for k in range(1, n_ctx):
                outs[i][lax.rem(here + n_ctx - k, n_ctx)] = came[k - 1].astype(F32)
        for i in range(4):
            outs[many + i][...] = ins[2 * many][:, i * block : (i + 1) * block]
        for i in range(len(plain)):
            outs[many + 4 + i][...] = ins[2 * many + 1 + i][...]

    def flat(array):
        return pl.BlockSpec((array.shape[0] // steps, array.shape[1]), lambda i, rank: (i, 0))

    in_specs, out_specs, out_shape = [], [], []
    for _ in experts_grads:
        in_specs.append(pl.BlockSpec((tile, size), lambda i, rank: (rank[0] * steps + i, 0)))
        in_specs.append(pl.BlockSpec((n_ctx - 1, tile, size), lambda i, rank: (0, i, 0)))
        out_specs.append(pl.BlockSpec((n_ctx, tile, size), lambda i, rank: (0, i, 0)))
        out_shape.append(shape((n_ctx, rows, size), F32))
    in_specs.append(flat(attn_grad))
    quarter = jax.ShapeDtypeStruct((attn_grad.shape[0], block), F32)
    for array in [quarter] * 4 + list(plain):
        out_specs.append(flat(array))
        out_shape.append(shape(array.shape, array.dtype))
    in_specs += [flat(array) for array in plain]
    inputs = [array for pair in experts_grads for array in pair] + [attn_grad, *plain]
    return pl.pallas_call(
        kernel,
        grid_spec=pltpu.PrefetchScalarGridSpec(
            num_scalar_prefetch=1, grid=(steps,), in_specs=in_specs, out_specs=out_specs
        ),
        out_shape=out_shape,
        cost_estimate=pl.CostEstimate(
            flops=0, bytes_accessed=6 * many * n_ctx * rows * size, transcendentals=0
        ),
        name="write_out",
    )(lax.axis_index("ctx").reshape(1), *inputs)


def after(value, *needed):
    return lax.optimization_barrier((value, *needed))[0]


def shards(
    hidden_in,
    out_grad,
    attn_gain,
    w_query,
    w_key,
    w_value,
    w_output,
    ffn_gain,
    w_router,
    w_gate,
    w_up,
    w_down,
    routes,
):
    rows_here, width_tp = hidden_in.shape
    here_tp = lax.axis_index("tp")
    here_ctx = lax.axis_index("ctx")
    here_fsdp = lax.axis_index("fsdp")
    n_fsdp = lax.axis_size("fsdp")
    n_ctx = lax.axis_size("ctx")
    n_tp = lax.axis_size("tp")
    experts = w_gate.shape[0]
    assert experts == n_ctx == 4
    width = width_tp * n_tp
    part = width // n_fsdp
    pair = n_fsdp == 2
    heads_width = w_query.shape[1]

    def swap_fsdp(value):
        return lax.ppermute(value, "fsdp", [(0, 1), (1, 0)])

    def other_parts(weight):
        if pair:
            return [weight, swap_fsdp(weight)]
        return [lax.all_gather(weight, "fsdp", axis=0, tiled=True)]

    def split(values):
        if pair:
            return [
                lax.dynamic_slice_in_dim(values, here_fsdp * part, part, 1),
                lax.dynamic_slice_in_dim(values, (1 - here_fsdp) * part, part, 1),
            ]
        return [values]

    def join(pieces):
        if pair:
            first = here_fsdp == 0
            return jnp.concatenate(
                [jnp.where(first, pieces[0], pieces[1]), jnp.where(first, pieces[1], pieces[0])],
                axis=1,
            )
        return pieces[0]

    def into(values, weights):
        return sum(mm(x, w) for x, w in zip(split(values), weights))

    def back(values, weights):
        return join([mm_t(values, w) for w in weights])

    def my_features(values):
        return lax.dynamic_slice_in_dim(values, here_tp * width_tp, width_tp, values.ndim - 1)

    attn_w = (w_query, w_key, w_value, w_output)
    small = jnp.concatenate(
        [attn_gain[None], ffn_gain[None], w_router.T, jnp.zeros((2, part), BF)], axis=0
    )
    if pair:
        quarter = part // n_ctx
        own_quarter = jnp.concatenate(
            [lax.dynamic_slice_in_dim(w, here_ctx * quarter, quarter, 0) for w in attn_w], axis=1
        )
        other_quarter = swap_fsdp(own_quarter)
        other_small = swap_fsdp(small)
        small_full = join([small, other_small]).astype(F32)
    else:
        other_quarter = None
        small_full = lax.all_gather(small, "fsdp", axis=1, tiled=True).astype(F32)
    inputs_full, up_mine, down_mine = gather_tp(hidden_in, (w_up, w_down), n_tp)
    gate_w = other_parts(lax.dynamic_index_in_dim(w_gate, here_ctx, 0, False))
    up_w = other_parts(up_mine)
    down_w = other_parts(down_mine)
    small_here = my_features(small_full)
    gain_one_here = jnp.broadcast_to(small_here[0:1], small_here.shape)
    gain_two_here = jnp.broadcast_to(small_here[1:2], small_here.shape)
    nothing = [(0, 8 - experts), (0, 0)]
    router_here = jnp.pad(small_here[2 : 2 + experts], nothing)

    relative = (jnp.arange(experts, dtype=jnp.int32) + here_ctx) % experts
    numbers = jnp.arange(8, dtype=jnp.int32)
    onehot = (routes.T[:, None, :] == numbers[None, :, None]).astype(F32)
    named = (routes.T[:, None, :] == relative[None, :, None]).astype(F32)
    names = jnp.pad(named, [(0, 0)] + nothing)
    chosen = jnp.sum(named, axis=0)
    earlier = jnp.triu(jnp.ones((rows_here, rows_here), BF), 1)
    slot_of = mm(chosen.astype(BF), earlier).astype(jnp.int32)
    slots = jnp.arange(CAP, dtype=jnp.int32)
    picks = (slot_of[:, None, :] == slots[None, :, None]) & (chosen[:, None, :] > 0)
    picks = picks.astype(BF).reshape(experts * CAP, rows_here)

    gathered = first_norm(
        inputs_full, out_grad, small_full, attn_w, other_quarter, n_tp, n_ctx
    )
    normed_one, scale_one, grad_full = gathered[:3]
    if pair:
        qkv_w, output_w = gathered[3:]
    else:
        qkv_w, output_w = (
            lax.all_gather(w, "fsdp", axis=0, tiled=True)
            for w in (jnp.concatenate(attn_w[:3], axis=1), w_output)
        )
    positions = here_ctx * rows_here + jnp.arange(rows_here, dtype=jnp.int32)
    cosine, sine = rotary_tables(positions)
    attended, query, kv = attention_forward(mm(normed_one, qkv_w), cosine, sine, n_ctx)
    resid, scale_two, normed_two, grad_rows, token_rows, slot_gates, gates, mix = second_norm(
        mm_t(attended, output_w).astype(BF),
        hidden_in,
        gain_two_here,
        mm(picks, grad_full).astype(BF),
        picks,
        router_here,
        onehot,
        names,
        n_tp,
        n_ctx,
    )
    gate_rows = slot_gates[:, 0, :CAP].reshape(experts * CAP, 1)

    gate_act = into(token_rows, gate_w)
    up_act = into(token_rows, up_w)
    sigma_act = jax.nn.sigmoid(gate_act)
    hidden_act = (gate_act * sigma_act * up_act).astype(BF)
    d_result = (gate_rows * grad_rows.astype(F32)).astype(BF)

    def grad_send(left, right):
        halves = split(left)
        if pair:
            away = t_mm(halves[1], right).astype(BF)
            return halves[0], right, away, swap_fsdp(away)
        return halves[0], right, None, None

    def grad_sum(mine, right, away, other):
        if pair:
            return (t_mm(mine, right) + other.astype(F32)).astype(BF)
        return lax.psum_scatter(
            t_mm(mine, right).astype(BF), "fsdp", scatter_dimension=0, tiled=True
        )

    down_sent = grad_send(d_result, hidden_act)
    if pair:
        grad_rows = after(grad_rows, down_sent[2])
    d_hidden = into(grad_rows, down_w)
    gate_dot = jnp.sum(hidden_act.astype(F32) * d_hidden, axis=-1).reshape(experts, CAP)
    gate_dot = jnp.broadcast_to(
        jnp.pad(gate_dot, [(0, 0), (0, rows_here - CAP)])[:, None, :], (experts, 8, rows_here)
    )
    d_hidden = gate_rows * d_hidden
    d_gate_act = (d_hidden * up_act * sigma_act * (1.0 + gate_act * (1.0 - sigma_act))).astype(BF)
    d_up_act = (d_hidden * gate_act * sigma_act).astype(BF)
    gate_sent = grad_send(token_rows, d_gate_act)

    acts = (d_gate_act, d_up_act, hidden_act)
    if pair:
        acts = lax.optimization_barrier((*acts, gate_sent[2]))[:3]
    d_resid, d_attn_here, gain_two_part, d_logits, returned, *up_away = second_norm_back(
        acts,
        (gate_w, up_w, down_w),
        token_rows,
        gate_dot,
        picks,
        gates,
        onehot,
        names,
        router_here,
        resid,
        scale_two,
        gain_two_here,
        out_grad,
        n_tp,
        n_ctx,
    )
    if pair:
        up_sent = (split(token_rows)[0], d_up_act, up_away[0], swap_fsdp(up_away[0]))
        d_attn_here, *down_sent = lax.optimization_barrier((d_attn_here, *down_sent))
    else:
        up_sent = grad_send(token_rows, d_up_act)
    grad_down = grad_sum(*down_sent)

    d_attn, d_qkv, down_came = attention_backward(
        d_attn_here, output_w, query, kv, cosine, -sine, grad_down, n_tp, n_ctx
    )
    if pair:
        d_qkv, *gate_sent = lax.optimization_barrier((d_qkv, *gate_sent))
    grad_gate = grad_sum(*gate_sent)
    in_grad, gain_one_part, gate_came = first_norm_back(
        mm_t(d_qkv, qkv_w).astype(BF),
        hidden_in,
        scale_one,
        gain_one_here,
        d_resid,
        grad_gate,
        n_tp,
        n_ctx,
    )
    if pair:
        in_grad, *up_sent = lax.optimization_barrier((in_grad, *up_sent))
    grad_up = grad_sum(*up_sent)

    grad_qkv = t_mm(normed_one, d_qkv).astype(BF)
    grad_output = t_mm(d_attn, attended).astype(BF)
    small_part = jnp.concatenate(
        [
            gain_one_part[:1],
            gain_two_part[:1],
            mm(d_logits[:experts].astype(BF), my_features(normed_two)),
            jnp.zeros((6 - experts, width_tp), F32),
        ],
        axis=0,
    )
    mixing = (returned, picks, mix, resid)
    if pair:
        grad_attn, small_grad, block_out, up_came = weight_grads(
            [value.reshape(n_fsdp, n_ctx, quarter, -1) for value in (grad_qkv, grad_output)],
            [
                (1, 0, heads_width, False),
                (0, 0, 2 * heads_width, False),
                (0, 2 * heads_width, heads_width, False),
            ],
            small_part,
            grad_up,
            *mixing,
            n_tp,
            n_ctx,
        )
    else:
        scatter = partial(
            lax.psum_scatter, axis_name=("fsdp", "ctx"), scatter_dimension=0, tiled=True
        )
        grad_attn = scatter(jnp.concatenate([grad_output, grad_qkv], axis=1)).astype(F32)
        small_grad = lax.all_gather(small_part, "tp", axis=1, tiled=True)
        small_grad = scatter(small_grad.T).T
        block_out, up_came = experts_out(*mixing, grad_up, n_tp, n_ctx)
    pieces = [(grad_gate, gate_came), (grad_up, up_came), (grad_down, down_came)]
    (
        grad_gate, grad_up, grad_down, grad_output, grad_query, grad_key, grad_value,
        block_out, in_grad,
    ) = write_out(pieces, grad_attn, (block_out, in_grad), n_ctx)
    return (
        block_out,
        in_grad,
        small_grad[0],
        grad_query,
        grad_key,
        grad_value,
        grad_output,
        small_grad[1],
        small_grad[2 : 2 + experts].T,
        grad_gate,
        grad_up,
        grad_down,
    )


def solution(mesh):
    rows = ("fsdp", "ctx")
    placed = (
        P(rows, "tp"),
        P(rows, "tp"),
        P("fsdp"),
        P("fsdp", "tp"),
        P("fsdp", "tp"),
        P("fsdp", "tp"),
        P("fsdp", "tp"),
        P("fsdp"),
        P("fsdp", None),
        P(None, "fsdp", "tp"),
        P(None, "fsdp", "tp"),
        P(None, "fsdp", "tp"),
        P(rows, None),
    )
    return jax.shard_map(
        shards,
        mesh=mesh,
        in_specs=placed,
        out_specs=(
            P(rows, "tp"),
            P(rows, "tp"),
            P(rows),
            P(rows, "tp"),
            P(rows, "tp"),
            P(rows, "tp"),
            P(rows, "tp"),
            P(rows),
            P(rows, None),
            P(None, rows, "tp"),
            P(None, rows, "tp"),
            P(None, rows, "tp"),
        ),
        check_vma=False,
    )
```

```python
from functools import partial
import math

import jax
import jax.numpy as jnp
from jax import lax
from jax.experimental import pallas as pl
from jax.experimental.pallas import tpu as pltpu
from jax.sharding import PartitionSpec as P

HD = 128
CAP = 160


EPS = 1e-05
THETA = 10000.0
NEG = -1e30
BF = jnp.bfloat16
F32 = jnp.float32


def mm(left, right):
    return jnp.dot(left, right, preferred_element_type=F32)


def mm_t(left, right):
    return lax.dot_general(left, right, (((1,), (1,)), ((), ())), preferred_element_type=F32)


def t_mm(left, right):
    return lax.dot_general(left, right, (((0,), (0,)), ((), ())), preferred_element_type=F32)


def rotary_tables(positions):
    half_size = HD // 2
    frequency = THETA ** (-(jnp.arange(half_size, dtype=F32) * 2.0 / HD))
    angles = positions.astype(F32)[:, None] * frequency[None, :]
    cosine, sine = jnp.cos(angles), jnp.sin(angles)
    return jnp.concatenate([cosine, cosine], axis=1), jnp.concatenate([-sine, sine], axis=1)


MESH = pl.DeviceIdType.MESH
VM = pl.BlockSpec(memory_space=pltpu.VMEM)
DMA = pltpu.SemaphoreType.DMA


def peer(axis, n, k):
    return lax.rem(lax.axis_index(axis) + k, n)


def greet(groups):
    barrier = pltpu.get_barrier_semaphore()
    for axis, n in groups:
        for k in range(1, n):
            pl.semaphore_signal(
                barrier, inc=1, device_id={axis: peer(axis, n, k)}, device_id_type=MESH
            )
    pl.semaphore_wait(barrier, sum(n - 1 for _, n in groups))


def described(source, target, sems, i, to):
    return pltpu.make_async_remote_copy(
        src_ref=source,
        dst_ref=target,
        send_sem=sems[0].at[i],
        recv_sem=sems[1].at[i],
        device_id=to,
        device_id_type=MESH,
    )


def remote(source, target, sems, i, to):
    copy = described(source, target, sems, i, to)
    copy.start()
    return copy


def send(source, target, axis, n, k, sems):
    return remote(source, target, sems, k - 1, {axis: peer(axis, n, k)})


def columns(n, size):
    return pl.ds(pl.multiple_of(n * size, 128), size)


def stretch(n, size):
    return pl.ds(pl.multiple_of(n * size, 16), size)


def gather_columns(own, full, axis, n, sems):
    size = own.shape[1]
    place = full.at[:, columns(lax.axis_index(axis), size)]
    copies = [send(own, place, axis, n, k, sems) for k in range(1, n)]
    place[...] = own[...]
    return copies


def scatter_columns(part, slots, axis, n, sems):
    size = slots.shape[2]
    return [
        send(part.at[:, columns(peer(axis, n, k), size)], slots.at[k - 1], axis, n, k, sems)
        for k in range(1, n)
    ]


def finish(copies):
    for copy in copies:
        copy.wait()


class Payload:

    def __init__(self, n_ctx, rows=None, product=None):
        self.n_ctx = n_ctx
        self.product = product is not None
        self.inputs = list(product) if self.product else [rows]
        last = self.inputs[-1]
        self.rows, self.hidden = last.shape
        self.cut = self.rows // n_ctx
        self.outs = [shape((n_ctx - 1, self.cut, self.hidden), BF)]
        self.scratch = pair_of_sems(n_ctx)
        if self.product:
            self.outs.append(shape((self.cut, self.hidden), BF))
            self.scratch += [
                pltpu.VMEM((self.rows, self.hidden), BF),
                pltpu.VMEM((self.rows, self.hidden), BF),
                DMA,
            ]

    def take(self, ins, outs, scratch):
        self.ins, self.out_refs, self.held = ins, outs, scratch

    def load(self):
        if self.product:
            pltpu.make_async_copy(self.ins[2], self.held[2], self.held[4]).start()

    def copy(self, k):
        to = peer("ctx", self.n_ctx, k)
        source = self.held[3] if self.product else self.ins[0]
        return described(
            source.at[stretch(to, self.cut), :], self.out_refs[0].at[k - 1],
            self.held[0:2], k - 1, {"ctx": to},
        )

    def go(self, first=0, last=4):
        n_ctx, cut = self.n_ctx, self.cut
        if not self.product:
            for j in range(first, last):
                if (j + 2) % n_ctx:
                    self.copy((j + 2) % n_ctx).start()
            return
        left, right, other = self.ins
        if first == 0:
            pltpu.make_async_copy(other, self.held[2], self.held[4]).wait()
        base = lax.axis_index("fsdp") * self.rows

        @pl.loop(first, last)
        def _(j):
            k = lax.rem(j + 2, n_ctx)
            to = peer("ctx", n_ctx, k)
            value = t_mm(left[:, pl.ds(pl.multiple_of(base + to * cut, 128), cut)], right[...])
            value = value + self.held[2][stretch(to, cut), :].astype(F32)
            self.held[3][stretch(to, cut), :] = value.astype(BF)

            @pl.when(j != n_ctx - 2)
            def _():
                self.copy(k).start()

    def wait(self):
        if self.product:
            self.out_refs[1][...] = self.held[3][stretch(lax.axis_index("ctx"), self.cut), :]
        for k in range(1, self.n_ctx):
            self.copy(k).wait()


class RowSums:

    def __init__(self, made, first, count, n_tp):
        self.n_tp, self.first = n_tp, first
        self.shape = (count, made.shape[1] // n_tp)
        self.scratch = [
            pltpu.VMEM((n_tp - 1, *self.shape), BF),
            pltpu.VMEM(self.shape, BF),
            DMA,
        ] + pair_of_sems(n_tp)

    def take(self, made, scratch):
        self.made, self.held = made, scratch

    def rows(self, rank):
        return self.made.at[pl.ds(self.first, self.shape[0]), columns(rank, self.shape[1])]

    def mine(self):
        return pltpu.make_async_copy(
            self.rows(lax.axis_index("tp")), self.held[1], self.held[2]
        )

    def start(self):
        self.mine().start()
        n = self.n_tp
        self.copies = [
            send(self.rows(peer("tp", n, k)), self.held[0].at[k - 1], "tp", n, k, self.held[3:5])
            for k in range(1, n)
        ]

    def total(self):
        self.mine().wait()
        finish(self.copies)
        value = self.held[1][...].astype(F32)
        for k in range(1, self.n_tp):
            value = value + self.held[0][k - 1].astype(F32)
        return value


def quad():
    here = lax.axis_index("ctx")
    return here, here + 1 - 2 * lax.rem(here, 2), lax.rem(here + 2, 4)


def gather_square(own, places, sems, between, local=None):
    cuts = own.shape[1] // 512
    here, beside, across = quad()
    first, second, third = [], [], []
    for i in range(cuts):
        piece = own.at[:, pl.ds(i * 512, 512)]
        first.append(remote(piece, places(here, i), sems, 3 * i, {"ctx": across}))
        second.append(remote(piece, places(here, i), sems, 3 * i + 1, {"ctx": beside}))
        if local is None:
            places(here, i)[...] = piece[...]
        else:
            pltpu.make_async_copy(piece, places(here, i), local.at[i]).start()
    between()
    for i in range(cuts):
        first[i].wait()
        third.append(
            remote(places(across, i), places(across, i), sems, 3 * i + 2, {"ctx": beside})
        )
    finish(second)
    finish(third)
    if local is not None:
        for i in range(cuts):
            piece = own.at[:, pl.ds(i * 512, 512)]
            pltpu.make_async_copy(piece, places(here, i), local.at[i]).wait()


def row_sums(values):
    ones = jnp.ones((8, values.shape[1]), F32)
    return lax.dot_general(
        ones,
        values,
        (((1,), (1,)), ((), ())),
        precision=lax.Precision.HIGHEST,
        preferred_element_type=F32,
    )


def as_column(rows, weight):
    return lax.dot_general(
        rows,
        weight,
        (((0,), (0,)), ((), ())),
        precision=lax.Precision.HIGHEST,
        preferred_element_type=F32,
    )


def eighth():
    return jnp.full((8, 128), 0.125, F32)


def total_over(sums, mine, slots, axis, n, sems):
    mine[...] = sums
    copies = [send(mine, slots.at[k - 1], axis, n, k, sems) for k in range(1, n)]
    finish(copies)
    total = sums
    for k in range(1, n):
        total = total + slots[k - 1]
    return total


def call(kernel, out_shape, inputs, scratch, collective, name, left=()):
    anywhere = pl.BlockSpec(memory_space=pl.ANY)
    outs = out_shape if isinstance(out_shape, tuple) else (out_shape,)
    specs = [anywhere if i - len(outs) in left else VM for i in range(len(outs))]
    return pl.pallas_call(
        kernel,
        out_shape=out_shape,
        in_specs=[anywhere if i in left else VM for i in range(len(inputs))],
        out_specs=tuple(specs) if isinstance(out_shape, tuple) else specs[0],
        scratch_shapes=scratch,
        compiler_params=pltpu.CompilerParams(collective_id=collective, has_side_effects=True),
        cost_estimate=pl.CostEstimate(flops=0, bytes_accessed=0, transcendentals=0),
        name=name,
    )(*inputs)


def shape(dims, dtype):
    return jax.ShapeDtypeStruct(dims, dtype)


def pair_of_sems(n):
    return [DMA((n,)), DMA((n,))]


def gather_tp(value, stacks, n_tp):
    rows, size = value.shape
    many = len(stacks)
    member = stacks[0].shape[1:]

    def kernel(own, *refs):
        stk, full, outs = refs[:many], refs[many], refs[many + 1 : 2 * many + 1]
        held, loads, stores = refs[2 * many + 1 : 2 * many + 4]
        sems = refs[2 * many + 4 :]
        here = lax.axis_index("ctx")
        into = [
            pltpu.make_async_copy(stk[i].at[here], held.at[i], loads.at[i]) for i in range(many)
        ]
        away = [pltpu.make_async_copy(held.at[i], outs[i], stores.at[i]) for i in range(many)]
        for copy in into:
            copy.start()
        greet([("tp", n_tp)])
        copies = gather_columns(own, full, "tp", n_tp, sems)
        for i in range(many):
            into[i].wait()
            away[i].start()
        finish(copies)
        finish(away)

    return call(
        kernel,
        (
            shape((rows, size * n_tp), value.dtype),
            *(shape(member, stack.dtype) for stack in stacks),
        ),
        (value, *stacks),
        [pltpu.VMEM((many, *member), BF), DMA((many,)), DMA((many,))] + pair_of_sems(n_tp),
        1,
        "gather_tp",
        left=tuple(range(1, many + 1)) + tuple(range(-many, 0)),
    )


def first_norm(full, grad, gain, weights, quarter, n_tp, n_ctx):
    rows, width = full.shape
    with_quarter = quarter is not None

    def kernel(*refs):
        hid, grd, gn = refs[:3]
        refs = refs[3:]
        if with_quarter:
            wgts, refs = refs[: len(weights)], refs[len(weights) :]
            qrt, out, scale, grd_full, many_full, last_full, held, local, loads, stores = refs[:10]
            sems = refs[10:]
            half, inner = wgts[0].shape
            last = len(wgts) - 1
            mine = lax.axis_index("fsdp")

            def target(i, first_row, count):
                at = pl.ds(pl.multiple_of(first_row, 16), count)
                if i == last:
                    return last_full.at[at, :]
                return many_full.at[at, pl.ds(i * inner, inner)]

            into = [
                pltpu.make_async_copy(wgts[i], held.at[i], loads.at[i]) for i in range(len(wgts))
            ]
            away = [
                pltpu.make_async_copy(held.at[i], target(i, mine * half, half), stores.at[i])
                for i in range(len(wgts))
            ]
            for copy in into:
                copy.start()
            greet([("tp", n_tp), ("ctx", n_ctx)])
        else:
            out, scale, grd_full = refs[:3]
            sems = refs[3:]
            greet([("tp", n_tp)])
        grads = gather_columns(grd, grd_full, "tp", n_tp, sems[0:2])

        def norm():
            values = hid[...].astype(F32)
            mean = jnp.sum(values * values, axis=-1, keepdims=True) * (1.0 / width)
            factor = lax.rsqrt(mean + EPS)
            scale[...] = jnp.broadcast_to(factor, scale.shape)
            out[...] = (values * factor * gn[0:1, :]).astype(BF)

        if with_quarter:
            count = qrt.shape[0]

            def work():
                for i in range(len(wgts)):
                    into[i].wait()
                    away[i].start()
                norm()

            def places(rank, i):
                return target(i, (1 - mine) * half + rank * count, count)

            gather_square(qrt, places, sems[2:4], work, local)
            finish(away)
        else:
            norm()
        finish(grads)

    outs = [shape((rows, width), BF), shape((rows, 128), F32), shape((rows, width), BF)]
    inputs = [full, grad, gain]
    scratch, left = [], ()
    if with_quarter:
        half, inner = weights[0].shape
        many = len(weights)
        assert inner == 512
        outs.append(shape((2 * half, (many - 1) * inner), BF))
        outs.append(shape((2 * half, inner), BF))
        inputs += [*weights, quarter]
        scratch = [pltpu.VMEM((many, half, inner), BF), DMA((many,)), DMA((many,)), DMA((many,))]
        left = tuple(range(3, 3 + many)) + (-2, -1)
    return call(
        kernel,
        tuple(outs),
        inputs,
        scratch + pair_of_sems(n_tp) + pair_of_sems(12),
        7,
        "first_norm",
        left=left,
    )


def turn(values, cosine, sine):
    return values * cosine + pltpu.roll(values, HD // 2, axis=1) * sine


def softmax_rows(query, key, first_row):
    scores = mm_t(query, key) * (1.0 / math.sqrt(HD))
    rows = first_row + lax.broadcasted_iota(jnp.int32, scores.shape, 0)
    cols = lax.broadcasted_iota(jnp.int32, scores.shape, 1)
    scores = jnp.where(cols <= rows, scores, NEG)
    top = jnp.max(scores, axis=-1, keepdims=True)
    weights = jnp.exp(scores - top)
    return weights / jnp.sum(weights, axis=-1, keepdims=True)


def attention_forward(qkv, cosine, sine, n_ctx):
    rows = qkv.shape[0]
    width = qkv.shape[1] // 3
    heads = width // HD

    def kernel(prj, cs, sn, out, qry, full, own, *sems):
        greet([("ctx", n_ctx)])
        here = lax.axis_index("ctx")

        @pl.loop(0, heads)
        def _(h):
            own[:, columns(h, HD)] = turn(
                prj[:, columns(h + heads, HD)], cs[...], sn[...]
            ).astype(BF)
            own[:, columns(h + heads, HD)] = prj[:, columns(h + 2 * heads, HD)].astype(BF)

        def queries():
            @pl.loop(0, heads)
            def _(h):
                qry[:, columns(h, HD)] = turn(prj[:, columns(h, HD)], cs[...], sn[...]).astype(BF)

        def places(rank, i):
            return full.at[stretch(rank, rows), pl.ds(i * 512, 512)]

        gather_square(own, places, sems, queries)

        @pl.loop(0, heads)
        def _(h):
            probs = softmax_rows(qry[:, columns(h, HD)], full[:, columns(h, HD)], here * rows)
            out[:, columns(h, HD)] = mm(
                probs.astype(BF), full[:, columns(h + heads, HD)]
            ).astype(BF)

    return call(
        kernel,
        (
            shape((rows, width), BF),
            shape((rows, width), BF),
            shape((rows * n_ctx, 2 * width), BF),
        ),
        (qkv, cosine, sine),
        [pltpu.VMEM((rows, 2 * width), BF)] + pair_of_sems(6 * width // 512),
        2,
        "attention_forward",
    )


def second_norm(part, hidden, gain, slabs, picks, router, onehot, names, n_tp, n_ctx):
    rows, size = hidden.shape
    width = size * n_tp
    experts = n_ctx

    def kernel(
        prt, hid, gn, slb, pck, rtr, one, nms,
        resid, scale, out, moved, tokens, slot_gates, gates, mix,
        slots, mine, sums, mine_two, sums_two, low, sent, own_gates, *sems
    ):
        greet([("tp", n_tp), ("ctx", n_ctx)])
        here = lax.axis_index("tp")
        copies = scatter_columns(prt, slots, "tp", n_tp, sems[0:2])
        others = [
            send(
                slb.at[pl.ds(k * CAP, CAP)], moved.at[pl.ds(k * CAP, CAP)],
                "ctx", n_ctx, k, sems[6:8],
            )
            for k in range(1, n_ctx)
        ]
        moved[0:CAP] = slb[0:CAP]
        total = prt[:, columns(here, size)].astype(F32)
        finish(copies)
        for k in range(1, n_tp):
            total = total + slots[k - 1].astype(F32)
        total = hid[...].astype(F32) + total
        resid[...] = total
        square = total_over(row_sums(total * total), mine, sums, "tp", n_tp, sems[2:4])
        factor = lax.rsqrt(as_column(square, eighth()) * (1.0 / width) + EPS)
        scale[...] = factor
        low[...] = (resid[...] * factor[:, 0:1] * gn[0:1, :]).astype(BF)
        partial_logits = mm_t(rtr[...].astype(BF), low[...])
        mine_two[...] = partial_logits
        logit_copies = [
            send(mine_two, sums_two.at[k - 1], "tp", n_tp, k, sems[12:14]) for k in range(1, n_tp)
        ]
        gather_columns(low, out, "tp", n_tp, sems[4:6])

        def route():
            finish(logit_copies)
            logits = partial_logits
            for k in range(1, n_tp):
                logits = logits + sums_two[k - 1]
            named = [jnp.sum(one[j] * logits, axis=0, keepdims=True) for j in range(2)]
            top = jnp.maximum(named[0], named[1])
            powers = [jnp.exp(value - top) for value in named]
            both = powers[0] + powers[1]
            gate = [value / both for value in powers]
            mixed = gate[0] * nms[0] + gate[1] * nms[1]
            mix[...] = mixed
            order = lax.broadcasted_iota(jnp.int32, (8, rows), 0)
            gates[...] = jnp.where(order == 0, gate[0], jnp.where(order == 1, gate[1], 0.0))
            own_gates[...] = jnp.zeros(own_gates.shape, F32)
            for k in range(experts):
                own_gates[k, :, 0:CAP] = lax.dot_general(
                    jnp.broadcast_to(mixed[k : k + 1], (8, rows)),
                    pck[k * CAP : (k + 1) * CAP].astype(F32),
                    (((1,), (1,)), ((), ())),
                    precision=lax.Precision.HIGHEST,
                    preferred_element_type=F32,
                )
            slot_gates[0] = own_gates[0]
            for k in range(1, n_ctx):
                others.append(
                    send(own_gates.at[k], slot_gates.at[k], "ctx", n_ctx, k, sems[10:12])
                )


        def slab(k, step):
            at = columns(peer("tp", n_tp, n_tp - step), size)
            return described(
                sent.at[step, pl.ds(k * CAP, CAP)], tokens.at[pl.ds(k * CAP, CAP), at],
                sems[8:10], step * n_ctx + k, {"ctx": peer("ctx", n_ctx, k)},
            )

        def dispatch(step, block):
            sent[step] = mm(pck[...], block).astype(BF)
            tokens[0:CAP, columns(peer("tp", n_tp, n_tp - step), size)] = sent[step, 0:CAP]
            for k in (2, 3, 1):
                slab(k, step).start()

        dispatch(0, low[...])
        route()

        @pl.loop(1, n_tp)
        def _(step):
            place = out.at[:, columns(here, size)]
            described(
                low, place, sems[4:6], step - 1, {"tp": peer("tp", n_tp, step)}
            ).wait()
            dispatch(step, out[:, columns(peer("tp", n_tp, n_tp - step), size)])

        for step in range(n_tp):
            for k in (2, 3, 1):
                slab(k, step).wait()
        finish(others)

    return call(
        kernel,
        (
            shape((rows, size), F32),
            shape((rows, 128), F32),
            shape((rows, width), BF),
            shape(slabs.shape, BF),
            shape(slabs.shape, BF),
            shape((experts, 8, rows), F32),
            shape((8, rows), F32),
            shape((8, rows), F32),
        ),
        (part, hidden, gain, slabs, picks, router, onehot, names),
        [
            pltpu.VMEM((n_tp - 1, rows, size), BF),
            pltpu.VMEM((8, rows), F32),
            pltpu.VMEM((n_tp - 1, 8, rows), F32),
            pltpu.VMEM((8, rows), F32),
            pltpu.VMEM((n_tp - 1, 8, rows), F32),
            pltpu.VMEM((rows, size), BF),
            pltpu.VMEM((n_tp, experts * CAP, size), BF),
            pltpu.VMEM((experts, 8, rows), F32),
        ]
        + pair_of_sems(n_tp) * 3
        + pair_of_sems(n_ctx)
        + pair_of_sems(n_tp * n_ctx)
        + pair_of_sems(n_ctx)
        + pair_of_sems(n_tp),
        3,
        "second_norm",
    )


def second_norm_back(
    acts, weights, tokens, dots, picks, gates, onehot, names, router, resid, scale, gain, grad,
    n_tp, n_ctx,
):
    rows, size = resid.shape
    width = size * n_tp
    experts = n_ctx
    hidden = acts[0].shape[1]
    count = len(weights[0])
    part = weights[0][0].shape[0]

    def kernel(*refs):
        dga, dup, hid = refs[:3]
        wgt = [refs[3 + i * count : 3 + (i + 1) * count] for i in range(3)]
        refs = refs[3 + 3 * count :]
        tok, dts, pck, gts, one, nms, rtr, rsd, scl, gn, grd = refs[:11]
        d_resid, low, d_gain, d_logits, out_rows = refs[11:16]
        refs = refs[16:]
        if count == 2:
            up_away, up_held, up_sem = refs[:1] + refs[1:3]
            refs = refs[3:]
        (
            drw, eo, buffer, back, back_dots, parts, slots, mine, sums, mine_two, sums_two, loads,
            out_sem,
        ) = refs[:13]
        sems = refs[13:]
        here = lax.axis_index("tp")
        first = lax.axis_index("fsdp")

        def load(which, rank, slot, lane):
            feature = rank * size
            inside = pl.ds(pl.multiple_of(lax.rem(feature, part), 16), size)
            target = buffer.at[slot, lane]
            if count == 1:
                pltpu.make_async_copy(
                    wgt[which][0].at[inside], target, loads.at[slot, lane]
                ).start()
                return
            own = feature // part == first

            @pl.when(own)
            def _():
                pltpu.make_async_copy(
                    wgt[which][0].at[inside], target, loads.at[slot, lane]
                ).start()

            @pl.when(jnp.logical_not(own))
            def _():
                pltpu.make_async_copy(
                    wgt[which][1].at[inside], target, loads.at[slot, lane]
                ).start()

        def loaded(which, slot, lane):
            pltpu.make_async_copy(
                wgt[which][0].at[pl.ds(0, size)], buffer.at[slot, lane], loads.at[slot, lane]
            ).wait()

        load(0, peer("tp", n_tp, 1), 0, 0)
        load(1, peer("tp", n_tp, 1), 0, 1)
        greet([("tp", n_tp), ("ctx", n_ctx)])
        small = []
        for k in range(1, n_ctx):
            small.append(
                send(dts.at[k], back_dots.at[k - 1], "ctx", n_ctx, n_ctx - k, sems[0:2])
            )

        def slab(k, rank, step):
            at = columns(rank, size)
            return described(
                drw.at[pl.ds(k * CAP, CAP), at], back.at[k - 1, :, at],
                sems[2:4], step * n_ctx + k - 1, {"ctx": peer("ctx", n_ctx, n_ctx - k)},
            )

        @pl.loop(0, n_tp)
        def _(step):
            rank = peer("tp", n_tp, step + 1)
            slot = lax.rem(step, 2)
            loaded(0, slot, 0)
            loaded(1, slot, 1)

            @pl.when(step + 1 < n_tp)
            def _():
                load(0, peer("tp", n_tp, step + 2), 1 - slot, 0)
                load(1, peer("tp", n_tp, step + 2), 1 - slot, 1)

            drw[:, columns(rank, size)] = (
                mm_t(dga[...], buffer[slot, 0]) + mm_t(dup[...], buffer[slot, 1])
            ).astype(BF)
            for k in (2, 3, 1):
                slab(k, rank, step).start()

        load(2, 0, 0, 0)

        @pl.loop(0, n_tp)
        def _(rank):
            slot = lax.rem(rank, 2)
            loaded(2, slot, 0)

            @pl.when(rank + 1 < n_tp)
            def _():
                load(2, rank + 1, 1 - slot, 0)

            eo[:, columns(rank, size)] = mm_t(hid[...], buffer[slot, 0]).astype(BF)

        pltpu.make_async_copy(eo, out_rows, out_sem).start()
        if count == 2:

            @pl.loop(0, part // 256)
            def _(i):
                at = pl.ds(pl.multiple_of((1 - first) * part + i * 256, 128), 256)
                up_held[stretch(i, 256), :] = t_mm(tok[:, at], dup[...]).astype(BF)

            pltpu.make_async_copy(up_held, up_away, up_sem).start()
        finish(small)
        order = lax.broadcasted_iota(jnp.int32, (8, rows), 0)
        own = jnp.zeros((8, rows), F32)
        for k in range(experts):
            by_slot = dts[0] if k == 0 else back_dots[k - 1]
            by_row = lax.dot_general(
                by_slot[:, 0:CAP],
                pck[k * CAP : (k + 1) * CAP].astype(F32),
                (((1,), (0,)), ((), ())),
                precision=lax.Precision.HIGHEST,
                preferred_element_type=F32,
            )
            own = own + jnp.where(order == k, by_row, 0.0)
        gate_grad = total_over(own, mine, sums, "tp", n_tp, sems[4:6])
        both = [jnp.sum(nms[j] * gate_grad, axis=0, keepdims=True) for j in range(2)]
        gate = [gts[j : j + 1, :] for j in range(2)]
        mean = gate[0] * both[0] + gate[1] * both[1]
        logits = sum(gate[j] * (both[j] - mean) * one[j] for j in range(2))
        d_logits[...] = logits

        def combined(step):
            rank = peer("tp", n_tp, step)
            at = columns(rank, size)
            for k in (2, 3, 1):
                slab(k, rank, step - 1).wait()
            block = t_mm(pck[0:CAP], drw[0:CAP, at])
            for k in range(1, experts):
                block = block + t_mm(pck[k * CAP : (k + 1) * CAP], back[k - 1, :, at])
            return block

        def give(step):
            return described(
                parts.at[step - 1], slots.at[step - 1], sems[6:8], step - 1,
                {"tp": peer("tp", n_tp, step)},
            )

        @pl.loop(1, n_tp)
        def _(step):
            parts[step - 1] = combined(step).astype(BF)
            give(step).start()

        copies = [give(step) for step in range(1, n_tp)]
        total = combined(n_tp)
        total = total + lax.dot_general(
            logits.astype(BF),
            rtr[...].astype(BF),
            (((0,), (0,)), ((), ())),
            preferred_element_type=F32,
        )
        finish(copies)
        for k in range(1, n_tp):
            total = total + slots[k - 1].astype(F32)
        factor = scl[:, 0:1]
        unit = rsd[...] * factor
        d_gain[...] = jnp.broadcast_to(jnp.sum(total * unit, axis=0, keepdims=True), d_gain.shape)
        gained = total * gn[0:1, :]
        d_resid[...] = gained
        dot = total_over(row_sums(unit * gained), mine_two, sums_two, "tp", n_tp, sems[8:10])
        dot = as_column(dot, eighth())[:, 0:1] * (1.0 / width)
        result = grd[...].astype(F32) + factor * (d_resid[...] - rsd[...] * factor * dot)
        d_resid[...] = result
        low[...] = result.astype(BF)
        pltpu.make_async_copy(eo, out_rows, out_sem).wait()
        if count == 2:
            pltpu.make_async_copy(up_held, up_away, up_sem).wait()

    outs = [
        shape((rows, size), F32),
        shape((rows, size), BF),
        shape((8, size), F32),
        shape((8, rows), F32),
        shape((experts * CAP, width), BF),
    ]
    held = []
    if count == 2:
        outs.append(shape((part, hidden), BF))
        held = [pltpu.VMEM((part, hidden), BF), DMA]
    flat = [array for group in weights for array in group]
    return call(
        kernel,
        tuple(outs),
        (*acts, *flat, tokens, dots, picks, gates, onehot, names, router, resid, scale, gain, grad),
        held
        + [
            pltpu.VMEM((experts * CAP, width), BF),
            pltpu.VMEM((experts * CAP, width), BF),
            pltpu.VMEM((2, 2, size, hidden), BF),
            pltpu.VMEM((n_ctx - 1, CAP, width), BF),
            pltpu.VMEM((n_ctx - 1, 8, rows), F32),
            pltpu.VMEM((n_tp - 1, rows, size), BF),
            pltpu.VMEM((n_tp - 1, rows, size), BF),
            pltpu.VMEM((8, rows), F32),
            pltpu.VMEM((n_tp - 1, 8, rows), F32),
            pltpu.VMEM((8, rows), F32),
            pltpu.VMEM((n_tp - 1, 8, rows), F32),
            DMA((2, 2)),
            DMA,
        ]
        + pair_of_sems(n_ctx)
        + pair_of_sems(n_tp * n_ctx)
        + pair_of_sems(n_tp) * 3,
        4,
        "second_norm_back",
        left=tuple(range(3, 3 + 3 * count)) + ((-2, -1) if count == 2 else (-1,)),
    )


def attention_backward(
    low, output_w, query, kv, cosine, sine, sums, payload, n_tp, n_ctx
):
    rows, size = low.shape
    width = size * n_tp
    inner = query.shape[1]
    heads = inner // HD
    scale = 1.0 / math.sqrt(HD)

    half = heads // 2
    sums, sums_input = sums
    lane = 2 * half * HD

    def kernel(*refs):
        lw, wgt, qry, full, cs, sn, made = refs[:7]
        n_in, n_out = 7 + len(payload.inputs), len(payload.outs)
        d_attn, d_qkv, summed = refs[n_in : n_in + 3]
        scratch = refs[n_in + 3 + n_out :]
        dot, dqs, dkv, slots, last, both, total, kept = scratch[:8]
        sems = scratch[8:12]
        sums.take(made, scratch[12 : 12 + len(sums.scratch)])
        payload.take(
            refs[7:n_in], refs[n_in + 3 : n_in + 3 + n_out], scratch[12 + len(sums.scratch) :]
        )
        payload.load()
        greet([("tp", n_tp), ("ctx", n_ctx)])
        here, beside, across = quad()
        beyond = lax.rem(beside + 2, 4)
        copies = gather_columns(lw, d_attn, "tp", n_tp, sems[2:4])
        sums.start()
        payload.go()

        @pl.loop(0, heads)
        def _(h):
            at = columns(h, HD)
            kept[h] = softmax_rows(qry[:, at], full[:, at], here * rows)

        for step in range(n_tp):
            rank = peer("tp", n_tp, n_tp - step)
            weights = wgt[pl.ds(pl.multiple_of(rank * size, 16), size), :]
            if step:
                copies[step - 1].wait()
                total[...] += mm(d_attn[:, columns(rank, size)], weights)
            else:
                total[...] = mm(lw[...], weights)
        dot[...] = total[...].astype(BF)
        first, second, third = [], [], []
        for j in range(2):

            @pl.loop(0, half)
            def _(i):
                h = j * half + i
                at, at_v = columns(h, HD), columns(h + heads, HD)
                key_at = pl.ds(pl.multiple_of(j * lane + i * HD, 128), HD)
                value_at = pl.ds(pl.multiple_of(j * lane + (half + i) * HD, 128), HD)
                probs = kept[h]
                d_probs = mm_t(dot[:, at], full[:, at_v])
                delta = jnp.sum(probs * d_probs, axis=-1, keepdims=True)
                d_scores = (probs * (d_probs - delta)).astype(BF)
                dqs[:, at] = mm(d_scores, full[:, at]) * scale
                dkv[:, key_at] = (t_mm(d_scores, qry[:, at]) * scale).astype(BF)
                dkv[:, value_at] = t_mm(probs.astype(BF), dot[:, at]).astype(BF)

            at = pl.ds(j * lane, lane)
            first.append(
                remote(
                    dkv.at[stretch(beyond, rows), at], slots.at[0, :, at],
                    sems, 3 * j, {"ctx": beside},
                )
            )
            second.append(
                remote(
                    dkv.at[stretch(beside, rows), at], slots.at[1, :, at],
                    sems, 3 * j + 1, {"ctx": beside},
                )
            )
        for j in range(2):
            at = pl.ds(j * lane, lane)
            first[j].wait()
            both[:, at] = (
                dkv[stretch(across, rows), at].astype(F32) + slots[0, :, at].astype(F32)
            ).astype(BF)
            third.append(
                remote(both.at[:, at], last.at[:, at], sems, 3 * j + 2, {"ctx": across})
            )

        @pl.loop(0, heads)
        def _(h):
            d_qkv[:, columns(h, HD)] = turn(dqs[:, columns(h, HD)], cs[...], sn[...]).astype(BF)

        for j in range(2):
            second[j].wait()
            third[j].wait()

            @pl.loop(0, half)
            def _(i):
                h = j * half + i
                key_at = pl.ds(pl.multiple_of(j * lane + i * HD, 128), HD)
                value_at = pl.ds(pl.multiple_of(j * lane + (half + i) * HD, 128), HD)
                mine = stretch(here, rows)
                d_key = dkv[mine, key_at].astype(F32) + slots[1, :, key_at].astype(F32)
                d_key = d_key + last[:, key_at].astype(F32)
                d_qkv[:, columns(h + heads, HD)] = turn(d_key, cs[...], sn[...]).astype(BF)
                d_value = dkv[mine, value_at].astype(F32) + slots[1, :, value_at].astype(F32)
                d_value = d_value + last[:, value_at].astype(F32)
                d_qkv[:, columns(h + 2 * heads, HD)] = d_value.astype(BF)

        summed[...] = sums.total().astype(BF)
        payload.wait()

    return call(
        kernel,
        (
            shape((rows, width), BF),
            shape((rows, 3 * inner), BF),
            shape(sums.shape, BF),
            *payload.outs,
        ),
        (low, output_w, query, kv, cosine, sine, sums_input, *payload.inputs),
        [
            pltpu.VMEM((rows, inner), BF),
            pltpu.VMEM((rows, inner), F32),
            pltpu.VMEM((rows * n_ctx, 2 * inner), BF),
            pltpu.VMEM((2, rows, 2 * inner), BF),
            pltpu.VMEM((rows, 2 * inner), BF),
            pltpu.VMEM((rows, 2 * inner), BF),
            pltpu.VMEM((rows, inner), F32),
            pltpu.VMEM((heads, rows, rows * n_ctx), F32),
        ]
        + pair_of_sems(6)
        + pair_of_sems(n_tp)
        + sums.scratch
        + payload.scratch,
        5,
        "attention_backward",
        left=(6, 6 + len(payload.inputs), -len(payload.outs)),
    )


def first_norm_back(d_qkv, weights, hidden, scale, gain, d_resid, payload, n_tp, n_ctx):
    rows, size = hidden.shape
    width = size * n_tp

    def kernel(*refs):
        dpr, wgt, hid, scl, gn, dr = refs[:6]
        n_in, n_out = 6 + len(payload.inputs), len(payload.outs)
        out, d_gain = refs[n_in : n_in + 2]
        scratch = refs[n_in + 2 + n_out :]
        held, parts, slots, mine, sums, loads = scratch[:6]
        sems = scratch[6:10]
        payload.take(refs[6:n_in], refs[n_in + 2 : n_in + 2 + n_out], scratch[10:])

        def block(step):
            rank = peer("tp", n_tp, step)
            return pltpu.make_async_copy(
                wgt.at[stretch(rank, size), :], held.at[step - 1], loads.at[step - 1]
            )

        for step in range(1, n_tp + 1):
            block(step).start()
        payload.load()
        greet([("tp", n_tp), ("ctx", n_ctx)])

        def give(step):
            return described(
                parts.at[step - 1], slots.at[step - 1], sems[0:2], step - 1,
                {"tp": peer("tp", n_tp, step)},
            )

        @pl.loop(1, n_tp)
        def _(step):
            block(step).wait()
            parts[step - 1] = mm_t(dpr[...], held[step - 1]).astype(BF)
            give(step).start()

        copies = [give(step) for step in range(1, n_tp)]
        block(n_tp).wait()
        out[...] = mm_t(dpr[...], held[n_tp - 1])
        payload.go()
        finish(copies)
        total = out[...]
        for k in range(1, n_tp):
            total = total + slots[k - 1].astype(F32)
        factor = scl[:, 0:1]
        unit = hid[...].astype(F32) * factor
        d_gain[...] = jnp.broadcast_to(jnp.sum(total * unit, axis=0, keepdims=True), d_gain.shape)
        gained = total * gn[0:1, :]
        out[...] = gained
        dot = total_over(row_sums(unit * gained), mine, sums, "tp", n_tp, sems[2:4])
        dot = as_column(dot, eighth())[:, 0:1] * (1.0 / width)
        unit = hid[...].astype(F32) * factor
        out[...] = dr[...] + factor * (out[...] - unit * dot)
        payload.wait()

    return call(
        kernel,
        (shape((rows, size), F32), shape((8, size), F32), *payload.outs),
        (d_qkv, weights, hidden, scale, gain, d_resid, *payload.inputs),
        [
            pltpu.VMEM((n_tp, size, d_qkv.shape[1]), BF),
            pltpu.VMEM((n_tp - 1, rows, size), BF),
            pltpu.VMEM((n_tp - 1, rows, size), BF),
            pltpu.VMEM((8, rows), F32),
            pltpu.VMEM((n_tp - 1, 8, rows), F32),
            DMA((n_tp,)),
        ]
        + pair_of_sems(n_tp) * 2
        + payload.scratch,
        6,
        "first_norm_back",
        left=(1, 5 + len(payload.inputs), -len(payload.outs)),
    )


class ExpertsOut:

    def __init__(self, made, done, picks, mix, resid, n_tp, n_ctx):
        self.n_ctx = n_ctx
        self.sums = RowSums(made, done.shape[0], made.shape[0] - done.shape[0], n_tp)
        self.inputs = [made, done, picks, mix, resid]
        self.size = resid.shape[1]
        self.out = shape(resid.shape, BF)
        self.scratch = [
            pltpu.VMEM(self.sums.shape, BF),
            pltpu.VMEM((n_ctx - 1, CAP, self.size), BF),
        ]
        self.scratch += pair_of_sems(n_ctx) + self.sums.scratch

    def take(self, ins, out, scratch):
        self.ins, self.out_ref, self.held = ins, out, scratch[:4]
        self.sums.take(ins[0], scratch[4:])

    def block(self, k):
        done, share = self.ins[1], self.held[0]
        first = k * CAP
        if first < done.shape[0]:
            return done.at[pl.ds(first, CAP)]
        return share.at[pl.ds(first - done.shape[0], CAP)]

    def give_back(self):
        share, back = self.held[:2]
        share[...] = self.sums.total().astype(BF)
        n_ctx = self.n_ctx
        self.copies = [
            send(self.block(k), back.at[k - 1], "ctx", n_ctx, n_ctx - k, self.held[2:4])
            for k in range(1, n_ctx)
        ]

    def mix(self):
        made, done, picks, mix, resid = self.ins
        back = self.held[1]
        finish(self.copies)
        order = lax.broadcasted_iota(jnp.int32, (8, 128), 0)
        total = resid[...]
        for k in range(self.n_ctx):
            gate = as_column(mix[...], jnp.where(order == k, 1.0, 0.0))[:, 0:1]
            rows = self.block(0)[...] if k == 0 else back[k - 1]
            total = total + gate * t_mm(picks[k * CAP : (k + 1) * CAP], rows)
        self.out_ref[...] = total.astype(BF)


def weight_grads(products, groups, small, payload, experts_out, n_tp, n_ctx):
    width = products[0][0].shape[1]
    places = 2 * n_ctx
    cut = width // places
    total_columns = sum(size for _, _, size in groups)
    flat = [array for pair in products for array in pair]
    inputs = [*flat, small, *experts_out.inputs, *payload.inputs]

    def kernel(*refs):
        factors, refs = refs[: len(flat)], refs[len(flat) :]
        sml, refs = refs[0], refs[1:]
        given, refs = refs[: len(experts_out.inputs)], refs[len(experts_out.inputs) :]
        paid, refs = refs[: len(payload.inputs)], refs[len(payload.inputs) :]
        out, small_out, block_out = refs[:3]
        paid_out, refs = refs[3 : 3 + len(payload.outs)], refs[3 + len(payload.outs) :]
        sml_full, sml_slots, refs = refs[0], refs[1], refs[2:]
        scratch, refs = refs[: 6 * len(groups)], refs[6 * len(groups) :]
        experts_out.take(given, block_out, refs[: len(experts_out.scratch)])
        refs = refs[len(experts_out.scratch) :]
        payload.take(paid, paid_out, refs[: len(payload.scratch)])
        sems = refs[len(payload.scratch) :]
        payload.load()
        barrier = pltpu.get_barrier_semaphore()
        here, beside, across = quad()
        beyond = lax.rem(beside + 2, 4)
        mine = lax.axis_index("fsdp")
        other = 1 - mine
        place = mine * n_ctx + here
        others = []
        for i in range(1, places):
            to = lax.rem(place + i, places)
            others.append((to, {"fsdp": to // n_ctx, "ctx": lax.rem(to, n_ctx)}))
        ahead = [{"tp": peer("tp", n_tp, k)} for k in range(1, n_tp)]
        for device in ahead + [device for _, device in others]:
            pl.semaphore_signal(barrier, inc=1, device_id=device, device_id_type=MESH)
        pl.semaphore_wait(barrier, n_tp - 1 + places - 1)
        gathers = gather_columns(sml, sml_full, "tp", n_tp, sems[0:2])
        experts_out.sums.start()
        moves = []

        def near(g):
            which, start, size = groups[g]
            prt, come = scratch[6 * g : 6 * g + 2]
            left, right = factors[2 * which : 2 * which + 2]

            @pl.loop(0, places)
            def _(i):
                prt[i] = t_mm(left[:, columns(i, cut)], right[:, start : start + size]).astype(BF)

            blocks = [(other, beyond), (other, beside), (mine, beyond), (mine, beside)]
            moves.append(
                [
                    remote(
                        prt.at[rank * n_ctx + column], come.at[i],
                        sems[4 + 6 * g : 6 + 6 * g], i, {"ctx": beside},
                    )
                    for i, (rank, column) in enumerate(blocks)
                ]
            )

        def chip(g, i, rank, column):
            prt, come = scratch[6 * g : 6 * g + 2]
            moves[g][i].wait()
            return prt[rank * n_ctx + column].astype(F32) + come[i].astype(F32)

        hops = []

        def hop(g):
            two, far = scratch[6 * g + 2 : 6 * g + 4]
            sent = []
            for i, column in enumerate((across, here)):
                two[i] = chip(g, i, other, column).astype(BF)
                sent.append(
                    remote(
                        two.at[i], far.at[i], sems[6 + 6 * g : 8 + 6 * g], i, {"fsdp": other}
                    )
                )
            hops.append(sent)

        near(0)
        payload.go(0, 1)
        finish(gathers)
        totals = [
            remote(sml_full.at[:, columns(to, cut)], sml_slots.at[i], sems[2:4], i, device)
            for i, (to, device) in enumerate(others)
        ]
        hop(0)
        for g in range(1, len(groups)):
            near(g)
            hop(g)
            if g == 1:
                payload.go(1, 4)
        lasts = []
        for g in range(len(groups)):
            far, one, last = scratch[6 * g + 3 : 6 * g + 6]
            value = chip(g, 2, mine, across)
            hops[g][0].wait()
            one[...] = (value + far[0].astype(F32)).astype(BF)
            lasts.append(
                remote(one, last, sems[8 + 6 * g : 10 + 6 * g], 0, {"ctx": across})
            )
        finish(totals)
        sums = sml_full[:, columns(place, cut)]
        for i in range(places - 1):
            sums = sums + sml_slots[i]
        small_out[...] = sums
        experts_out.give_back()
        start = 0
        for g, (_, _, size) in enumerate(groups):
            far = scratch[6 * g + 3]
            value = chip(g, 3, mine, here)
            hops[g][1].wait()
            value = value + far[1].astype(F32)
            out[:, start : start + size] = value
            start += size
        experts_out.mix()
        payload.wait()
        start = 0
        for g, (_, _, size) in enumerate(groups):
            lasts[g].wait()
            at = pl.ds(start, size)
            out[:, at] = out[:, at] + scratch[6 * g + 5][...].astype(F32)
            start += size

    buffers = [pltpu.VMEM((8, width), F32), pltpu.VMEM((places - 1, 8, cut), F32)]
    sems = pair_of_sems(n_tp) + pair_of_sems(places)
    for _, _, size in groups:
        buffers += [
            pltpu.VMEM((places, cut, size), BF),
            pltpu.VMEM((4, cut, size), BF),
            pltpu.VMEM((2, cut, size), BF),
            pltpu.VMEM((2, cut, size), BF),
            pltpu.VMEM((cut, size), BF),
            pltpu.VMEM((cut, size), BF),
        ]
        sems += pair_of_sems(4) + pair_of_sems(2) + pair_of_sems(1)
    return call(
        kernel,
        (
            shape((cut, total_columns), F32),
            shape((8, cut), F32),
            experts_out.out,
            *payload.outs,
        ),
        inputs,
        buffers + experts_out.scratch + payload.scratch + sems,
        10,
        "weight_grads",
        left=(
            len(flat) + 1,
            len(inputs) - 1,
            -len(payload.outs),
        ),
    )


def experts_back(experts_out, payload, n_tp, n_ctx):
    inputs = [*experts_out.inputs, *payload.inputs]
    given = len(experts_out.inputs)

    def kernel(*refs):
        ins, refs = refs[: len(inputs)], refs[len(inputs) :]
        outs, scratch = refs[: 1 + len(payload.outs)], refs[1 + len(payload.outs) :]
        experts_out.take(ins[:given], outs[0], scratch[: len(experts_out.scratch)])
        payload.take(ins[given:], outs[1:], scratch[len(experts_out.scratch) :])
        greet([("tp", n_tp), ("ctx", n_ctx)])
        experts_out.sums.start()
        payload.go()
        experts_out.give_back()
        experts_out.mix()
        payload.wait()

    return call(
        kernel,
        (experts_out.out, *payload.outs),
        inputs,
        experts_out.scratch + payload.scratch,
        9,
        "experts_back",
        left=(0, len(inputs) - 1, -len(payload.outs)),
    )


def write_out(experts_grads, attn_grad, plain, n_ctx):
    _, rows, size = experts_grads[0][0].shape
    steps = max(1, rows // 32)
    tile = rows // steps
    many = len(experts_grads)
    plain = list(plain)
    blocks = []
    if attn_grad is not None:
        block = attn_grad.shape[1] // 4
        blocks = [shape((attn_grad.shape[0], block), F32)] * 4
        plain.append(attn_grad)

    def kernel(*refs):
        here = lax.axis_index("ctx")
        ins, outs = refs[: 2 * many + len(plain)], refs[2 * many + len(plain) :]
        for i in range(many):
            came, mine = ins[2 * i : 2 * i + 2]
            outs[i][here] = mine[...].astype(F32)
            for k in range(1, n_ctx):
                outs[i][lax.rem(here + n_ctx - k, n_ctx)] = came[k - 1].astype(F32)
        for i in range(len(plain) - (1 if blocks else 0)):
            outs[many + i][...] = ins[2 * many + i][...]
        for i in range(len(blocks)):
            outs[i - 4][...] = ins[-1][:, i * block : (i + 1) * block]

    def flat(array):
        return pl.BlockSpec((array.shape[0] // steps, array.shape[1]), lambda i: (i, 0))

    in_specs, out_specs, out_shape = [], [], []
    for _ in experts_grads:
        in_specs.append(pl.BlockSpec((n_ctx - 1, tile, size), lambda i: (0, i, 0)))
        in_specs.append(pl.BlockSpec((tile, size), lambda i: (i, 0)))
        out_specs.append(pl.BlockSpec((n_ctx, tile, size), lambda i: (0, i, 0)))
        out_shape.append(shape((n_ctx, rows, size), F32))
    for array in plain[: len(plain) - (1 if blocks else 0)] + blocks:
        out_specs.append(flat(array))
        out_shape.append(shape(array.shape, array.dtype))
    in_specs += [flat(array) for array in plain]
    inputs = [array for pair in experts_grads for array in pair] + plain
    return pl.pallas_call(
        kernel,
        grid=(steps,),
        in_specs=in_specs,
        out_specs=out_specs,
        out_shape=out_shape,
        cost_estimate=pl.CostEstimate(
            flops=0, bytes_accessed=6 * many * n_ctx * rows * size, transcendentals=0
        ),
        name="write_out",
    )(*inputs)


def after(value, *needed):
    return lax.optimization_barrier((value, *needed))[0]


def shards(
    hidden_in,
    out_grad,
    attn_gain,
    w_query,
    w_key,
    w_value,
    w_output,
    ffn_gain,
    w_router,
    w_gate,
    w_up,
    w_down,
    routes,
):
    rows_here, width_tp = hidden_in.shape
    here_tp = lax.axis_index("tp")
    here_ctx = lax.axis_index("ctx")
    here_fsdp = lax.axis_index("fsdp")
    n_fsdp = lax.axis_size("fsdp")
    n_ctx = lax.axis_size("ctx")
    n_tp = lax.axis_size("tp")
    experts = w_gate.shape[0]
    assert experts == n_ctx == 4
    width = width_tp * n_tp
    part = width // n_fsdp
    pair = n_fsdp == 2
    heads_width = w_query.shape[1]

    def swap_fsdp(value):
        return lax.ppermute(value, "fsdp", [(0, 1), (1, 0)])

    def other_parts(weight):
        if pair:
            return [weight, swap_fsdp(weight)]
        return [lax.all_gather(weight, "fsdp", axis=0, tiled=True)]

    def split(values):
        if pair:
            return [
                lax.dynamic_slice_in_dim(values, here_fsdp * part, part, 1),
                lax.dynamic_slice_in_dim(values, (1 - here_fsdp) * part, part, 1),
            ]
        return [values]

    def join(pieces):
        if pair:
            first = here_fsdp == 0
            return jnp.concatenate(
                [jnp.where(first, pieces[0], pieces[1]), jnp.where(first, pieces[1], pieces[0])],
                axis=1,
            )
        return pieces[0]

    def into(values, weights):
        return sum(mm(x, w) for x, w in zip(split(values), weights))

    def back(values, weights):
        return join([mm_t(values, w) for w in weights])

    def my_features(values):
        return lax.dynamic_slice_in_dim(values, here_tp * width_tp, width_tp, values.ndim - 1)

    attn_w = (w_query, w_key, w_value, w_output)
    small = jnp.concatenate(
        [attn_gain[None], ffn_gain[None], w_router.T, jnp.zeros((2, part), BF)], axis=0
    )
    if pair:
        quarter = part // n_ctx
        own_quarter = jnp.concatenate(
            [lax.dynamic_slice_in_dim(w, here_ctx * quarter, quarter, 0) for w in attn_w], axis=1
        )
        other_quarter = swap_fsdp(own_quarter)
        other_small = swap_fsdp(small)
        small_full = join([small, other_small]).astype(F32)
    else:
        other_quarter = None
        small_full = lax.all_gather(small, "fsdp", axis=1, tiled=True).astype(F32)
    inputs_full, up_mine, down_mine = gather_tp(hidden_in, (w_up, w_down), n_tp)
    gate_w = other_parts(lax.dynamic_index_in_dim(w_gate, here_ctx, 0, False))
    up_w = other_parts(up_mine)
    down_w = other_parts(down_mine)
    small_here = my_features(small_full)
    gain_one_here = jnp.broadcast_to(small_here[0:1], small_here.shape)
    gain_two_here = jnp.broadcast_to(small_here[1:2], small_here.shape)
    nothing = [(0, 8 - experts), (0, 0)]
    router_here = jnp.pad(small_here[2 : 2 + experts], nothing)

    relative = (jnp.arange(experts, dtype=jnp.int32) + here_ctx) % experts
    numbers = jnp.arange(8, dtype=jnp.int32)
    onehot = (routes.T[:, None, :] == numbers[None, :, None]).astype(F32)
    named = (routes.T[:, None, :] == relative[None, :, None]).astype(F32)
    names = jnp.pad(named, [(0, 0)] + nothing)
    chosen = jnp.sum(named, axis=0)
    earlier = jnp.triu(jnp.ones((rows_here, rows_here), BF), 1)
    slot_of = mm(chosen.astype(BF), earlier).astype(jnp.int32)
    slots = jnp.arange(CAP, dtype=jnp.int32)
    picks = (slot_of[:, None, :] == slots[None, :, None]) & (chosen[:, None, :] > 0)
    picks = picks.astype(BF).reshape(experts * CAP, rows_here)

    gathered = first_norm(
        inputs_full, out_grad, small_full, attn_w, other_quarter, n_tp, n_ctx
    )
    normed_one, scale_one, grad_full = gathered[:3]
    if pair:
        qkv_w, output_w = gathered[3:]
    else:
        qkv_w, output_w = (
            lax.all_gather(w, "fsdp", axis=0, tiled=True)
            for w in (jnp.concatenate(attn_w[:3], axis=1), w_output)
        )
    positions = here_ctx * rows_here + jnp.arange(rows_here, dtype=jnp.int32)
    cosine, sine = rotary_tables(positions)
    attended, query, kv = attention_forward(mm(normed_one, qkv_w), cosine, sine, n_ctx)
    resid, scale_two, normed_two, grad_rows, token_rows, slot_gates, gates, mix = second_norm(
        mm_t(attended, output_w).astype(BF),
        hidden_in,
        gain_two_here,
        mm(picks, grad_full).astype(BF),
        picks,
        router_here,
        onehot,
        names,
        n_tp,
        n_ctx,
    )
    gate_rows = slot_gates[:, 0, :CAP].reshape(experts * CAP, 1)

    gate_act = into(token_rows, gate_w)
    up_act = into(token_rows, up_w)
    sigma_act = jax.nn.sigmoid(gate_act)
    hidden_act = (gate_act * sigma_act * up_act).astype(BF)
    d_result = (gate_rows * grad_rows.astype(F32)).astype(BF)

    def away(left, right):
        value = t_mm(split(left)[1], right).astype(BF)
        return value, swap_fsdp(value)

    def payload_of(left, right, come):
        if pair:
            return Payload(n_ctx, product=(left, right, come))
        return Payload(
            n_ctx,
            rows=lax.psum_scatter(
                t_mm(left, right).astype(BF), "fsdp", scatter_dimension=0, tiled=True
            ),
        )

    def came_and_own(outs, payload):
        if pair:
            return tuple(outs)
        own = lax.dynamic_slice_in_dim(payload.inputs[0], here_ctx * payload.cut, payload.cut, 0)
        return outs[0], own

    down_come = gate_come = up_come = None
    if pair:
        down_away, down_come = away(d_result, hidden_act)
        grad_rows = after(grad_rows, down_away)
    d_hidden = into(grad_rows, down_w)
    gate_dot = jnp.sum(hidden_act.astype(F32) * d_hidden, axis=-1).reshape(experts, CAP)
    gate_dot = jnp.broadcast_to(
        jnp.pad(gate_dot, [(0, 0), (0, rows_here - CAP)])[:, None, :], (experts, 8, rows_here)
    )
    d_hidden = gate_rows * d_hidden
    d_gate_act = (d_hidden * up_act * sigma_act * (1.0 + gate_act * (1.0 - sigma_act))).astype(BF)
    d_up_act = (d_hidden * gate_act * sigma_act).astype(BF)
    if pair:
        gate_away, gate_come = away(token_rows, d_gate_act)

    acts = (d_gate_act, d_up_act, hidden_act)
    if pair:
        acts = lax.optimization_barrier((*acts, gate_away))[:3]
    d_resid, d_attn_here, gain_two_part, d_logits, made, *up_away = second_norm_back(
        acts,
        (gate_w, up_w, down_w),
        token_rows,
        gate_dot,
        picks,
        gates,
        onehot,
        names,
        router_here,
        resid,
        scale_two,
        gain_two_here,
        out_grad,
        n_tp,
        n_ctx,
    )
    if pair:
        up_come = swap_fsdp(up_away[0])

    payload = payload_of(d_result, hidden_act, down_come)
    early = (RowSums(made, 0, CAP, n_tp), made)
    d_attn, d_qkv, made_early, *outs = attention_backward(
        d_attn_here, output_w, query, kv, cosine, -sine, early, payload, n_tp, n_ctx
    )
    grad_down = came_and_own(outs, payload)
    payload = payload_of(token_rows, d_gate_act, gate_come)
    in_grad, gain_one_part, *outs = first_norm_back(
        d_qkv, qkv_w, hidden_in, scale_one, gain_one_here, d_resid, payload, n_tp, n_ctx
    )
    grad_gate = came_and_own(outs, payload)
    payload = payload_of(token_rows, d_up_act, up_come)

    small_part = jnp.concatenate(
        [
            gain_one_part[:1],
            gain_two_part[:1],
            mm(d_logits[:experts].astype(BF), my_features(normed_two)),
            jnp.zeros((6 - experts, width_tp), F32),
        ],
        axis=0,
    )
    written = write_out([grad_gate, grad_down], None, (), n_ctx)
    if pair:
        small_part = after(small_part, *written)
    grad_gate, grad_down = written
    experts_out = ExpertsOut(made, made_early, picks, mix, resid, n_tp, n_ctx)
    if pair:
        grad_attn, small_grad, block_out, *outs = weight_grads(
            [(d_attn, attended), (normed_one, d_qkv)],
            [(0, 0, heads_width), (1, 0, 2 * heads_width), (1, 2 * heads_width, heads_width)],
            small_part,
            payload,
            experts_out,
            n_tp,
            n_ctx,
        )
    else:
        grad_attn = jnp.concatenate([t_mm(d_attn, attended), t_mm(normed_one, d_qkv)], axis=1)
        scatter = partial(
            lax.psum_scatter, axis_name=("fsdp", "ctx"), scatter_dimension=0, tiled=True
        )
        grad_attn = scatter(grad_attn.astype(BF)).astype(F32)
        small_grad = lax.all_gather(small_part, "tp", axis=1, tiled=True)
        small_grad = scatter(small_grad.T).T
        block_out, *outs = experts_back(experts_out, payload, n_tp, n_ctx)
    grad_up = came_and_own(outs, payload)
    grad_up, block_out, in_grad, grad_output, grad_query, grad_key, grad_value = write_out(
        [grad_up], grad_attn, (block_out, in_grad), n_ctx
    )
    return (
        block_out,
        in_grad,
        small_grad[0],
        grad_query,
        grad_key,
        grad_value,
        grad_output,
        small_grad[1],
        small_grad[2 : 2 + experts].T,
        grad_gate,
        grad_up,
        grad_down,
    )


def solution(mesh):
    rows = ("fsdp", "ctx")
    placed = (
        P(rows, "tp"),
        P(rows, "tp"),
        P("fsdp"),
        P("fsdp", "tp"),
        P("fsdp", "tp"),
        P("fsdp", "tp"),
        P("fsdp", "tp"),
        P("fsdp"),
        P("fsdp", None),
        P(None, "fsdp", "tp"),
        P(None, "fsdp", "tp"),
        P(None, "fsdp", "tp"),
        P(rows, None),
    )
    return jax.shard_map(
        shards,
        mesh=mesh,
        in_specs=placed,
        out_specs=(
            P(rows, "tp"),
            P(rows, "tp"),
            P(rows),
            P(rows, "tp"),
            P(rows, "tp"),
            P(rows, "tp"),
            P(rows, "tp"),
            P(rows),
            P(rows, None),
            P(None, rows, "tp"),
            P(None, rows, "tp"),
            P(None, rows, "tp"),
        ),
        check_vma=False,
    )
```

```python
from functools import partial
import math

import jax
import jax.numpy as jnp
from jax import lax
from jax.experimental import pallas as pl
from jax.experimental.pallas import tpu as pltpu
from jax.sharding import PartitionSpec as P

HD = 128
CAP = 160


EPS = 1e-05
THETA = 10000.0
NEG = -1e30
BF = jnp.bfloat16
F32 = jnp.float32


def mm(left, right):
    return jnp.dot(left, right, preferred_element_type=F32)


def mm_t(left, right):
    return lax.dot_general(left, right, (((1,), (1,)), ((), ())), preferred_element_type=F32)


def t_mm(left, right):
    return lax.dot_general(left, right, (((0,), (0,)), ((), ())), preferred_element_type=F32)


def rotary_tables(positions):
    half_size = HD // 2
    frequency = THETA ** (-(jnp.arange(half_size, dtype=F32) * 2.0 / HD))
    angles = positions.astype(F32)[:, None] * frequency[None, :]
    cosine, sine = jnp.cos(angles), jnp.sin(angles)
    return jnp.concatenate([cosine, cosine], axis=1), jnp.concatenate([-sine, sine], axis=1)


MESH = pl.DeviceIdType.MESH
VM = pl.BlockSpec(memory_space=pltpu.VMEM)
DMA = pltpu.SemaphoreType.DMA


def peer(axis, n, k):
    return lax.rem(lax.axis_index(axis) + k, n)


def greet(groups):
    barrier = pltpu.get_barrier_semaphore()
    for axis, n in groups:
        for k in range(1, n):
            pl.semaphore_signal(
                barrier, inc=1, device_id={axis: peer(axis, n, k)}, device_id_type=MESH
            )
    pl.semaphore_wait(barrier, sum(n - 1 for _, n in groups))


def described(source, target, sems, i, to):
    return pltpu.make_async_remote_copy(
        src_ref=source,
        dst_ref=target,
        send_sem=sems[0].at[i],
        recv_sem=sems[1].at[i],
        device_id=to,
        device_id_type=MESH,
    )


def remote(source, target, sems, i, to):
    copy = described(source, target, sems, i, to)
    copy.start()
    return copy


def send(source, target, axis, n, k, sems):
    return remote(source, target, sems, k - 1, {axis: peer(axis, n, k)})


def columns(n, size):
    return pl.ds(pl.multiple_of(n * size, 128), size)


def stretch(n, size):
    return pl.ds(pl.multiple_of(n * size, 16), size)


def gather_columns(own, full, axis, n, sems):
    size = own.shape[1]
    place = full.at[:, columns(lax.axis_index(axis), size)]
    copies = [send(own, place, axis, n, k, sems) for k in range(1, n)]
    place[...] = own[...]
    return copies


def scatter_columns(part, slots, axis, n, sems):
    size = slots.shape[2]
    return [
        send(part.at[:, columns(peer(axis, n, k), size)], slots.at[k - 1], axis, n, k, sems)
        for k in range(1, n)
    ]


def finish(copies):
    for copy in copies:
        copy.wait()


class Payload:

    def __init__(self, n_ctx, rows=None, product=None):
        self.n_ctx = n_ctx
        self.product = product is not None
        self.inputs = list(product) if self.product else [rows]
        last = self.inputs[-1]
        self.rows, self.hidden = last.shape
        self.cut = self.rows // n_ctx
        self.outs = [shape((n_ctx - 1, self.cut, self.hidden), BF)]
        self.scratch = pair_of_sems(n_ctx)
        if self.product:
            self.outs.append(shape((self.cut, self.hidden), BF))
            self.scratch += [
                pltpu.VMEM((self.rows, self.hidden), BF),
                pltpu.VMEM((self.rows, self.hidden), BF),
                DMA,
            ]

    def take(self, ins, outs, scratch):
        self.ins, self.out_refs, self.held = ins, outs, scratch

    def load(self):
        if self.product:
            pltpu.make_async_copy(self.ins[2], self.held[2], self.held[4]).start()

    def copy(self, k):
        to = peer("ctx", self.n_ctx, k)
        source = self.held[3] if self.product else self.ins[0]
        return described(
            source.at[stretch(to, self.cut), :], self.out_refs[0].at[k - 1],
            self.held[0:2], k - 1, {"ctx": to},
        )

    def go(self, first=0, last=4):
        n_ctx, cut = self.n_ctx, self.cut
        if not self.product:
            for j in range(first, last):
                if (j + 2) % n_ctx:
                    self.copy((j + 2) % n_ctx).start()
            return
        left, right, other = self.ins
        if first == 0:
            pltpu.make_async_copy(other, self.held[2], self.held[4]).wait()
        base = lax.axis_index("fsdp") * self.rows

        @pl.loop(first, last)
        def _(j):
            k = lax.rem(j + 2, n_ctx)
            to = peer("ctx", n_ctx, k)
            value = t_mm(left[:, pl.ds(pl.multiple_of(base + to * cut, 128), cut)], right[...])
            value = value + self.held[2][stretch(to, cut), :].astype(F32)
            self.held[3][stretch(to, cut), :] = value.astype(BF)

            @pl.when(j != n_ctx - 2)
            def _():
                self.copy(k).start()

    def wait(self):
        if self.product:
            self.out_refs[1][...] = self.held[3][stretch(lax.axis_index("ctx"), self.cut), :]
        for k in range(1, self.n_ctx):
            self.copy(k).wait()


class RowSums:

    def __init__(self, made, first, count, n_tp):
        self.n_tp, self.first = n_tp, first
        self.shape = (count, made.shape[1] // n_tp)
        self.scratch = [
            pltpu.VMEM((n_tp - 1, *self.shape), BF),
            pltpu.VMEM(self.shape, BF),
            DMA,
        ] + pair_of_sems(n_tp)

    def take(self, made, scratch):
        self.made, self.held = made, scratch

    def rows(self, rank):
        return self.made.at[pl.ds(self.first, self.shape[0]), columns(rank, self.shape[1])]

    def mine(self):
        return pltpu.make_async_copy(
            self.rows(lax.axis_index("tp")), self.held[1], self.held[2]
        )

    def start(self):
        self.mine().start()
        n = self.n_tp
        self.copies = [
            send(self.rows(peer("tp", n, k)), self.held[0].at[k - 1], "tp", n, k, self.held[3:5])
            for k in range(1, n)
        ]

    def total(self):
        self.mine().wait()
        finish(self.copies)
        value = self.held[1][...].astype(F32)
        for k in range(1, self.n_tp):
            value = value + self.held[0][k - 1].astype(F32)
        return value


def quad():
    here = lax.axis_index("ctx")
    return here, here + 1 - 2 * lax.rem(here, 2), lax.rem(here + 2, 4)


def gather_square(own, places, sems, between, local=None):
    cuts = own.shape[1] // 512
    here, beside, across = quad()
    first, second, third = [], [], []
    for i in range(cuts):
        piece = own.at[:, pl.ds(i * 512, 512)]
        first.append(remote(piece, places(here, i), sems, 3 * i, {"ctx": across}))
        second.append(remote(piece, places(here, i), sems, 3 * i + 1, {"ctx": beside}))
        if local is None:
            places(here, i)[...] = piece[...]
        else:
            pltpu.make_async_copy(piece, places(here, i), local.at[i]).start()
    between()
    for i in range(cuts):
        first[i].wait()
        third.append(
            remote(places(across, i), places(across, i), sems, 3 * i + 2, {"ctx": beside})
        )
    finish(second)
    finish(third)
    if local is not None:
        for i in range(cuts):
            piece = own.at[:, pl.ds(i * 512, 512)]
            pltpu.make_async_copy(piece, places(here, i), local.at[i]).wait()


def row_sums(values):
    ones = jnp.ones((8, values.shape[1]), F32)
    return lax.dot_general(
        ones,
        values,
        (((1,), (1,)), ((), ())),
        precision=lax.Precision.HIGHEST,
        preferred_element_type=F32,
    )


def as_column(rows, weight):
    return lax.dot_general(
        rows,
        weight,
        (((0,), (0,)), ((), ())),
        precision=lax.Precision.HIGHEST,
        preferred_element_type=F32,
    )


def eighth():
    return jnp.full((8, 128), 0.125, F32)


def total_over(sums, mine, slots, axis, n, sems):
    mine[...] = sums
    copies = [send(mine, slots.at[k - 1], axis, n, k, sems) for k in range(1, n)]
    finish(copies)
    total = sums
    for k in range(1, n):
        total = total + slots[k - 1]
    return total


def call(kernel, out_shape, inputs, scratch, collective, name, left=()):
    anywhere = pl.BlockSpec(memory_space=pl.ANY)
    outs = out_shape if isinstance(out_shape, tuple) else (out_shape,)
    specs = [anywhere if i - len(outs) in left else VM for i in range(len(outs))]
    return pl.pallas_call(
        kernel,
        out_shape=out_shape,
        in_specs=[anywhere if i in left else VM for i in range(len(inputs))],
        out_specs=tuple(specs) if isinstance(out_shape, tuple) else specs[0],
        scratch_shapes=scratch,
        compiler_params=pltpu.CompilerParams(collective_id=collective, has_side_effects=True),
        cost_estimate=pl.CostEstimate(flops=0, bytes_accessed=0, transcendentals=0),
        name=name,
    )(*inputs)


def shape(dims, dtype):
    return jax.ShapeDtypeStruct(dims, dtype)


def pair_of_sems(n):
    return [DMA((n,)), DMA((n,))]


def gather_tp(value, stacks, n_tp):
    rows, size = value.shape
    many = len(stacks)
    member = stacks[0].shape[1:]

    def kernel(own, *refs):
        stk, full, outs = refs[:many], refs[many], refs[many + 1 : 2 * many + 1]
        held, loads, stores = refs[2 * many + 1 : 2 * many + 4]
        sems = refs[2 * many + 4 :]
        here = lax.axis_index("ctx")
        into = [
            pltpu.make_async_copy(stk[i].at[here], held.at[i], loads.at[i]) for i in range(many)
        ]
        away = [pltpu.make_async_copy(held.at[i], outs[i], stores.at[i]) for i in range(many)]
        for copy in into:
            copy.start()
        greet([("tp", n_tp)])
        copies = gather_columns(own, full, "tp", n_tp, sems)
        for i in range(many):
            into[i].wait()
            away[i].start()
        finish(copies)
        finish(away)

    return call(
        kernel,
        (
            shape((rows, size * n_tp), value.dtype),
            *(shape(member, stack.dtype) for stack in stacks),
        ),
        (value, *stacks),
        [pltpu.VMEM((many, *member), BF), DMA((many,)), DMA((many,))] + pair_of_sems(n_tp),
        1,
        "gather_tp",
        left=tuple(range(1, many + 1)) + tuple(range(-many, 0)),
    )


def first_norm(full, grad, gain, weights, quarter, n_tp, n_ctx):
    rows, width = full.shape
    with_quarter = quarter is not None

    def kernel(*refs):
        hid, grd, gn = refs[:3]
        refs = refs[3:]
        if with_quarter:
            wgts, refs = refs[: len(weights)], refs[len(weights) :]
            qrt, out, scale, grd_full, many_full, last_full, held, local, loads, stores = refs[:10]
            sems = refs[10:]
            half, inner = wgts[0].shape
            last = len(wgts) - 1
            mine = lax.axis_index("fsdp")

            def target(i, first_row, count):
                at = pl.ds(pl.multiple_of(first_row, 16), count)
                if i == last:
                    return last_full.at[at, :]
                return many_full.at[at, pl.ds(i * inner, inner)]

            into = [
                pltpu.make_async_copy(wgts[i], held.at[i], loads.at[i]) for i in range(len(wgts))
            ]
            away = [
                pltpu.make_async_copy(held.at[i], target(i, mine * half, half), stores.at[i])
                for i in range(len(wgts))
            ]
            for copy in into:
                copy.start()
            greet([("tp", n_tp), ("ctx", n_ctx)])
        else:
            out, scale, grd_full = refs[:3]
            sems = refs[3:]
            greet([("tp", n_tp)])
        grads = gather_columns(grd, grd_full, "tp", n_tp, sems[0:2])

        def norm():
            values = hid[...].astype(F32)
            mean = jnp.sum(values * values, axis=-1, keepdims=True) * (1.0 / width)
            factor = lax.rsqrt(mean + EPS)
            scale[...] = jnp.broadcast_to(factor, scale.shape)
            out[...] = (values * factor * gn[0:1, :]).astype(BF)

        if with_quarter:
            count = qrt.shape[0]

            def work():
                for i in range(len(wgts)):
                    into[i].wait()
                    away[i].start()
                norm()

            def places(rank, i):
                return target(i, (1 - mine) * half + rank * count, count)

            gather_square(qrt, places, sems[2:4], work, local)
            finish(away)
        else:
            norm()
        finish(grads)

    outs = [shape((rows, width), BF), shape((rows, 128), F32), shape((rows, width), BF)]
    inputs = [full, grad, gain]
    scratch, left = [], ()
    if with_quarter:
        half, inner = weights[0].shape
        many = len(weights)
        assert inner == 512
        outs.append(shape((2 * half, (many - 1) * inner), BF))
        outs.append(shape((2 * half, inner), BF))
        inputs += [*weights, quarter]
        scratch = [pltpu.VMEM((many, half, inner), BF), DMA((many,)), DMA((many,)), DMA((many,))]
        left = tuple(range(3, 3 + many)) + (-2, -1)
    return call(
        kernel,
        tuple(outs),
        inputs,
        scratch + pair_of_sems(n_tp) + pair_of_sems(12),
        7,
        "first_norm",
        left=left,
    )


def turn(values, cosine, sine):
    return values * cosine + pltpu.roll(values, HD // 2, axis=1) * sine


def softmax_rows(query, key, first_row):
    scores = mm_t(query, key) * (1.0 / math.sqrt(HD))
    rows = first_row + lax.broadcasted_iota(jnp.int32, scores.shape, 0)
    cols = lax.broadcasted_iota(jnp.int32, scores.shape, 1)
    scores = jnp.where(cols <= rows, scores, NEG)
    top = jnp.max(scores, axis=-1, keepdims=True)
    weights = jnp.exp(scores - top)
    return weights / jnp.sum(weights, axis=-1, keepdims=True)


def attention_forward(qkv, cosine, sine, n_ctx):
    rows = qkv.shape[0]
    width = qkv.shape[1] // 3
    heads = width // HD

    def kernel(prj, cs, sn, out, qry, full, own, *sems):
        greet([("ctx", n_ctx)])
        here = lax.axis_index("ctx")

        @pl.loop(0, heads)
        def _(h):
            own[:, columns(h, HD)] = turn(
                prj[:, columns(h + heads, HD)], cs[...], sn[...]
            ).astype(BF)
            own[:, columns(h + heads, HD)] = prj[:, columns(h + 2 * heads, HD)].astype(BF)

        def queries():
            @pl.loop(0, heads)
            def _(h):
                qry[:, columns(h, HD)] = turn(prj[:, columns(h, HD)], cs[...], sn[...]).astype(BF)

        def places(rank, i):
            return full.at[stretch(rank, rows), pl.ds(i * 512, 512)]

        gather_square(own, places, sems, queries)

        @pl.loop(0, heads)
        def _(h):
            probs = softmax_rows(qry[:, columns(h, HD)], full[:, columns(h, HD)], here * rows)
            out[:, columns(h, HD)] = mm(
                probs.astype(BF), full[:, columns(h + heads, HD)]
            ).astype(BF)

    return call(
        kernel,
        (
            shape((rows, width), BF),
            shape((rows, width), BF),
            shape((rows * n_ctx, 2 * width), BF),
        ),
        (qkv, cosine, sine),
        [pltpu.VMEM((rows, 2 * width), BF)] + pair_of_sems(6 * width // 512),
        2,
        "attention_forward",
    )


def second_norm(part, hidden, gain, slabs, picks, router, onehot, names, n_tp, n_ctx):
    rows, size = hidden.shape
    width = size * n_tp
    experts = n_ctx

    def kernel(
        prt, hid, gn, slb, pck, rtr, one, nms,
        resid, scale, out, moved, tokens, slot_gates, gates, mix,
        slots, mine, sums, mine_two, sums_two, low, sent, own_gates, *sems
    ):
        greet([("tp", n_tp), ("ctx", n_ctx)])
        here = lax.axis_index("tp")
        copies = scatter_columns(prt, slots, "tp", n_tp, sems[0:2])
        others = [
            send(
                slb.at[pl.ds(k * CAP, CAP)], moved.at[pl.ds(k * CAP, CAP)],
                "ctx", n_ctx, k, sems[6:8],
            )
            for k in range(1, n_ctx)
        ]
        moved[0:CAP] = slb[0:CAP]
        total = prt[:, columns(here, size)].astype(F32)
        finish(copies)
        for k in range(1, n_tp):
            total = total + slots[k - 1].astype(F32)
        total = hid[...].astype(F32) + total
        resid[...] = total
        square = total_over(row_sums(total * total), mine, sums, "tp", n_tp, sems[2:4])
        factor = lax.rsqrt(as_column(square, eighth()) * (1.0 / width) + EPS)
        scale[...] = factor
        low[...] = (resid[...] * factor[:, 0:1] * gn[0:1, :]).astype(BF)
        partial_logits = mm_t(rtr[...].astype(BF), low[...])
        mine_two[...] = partial_logits
        logit_copies = [
            send(mine_two, sums_two.at[k - 1], "tp", n_tp, k, sems[12:14]) for k in range(1, n_tp)
        ]
        gather_columns(low, out, "tp", n_tp, sems[4:6])

        def route():
            finish(logit_copies)
            logits = partial_logits
            for k in range(1, n_tp):
                logits = logits + sums_two[k - 1]
            named = [jnp.sum(one[j] * logits, axis=0, keepdims=True) for j in range(2)]
            top = jnp.maximum(named[0], named[1])
            powers = [jnp.exp(value - top) for value in named]
            both = powers[0] + powers[1]
            gate = [value / both for value in powers]
            mixed = gate[0] * nms[0] + gate[1] * nms[1]
            mix[...] = mixed
            order = lax.broadcasted_iota(jnp.int32, (8, rows), 0)
            gates[...] = jnp.where(order == 0, gate[0], jnp.where(order == 1, gate[1], 0.0))
            own_gates[...] = jnp.zeros(own_gates.shape, F32)
            for k in range(experts):
                own_gates[k, :, 0:CAP] = lax.dot_general(
                    jnp.broadcast_to(mixed[k : k + 1], (8, rows)),
                    pck[k * CAP : (k + 1) * CAP].astype(F32),
                    (((1,), (1,)), ((), ())),
                    precision=lax.Precision.HIGHEST,
                    preferred_element_type=F32,
                )
            slot_gates[0] = own_gates[0]
            for k in range(1, n_ctx):
                others.append(
                    send(own_gates.at[k], slot_gates.at[k], "ctx", n_ctx, k, sems[10:12])
                )


        def slab(k, step):
            at = columns(peer("tp", n_tp, n_tp - step), size)
            return described(
                sent.at[step, pl.ds(k * CAP, CAP)], tokens.at[pl.ds(k * CAP, CAP), at],
                sems[8:10], step * n_ctx + k, {"ctx": peer("ctx", n_ctx, k)},
            )

        def dispatch(step, block):
            sent[step] = mm(pck[...], block).astype(BF)
            tokens[0:CAP, columns(peer("tp", n_tp, n_tp - step), size)] = sent[step, 0:CAP]
            for k in (2, 3, 1):
                slab(k, step).start()

        route()

        @pl.loop(0, n_tp)
        def _(step):
            @pl.when(step > 0)
            def _():
                described(
                    low, out.at[:, columns(here, size)], sems[4:6], step - 1,
                    {"tp": peer("tp", n_tp, step)},
                ).wait()

            dispatch(step, out[:, columns(peer("tp", n_tp, n_tp - step), size)])

        for step in range(n_tp):
            for k in (2, 3, 1):
                slab(k, step).wait()
        finish(others)

    return call(
        kernel,
        (
            shape((rows, size), F32),
            shape((rows, 128), F32),
            shape((rows, width), BF),
            shape(slabs.shape, BF),
            shape(slabs.shape, BF),
            shape((experts, 8, rows), F32),
            shape((8, rows), F32),
            shape((8, rows), F32),
        ),
        (part, hidden, gain, slabs, picks, router, onehot, names),
        [
            pltpu.VMEM((n_tp - 1, rows, size), BF),
            pltpu.VMEM((8, rows), F32),
            pltpu.VMEM((n_tp - 1, 8, rows), F32),
            pltpu.VMEM((8, rows), F32),
            pltpu.VMEM((n_tp - 1, 8, rows), F32),
            pltpu.VMEM((rows, size), BF),
            pltpu.VMEM((n_tp, experts * CAP, size), BF),
            pltpu.VMEM((experts, 8, rows), F32),
        ]
        + pair_of_sems(n_tp) * 3
        + pair_of_sems(n_ctx)
        + pair_of_sems(n_tp * n_ctx)
        + pair_of_sems(n_ctx)
        + pair_of_sems(n_tp),
        3,
        "second_norm",
    )


def expert_acts(tokens, gate_w, up_w, n_fsdp):
    rows, width = tokens.shape
    hidden = gate_w[0].shape[1]
    count = len(gate_w)
    part = gate_w[0].shape[0]
    chunk = 256
    per = part // chunk
    steps = count * per
    pair = count == 2

    def kernel(tok, *refs):
        wgt = [refs[:count], refs[count : 2 * count]]
        to_gate, to_up, hid, buffer, loads = refs[2 * count :]
        first = lax.axis_index("fsdp") if pair else 0

        def load(step):
            slot = lax.rem(step, 2)
            at = stretch(lax.rem(step, per), chunk)
            for lane in range(2):
                for i in range(count):

                    @pl.when(step // per == i)
                    def _():
                        pltpu.make_async_copy(
                            wgt[lane][i].at[at], buffer.at[slot, lane], loads.at[slot, lane]
                        ).start()

        load(0)
        to_gate[...] = jnp.zeros_like(to_gate)
        to_up[...] = jnp.zeros_like(to_up)

        @pl.loop(0, steps)
        def _(step):
            slot = lax.rem(step, 2)
            for lane in range(2):
                pltpu.make_async_copy(
                    wgt[lane][0].at[pl.ds(0, chunk)], buffer.at[slot, lane], loads.at[slot, lane]
                ).wait()

            @pl.when(step + 1 < steps)
            def _():
                load(step + 1)

            which = lax.rem(first + step // per, count)
            column = which * part + lax.rem(step, per) * chunk
            values = tok[:, pl.ds(pl.multiple_of(column, 128), chunk)]
            to_gate[...] += mm(values, buffer[slot, 0])
            to_up[...] += mm(values, buffer[slot, 1])

        @pl.loop(0, rows // 32)
        def _(i):
            at = stretch(i, 32)
            a, b = to_gate[at, :], to_up[at, :]
            sigma = 1.0 / (1.0 + jnp.exp(-a))
            silu = a * sigma
            hid[at, :] = (silu * b).astype(BF)
            to_up[at, :] = silu
            to_gate[at, :] = b * sigma * (1.0 + a * (1.0 - sigma))

    anywhere = pl.BlockSpec(memory_space=pl.ANY)
    return pl.pallas_call(
        kernel,
        out_shape=(
            shape((rows, hidden), F32),
            shape((rows, hidden), F32),
            shape((rows, hidden), BF),
        ),
        in_specs=[VM] + [anywhere] * (2 * count),
        out_specs=(VM, VM, VM),
        scratch_shapes=[pltpu.VMEM((2, 2, chunk, hidden), BF), DMA((2, 2))],
        cost_estimate=pl.CostEstimate(flops=0, bytes_accessed=0, transcendentals=0),
        name="expert_acts",
    )(tokens, *gate_w, *up_w)


def second_norm_back(
    acts, weights, tokens, dots, picks, gates, onehot, names, router, resid, scale, gain, grad,
    n_tp, n_ctx,
):
    rows, size = resid.shape
    width = size * n_tp
    experts = n_ctx
    hidden = acts[0].shape[1]
    count = len(weights[0])
    part = weights[0][0].shape[0]

    def kernel(*refs):
        dga, dup, hid = refs[:3]
        wgt = [refs[3 + i * count : 3 + (i + 1) * count] for i in range(3)]
        refs = refs[3 + 3 * count :]
        tok, dts, pck, gts, one, nms, rtr, rsd, scl, gn, grd = refs[:11]
        d_resid, low, d_gain, d_logits, out_rows = refs[11:16]
        refs = refs[16:]
        if count == 2:
            up_away, up_held, up_sem = refs[:1] + refs[1:3]
            refs = refs[3:]
        (
            drw, eo, buffer, back, back_dots, parts, slots, mine, sums, mine_two, sums_two, loads,
            out_sem,
        ) = refs[:13]
        sems = refs[13:]
        here = lax.axis_index("tp")
        first = lax.axis_index("fsdp")

        def load(which, rank, slot, lane):
            feature = rank * size
            inside = pl.ds(pl.multiple_of(lax.rem(feature, part), 16), size)
            target = buffer.at[slot, lane]
            if count == 1:
                pltpu.make_async_copy(
                    wgt[which][0].at[inside], target, loads.at[slot, lane]
                ).start()
                return
            own = feature // part == first

            @pl.when(own)
            def _():
                pltpu.make_async_copy(
                    wgt[which][0].at[inside], target, loads.at[slot, lane]
                ).start()

            @pl.when(jnp.logical_not(own))
            def _():
                pltpu.make_async_copy(
                    wgt[which][1].at[inside], target, loads.at[slot, lane]
                ).start()

        def loaded(which, slot, lane):
            pltpu.make_async_copy(
                wgt[which][0].at[pl.ds(0, size)], buffer.at[slot, lane], loads.at[slot, lane]
            ).wait()

        load(0, peer("tp", n_tp, 1), 0, 0)
        load(1, peer("tp", n_tp, 1), 0, 1)
        greet([("tp", n_tp), ("ctx", n_ctx)])
        small = []
        for k in range(1, n_ctx):
            small.append(
                send(dts.at[k], back_dots.at[k - 1], "ctx", n_ctx, n_ctx - k, sems[0:2])
            )

        def slab(k, rank, step):
            at = columns(rank, size)
            return described(
                drw.at[pl.ds(k * CAP, CAP), at], back.at[k - 1, :, at],
                sems[2:4], step * n_ctx + k - 1, {"ctx": peer("ctx", n_ctx, n_ctx - k)},
            )

        @pl.loop(0, n_tp)
        def _(step):
            rank = peer("tp", n_tp, step + 1)
            slot = lax.rem(step, 2)
            loaded(0, slot, 0)
            loaded(1, slot, 1)

            @pl.when(step + 1 < n_tp)
            def _():
                load(0, peer("tp", n_tp, step + 2), 1 - slot, 0)
                load(1, peer("tp", n_tp, step + 2), 1 - slot, 1)

            drw[:, columns(rank, size)] = (
                mm_t(dga[...], buffer[slot, 0]) + mm_t(dup[...], buffer[slot, 1])
            ).astype(BF)
            for k in (2, 3, 1):
                slab(k, rank, step).start()

        load(2, 0, 0, 0)

        @pl.loop(0, n_tp)
        def _(rank):
            slot = lax.rem(rank, 2)
            loaded(2, slot, 0)

            @pl.when(rank + 1 < n_tp)
            def _():
                load(2, rank + 1, 1 - slot, 0)

            eo[:, columns(rank, size)] = mm_t(hid[...], buffer[slot, 0]).astype(BF)

        pltpu.make_async_copy(eo, out_rows, out_sem).start()
        if count == 2:

            @pl.loop(0, part // 256)
            def _(i):
                at = pl.ds(pl.multiple_of((1 - first) * part + i * 256, 128), 256)
                up_held[stretch(i, 256), :] = t_mm(tok[:, at], dup[...]).astype(BF)

            pltpu.make_async_copy(up_held, up_away, up_sem).start()
        finish(small)
        order = lax.broadcasted_iota(jnp.int32, (8, rows), 0)
        own = jnp.zeros((8, rows), F32)
        for k in range(experts):
            by_slot = dts[0] if k == 0 else back_dots[k - 1]
            by_row = lax.dot_general(
                by_slot[:, 0:CAP],
                pck[k * CAP : (k + 1) * CAP].astype(F32),
                (((1,), (0,)), ((), ())),
                precision=lax.Precision.HIGHEST,
                preferred_element_type=F32,
            )
            own = own + jnp.where(order == k, by_row, 0.0)
        gate_grad = total_over(own, mine, sums, "tp", n_tp, sems[4:6])
        both = [jnp.sum(nms[j] * gate_grad, axis=0, keepdims=True) for j in range(2)]
        gate = [gts[j : j + 1, :] for j in range(2)]
        mean = gate[0] * both[0] + gate[1] * both[1]
        logits = sum(gate[j] * (both[j] - mean) * one[j] for j in range(2))
        d_logits[...] = logits

        def combined(step):
            rank = peer("tp", n_tp, step)
            at = columns(rank, size)
            for k in (2, 3, 1):
                slab(k, rank, step - 1).wait()
            block = t_mm(pck[0:CAP], drw[0:CAP, at])
            for k in range(1, experts):
                block = block + t_mm(pck[k * CAP : (k + 1) * CAP], back[k - 1, :, at])
            return block

        def give(step):
            return described(
                parts.at[step - 1], slots.at[step - 1], sems[6:8], step - 1,
                {"tp": peer("tp", n_tp, step)},
            )

        @pl.loop(1, n_tp + 1)
        def _(step):
            d_resid[...] = combined(step)

            @pl.when(step < n_tp)
            def _():
                parts[step - 1] = d_resid[...].astype(BF)
                give(step).start()

        copies = [give(step) for step in range(1, n_tp)]
        total = d_resid[...]
        total = total + lax.dot_general(
            logits.astype(BF),
            rtr[...].astype(BF),
            (((0,), (0,)), ((), ())),
            preferred_element_type=F32,
        )
        finish(copies)
        for k in range(1, n_tp):
            total = total + slots[k - 1].astype(F32)
        factor = scl[:, 0:1]
        unit = rsd[...] * factor
        d_gain[...] = jnp.broadcast_to(jnp.sum(total * unit, axis=0, keepdims=True), d_gain.shape)
        gained = total * gn[0:1, :]
        d_resid[...] = gained
        dot = total_over(row_sums(unit * gained), mine_two, sums_two, "tp", n_tp, sems[8:10])
        dot = as_column(dot, eighth())[:, 0:1] * (1.0 / width)
        result = grd[...].astype(F32) + factor * (d_resid[...] - rsd[...] * factor * dot)
        d_resid[...] = result
        low[...] = result.astype(BF)
        pltpu.make_async_copy(eo, out_rows, out_sem).wait()
        if count == 2:
            pltpu.make_async_copy(up_held, up_away, up_sem).wait()

    outs = [
        shape((rows, size), F32),
        shape((rows, size), BF),
        shape((8, size), F32),
        shape((8, rows), F32),
        shape((experts * CAP, width), BF),
    ]
    held = []
    if count == 2:
        outs.append(shape((part, hidden), BF))
        held = [pltpu.VMEM((part, hidden), BF), DMA]
    flat = [array for group in weights for array in group]
    return call(
        kernel,
        tuple(outs),
        (*acts, *flat, tokens, dots, picks, gates, onehot, names, router, resid, scale, gain, grad),
        held
        + [
            pltpu.VMEM((experts * CAP, width), BF),
            pltpu.VMEM((experts * CAP, width), BF),
            pltpu.VMEM((2, 2, size, hidden), BF),
            pltpu.VMEM((n_ctx - 1, CAP, width), BF),
            pltpu.VMEM((n_ctx - 1, 8, rows), F32),
            pltpu.VMEM((n_tp - 1, rows, size), BF),
            pltpu.VMEM((n_tp - 1, rows, size), BF),
            pltpu.VMEM((8, rows), F32),
            pltpu.VMEM((n_tp - 1, 8, rows), F32),
            pltpu.VMEM((8, rows), F32),
            pltpu.VMEM((n_tp - 1, 8, rows), F32),
            DMA((2, 2)),
            DMA,
        ]
        + pair_of_sems(n_ctx)
        + pair_of_sems(n_tp * n_ctx)
        + pair_of_sems(n_tp) * 3,
        4,
        "second_norm_back",
        left=tuple(range(3, 3 + 3 * count)) + ((-2, -1) if count == 2 else (-1,)),
    )


def attention_backward(
    low, output_w, query, kv, cosine, sine, sums, payload, n_tp, n_ctx
):
    rows, size = low.shape
    width = size * n_tp
    inner = query.shape[1]
    heads = inner // HD
    scale = 1.0 / math.sqrt(HD)

    half = heads // 2
    sums, sums_input = sums
    lane = 2 * half * HD

    def kernel(*refs):
        lw, wgt, qry, full, cs, sn, made = refs[:7]
        n_in, n_out = 7 + len(payload.inputs), len(payload.outs)
        d_attn, d_qkv, summed = refs[n_in : n_in + 3]
        scratch = refs[n_in + 3 + n_out :]
        dot, dqs, dkv, slots, last, both, total, kept = scratch[:8]
        sems = scratch[8:12]
        sums.take(made, scratch[12 : 12 + len(sums.scratch)])
        payload.take(
            refs[7:n_in], refs[n_in + 3 : n_in + 3 + n_out], scratch[12 + len(sums.scratch) :]
        )
        payload.load()
        greet([("tp", n_tp), ("ctx", n_ctx)])
        here, beside, across = quad()
        beyond = lax.rem(beside + 2, 4)
        copies = gather_columns(lw, d_attn, "tp", n_tp, sems[2:4])
        sums.start()
        payload.go()

        @pl.loop(0, heads)
        def _(h):
            at = columns(h, HD)
            kept[h] = softmax_rows(qry[:, at], full[:, at], here * rows)

        for step in range(n_tp):
            rank = peer("tp", n_tp, n_tp - step)
            weights = wgt[pl.ds(pl.multiple_of(rank * size, 16), size), :]
            if step:
                copies[step - 1].wait()
                total[...] += mm(d_attn[:, columns(rank, size)], weights)
            else:
                total[...] = mm(lw[...], weights)
        dot[...] = total[...].astype(BF)
        first, second, third = [], [], []
        for j in range(2):

            @pl.loop(0, half)
            def _(i):
                h = j * half + i
                at, at_v = columns(h, HD), columns(h + heads, HD)
                key_at = pl.ds(pl.multiple_of(j * lane + i * HD, 128), HD)
                value_at = pl.ds(pl.multiple_of(j * lane + (half + i) * HD, 128), HD)
                probs = kept[h]
                d_probs = mm_t(dot[:, at], full[:, at_v])
                delta = jnp.sum(probs * d_probs, axis=-1, keepdims=True)
                d_scores = (probs * (d_probs - delta)).astype(BF)
                dqs[:, at] = mm(d_scores, full[:, at]) * scale
                dkv[:, key_at] = (t_mm(d_scores, qry[:, at]) * scale).astype(BF)
                dkv[:, value_at] = t_mm(probs.astype(BF), dot[:, at]).astype(BF)

            at = pl.ds(j * lane, lane)
            first.append(
                remote(
                    dkv.at[stretch(beyond, rows), at], slots.at[0, :, at],
                    sems, 3 * j, {"ctx": beside},
                )
            )
            second.append(
                remote(
                    dkv.at[stretch(beside, rows), at], slots.at[1, :, at],
                    sems, 3 * j + 1, {"ctx": beside},
                )
            )
        for j in range(2):
            at = pl.ds(j * lane, lane)
            first[j].wait()
            both[:, at] = (
                dkv[stretch(across, rows), at].astype(F32) + slots[0, :, at].astype(F32)
            ).astype(BF)
            third.append(
                remote(both.at[:, at], last.at[:, at], sems, 3 * j + 2, {"ctx": across})
            )

        @pl.loop(0, heads)
        def _(h):
            d_qkv[:, columns(h, HD)] = turn(dqs[:, columns(h, HD)], cs[...], sn[...]).astype(BF)

        for j in range(2):
            second[j].wait()
            third[j].wait()

            @pl.loop(0, half)
            def _(i):
                h = j * half + i
                key_at = pl.ds(pl.multiple_of(j * lane + i * HD, 128), HD)
                value_at = pl.ds(pl.multiple_of(j * lane + (half + i) * HD, 128), HD)
                mine = stretch(here, rows)
                d_key = dkv[mine, key_at].astype(F32) + slots[1, :, key_at].astype(F32)
                d_key = d_key + last[:, key_at].astype(F32)
                d_qkv[:, columns(h + heads, HD)] = turn(d_key, cs[...], sn[...]).astype(BF)
                d_value = dkv[mine, value_at].astype(F32) + slots[1, :, value_at].astype(F32)
                d_value = d_value + last[:, value_at].astype(F32)
                d_qkv[:, columns(h + 2 * heads, HD)] = d_value.astype(BF)

        summed[...] = sums.total().astype(BF)
        payload.wait()

    return call(
        kernel,
        (
            shape((rows, width), BF),
            shape((rows, 3 * inner), BF),
            shape(sums.shape, BF),
            *payload.outs,
        ),
        (low, output_w, query, kv, cosine, sine, sums_input, *payload.inputs),
        [
            pltpu.VMEM((rows, inner), BF),
            pltpu.VMEM((rows, inner), F32),
            pltpu.VMEM((rows * n_ctx, 2 * inner), BF),
            pltpu.VMEM((2, rows, 2 * inner), BF),
            pltpu.VMEM((rows, 2 * inner), BF),
            pltpu.VMEM((rows, 2 * inner), BF),
            pltpu.VMEM((rows, inner), F32),
            pltpu.VMEM((heads, rows, rows * n_ctx), F32),
        ]
        + pair_of_sems(6)
        + pair_of_sems(n_tp)
        + sums.scratch
        + payload.scratch,
        5,
        "attention_backward",
        left=(6, 6 + len(payload.inputs), -len(payload.outs)),
    )


def first_norm_back(d_qkv, weights, hidden, scale, gain, d_resid, sums, payload, n_tp, n_ctx):
    more, more_input = sums
    rows, size = hidden.shape
    width = size * n_tp

    def kernel(*refs):
        dpr, wgt, hid, scl, gn, dr, made = refs[:7]
        n_in, n_out = 7 + len(payload.inputs), len(payload.outs)
        out, d_gain, summed = refs[n_in : n_in + 3]
        scratch = refs[n_in + 3 + n_out :]
        held, parts, slots, mine, sums, loads = scratch[:6]
        sems = scratch[6:10]
        more.take(made, scratch[10 : 10 + len(more.scratch)])
        payload.take(
            refs[7:n_in], refs[n_in + 3 : n_in + 3 + n_out], scratch[10 + len(more.scratch) :]
        )

        def block(step):
            rank = peer("tp", n_tp, step)
            return pltpu.make_async_copy(
                wgt.at[stretch(rank, size), :], held.at[step - 1], loads.at[step - 1]
            )

        for step in range(1, n_tp + 1):
            block(step).start()
        payload.load()
        greet([("tp", n_tp), ("ctx", n_ctx)])

        def give(step):
            return described(
                parts.at[step - 1], slots.at[step - 1], sems[0:2], step - 1,
                {"tp": peer("tp", n_tp, step)},
            )

        @pl.loop(1, n_tp + 1)
        def _(step):
            block(step).wait()
            out[...] = mm_t(dpr[...], held[step - 1])

            @pl.when(step < n_tp)
            def _():
                parts[step - 1] = out[...].astype(BF)
                give(step).start()

        copies = [give(step) for step in range(1, n_tp)]
        more.start()
        payload.go()
        finish(copies)
        total = out[...]
        for k in range(1, n_tp):
            total = total + slots[k - 1].astype(F32)
        factor = scl[:, 0:1]
        unit = hid[...].astype(F32) * factor
        d_gain[...] = jnp.broadcast_to(jnp.sum(total * unit, axis=0, keepdims=True), d_gain.shape)
        gained = total * gn[0:1, :]
        out[...] = gained
        dot = total_over(row_sums(unit * gained), mine, sums, "tp", n_tp, sems[2:4])
        dot = as_column(dot, eighth())[:, 0:1] * (1.0 / width)
        unit = hid[...].astype(F32) * factor
        out[...] = dr[...] + factor * (out[...] - unit * dot)
        summed[...] = more.total().astype(BF)
        payload.wait()

    return call(
        kernel,
        (shape((rows, size), F32), shape((8, size), F32), shape(more.shape, BF), *payload.outs),
        (d_qkv, weights, hidden, scale, gain, d_resid, more_input, *payload.inputs),
        [
            pltpu.VMEM((n_tp, size, d_qkv.shape[1]), BF),
            pltpu.VMEM((n_tp - 1, rows, size), BF),
            pltpu.VMEM((n_tp - 1, rows, size), BF),
            pltpu.VMEM((8, rows), F32),
            pltpu.VMEM((n_tp - 1, 8, rows), F32),
            DMA((n_tp,)),
        ]
        + pair_of_sems(n_tp) * 2
        + more.scratch
        + payload.scratch,
        6,
        "first_norm_back",
        left=(1, 6, 6 + len(payload.inputs), -len(payload.outs)),
    )


class ExpertsOut:

    def __init__(self, made, done, picks, mix, resid, n_tp, n_ctx):
        self.n_ctx, self.n_done = n_ctx, len(done)
        first = CAP * len(done)
        self.sums = RowSums(made, first, made.shape[0] - first, n_tp)
        self.inputs = [made, *done, picks, mix, resid]
        self.size = resid.shape[1]
        self.out = shape(resid.shape, BF)
        self.scratch = [
            pltpu.VMEM(self.sums.shape, BF),
            pltpu.VMEM((n_ctx - 1, CAP, self.size), BF),
        ]
        self.scratch += pair_of_sems(n_ctx) + self.sums.scratch

    def take(self, ins, out, scratch):
        self.ins, self.out_ref, self.held = ins, out, scratch[:4]
        self.sums.take(ins[0], scratch[4:])

    def block(self, k):
        if k < self.n_done:
            return self.ins[1 + k]
        return self.held[0].at[pl.ds((k - self.n_done) * CAP, CAP)]

    def give_back(self):
        share, back = self.held[:2]
        share[...] = self.sums.total().astype(BF)
        n_ctx = self.n_ctx
        self.copies = [
            send(self.block(k), back.at[k - 1], "ctx", n_ctx, n_ctx - k, self.held[2:4])
            for k in range(1, n_ctx)
        ]

    def mix(self):
        picks, mix, resid = self.ins[-3:]
        back = self.held[1]
        finish(self.copies)
        order = lax.broadcasted_iota(jnp.int32, (8, 128), 0)
        total = resid[...]
        for k in range(self.n_ctx):
            gate = as_column(mix[...], jnp.where(order == k, 1.0, 0.0))[:, 0:1]
            rows = self.block(0)[...] if k == 0 else back[k - 1]
            total = total + gate * t_mm(picks[k * CAP : (k + 1) * CAP], rows)
        self.out_ref[...] = total.astype(BF)


def weight_grads(products, groups, small, payload, experts_out, n_tp, n_ctx):
    width = products[0][0].shape[1]
    places = 2 * n_ctx
    cut = width // places
    total_columns = sum(size for _, _, size in groups)
    flat = [array for pair in products for array in pair]
    inputs = [*flat, small, *experts_out.inputs, *payload.inputs]

    def kernel(*refs):
        factors, refs = refs[: len(flat)], refs[len(flat) :]
        sml, refs = refs[0], refs[1:]
        given, refs = refs[: len(experts_out.inputs)], refs[len(experts_out.inputs) :]
        paid, refs = refs[: len(payload.inputs)], refs[len(payload.inputs) :]
        out, small_out, block_out = refs[:3]
        paid_out, refs = refs[3 : 3 + len(payload.outs)], refs[3 + len(payload.outs) :]
        sml_full, sml_slots, refs = refs[0], refs[1], refs[2:]
        scratch, refs = refs[: 6 * len(groups)], refs[6 * len(groups) :]
        experts_out.take(given, block_out, refs[: len(experts_out.scratch)])
        refs = refs[len(experts_out.scratch) :]
        payload.take(paid, paid_out, refs[: len(payload.scratch)])
        sems = refs[len(payload.scratch) :]
        payload.load()
        barrier = pltpu.get_barrier_semaphore()
        here, beside, across = quad()
        beyond = lax.rem(beside + 2, 4)
        mine = lax.axis_index("fsdp")
        other = 1 - mine
        place = mine * n_ctx + here
        others = []
        for i in range(1, places):
            to = lax.rem(place + i, places)
            others.append((to, {"fsdp": to // n_ctx, "ctx": lax.rem(to, n_ctx)}))
        ahead = [{"tp": peer("tp", n_tp, k)} for k in range(1, n_tp)]
        for device in ahead + [device for _, device in others]:
            pl.semaphore_signal(barrier, inc=1, device_id=device, device_id_type=MESH)
        pl.semaphore_wait(barrier, n_tp - 1 + places - 1)
        gathers = gather_columns(sml, sml_full, "tp", n_tp, sems[0:2])
        experts_out.sums.start()
        moves = []

        def near(g):
            which, start, size = groups[g]
            prt, come = scratch[6 * g : 6 * g + 2]
            left, right = factors[2 * which : 2 * which + 2]

            @pl.loop(0, places)
            def _(i):
                prt[i] = t_mm(left[:, columns(i, cut)], right[:, start : start + size]).astype(BF)

            blocks = [(other, beyond), (other, beside), (mine, beyond), (mine, beside)]
            moves.append(
                [
                    remote(
                        prt.at[rank * n_ctx + column], come.at[i],
                        sems[4 + 6 * g : 6 + 6 * g], i, {"ctx": beside},
                    )
                    for i, (rank, column) in enumerate(blocks)
                ]
            )

        def chip(g, i, rank, column):
            prt, come = scratch[6 * g : 6 * g + 2]
            moves[g][i].wait()
            return prt[rank * n_ctx + column].astype(F32) + come[i].astype(F32)

        hops = []

        def hop(g):
            two, far = scratch[6 * g + 2 : 6 * g + 4]
            sent = []
            for i, column in enumerate((across, here)):
                two[i] = chip(g, i, other, column).astype(BF)
                sent.append(
                    remote(
                        two.at[i], far.at[i], sems[6 + 6 * g : 8 + 6 * g], i, {"fsdp": other}
                    )
                )
            hops.append(sent)

        near(0)
        payload.go()
        finish(gathers)
        totals = [
            remote(sml_full.at[:, columns(to, cut)], sml_slots.at[i], sems[2:4], i, device)
            for i, (to, device) in enumerate(others)
        ]
        hop(0)
        for g in range(1, len(groups)):
            near(g)
            hop(g)
        lasts = []
        for g in range(len(groups)):
            far, one, last = scratch[6 * g + 3 : 6 * g + 6]
            value = chip(g, 2, mine, across)
            hops[g][0].wait()
            one[...] = (value + far[0].astype(F32)).astype(BF)
            lasts.append(
                remote(one, last, sems[8 + 6 * g : 10 + 6 * g], 0, {"ctx": across})
            )
            if g == 0:
                experts_out.give_back()
        finish(totals)
        sums = sml_full[:, columns(place, cut)]
        for i in range(places - 1):
            sums = sums + sml_slots[i]
        small_out[...] = sums
        start = 0
        for g, (_, _, size) in enumerate(groups):
            far = scratch[6 * g + 3]
            value = chip(g, 3, mine, here)
            hops[g][1].wait()
            value = value + far[1].astype(F32)
            out[:, start : start + size] = value
            start += size
        experts_out.mix()
        payload.wait()
        start = 0
        for g, (_, _, size) in enumerate(groups):
            lasts[g].wait()
            at = pl.ds(start, size)
            out[:, at] = out[:, at] + scratch[6 * g + 5][...].astype(F32)
            start += size

    buffers = [pltpu.VMEM((8, width), F32), pltpu.VMEM((places - 1, 8, cut), F32)]
    sems = pair_of_sems(n_tp) + pair_of_sems(places)
    for _, _, size in groups:
        buffers += [
            pltpu.VMEM((places, cut, size), BF),
            pltpu.VMEM((4, cut, size), BF),
            pltpu.VMEM((2, cut, size), BF),
            pltpu.VMEM((2, cut, size), BF),
            pltpu.VMEM((cut, size), BF),
            pltpu.VMEM((cut, size), BF),
        ]
        sems += pair_of_sems(4) + pair_of_sems(2) + pair_of_sems(1)
    return call(
        kernel,
        (
            shape((cut, total_columns), F32),
            shape((8, cut), F32),
            experts_out.out,
            *payload.outs,
        ),
        inputs,
        buffers + experts_out.scratch + payload.scratch + sems,
        10,
        "weight_grads",
        left=(
            len(flat) + 1,
            len(inputs) - 1,
            -len(payload.outs),
        ),
    )


def experts_back(experts_out, payload, n_tp, n_ctx):
    inputs = [*experts_out.inputs, *payload.inputs]
    given = len(experts_out.inputs)

    def kernel(*refs):
        ins, refs = refs[: len(inputs)], refs[len(inputs) :]
        outs, scratch = refs[: 1 + len(payload.outs)], refs[1 + len(payload.outs) :]
        experts_out.take(ins[:given], outs[0], scratch[: len(experts_out.scratch)])
        payload.take(ins[given:], outs[1:], scratch[len(experts_out.scratch) :])
        greet([("tp", n_tp), ("ctx", n_ctx)])
        experts_out.sums.start()
        payload.go()
        experts_out.give_back()
        experts_out.mix()
        payload.wait()

    return call(
        kernel,
        (experts_out.out, *payload.outs),
        inputs,
        experts_out.scratch + payload.scratch,
        9,
        "experts_back",
        left=(0, len(inputs) - 1, -len(payload.outs)),
    )


def write_out(experts_grads, attn_grad, plain, n_ctx):
    _, rows, size = experts_grads[0][0].shape
    steps = max(1, rows // 32)
    tile = rows // steps
    many = len(experts_grads)
    plain = list(plain)
    blocks = []
    if attn_grad is not None:
        block = attn_grad.shape[1] // 4
        blocks = [shape((attn_grad.shape[0], block), F32)] * 4
        plain.append(attn_grad)

    def kernel(*refs):
        here = lax.axis_index("ctx")
        ins, outs = refs[: 2 * many + len(plain)], refs[2 * many + len(plain) :]
        for i in range(many):
            came, mine = ins[2 * i : 2 * i + 2]
            outs[i][here] = mine[...].astype(F32)
            for k in range(1, n_ctx):
                outs[i][lax.rem(here + n_ctx - k, n_ctx)] = came[k - 1].astype(F32)
        for i in range(len(plain) - (1 if blocks else 0)):
            outs[many + i][...] = ins[2 * many + i][...]
        for i in range(len(blocks)):
            outs[i - 4][...] = ins[-1][:, i * block : (i + 1) * block]

    def flat(array):
        return pl.BlockSpec((array.shape[0] // steps, array.shape[1]), lambda i: (i, 0))

    in_specs, out_specs, out_shape = [], [], []
    for _ in experts_grads:
        in_specs.append(pl.BlockSpec((n_ctx - 1, tile, size), lambda i: (0, i, 0)))
        in_specs.append(pl.BlockSpec((tile, size), lambda i: (i, 0)))
        out_specs.append(pl.BlockSpec((n_ctx, tile, size), lambda i: (0, i, 0)))
        out_shape.append(shape((n_ctx, rows, size), F32))
    for array in plain[: len(plain) - (1 if blocks else 0)] + blocks:
        out_specs.append(flat(array))
        out_shape.append(shape(array.shape, array.dtype))
    in_specs += [flat(array) for array in plain]
    inputs = [array for pair in experts_grads for array in pair] + plain
    return pl.pallas_call(
        kernel,
        grid=(steps,),
        in_specs=in_specs,
        out_specs=out_specs,
        out_shape=out_shape,
        cost_estimate=pl.CostEstimate(
            flops=0, bytes_accessed=6 * many * n_ctx * rows * size, transcendentals=0
        ),
        name="write_out",
    )(*inputs)


def after(value, *needed):
    return lax.optimization_barrier((value, *needed))[0]


def shards(
    hidden_in,
    out_grad,
    attn_gain,
    w_query,
    w_key,
    w_value,
    w_output,
    ffn_gain,
    w_router,
    w_gate,
    w_up,
    w_down,
    routes,
):
    rows_here, width_tp = hidden_in.shape
    here_tp = lax.axis_index("tp")
    here_ctx = lax.axis_index("ctx")
    here_fsdp = lax.axis_index("fsdp")
    n_fsdp = lax.axis_size("fsdp")
    n_ctx = lax.axis_size("ctx")
    n_tp = lax.axis_size("tp")
    experts = w_gate.shape[0]
    assert experts == n_ctx == 4
    width = width_tp * n_tp
    part = width // n_fsdp
    pair = n_fsdp == 2
    heads_width = w_query.shape[1]

    def swap_fsdp(value):
        return lax.ppermute(value, "fsdp", [(0, 1), (1, 0)])

    def other_parts(weight):
        if pair:
            return [weight, swap_fsdp(weight)]
        return [lax.all_gather(weight, "fsdp", axis=0, tiled=True)]

    def split(values):
        if pair:
            return [
                lax.dynamic_slice_in_dim(values, here_fsdp * part, part, 1),
                lax.dynamic_slice_in_dim(values, (1 - here_fsdp) * part, part, 1),
            ]
        return [values]

    def join(pieces):
        if pair:
            first = here_fsdp == 0
            return jnp.concatenate(
                [jnp.where(first, pieces[0], pieces[1]), jnp.where(first, pieces[1], pieces[0])],
                axis=1,
            )
        return pieces[0]

    def into(values, weights):
        return sum(mm(x, w) for x, w in zip(split(values), weights))

    def back(values, weights):
        return join([mm_t(values, w) for w in weights])

    def my_features(values):
        return lax.dynamic_slice_in_dim(values, here_tp * width_tp, width_tp, values.ndim - 1)

    attn_w = (w_query, w_key, w_value, w_output)
    small = jnp.concatenate(
        [attn_gain[None], ffn_gain[None], w_router.T, jnp.zeros((2, part), BF)], axis=0
    )
    if pair:
        quarter = part // n_ctx
        own_quarter = jnp.concatenate(
            [lax.dynamic_slice_in_dim(w, here_ctx * quarter, quarter, 0) for w in attn_w], axis=1
        )
        other_quarter = swap_fsdp(own_quarter)
        other_small = swap_fsdp(small)
        small_full = join([small, other_small]).astype(F32)
    else:
        other_quarter = None
        small_full = lax.all_gather(small, "fsdp", axis=1, tiled=True).astype(F32)
    inputs_full, up_mine, down_mine = gather_tp(hidden_in, (w_up, w_down), n_tp)
    gate_w = other_parts(lax.dynamic_index_in_dim(w_gate, here_ctx, 0, False))
    up_w = other_parts(up_mine)
    down_w = other_parts(down_mine)
    small_here = my_features(small_full)
    gain_one_here = jnp.broadcast_to(small_here[0:1], small_here.shape)
    gain_two_here = jnp.broadcast_to(small_here[1:2], small_here.shape)
    nothing = [(0, 8 - experts), (0, 0)]
    router_here = jnp.pad(small_here[2 : 2 + experts], nothing)

    relative = (jnp.arange(experts, dtype=jnp.int32) + here_ctx) % experts
    numbers = jnp.arange(8, dtype=jnp.int32)
    onehot = (routes.T[:, None, :] == numbers[None, :, None]).astype(F32)
    named = (routes.T[:, None, :] == relative[None, :, None]).astype(F32)
    names = jnp.pad(named, [(0, 0)] + nothing)
    chosen = jnp.sum(named, axis=0)
    earlier = jnp.triu(jnp.ones((rows_here, rows_here), BF), 1)
    slot_of = mm(chosen.astype(BF), earlier).astype(jnp.int32)
    slots = jnp.arange(CAP, dtype=jnp.int32)
    picks = (slot_of[:, None, :] == slots[None, :, None]) & (chosen[:, None, :] > 0)
    picks = picks.astype(BF).reshape(experts * CAP, rows_here)

    gathered = first_norm(
        inputs_full, out_grad, small_full, attn_w, other_quarter, n_tp, n_ctx
    )
    normed_one, scale_one, grad_full = gathered[:3]
    if pair:
        qkv_w, output_w = gathered[3:]
    else:
        qkv_w, output_w = (
            lax.all_gather(w, "fsdp", axis=0, tiled=True)
            for w in (jnp.concatenate(attn_w[:3], axis=1), w_output)
        )
    positions = here_ctx * rows_here + jnp.arange(rows_here, dtype=jnp.int32)
    cosine, sine = rotary_tables(positions)
    attended, query, kv = attention_forward(mm(normed_one, qkv_w), cosine, sine, n_ctx)
    resid, scale_two, normed_two, grad_rows, token_rows, slot_gates, gates, mix = second_norm(
        mm_t(attended, output_w).astype(BF),
        hidden_in,
        gain_two_here,
        mm(picks, grad_full).astype(BF),
        picks,
        router_here,
        onehot,
        names,
        n_tp,
        n_ctx,
    )
    gate_rows = slot_gates[:, 0, :CAP].reshape(experts * CAP, 1)

    to_gate, to_up, hidden_act = expert_acts(token_rows, gate_w, up_w, n_fsdp)
    d_result = (gate_rows * grad_rows.astype(F32)).astype(BF)

    def away(left, right):
        value = t_mm(split(left)[1], right).astype(BF)
        return value, swap_fsdp(value)

    def payload_of(left, right, come):
        if pair:
            return Payload(n_ctx, product=(left, right, come))
        return Payload(
            n_ctx,
            rows=lax.psum_scatter(
                t_mm(left, right).astype(BF), "fsdp", scatter_dimension=0, tiled=True
            ),
        )

    def came_and_own(outs, payload):
        if pair:
            return tuple(outs)
        own = lax.dynamic_slice_in_dim(payload.inputs[0], here_ctx * payload.cut, payload.cut, 0)
        return outs[0], own

    down_come = gate_come = up_come = None
    if pair:
        down_away, down_come = away(d_result, hidden_act)
        grad_rows = after(grad_rows, down_away)
    d_hidden = into(grad_rows, down_w)
    gate_dot = jnp.sum(hidden_act.astype(F32) * d_hidden, axis=-1).reshape(experts, CAP)
    gate_dot = jnp.broadcast_to(
        jnp.pad(gate_dot, [(0, 0), (0, rows_here - CAP)])[:, None, :], (experts, 8, rows_here)
    )
    d_hidden = gate_rows * d_hidden
    d_gate_act = (d_hidden * to_gate).astype(BF)
    d_up_act = (d_hidden * to_up).astype(BF)
    if pair:
        gate_away, gate_come = away(token_rows, d_gate_act)

    acts = (d_gate_act, d_up_act, hidden_act)
    if pair:
        acts = lax.optimization_barrier((*acts, gate_away))[:3]
    d_resid, d_attn_here, gain_two_part, d_logits, made, *up_away = second_norm_back(
        acts,
        (gate_w, up_w, down_w),
        token_rows,
        gate_dot,
        picks,
        gates,
        onehot,
        names,
        router_here,
        resid,
        scale_two,
        gain_two_here,
        out_grad,
        n_tp,
        n_ctx,
    )
    if pair:
        up_come = swap_fsdp(up_away[0])

    payload = payload_of(d_result, hidden_act, down_come)
    early = (RowSums(made, 0, CAP, n_tp), made)
    d_attn, d_qkv, made_early, *outs = attention_backward(
        d_attn_here, output_w, query, kv, cosine, -sine, early, payload, n_tp, n_ctx
    )
    grad_down = came_and_own(outs, payload)
    payload = payload_of(token_rows, d_gate_act, gate_come)
    later = (RowSums(made, CAP, CAP, n_tp), made)
    in_grad, gain_one_part, made_later, *outs = first_norm_back(
        d_qkv, qkv_w, hidden_in, scale_one, gain_one_here, d_resid, later, payload, n_tp, n_ctx
    )
    grad_gate = came_and_own(outs, payload)
    payload = payload_of(token_rows, d_up_act, up_come)

    small_part = jnp.concatenate(
        [
            gain_one_part[:1],
            gain_two_part[:1],
            mm(d_logits[:experts].astype(BF), my_features(normed_two)),
            jnp.zeros((6 - experts, width_tp), F32),
        ],
        axis=0,
    )
    written = write_out([grad_gate, grad_down], None, (), n_ctx)
    if pair:
        small_part = after(small_part, *written)
    grad_gate, grad_down = written
    experts_out = ExpertsOut(made, (made_early, made_later), picks, mix, resid, n_tp, n_ctx)
    if pair:
        grad_attn, small_grad, block_out, *outs = weight_grads(
            [(d_attn, attended), (normed_one, d_qkv)],
            [(0, 0, heads_width), (1, 0, 2 * heads_width), (1, 2 * heads_width, heads_width)],
            small_part,
            payload,
            experts_out,
            n_tp,
            n_ctx,
        )
    else:
        grad_attn = jnp.concatenate([t_mm(d_attn, attended), t_mm(normed_one, d_qkv)], axis=1)
        scatter = partial(
            lax.psum_scatter, axis_name=("fsdp", "ctx"), scatter_dimension=0, tiled=True
        )
        grad_attn = scatter(grad_attn.astype(BF)).astype(F32)
        small_grad = lax.all_gather(small_part, "tp", axis=1, tiled=True)
        small_grad = scatter(small_grad.T).T
        block_out, *outs = experts_back(experts_out, payload, n_tp, n_ctx)
    grad_up = came_and_own(outs, payload)
    grad_up, block_out, in_grad, grad_output, grad_query, grad_key, grad_value = write_out(
        [grad_up], grad_attn, (block_out, in_grad), n_ctx
    )
    return (
        block_out,
        in_grad,
        small_grad[0],
        grad_query,
        grad_key,
        grad_value,
        grad_output,
        small_grad[1],
        small_grad[2 : 2 + experts].T,
        grad_gate,
        grad_up,
        grad_down,
    )


def solution(mesh):
    rows = ("fsdp", "ctx")
    placed = (
        P(rows, "tp"),
        P(rows, "tp"),
        P("fsdp"),
        P("fsdp", "tp"),
        P("fsdp", "tp"),
        P("fsdp", "tp"),
        P("fsdp", "tp"),
        P("fsdp"),
        P("fsdp", None),
        P(None, "fsdp", "tp"),
        P(None, "fsdp", "tp"),
        P(None, "fsdp", "tp"),
        P(rows, None),
    )
    return jax.shard_map(
        shards,
        mesh=mesh,
        in_specs=placed,
        out_specs=(
            P(rows, "tp"),
            P(rows, "tp"),
            P(rows),
            P(rows, "tp"),
            P(rows, "tp"),
            P(rows, "tp"),
            P(rows, "tp"),
            P(rows),
            P(rows, None),
            P(None, rows, "tp"),
            P(None, rows, "tp"),
            P(None, rows, "tp"),
        ),
        check_vma=False,
    )
```

```python
from functools import partial
import math

import jax
import jax.numpy as jnp
from jax import lax
from jax.experimental import pallas as pl
from jax.experimental.pallas import tpu as pltpu
from jax.sharding import PartitionSpec as P

HD = 128
CAP = 160


EPS = 1e-05
THETA = 10000.0
NEG = -1e30
BF = jnp.bfloat16
F32 = jnp.float32


def mm(left, right):
    return jnp.dot(left, right, preferred_element_type=F32)


def mm_t(left, right):
    return lax.dot_general(left, right, (((1,), (1,)), ((), ())), preferred_element_type=F32)


def t_mm(left, right):
    return lax.dot_general(left, right, (((0,), (0,)), ((), ())), preferred_element_type=F32)


def rotary_tables(positions):
    half_size = HD // 2
    frequency = THETA ** (-(jnp.arange(half_size, dtype=F32) * 2.0 / HD))
    angles = positions.astype(F32)[:, None] * frequency[None, :]
    cosine, sine = jnp.cos(angles), jnp.sin(angles)
    return jnp.concatenate([cosine, cosine], axis=1), jnp.concatenate([-sine, sine], axis=1)


MESH = pl.DeviceIdType.MESH
VM = pl.BlockSpec(memory_space=pltpu.VMEM)
DMA = pltpu.SemaphoreType.DMA


def peer(axis, n, k):
    return lax.rem(lax.axis_index(axis) + k, n)


def greet(groups):
    barrier = pltpu.get_barrier_semaphore()
    for axis, n in groups:
        for k in range(1, n):
            pl.semaphore_signal(
                barrier, inc=1, device_id={axis: peer(axis, n, k)}, device_id_type=MESH
            )
    pl.semaphore_wait(barrier, sum(n - 1 for _, n in groups))


def described(source, target, sems, i, to):
    return pltpu.make_async_remote_copy(
        src_ref=source,
        dst_ref=target,
        send_sem=sems[0].at[i],
        recv_sem=sems[1].at[i],
        device_id=to,
        device_id_type=MESH,
    )


def remote(source, target, sems, i, to):
    copy = described(source, target, sems, i, to)
    copy.start()
    return copy


def send(source, target, axis, n, k, sems):
    return remote(source, target, sems, k - 1, {axis: peer(axis, n, k)})


def columns(n, size):
    return pl.ds(pl.multiple_of(n * size, 128), size)


def stretch(n, size):
    return pl.ds(pl.multiple_of(n * size, 16), size)


def gather_columns(own, full, axis, n, sems):
    size = own.shape[1]
    place = full.at[:, columns(lax.axis_index(axis), size)]
    copies = [send(own, place, axis, n, k, sems) for k in range(1, n)]
    place[...] = own[...]
    return copies


def scatter_columns(part, slots, axis, n, sems):
    size = slots.shape[2]
    return [
        send(part.at[:, columns(peer(axis, n, k), size)], slots.at[k - 1], axis, n, k, sems)
        for k in range(1, n)
    ]


def finish(copies):
    for copy in copies:
        copy.wait()


class Payload:

    def __init__(self, n_ctx, rows=None, product=None):
        self.n_ctx = n_ctx
        self.product = product is not None
        self.inputs = list(product) if self.product else [rows]
        last = self.inputs[-1]
        self.rows, self.hidden = last.shape
        self.cut = self.rows // n_ctx
        self.outs = [shape((n_ctx - 1, self.cut, self.hidden), BF)]
        self.scratch = pair_of_sems(n_ctx)
        if self.product:
            self.outs.append(shape((self.cut, self.hidden), BF))
            self.scratch += [
                pltpu.VMEM((self.rows, self.hidden), BF),
                pltpu.VMEM((self.rows, self.hidden), BF),
                DMA,
            ]

    def take(self, ins, outs, scratch):
        self.ins, self.out_refs, self.held = ins, outs, scratch

    def load(self):
        if self.product:
            pltpu.make_async_copy(self.ins[2], self.held[2], self.held[4]).start()

    def copy(self, k):
        to = peer("ctx", self.n_ctx, k)
        source = self.held[3] if self.product else self.ins[0]
        return described(
            source.at[stretch(to, self.cut), :], self.out_refs[0].at[k - 1],
            self.held[0:2], k - 1, {"ctx": to},
        )

    def go(self, first=0, last=4):
        n_ctx, cut = self.n_ctx, self.cut
        if not self.product:
            for j in range(first, last):
                if (j + 2) % n_ctx:
                    self.copy((j + 2) % n_ctx).start()
            return
        left, right, other = self.ins
        if first == 0:
            pltpu.make_async_copy(other, self.held[2], self.held[4]).wait()
        base = lax.axis_index("fsdp") * self.rows

        @pl.loop(first, last)
        def _(j):
            k = lax.rem(j + 2, n_ctx)
            to = peer("ctx", n_ctx, k)
            value = t_mm(left[:, pl.ds(pl.multiple_of(base + to * cut, 128), cut)], right[...])
            value = value + self.held[2][stretch(to, cut), :].astype(F32)
            self.held[3][stretch(to, cut), :] = value.astype(BF)

            @pl.when(j != n_ctx - 2)
            def _():
                self.copy(k).start()

    def wait(self):
        if self.product:
            self.out_refs[1][...] = self.held[3][stretch(lax.axis_index("ctx"), self.cut), :]
        for k in range(1, self.n_ctx):
            self.copy(k).wait()


class RowSums:

    def __init__(self, made, first, count, n_tp):
        self.n_tp, self.first = n_tp, first
        self.shape = (count, made.shape[1] // n_tp)
        self.scratch = [
            pltpu.VMEM((n_tp - 1, *self.shape), BF),
            pltpu.VMEM(self.shape, BF),
            DMA,
        ] + pair_of_sems(n_tp)

    def take(self, made, scratch):
        self.made, self.held = made, scratch

    def rows(self, rank):
        return self.made.at[pl.ds(self.first, self.shape[0]), columns(rank, self.shape[1])]

    def mine(self):
        return pltpu.make_async_copy(
            self.rows(lax.axis_index("tp")), self.held[1], self.held[2]
        )

    def start(self):
        self.mine().start()
        n = self.n_tp
        self.copies = [
            send(self.rows(peer("tp", n, k)), self.held[0].at[k - 1], "tp", n, k, self.held[3:5])
            for k in range(1, n)
        ]

    def total(self):
        self.mine().wait()
        finish(self.copies)
        value = self.held[1][...].astype(F32)
        for k in range(1, self.n_tp):
            value = value + self.held[0][k - 1].astype(F32)
        return value


def quad():
    here = lax.axis_index("ctx")
    return here, here + 1 - 2 * lax.rem(here, 2), lax.rem(here + 2, 4)


def gather_square(own, places, sems, between, local=None):
    cuts = own.shape[1] // 512
    here, beside, across = quad()
    first, second, third = [], [], []
    for i in range(cuts):
        piece = own.at[:, pl.ds(i * 512, 512)]
        first.append(remote(piece, places(here, i), sems, 3 * i, {"ctx": across}))
        second.append(remote(piece, places(here, i), sems, 3 * i + 1, {"ctx": beside}))
        if local is None:
            places(here, i)[...] = piece[...]
        else:
            pltpu.make_async_copy(piece, places(here, i), local.at[i]).start()
    between()
    for i in range(cuts):
        first[i].wait()
        third.append(
            remote(places(across, i), places(across, i), sems, 3 * i + 2, {"ctx": beside})
        )
    finish(second)
    finish(third)
    if local is not None:
        for i in range(cuts):
            piece = own.at[:, pl.ds(i * 512, 512)]
            pltpu.make_async_copy(piece, places(here, i), local.at[i]).wait()


def row_sums(values):
    ones = jnp.ones((8, values.shape[1]), F32)
    return lax.dot_general(
        ones,
        values,
        (((1,), (1,)), ((), ())),
        precision=lax.Precision.HIGHEST,
        preferred_element_type=F32,
    )


def as_column(rows, weight):
    return lax.dot_general(
        rows,
        weight,
        (((0,), (0,)), ((), ())),
        precision=lax.Precision.HIGHEST,
        preferred_element_type=F32,
    )


def eighth():
    return jnp.full((8, 128), 0.125, F32)


def total_over(sums, mine, slots, axis, n, sems):
    mine[...] = sums
    copies = [send(mine, slots.at[k - 1], axis, n, k, sems) for k in range(1, n)]
    finish(copies)
    total = sums
    for k in range(1, n):
        total = total + slots[k - 1]
    return total


def call(kernel, out_shape, inputs, scratch, collective, name, left=()):
    anywhere = pl.BlockSpec(memory_space=pl.ANY)
    outs = out_shape if isinstance(out_shape, tuple) else (out_shape,)
    specs = [anywhere if i - len(outs) in left else VM for i in range(len(outs))]
    return pl.pallas_call(
        kernel,
        out_shape=out_shape,
        in_specs=[anywhere if i in left else VM for i in range(len(inputs))],
        out_specs=tuple(specs) if isinstance(out_shape, tuple) else specs[0],
        scratch_shapes=scratch,
        compiler_params=pltpu.CompilerParams(collective_id=collective, has_side_effects=True),
        cost_estimate=pl.CostEstimate(flops=0, bytes_accessed=0, transcendentals=0),
        name=name,
    )(*inputs)


def shape(dims, dtype):
    return jax.ShapeDtypeStruct(dims, dtype)


def pair_of_sems(n):
    return [DMA((n,)), DMA((n,))]


def gather_tp(value, stacks, n_tp):
    rows, size = value.shape
    many = len(stacks)
    member = stacks[0].shape[1:]

    def kernel(own, *refs):
        stk, full, outs = refs[:many], refs[many], refs[many + 1 : 2 * many + 1]
        held, loads, stores = refs[2 * many + 1 : 2 * many + 4]
        sems = refs[2 * many + 4 :]
        here = lax.axis_index("ctx")
        into = [
            pltpu.make_async_copy(stk[i].at[here], held.at[i], loads.at[i]) for i in range(many)
        ]
        away = [pltpu.make_async_copy(held.at[i], outs[i], stores.at[i]) for i in range(many)]
        for copy in into:
            copy.start()
        greet([("tp", n_tp)])
        copies = gather_columns(own, full, "tp", n_tp, sems)
        for i in range(many):
            into[i].wait()
            away[i].start()
        finish(copies)
        finish(away)

    return call(
        kernel,
        (
            shape((rows, size * n_tp), value.dtype),
            *(shape(member, stack.dtype) for stack in stacks),
        ),
        (value, *stacks),
        [pltpu.VMEM((many, *member), BF), DMA((many,)), DMA((many,))] + pair_of_sems(n_tp),
        1,
        "gather_tp",
        left=tuple(range(1, many + 1)) + tuple(range(-many, 0)),
    )


def first_norm(full, grad, gain, weights, quarter, n_tp, n_ctx):
    rows, width = full.shape
    with_quarter = quarter is not None

    def kernel(*refs):
        hid, grd, gn = refs[:3]
        refs = refs[3:]
        if with_quarter:
            wgts, refs = refs[: len(weights)], refs[len(weights) :]
            qrt, out, scale, grd_full, many_full, last_full, held, local, loads, stores = refs[:10]
            sems = refs[10:]
            half, inner = wgts[0].shape
            last = len(wgts) - 1
            mine = lax.axis_index("fsdp")

            def target(i, first_row, count):
                at = pl.ds(pl.multiple_of(first_row, 16), count)
                if i == last:
                    return last_full.at[at, :]
                return many_full.at[at, pl.ds(i * inner, inner)]

            into = [
                pltpu.make_async_copy(wgts[i], held.at[i], loads.at[i]) for i in range(len(wgts))
            ]
            away = [
                pltpu.make_async_copy(held.at[i], target(i, mine * half, half), stores.at[i])
                for i in range(len(wgts))
            ]
            for copy in into:
                copy.start()
            greet([("tp", n_tp), ("ctx", n_ctx)])
        else:
            out, scale, grd_full = refs[:3]
            sems = refs[3:]
            greet([("tp", n_tp)])
        grads = gather_columns(grd, grd_full, "tp", n_tp, sems[0:2])

        def norm():
            values = hid[...].astype(F32)
            mean = jnp.sum(values * values, axis=-1, keepdims=True) * (1.0 / width)
            factor = lax.rsqrt(mean + EPS)
            scale[...] = jnp.broadcast_to(factor, scale.shape)
            out[...] = (values * factor * gn[0:1, :]).astype(BF)

        if with_quarter:
            count = qrt.shape[0]

            def work():
                for i in range(len(wgts)):
                    into[i].wait()
                    away[i].start()
                norm()

            def places(rank, i):
                return target(i, (1 - mine) * half + rank * count, count)

            gather_square(qrt, places, sems[2:4], work, local)
            finish(away)
        else:
            norm()
        finish(grads)

    outs = [shape((rows, width), BF), shape((rows, 128), F32), shape((rows, width), BF)]
    inputs = [full, grad, gain]
    scratch, left = [], ()
    if with_quarter:
        half, inner = weights[0].shape
        many = len(weights)
        assert inner == 512
        outs.append(shape((2 * half, (many - 1) * inner), BF))
        outs.append(shape((2 * half, inner), BF))
        inputs += [*weights, quarter]
        scratch = [pltpu.VMEM((many, half, inner), BF), DMA((many,)), DMA((many,)), DMA((many,))]
        left = tuple(range(3, 3 + many)) + (-2, -1)
    return call(
        kernel,
        tuple(outs),
        inputs,
        scratch + pair_of_sems(n_tp) + pair_of_sems(12),
        7,
        "first_norm",
        left=left,
    )


def turn(values, cosine, sine):
    return values * cosine + pltpu.roll(values, HD // 2, axis=1) * sine


def softmax_rows(query, key, first_row):
    scores = mm_t(query, key) * (1.0 / math.sqrt(HD))
    rows = first_row + lax.broadcasted_iota(jnp.int32, scores.shape, 0)
    cols = lax.broadcasted_iota(jnp.int32, scores.shape, 1)
    scores = jnp.where(cols <= rows, scores, NEG)
    top = jnp.max(scores, axis=-1, keepdims=True)
    weights = jnp.exp(scores - top)
    return weights / jnp.sum(weights, axis=-1, keepdims=True)


def attention_forward(qkv, cosine, sine, n_ctx):
    rows = qkv.shape[0]
    width = qkv.shape[1] // 3
    heads = width // HD

    def kernel(prj, cs, sn, out, qry, full, own, *sems):
        greet([("ctx", n_ctx)])
        here = lax.axis_index("ctx")

        @pl.loop(0, heads)
        def _(h):
            own[:, columns(h, HD)] = turn(
                prj[:, columns(h + heads, HD)], cs[...], sn[...]
            ).astype(BF)
            own[:, columns(h + heads, HD)] = prj[:, columns(h + 2 * heads, HD)].astype(BF)

        def queries():
            @pl.loop(0, heads)
            def _(h):
                qry[:, columns(h, HD)] = turn(prj[:, columns(h, HD)], cs[...], sn[...]).astype(BF)

        def places(rank, i):
            return full.at[stretch(rank, rows), pl.ds(i * 512, 512)]

        gather_square(own, places, sems, queries)

        @pl.loop(0, heads)
        def _(h):
            probs = softmax_rows(qry[:, columns(h, HD)], full[:, columns(h, HD)], here * rows)
            out[:, columns(h, HD)] = mm(
                probs.astype(BF), full[:, columns(h + heads, HD)]
            ).astype(BF)

    return call(
        kernel,
        (
            shape((rows, width), BF),
            shape((rows, width), BF),
            shape((rows * n_ctx, 2 * width), BF),
        ),
        (qkv, cosine, sine),
        [pltpu.VMEM((rows, 2 * width), BF)] + pair_of_sems(6 * width // 512),
        2,
        "attention_forward",
    )


def second_norm(part, hidden, gain, slabs, picks, router, onehot, names, n_tp, n_ctx):
    rows, size = hidden.shape
    width = size * n_tp
    experts = n_ctx

    def kernel(
        prt, hid, gn, slb, pck, rtr, one, nms,
        resid, scale, out, moved, tokens, slot_gates, gates, mix,
        slots, mine, sums, mine_two, sums_two, low, sent, own_gates, *sems
    ):
        greet([("tp", n_tp), ("ctx", n_ctx)])
        here = lax.axis_index("tp")
        copies = scatter_columns(prt, slots, "tp", n_tp, sems[0:2])
        others = [
            send(
                slb.at[pl.ds(k * CAP, CAP)], moved.at[pl.ds(k * CAP, CAP)],
                "ctx", n_ctx, k, sems[6:8],
            )
            for k in range(1, n_ctx)
        ]
        moved[0:CAP] = slb[0:CAP]
        total = prt[:, columns(here, size)].astype(F32)
        finish(copies)
        for k in range(1, n_tp):
            total = total + slots[k - 1].astype(F32)
        total = hid[...].astype(F32) + total
        resid[...] = total
        square = total_over(row_sums(total * total), mine, sums, "tp", n_tp, sems[2:4])
        factor = lax.rsqrt(as_column(square, eighth()) * (1.0 / width) + EPS)
        scale[...] = factor
        low[...] = (resid[...] * factor[:, 0:1] * gn[0:1, :]).astype(BF)
        partial_logits = mm_t(rtr[...].astype(BF), low[...])
        mine_two[...] = partial_logits
        logit_copies = [
            send(mine_two, sums_two.at[k - 1], "tp", n_tp, k, sems[12:14]) for k in range(1, n_tp)
        ]
        gather_columns(low, out, "tp", n_tp, sems[4:6])

        def route():
            finish(logit_copies)
            logits = partial_logits
            for k in range(1, n_tp):
                logits = logits + sums_two[k - 1]
            named = [jnp.sum(one[j] * logits, axis=0, keepdims=True) for j in range(2)]
            top = jnp.maximum(named[0], named[1])
            powers = [jnp.exp(value - top) for value in named]
            both = powers[0] + powers[1]
            gate = [value / both for value in powers]
            mixed = gate[0] * nms[0] + gate[1] * nms[1]
            mix[...] = mixed
            order = lax.broadcasted_iota(jnp.int32, (8, rows), 0)
            gates[...] = jnp.where(order == 0, gate[0], jnp.where(order == 1, gate[1], 0.0))
            own_gates[...] = jnp.zeros(own_gates.shape, F32)
            for k in range(experts):
                own_gates[k, :, 0:CAP] = lax.dot_general(
                    jnp.broadcast_to(mixed[k : k + 1], (8, rows)),
                    pck[k * CAP : (k + 1) * CAP].astype(F32),
                    (((1,), (1,)), ((), ())),
                    precision=lax.Precision.HIGHEST,
                    preferred_element_type=F32,
                )
            slot_gates[0] = own_gates[0]
            for k in range(1, n_ctx):
                others.append(
                    send(own_gates.at[k], slot_gates.at[k], "ctx", n_ctx, k, sems[10:12])
                )


        def slab(k, step):
            at = columns(peer("tp", n_tp, n_tp - step), size)
            return described(
                sent.at[step, pl.ds(k * CAP, CAP)], tokens.at[pl.ds(k * CAP, CAP), at],
                sems[8:10], step * n_ctx + k, {"ctx": peer("ctx", n_ctx, k)},
            )

        def dispatch(step, block):
            sent[step] = mm(pck[...], block).astype(BF)
            tokens[0:CAP, columns(peer("tp", n_tp, n_tp - step), size)] = sent[step, 0:CAP]
            for k in (2, 3, 1):
                slab(k, step).start()

        route()

        @pl.loop(0, n_tp)
        def _(step):
            @pl.when(step > 0)
            def _():
                described(
                    low, out.at[:, columns(here, size)], sems[4:6], step - 1,
                    {"tp": peer("tp", n_tp, step)},
                ).wait()

            dispatch(step, out[:, columns(peer("tp", n_tp, n_tp - step), size)])

        for step in range(n_tp):
            for k in (2, 3, 1):
                slab(k, step).wait()
        finish(others)

    return call(
        kernel,
        (
            shape((rows, size), F32),
            shape((rows, 128), F32),
            shape((rows, width), BF),
            shape(slabs.shape, BF),
            shape(slabs.shape, BF),
            shape((experts, 8, rows), F32),
            shape((8, rows), F32),
            shape((8, rows), F32),
        ),
        (part, hidden, gain, slabs, picks, router, onehot, names),
        [
            pltpu.VMEM((n_tp - 1, rows, size), BF),
            pltpu.VMEM((8, rows), F32),
            pltpu.VMEM((n_tp - 1, 8, rows), F32),
            pltpu.VMEM((8, rows), F32),
            pltpu.VMEM((n_tp - 1, 8, rows), F32),
            pltpu.VMEM((rows, size), BF),
            pltpu.VMEM((n_tp, experts * CAP, size), BF),
            pltpu.VMEM((experts, 8, rows), F32),
        ]
        + pair_of_sems(n_tp) * 3
        + pair_of_sems(n_ctx)
        + pair_of_sems(n_tp * n_ctx)
        + pair_of_sems(n_ctx)
        + pair_of_sems(n_tp),
        3,
        "second_norm",
    )


def expert_acts(tokens, gate_w, up_w, n_fsdp):
    rows, width = tokens.shape
    hidden = gate_w[0].shape[1]
    count = len(gate_w)
    part = gate_w[0].shape[0]
    chunk = 256
    per = part // chunk
    steps = count * per
    pair = count == 2

    def kernel(tok, *refs):
        wgt = [refs[:count], refs[count : 2 * count]]
        to_gate, to_up, hid, buffer, loads = refs[2 * count :]
        first = lax.axis_index("fsdp") if pair else 0

        def load(step):
            slot = lax.rem(step, 2)
            at = stretch(lax.rem(step, per), chunk)
            for lane in range(2):
                for i in range(count):

                    @pl.when(step // per == i)
                    def _():
                        pltpu.make_async_copy(
                            wgt[lane][i].at[at], buffer.at[slot, lane], loads.at[slot, lane]
                        ).start()

        load(0)
        to_gate[...] = jnp.zeros_like(to_gate)
        to_up[...] = jnp.zeros_like(to_up)

        @pl.loop(0, steps)
        def _(step):
            slot = lax.rem(step, 2)
            for lane in range(2):
                pltpu.make_async_copy(
                    wgt[lane][0].at[pl.ds(0, chunk)], buffer.at[slot, lane], loads.at[slot, lane]
                ).wait()

            @pl.when(step + 1 < steps)
            def _():
                load(step + 1)

            which = lax.rem(first + step // per, count)
            column = which * part + lax.rem(step, per) * chunk
            values = tok[:, pl.ds(pl.multiple_of(column, 128), chunk)]
            to_gate[...] += mm(values, buffer[slot, 0])
            to_up[...] += mm(values, buffer[slot, 1])

        @pl.loop(0, rows // 32)
        def _(i):
            at = stretch(i, 32)
            a, b = to_gate[at, :], to_up[at, :]
            sigma = 1.0 / (1.0 + jnp.exp(-a))
            silu = a * sigma
            hid[at, :] = (silu * b).astype(BF)
            to_up[at, :] = silu
            to_gate[at, :] = b * sigma * (1.0 + a * (1.0 - sigma))

    anywhere = pl.BlockSpec(memory_space=pl.ANY)
    return pl.pallas_call(
        kernel,
        out_shape=(
            shape((rows, hidden), F32),
            shape((rows, hidden), F32),
            shape((rows, hidden), BF),
        ),
        in_specs=[VM] + [anywhere] * (2 * count),
        out_specs=(VM, VM, VM),
        scratch_shapes=[pltpu.VMEM((2, 2, chunk, hidden), BF), DMA((2, 2))],
        cost_estimate=pl.CostEstimate(flops=0, bytes_accessed=0, transcendentals=0),
        name="expert_acts",
    )(tokens, *gate_w, *up_w)


def second_norm_back(
    acts, weights, tokens, dots, picks, gates, onehot, names, router, resid, scale, gain, grad,
    n_tp, n_ctx,
):
    rows, size = resid.shape
    width = size * n_tp
    experts = n_ctx
    hidden = acts[0].shape[1]
    count = len(weights[0])
    part = weights[0][0].shape[0]

    def kernel(*refs):
        dga, dup, hid = refs[:3]
        wgt = [refs[3 + i * count : 3 + (i + 1) * count] for i in range(3)]
        refs = refs[3 + 3 * count :]
        tok, dts, pck, gts, one, nms, rtr, rsd, scl, gn, grd = refs[:11]
        d_resid, low, d_gain, d_logits, out_rows = refs[11:16]
        refs = refs[16:]
        if count == 2:
            up_away, up_held, up_sem = refs[:1] + refs[1:3]
            refs = refs[3:]
        (
            drw, eo, buffer, back, back_dots, parts, slots, mine, sums, mine_two, sums_two, loads,
            out_sem,
        ) = refs[:13]
        sems = refs[13:]
        here = lax.axis_index("tp")
        first = lax.axis_index("fsdp")

        def load(which, rank, slot, lane):
            feature = rank * size
            inside = pl.ds(pl.multiple_of(lax.rem(feature, part), 16), size)
            target = buffer.at[slot, lane]
            if count == 1:
                pltpu.make_async_copy(
                    wgt[which][0].at[inside], target, loads.at[slot, lane]
                ).start()
                return
            own = feature // part == first

            @pl.when(own)
            def _():
                pltpu.make_async_copy(
                    wgt[which][0].at[inside], target, loads.at[slot, lane]
                ).start()

            @pl.when(jnp.logical_not(own))
            def _():
                pltpu.make_async_copy(
                    wgt[which][1].at[inside], target, loads.at[slot, lane]
                ).start()

        def loaded(which, slot, lane):
            pltpu.make_async_copy(
                wgt[which][0].at[pl.ds(0, size)], buffer.at[slot, lane], loads.at[slot, lane]
            ).wait()

        load(0, peer("tp", n_tp, 1), 0, 0)
        load(1, peer("tp", n_tp, 1), 0, 1)
        greet([("tp", n_tp), ("ctx", n_ctx)])
        small = []
        for k in range(1, n_ctx):
            small.append(
                send(dts.at[k], back_dots.at[k - 1], "ctx", n_ctx, n_ctx - k, sems[0:2])
            )

        def slab(k, rank, step):
            at = columns(rank, size)
            return described(
                drw.at[pl.ds(k * CAP, CAP), at], back.at[k - 1, :, at],
                sems[2:4], step * n_ctx + k - 1, {"ctx": peer("ctx", n_ctx, n_ctx - k)},
            )

        @pl.loop(0, n_tp)
        def _(step):
            rank = peer("tp", n_tp, step + 1)
            slot = lax.rem(step, 2)
            loaded(0, slot, 0)
            loaded(1, slot, 1)

            @pl.when(step + 1 < n_tp)
            def _():
                load(0, peer("tp", n_tp, step + 2), 1 - slot, 0)
                load(1, peer("tp", n_tp, step + 2), 1 - slot, 1)

            drw[:, columns(rank, size)] = (
                mm_t(dga[...], buffer[slot, 0]) + mm_t(dup[...], buffer[slot, 1])
            ).astype(BF)
            for k in (2, 3, 1):
                slab(k, rank, step).start()

        def combined(step):
            rank = peer("tp", n_tp, step)
            at = columns(rank, size)
            for k in (2, 3, 1):
                slab(k, rank, step - 1).wait()
            block = t_mm(pck[0:CAP], drw[0:CAP, at])
            for k in range(1, experts):
                block = block + t_mm(pck[k * CAP : (k + 1) * CAP], back[k - 1, :, at])
            return block

        def give(step):
            return described(
                parts.at[step - 1], slots.at[step - 1], sems[6:8], step - 1,
                {"tp": peer("tp", n_tp, step)},
            )

        def pass_on(begin, end):
            @pl.loop(begin, end)
            def _(step):
                parts[step - 1] = combined(step).astype(BF)
                give(step).start()

        load(2, 0, 0, 0)
        finish(small)
        order = lax.broadcasted_iota(jnp.int32, (8, rows), 0)
        own = jnp.zeros((8, rows), F32)
        for k in range(experts):
            by_slot = dts[0] if k == 0 else back_dots[k - 1]
            by_row = lax.dot_general(
                by_slot[:, 0:CAP],
                pck[k * CAP : (k + 1) * CAP].astype(F32),
                (((1,), (0,)), ((), ())),
                precision=lax.Precision.HIGHEST,
                preferred_element_type=F32,
            )
            own = own + jnp.where(order == k, by_row, 0.0)
        mine[...] = own
        shared = [
            send(mine, sums.at[k - 1], "tp", n_tp, k, sems[4:6]) for k in range(1, n_tp)
        ]
        pass_on(1, n_tp - 1)


        @pl.loop(0, n_tp)
        def _(rank):
            slot = lax.rem(rank, 2)
            loaded(2, slot, 0)

            @pl.when(rank + 1 < n_tp)
            def _():
                load(2, rank + 1, 1 - slot, 0)

            eo[:, columns(rank, size)] = mm_t(hid[...], buffer[slot, 0]).astype(BF)

        pltpu.make_async_copy(eo, out_rows, out_sem).start()
        pass_on(n_tp - 1, n_tp)
        if count == 2:

            @pl.loop(0, part // 256)
            def _(i):
                at = pl.ds(pl.multiple_of((1 - first) * part + i * 256, 128), 256)
                up_held[stretch(i, 256), :] = t_mm(tok[:, at], dup[...]).astype(BF)

            pltpu.make_async_copy(up_held, up_away, up_sem).start()
        finish(shared)
        gate_grad = mine[...]
        for k in range(1, n_tp):
            gate_grad = gate_grad + sums[k - 1]
        both = [jnp.sum(nms[j] * gate_grad, axis=0, keepdims=True) for j in range(2)]
        gate = [gts[j : j + 1, :] for j in range(2)]
        mean = gate[0] * both[0] + gate[1] * both[1]
        logits = sum(gate[j] * (both[j] - mean) * one[j] for j in range(2))
        d_logits[...] = logits

        copies = [give(step) for step in range(1, n_tp)]
        total = combined(n_tp)
        total = total + lax.dot_general(
            logits.astype(BF),
            rtr[...].astype(BF),
            (((0,), (0,)), ((), ())),
            preferred_element_type=F32,
        )
        finish(copies)
        for k in range(1, n_tp):
            total = total + slots[k - 1].astype(F32)
        factor = scl[:, 0:1]
        unit = rsd[...] * factor
        d_gain[...] = jnp.broadcast_to(jnp.sum(total * unit, axis=0, keepdims=True), d_gain.shape)
        gained = total * gn[0:1, :]
        d_resid[...] = gained
        dot = total_over(row_sums(unit * gained), mine_two, sums_two, "tp", n_tp, sems[8:10])
        dot = as_column(dot, eighth())[:, 0:1] * (1.0 / width)
        result = grd[...].astype(F32) + factor * (d_resid[...] - rsd[...] * factor * dot)
        d_resid[...] = result
        low[...] = result.astype(BF)
        pltpu.make_async_copy(eo, out_rows, out_sem).wait()
        if count == 2:
            pltpu.make_async_copy(up_held, up_away, up_sem).wait()

    outs = [
        shape((rows, size), F32),
        shape((rows, size), BF),
        shape((8, size), F32),
        shape((8, rows), F32),
        shape((experts * CAP, width), BF),
    ]
    held = []
    if count == 2:
        outs.append(shape((part, hidden), BF))
        held = [pltpu.VMEM((part, hidden), BF), DMA]
    flat = [array for group in weights for array in group]
    return call(
        kernel,
        tuple(outs),
        (*acts, *flat, tokens, dots, picks, gates, onehot, names, router, resid, scale, gain, grad),
        held
        + [
            pltpu.VMEM((experts * CAP, width), BF),
            pltpu.VMEM((experts * CAP, width), BF),
            pltpu.VMEM((2, 2, size, hidden), BF),
            pltpu.VMEM((n_ctx - 1, CAP, width), BF),
            pltpu.VMEM((n_ctx - 1, 8, rows), F32),
            pltpu.VMEM((n_tp - 1, rows, size), BF),
            pltpu.VMEM((n_tp - 1, rows, size), BF),
            pltpu.VMEM((8, rows), F32),
            pltpu.VMEM((n_tp - 1, 8, rows), F32),
            pltpu.VMEM((8, rows), F32),
            pltpu.VMEM((n_tp - 1, 8, rows), F32),
            DMA((2, 2)),
            DMA,
        ]
        + pair_of_sems(n_ctx)
        + pair_of_sems(n_tp * n_ctx)
        + pair_of_sems(n_tp) * 3,
        4,
        "second_norm_back",
        left=tuple(range(3, 3 + 3 * count)) + ((-2, -1) if count == 2 else (-1,)),
    )


def attention_backward(
    low, output_w, query, kv, cosine, sine, sums, payload, n_tp, n_ctx
):
    rows, size = low.shape
    width = size * n_tp
    inner = query.shape[1]
    heads = inner // HD
    scale = 1.0 / math.sqrt(HD)

    half = heads // 2
    sums, sums_input = sums
    lane = 2 * half * HD

    def kernel(*refs):
        lw, wgt, qry, full, cs, sn, made = refs[:7]
        n_in, n_out = 7 + len(payload.inputs), len(payload.outs)
        d_attn, d_qkv, summed = refs[n_in : n_in + 3]
        scratch = refs[n_in + 3 + n_out :]
        dot, dqs, dkv, slots, last, both, total, kept = scratch[:8]
        sems = scratch[8:12]
        sums.take(made, scratch[12 : 12 + len(sums.scratch)])
        payload.take(
            refs[7:n_in], refs[n_in + 3 : n_in + 3 + n_out], scratch[12 + len(sums.scratch) :]
        )
        payload.load()
        greet([("tp", n_tp), ("ctx", n_ctx)])
        here, beside, across = quad()
        beyond = lax.rem(beside + 2, 4)
        copies = gather_columns(lw, d_attn, "tp", n_tp, sems[2:4])
        sums.start()
        payload.go()

        @pl.loop(0, heads)
        def _(h):
            at = columns(h, HD)
            kept[h] = softmax_rows(qry[:, at], full[:, at], here * rows)

        for step in range(n_tp):
            rank = peer("tp", n_tp, n_tp - step)
            weights = wgt[pl.ds(pl.multiple_of(rank * size, 16), size), :]
            if step:
                copies[step - 1].wait()
                total[...] += mm(d_attn[:, columns(rank, size)], weights)
            else:
                total[...] = mm(lw[...], weights)
        dot[...] = total[...].astype(BF)
        first, second, third = [], [], []
        for j in range(2):

            @pl.loop(0, half)
            def _(i):
                h = j * half + i
                at, at_v = columns(h, HD), columns(h + heads, HD)
                key_at = pl.ds(pl.multiple_of(j * lane + i * HD, 128), HD)
                value_at = pl.ds(pl.multiple_of(j * lane + (half + i) * HD, 128), HD)
                probs = kept[h]
                d_probs = mm_t(dot[:, at], full[:, at_v])
                delta = jnp.sum(probs * d_probs, axis=-1, keepdims=True)
                d_scores = (probs * (d_probs - delta)).astype(BF)
                dqs[:, at] = mm(d_scores, full[:, at]) * scale
                dkv[:, key_at] = (t_mm(d_scores, qry[:, at]) * scale).astype(BF)
                dkv[:, value_at] = t_mm(probs.astype(BF), dot[:, at]).astype(BF)

            at = pl.ds(j * lane, lane)
            first.append(
                remote(
                    dkv.at[stretch(beyond, rows), at], slots.at[0, :, at],
                    sems, 3 * j, {"ctx": beside},
                )
            )
            second.append(
                remote(
                    dkv.at[stretch(beside, rows), at], slots.at[1, :, at],
                    sems, 3 * j + 1, {"ctx": beside},
                )
            )
        for j in range(2):
            at = pl.ds(j * lane, lane)
            first[j].wait()
            both[:, at] = (
                dkv[stretch(across, rows), at].astype(F32) + slots[0, :, at].astype(F32)
            ).astype(BF)
            third.append(
                remote(both.at[:, at], last.at[:, at], sems, 3 * j + 2, {"ctx": across})
            )

        @pl.loop(0, heads)
        def _(h):
            d_qkv[:, columns(h, HD)] = turn(dqs[:, columns(h, HD)], cs[...], sn[...]).astype(BF)

        for j in range(2):
            second[j].wait()
            third[j].wait()

            @pl.loop(0, half)
            def _(i):
                h = j * half + i
                key_at = pl.ds(pl.multiple_of(j * lane + i * HD, 128), HD)
                value_at = pl.ds(pl.multiple_of(j * lane + (half + i) * HD, 128), HD)
                mine = stretch(here, rows)
                d_key = dkv[mine, key_at].astype(F32) + slots[1, :, key_at].astype(F32)
                d_key = d_key + last[:, key_at].astype(F32)
                d_qkv[:, columns(h + heads, HD)] = turn(d_key, cs[...], sn[...]).astype(BF)
                d_value = dkv[mine, value_at].astype(F32) + slots[1, :, value_at].astype(F32)
                d_value = d_value + last[:, value_at].astype(F32)
                d_qkv[:, columns(h + 2 * heads, HD)] = d_value.astype(BF)

        summed[...] = sums.total().astype(BF)
        payload.wait()

    return call(
        kernel,
        (
            shape((rows, width), BF),
            shape((rows, 3 * inner), BF),
            shape(sums.shape, BF),
            *payload.outs,
        ),
        (low, output_w, query, kv, cosine, sine, sums_input, *payload.inputs),
        [
            pltpu.VMEM((rows, inner), BF),
            pltpu.VMEM((rows, inner), F32),
            pltpu.VMEM((rows * n_ctx, 2 * inner), BF),
            pltpu.VMEM((2, rows, 2 * inner), BF),
            pltpu.VMEM((rows, 2 * inner), BF),
            pltpu.VMEM((rows, 2 * inner), BF),
            pltpu.VMEM((rows, inner), F32),
            pltpu.VMEM((heads, rows, rows * n_ctx), F32),
        ]
        + pair_of_sems(6)
        + pair_of_sems(n_tp)
        + sums.scratch
        + payload.scratch,
        5,
        "attention_backward",
        left=(6, 6 + len(payload.inputs), -len(payload.outs)),
    )


def first_norm_back(d_qkv, weights, hidden, scale, gain, d_resid, payload, n_tp, n_ctx):
    rows, size = hidden.shape
    width = size * n_tp

    def kernel(*refs):
        dpr, wgt, hid, scl, gn, dr = refs[:6]
        n_in, n_out = 6 + len(payload.inputs), len(payload.outs)
        out, d_gain = refs[n_in : n_in + 2]
        scratch = refs[n_in + 2 + n_out :]
        held, parts, slots, mine, sums, loads = scratch[:6]
        sems = scratch[6:10]
        payload.take(refs[6:n_in], refs[n_in + 2 : n_in + 2 + n_out], scratch[10:])

        def block(step):
            rank = peer("tp", n_tp, step)
            return pltpu.make_async_copy(
                wgt.at[stretch(rank, size), :], held.at[step - 1], loads.at[step - 1]
            )

        for step in range(1, n_tp + 1):
            block(step).start()
        payload.load()
        greet([("tp", n_tp), ("ctx", n_ctx)])

        def give(step):
            return described(
                parts.at[step - 1], slots.at[step - 1], sems[0:2], step - 1,
                {"tp": peer("tp", n_tp, step)},
            )

        @pl.loop(1, n_tp + 1)
        def _(step):
            block(step).wait()
            out[...] = mm_t(dpr[...], held[step - 1])

            @pl.when(step < n_tp)
            def _():
                parts[step - 1] = out[...].astype(BF)
                give(step).start()

        copies = [give(step) for step in range(1, n_tp)]
        payload.go()
        finish(copies)
        total = out[...]
        for k in range(1, n_tp):
            total = total + slots[k - 1].astype(F32)
        factor = scl[:, 0:1]
        unit = hid[...].astype(F32) * factor
        d_gain[...] = jnp.broadcast_to(jnp.sum(total * unit, axis=0, keepdims=True), d_gain.shape)
        gained = total * gn[0:1, :]
        out[...] = gained
        dot = total_over(row_sums(unit * gained), mine, sums, "tp", n_tp, sems[2:4])
        dot = as_column(dot, eighth())[:, 0:1] * (1.0 / width)
        unit = hid[...].astype(F32) * factor
        out[...] = dr[...] + factor * (out[...] - unit * dot)
        payload.wait()

    return call(
        kernel,
        (shape((rows, size), F32), shape((8, size), F32), *payload.outs),
        (d_qkv, weights, hidden, scale, gain, d_resid, *payload.inputs),
        [
            pltpu.VMEM((n_tp, size, d_qkv.shape[1]), BF),
            pltpu.VMEM((n_tp - 1, rows, size), BF),
            pltpu.VMEM((n_tp - 1, rows, size), BF),
            pltpu.VMEM((8, rows), F32),
            pltpu.VMEM((n_tp - 1, 8, rows), F32),
            DMA((n_tp,)),
        ]
        + pair_of_sems(n_tp) * 2
        + payload.scratch,
        6,
        "first_norm_back",
        left=(1, 5 + len(payload.inputs), -len(payload.outs)),
    )


class ExpertsOut:

    def __init__(self, made, done, picks, mix, resid, n_tp, n_ctx):
        self.n_ctx, self.n_done = n_ctx, len(done)
        first = CAP * len(done)
        self.sums = RowSums(made, first, made.shape[0] - first, n_tp)
        self.inputs = [made, *done, picks, mix, resid]
        self.size = resid.shape[1]
        self.out = shape(resid.shape, BF)
        self.scratch = [
            pltpu.VMEM(self.sums.shape, BF),
            pltpu.VMEM((n_ctx - 1, CAP, self.size), BF),
        ]
        self.scratch += pair_of_sems(n_ctx) + self.sums.scratch

    def take(self, ins, out, scratch):
        self.ins, self.out_ref, self.held = ins, out, scratch[:4]
        self.sums.take(ins[0], scratch[4:])

    def block(self, k):
        if k < self.n_done:
            return self.ins[1 + k]
        return self.held[0].at[pl.ds((k - self.n_done) * CAP, CAP)]

    def give_back(self):
        share, back = self.held[:2]
        share[...] = self.sums.total().astype(BF)
        n_ctx = self.n_ctx
        self.copies = [
            send(self.block(k), back.at[k - 1], "ctx", n_ctx, n_ctx - k, self.held[2:4])
            for k in range(1, n_ctx)
        ]

    def mix(self):
        picks, mix, resid = self.ins[-3:]
        back = self.held[1]
        finish(self.copies)
        order = lax.broadcasted_iota(jnp.int32, (8, 128), 0)
        total = resid[...]
        for k in range(self.n_ctx):
            gate = as_column(mix[...], jnp.where(order == k, 1.0, 0.0))[:, 0:1]
            rows = self.block(0)[...] if k == 0 else back[k - 1]
            total = total + gate * t_mm(picks[k * CAP : (k + 1) * CAP], rows)
        self.out_ref[...] = total.astype(BF)


def weight_grads(products, groups, small, payload, experts_out, n_tp, n_ctx):
    width = products[0][0].shape[1]
    places = 2 * n_ctx
    cut = width // places
    total_columns = sum(size for _, _, size in groups)
    flat = [array for pair in products for array in pair]
    inputs = [*flat, small, *experts_out.inputs, *payload.inputs]

    def kernel(*refs):
        factors, refs = refs[: len(flat)], refs[len(flat) :]
        sml, refs = refs[0], refs[1:]
        given, refs = refs[: len(experts_out.inputs)], refs[len(experts_out.inputs) :]
        paid, refs = refs[: len(payload.inputs)], refs[len(payload.inputs) :]
        out, small_out, block_out = refs[:3]
        paid_out, refs = refs[3 : 3 + len(payload.outs)], refs[3 + len(payload.outs) :]
        sml_full, sml_slots, refs = refs[0], refs[1], refs[2:]
        scratch, refs = refs[: 6 * len(groups)], refs[6 * len(groups) :]
        experts_out.take(given, block_out, refs[: len(experts_out.scratch)])
        refs = refs[len(experts_out.scratch) :]
        payload.take(paid, paid_out, refs[: len(payload.scratch)])
        sems = refs[len(payload.scratch) :]
        payload.load()
        barrier = pltpu.get_barrier_semaphore()
        here, beside, across = quad()
        beyond = lax.rem(beside + 2, 4)
        mine = lax.axis_index("fsdp")
        other = 1 - mine
        place = mine * n_ctx + here
        others = []
        for i in range(1, places):
            to = lax.rem(place + i, places)
            others.append((to, {"fsdp": to // n_ctx, "ctx": lax.rem(to, n_ctx)}))
        ahead = [{"tp": peer("tp", n_tp, k)} for k in range(1, n_tp)]
        for device in ahead + [device for _, device in others]:
            pl.semaphore_signal(barrier, inc=1, device_id=device, device_id_type=MESH)
        pl.semaphore_wait(barrier, n_tp - 1 + places - 1)
        gathers = gather_columns(sml, sml_full, "tp", n_tp, sems[0:2])
        experts_out.sums.start()
        moves = []

        def near(g):
            which, start, size = groups[g]
            prt, come = scratch[6 * g : 6 * g + 2]
            left, right = factors[2 * which : 2 * which + 2]

            @pl.loop(0, places)
            def _(i):
                prt[i] = t_mm(left[:, columns(i, cut)], right[:, start : start + size]).astype(BF)

            blocks = [(other, beyond), (other, beside), (mine, beyond), (mine, beside)]
            moves.append(
                [
                    remote(
                        prt.at[rank * n_ctx + column], come.at[i],
                        sems[4 + 6 * g : 6 + 6 * g], i, {"ctx": beside},
                    )
                    for i, (rank, column) in enumerate(blocks)
                ]
            )

        def chip(g, i, rank, column):
            prt, come = scratch[6 * g : 6 * g + 2]
            moves[g][i].wait()
            return prt[rank * n_ctx + column].astype(F32) + come[i].astype(F32)

        hops = []

        def hop(g):
            two, far = scratch[6 * g + 2 : 6 * g + 4]
            sent = []
            for i, column in enumerate((across, here)):
                two[i] = chip(g, i, other, column).astype(BF)
                sent.append(
                    remote(
                        two.at[i], far.at[i], sems[6 + 6 * g : 8 + 6 * g], i, {"fsdp": other}
                    )
                )
            hops.append(sent)

        payload.go()
        near(0)
        finish(gathers)
        totals = [
            remote(sml_full.at[:, columns(to, cut)], sml_slots.at[i], sems[2:4], i, device)
            for i, (to, device) in enumerate(others)
        ]
        hop(0)
        for g in range(1, len(groups)):
            near(g)
            hop(g)
        lasts = []
        for g in range(len(groups)):
            far, one, last = scratch[6 * g + 3 : 6 * g + 6]
            value = chip(g, 2, mine, across)
            hops[g][0].wait()
            one[...] = (value + far[0].astype(F32)).astype(BF)
            lasts.append(
                remote(one, last, sems[8 + 6 * g : 10 + 6 * g], 0, {"ctx": across})
            )
            if g == 1:
                experts_out.give_back()
        finish(totals)
        sums = sml_full[:, columns(place, cut)]
        for i in range(places - 1):
            sums = sums + sml_slots[i]
        small_out[...] = sums
        start = 0
        for g, (_, _, size) in enumerate(groups):
            far = scratch[6 * g + 3]
            value = chip(g, 3, mine, here)
            hops[g][1].wait()
            value = value + far[1].astype(F32)
            out[:, start : start + size] = value
            start += size
        experts_out.mix()
        payload.wait()
        start = 0
        for g, (_, _, size) in enumerate(groups):
            lasts[g].wait()
            at = pl.ds(start, size)
            out[:, at] = out[:, at] + scratch[6 * g + 5][...].astype(F32)
            start += size

    buffers = [pltpu.VMEM((8, width), F32), pltpu.VMEM((places - 1, 8, cut), F32)]
    sems = pair_of_sems(n_tp) + pair_of_sems(places)
    for _, _, size in groups:
        buffers += [
            pltpu.VMEM((places, cut, size), BF),
            pltpu.VMEM((4, cut, size), BF),
            pltpu.VMEM((2, cut, size), BF),
            pltpu.VMEM((2, cut, size), BF),
            pltpu.VMEM((cut, size), BF),
            pltpu.VMEM((cut, size), BF),
        ]
        sems += pair_of_sems(4) + pair_of_sems(2) + pair_of_sems(1)
    return call(
        kernel,
        (
            shape((cut, total_columns), F32),
            shape((8, cut), F32),
            experts_out.out,
            *payload.outs,
        ),
        inputs,
        buffers + experts_out.scratch + payload.scratch + sems,
        10,
        "weight_grads",
        left=(
            len(flat) + 1,
            len(inputs) - 1,
            -len(payload.outs),
        ),
    )


def experts_back(experts_out, payload, n_tp, n_ctx):
    inputs = [*experts_out.inputs, *payload.inputs]
    given = len(experts_out.inputs)

    def kernel(*refs):
        ins, refs = refs[: len(inputs)], refs[len(inputs) :]
        outs, scratch = refs[: 1 + len(payload.outs)], refs[1 + len(payload.outs) :]
        experts_out.take(ins[:given], outs[0], scratch[: len(experts_out.scratch)])
        payload.take(ins[given:], outs[1:], scratch[len(experts_out.scratch) :])
        greet([("tp", n_tp), ("ctx", n_ctx)])
        experts_out.sums.start()
        payload.go()
        experts_out.give_back()
        experts_out.mix()
        payload.wait()

    return call(
        kernel,
        (experts_out.out, *payload.outs),
        inputs,
        experts_out.scratch + payload.scratch,
        9,
        "experts_back",
        left=(0, len(inputs) - 1, -len(payload.outs)),
    )


def write_out(experts_grads, attn_grad, plain, n_ctx):
    _, rows, size = experts_grads[0][0].shape
    steps = max(1, rows // 32)
    tile = rows // steps
    many = len(experts_grads)
    plain = list(plain)
    blocks = []
    if attn_grad is not None:
        block = attn_grad.shape[1] // 4
        blocks = [shape((attn_grad.shape[0], block), F32)] * 4
        plain.append(attn_grad)

    def kernel(*refs):
        here = lax.axis_index("ctx")
        ins, outs = refs[: 2 * many + len(plain)], refs[2 * many + len(plain) :]
        for i in range(many):
            came, mine = ins[2 * i : 2 * i + 2]
            outs[i][here] = mine[...].astype(F32)
            for k in range(1, n_ctx):
                outs[i][lax.rem(here + n_ctx - k, n_ctx)] = came[k - 1].astype(F32)
        for i in range(len(plain) - (1 if blocks else 0)):
            outs[many + i][...] = ins[2 * many + i][...]
        for i in range(len(blocks)):
            outs[i - 4][...] = ins[-1][:, i * block : (i + 1) * block]

    def flat(array):
        return pl.BlockSpec((array.shape[0] // steps, array.shape[1]), lambda i: (i, 0))

    in_specs, out_specs, out_shape = [], [], []
    for _ in experts_grads:
        in_specs.append(pl.BlockSpec((n_ctx - 1, tile, size), lambda i: (0, i, 0)))
        in_specs.append(pl.BlockSpec((tile, size), lambda i: (i, 0)))
        out_specs.append(pl.BlockSpec((n_ctx, tile, size), lambda i: (0, i, 0)))
        out_shape.append(shape((n_ctx, rows, size), F32))
    for array in plain[: len(plain) - (1 if blocks else 0)] + blocks:
        out_specs.append(flat(array))
        out_shape.append(shape(array.shape, array.dtype))
    in_specs += [flat(array) for array in plain]
    inputs = [array for pair in experts_grads for array in pair] + plain
    return pl.pallas_call(
        kernel,
        grid=(steps,),
        in_specs=in_specs,
        out_specs=out_specs,
        out_shape=out_shape,
        cost_estimate=pl.CostEstimate(
            flops=0, bytes_accessed=6 * many * n_ctx * rows * size, transcendentals=0
        ),
        name="write_out",
    )(*inputs)


def after(value, *needed):
    return lax.optimization_barrier((value, *needed))[0]


def shards(
    hidden_in,
    out_grad,
    attn_gain,
    w_query,
    w_key,
    w_value,
    w_output,
    ffn_gain,
    w_router,
    w_gate,
    w_up,
    w_down,
    routes,
):
    rows_here, width_tp = hidden_in.shape
    here_tp = lax.axis_index("tp")
    here_ctx = lax.axis_index("ctx")
    here_fsdp = lax.axis_index("fsdp")
    n_fsdp = lax.axis_size("fsdp")
    n_ctx = lax.axis_size("ctx")
    n_tp = lax.axis_size("tp")
    experts = w_gate.shape[0]
    assert experts == n_ctx == 4
    width = width_tp * n_tp
    part = width // n_fsdp
    pair = n_fsdp == 2
    heads_width = w_query.shape[1]

    def swap_fsdp(value):
        return lax.ppermute(value, "fsdp", [(0, 1), (1, 0)])

    def other_parts(weight):
        if pair:
            return [weight, swap_fsdp(weight)]
        return [lax.all_gather(weight, "fsdp", axis=0, tiled=True)]

    def split(values):
        if pair:
            return [
                lax.dynamic_slice_in_dim(values, here_fsdp * part, part, 1),
                lax.dynamic_slice_in_dim(values, (1 - here_fsdp) * part, part, 1),
            ]
        return [values]

    def join(pieces):
        if pair:
            first = here_fsdp == 0
            return jnp.concatenate(
                [jnp.where(first, pieces[0], pieces[1]), jnp.where(first, pieces[1], pieces[0])],
                axis=1,
            )
        return pieces[0]

    def into(values, weights):
        return sum(mm(x, w) for x, w in zip(split(values), weights))

    def back(values, weights):
        return join([mm_t(values, w) for w in weights])

    def my_features(values):
        return lax.dynamic_slice_in_dim(values, here_tp * width_tp, width_tp, values.ndim - 1)

    attn_w = (w_query, w_key, w_value, w_output)
    small = jnp.concatenate(
        [attn_gain[None], ffn_gain[None], w_router.T, jnp.zeros((2, part), BF)], axis=0
    )
    if pair:
        quarter = part // n_ctx
        own_quarter = jnp.concatenate(
            [lax.dynamic_slice_in_dim(w, here_ctx * quarter, quarter, 0) for w in attn_w], axis=1
        )
        other_quarter = swap_fsdp(own_quarter)
        other_small = swap_fsdp(small)
        small_full = join([small, other_small]).astype(F32)
    else:
        other_quarter = None
        small_full = lax.all_gather(small, "fsdp", axis=1, tiled=True).astype(F32)
    inputs_full, up_mine, down_mine = gather_tp(hidden_in, (w_up, w_down), n_tp)
    gate_w = other_parts(lax.dynamic_index_in_dim(w_gate, here_ctx, 0, False))
    up_w = other_parts(up_mine)
    down_w = other_parts(down_mine)
    small_here = my_features(small_full)
    gain_one_here = jnp.broadcast_to(small_here[0:1], small_here.shape)
    gain_two_here = jnp.broadcast_to(small_here[1:2], small_here.shape)
    nothing = [(0, 8 - experts), (0, 0)]
    router_here = jnp.pad(small_here[2 : 2 + experts], nothing)

    relative = (jnp.arange(experts, dtype=jnp.int32) + here_ctx) % experts
    numbers = jnp.arange(8, dtype=jnp.int32)
    onehot = (routes.T[:, None, :] == numbers[None, :, None]).astype(F32)
    named = (routes.T[:, None, :] == relative[None, :, None]).astype(F32)
    names = jnp.pad(named, [(0, 0)] + nothing)
    chosen = jnp.sum(named, axis=0)
    earlier = jnp.triu(jnp.ones((rows_here, rows_here), BF), 1)
    slot_of = mm(chosen.astype(BF), earlier).astype(jnp.int32)
    slots = jnp.arange(CAP, dtype=jnp.int32)
    picks = (slot_of[:, None, :] == slots[None, :, None]) & (chosen[:, None, :] > 0)
    picks = picks.astype(BF).reshape(experts * CAP, rows_here)

    gathered = first_norm(
        inputs_full, out_grad, small_full, attn_w, other_quarter, n_tp, n_ctx
    )
    normed_one, scale_one, grad_full = gathered[:3]
    if pair:
        qkv_w, output_w = gathered[3:]
    else:
        qkv_w, output_w = (
            lax.all_gather(w, "fsdp", axis=0, tiled=True)
            for w in (jnp.concatenate(attn_w[:3], axis=1), w_output)
        )
    positions = here_ctx * rows_here + jnp.arange(rows_here, dtype=jnp.int32)
    cosine, sine = rotary_tables(positions)
    attended, query, kv = attention_forward(mm(normed_one, qkv_w), cosine, sine, n_ctx)
    resid, scale_two, normed_two, grad_rows, token_rows, slot_gates, gates, mix = second_norm(
        mm_t(attended, output_w).astype(BF),
        hidden_in,
        gain_two_here,
        mm(picks, grad_full).astype(BF),
        picks,
        router_here,
        onehot,
        names,
        n_tp,
        n_ctx,
    )
    gate_rows = slot_gates[:, 0, :CAP].reshape(experts * CAP, 1)

    to_gate, to_up, hidden_act = expert_acts(token_rows, gate_w, up_w, n_fsdp)
    d_result = (gate_rows * grad_rows.astype(F32)).astype(BF)

    def away(left, right):
        value = t_mm(split(left)[1], right).astype(BF)
        return value, swap_fsdp(value)

    def payload_of(left, right, come):
        if pair:
            return Payload(n_ctx, product=(left, right, come))
        return Payload(
            n_ctx,
            rows=lax.psum_scatter(
                t_mm(left, right).astype(BF), "fsdp", scatter_dimension=0, tiled=True
            ),
        )

    def came_and_own(outs, payload):
        if pair:
            return tuple(outs)
        own = lax.dynamic_slice_in_dim(payload.inputs[0], here_ctx * payload.cut, payload.cut, 0)
        return outs[0], own

    down_come = gate_come = up_come = None
    if pair:
        down_away, down_come = away(d_result, hidden_act)
        grad_rows = after(grad_rows, down_away)
    d_hidden = into(grad_rows, down_w)
    gate_dot = jnp.sum(hidden_act.astype(F32) * d_hidden, axis=-1).reshape(experts, CAP)
    gate_dot = jnp.broadcast_to(
        jnp.pad(gate_dot, [(0, 0), (0, rows_here - CAP)])[:, None, :], (experts, 8, rows_here)
    )
    d_hidden = gate_rows * d_hidden
    d_gate_act = (d_hidden * to_gate).astype(BF)
    d_up_act = (d_hidden * to_up).astype(BF)
    if pair:
        gate_away, gate_come = away(token_rows, d_gate_act)

    acts = (d_gate_act, d_up_act, hidden_act)
    if pair:
        acts = lax.optimization_barrier((*acts, gate_away))[:3]
    d_resid, d_attn_here, gain_two_part, d_logits, made, *up_away = second_norm_back(
        acts,
        (gate_w, up_w, down_w),
        token_rows,
        gate_dot,
        picks,
        gates,
        onehot,
        names,
        router_here,
        resid,
        scale_two,
        gain_two_here,
        out_grad,
        n_tp,
        n_ctx,
    )
    if pair:
        up_come = swap_fsdp(up_away[0])

    payload = payload_of(d_result, hidden_act, down_come)
    early = (RowSums(made, 0, CAP, n_tp), made)
    d_attn, d_qkv, made_early, *outs = attention_backward(
        d_attn_here, output_w, query, kv, cosine, -sine, early, payload, n_tp, n_ctx
    )
    grad_down = came_and_own(outs, payload)
    payload = payload_of(token_rows, d_gate_act, gate_come)
    in_grad, gain_one_part, *outs = first_norm_back(
        d_qkv, qkv_w, hidden_in, scale_one, gain_one_here, d_resid, payload, n_tp, n_ctx
    )
    grad_gate = came_and_own(outs, payload)
    payload = payload_of(token_rows, d_up_act, up_come)

    small_part = jnp.concatenate(
        [
            gain_one_part[:1],
            gain_two_part[:1],
            mm(d_logits[:experts].astype(BF), my_features(normed_two)),
            jnp.zeros((6 - experts, width_tp), F32),
        ],
        axis=0,
    )
    written = write_out([grad_gate, grad_down], None, (), n_ctx)
    if pair:
        small_part = after(small_part, *written)
    grad_gate, grad_down = written
    experts_out = ExpertsOut(made, (made_early,), picks, mix, resid, n_tp, n_ctx)
    if pair:
        grad_attn, small_grad, block_out, *outs = weight_grads(
            [(d_attn, attended), (normed_one, d_qkv)],
            [(0, 0, heads_width), (1, 0, 2 * heads_width), (1, 2 * heads_width, heads_width)],
            small_part,
            payload,
            experts_out,
            n_tp,
            n_ctx,
        )
    else:
        grad_attn = jnp.concatenate([t_mm(d_attn, attended), t_mm(normed_one, d_qkv)], axis=1)
        scatter = partial(
            lax.psum_scatter, axis_name=("fsdp", "ctx"), scatter_dimension=0, tiled=True
        )
        grad_attn = scatter(grad_attn.astype(BF)).astype(F32)
        small_grad = lax.all_gather(small_part, "tp", axis=1, tiled=True)
        small_grad = scatter(small_grad.T).T
        block_out, *outs = experts_back(experts_out, payload, n_tp, n_ctx)
    grad_up = came_and_own(outs, payload)
    grad_up, block_out, in_grad, grad_output, grad_query, grad_key, grad_value = write_out(
        [grad_up], grad_attn, (block_out, in_grad), n_ctx
    )
    return (
        block_out,
        in_grad,
        small_grad[0],
        grad_query,
        grad_key,
        grad_value,
        grad_output,
        small_grad[1],
        small_grad[2 : 2 + experts].T,
        grad_gate,
        grad_up,
        grad_down,
    )


def solution(mesh):
    rows = ("fsdp", "ctx")
    placed = (
        P(rows, "tp"),
        P(rows, "tp"),
        P("fsdp"),
        P("fsdp", "tp"),
        P("fsdp", "tp"),
        P("fsdp", "tp"),
        P("fsdp", "tp"),
        P("fsdp"),
        P("fsdp", None),
        P(None, "fsdp", "tp"),
        P(None, "fsdp", "tp"),
        P(None, "fsdp", "tp"),
        P(rows, None),
    )
    return jax.shard_map(
        shards,
        mesh=mesh,
        in_specs=placed,
        out_specs=(
            P(rows, "tp"),
            P(rows, "tp"),
            P(rows),
            P(rows, "tp"),
            P(rows, "tp"),
            P(rows, "tp"),
            P(rows, "tp"),
            P(rows),
            P(rows, None),
            P(None, rows, "tp"),
            P(None, rows, "tp"),
            P(None, rows, "tp"),
        ),
        check_vma=False,
    )
```

```python
from functools import partial
import math

import jax
import jax.numpy as jnp
from jax import lax
from jax.experimental import pallas as pl
from jax.experimental.pallas import tpu as pltpu
from jax.sharding import PartitionSpec as P

HD = 128
CAP = 160


EPS = 1e-05
THETA = 10000.0
NEG = -1e30
BF = jnp.bfloat16
F32 = jnp.float32


def mm(left, right):
    return jnp.dot(left, right, preferred_element_type=F32)


def mm_t(left, right):
    return lax.dot_general(left, right, (((1,), (1,)), ((), ())), preferred_element_type=F32)


def t_mm(left, right):
    return lax.dot_general(left, right, (((0,), (0,)), ((), ())), preferred_element_type=F32)


def rotary_tables(positions):
    half_size = HD // 2
    frequency = THETA ** (-(jnp.arange(half_size, dtype=F32) * 2.0 / HD))
    angles = positions.astype(F32)[:, None] * frequency[None, :]
    cosine, sine = jnp.cos(angles), jnp.sin(angles)
    return jnp.concatenate([cosine, cosine], axis=1), jnp.concatenate([-sine, sine], axis=1)


MESH = pl.DeviceIdType.MESH
VM = pl.BlockSpec(memory_space=pltpu.VMEM)
DMA = pltpu.SemaphoreType.DMA


def peer(axis, n, k):
    return lax.rem(lax.axis_index(axis) + k, n)


def greet(groups):
    barrier = pltpu.get_barrier_semaphore()
    for axis, n in groups:
        for k in range(1, n):
            pl.semaphore_signal(
                barrier, inc=1, device_id={axis: peer(axis, n, k)}, device_id_type=MESH
            )
    pl.semaphore_wait(barrier, sum(n - 1 for _, n in groups))


def described(source, target, sems, i, to):
    return pltpu.make_async_remote_copy(
        src_ref=source,
        dst_ref=target,
        send_sem=sems[0].at[i],
        recv_sem=sems[1].at[i],
        device_id=to,
        device_id_type=MESH,
    )


def remote(source, target, sems, i, to):
    copy = described(source, target, sems, i, to)
    copy.start()
    return copy


def send(source, target, axis, n, k, sems):
    return remote(source, target, sems, k - 1, {axis: peer(axis, n, k)})


def columns(n, size):
    return pl.ds(pl.multiple_of(n * size, 128), size)


def stretch(n, size):
    return pl.ds(pl.multiple_of(n * size, 16), size)


def gather_columns(own, full, axis, n, sems):
    size = own.shape[1]
    place = full.at[:, columns(lax.axis_index(axis), size)]
    copies = [send(own, place, axis, n, k, sems) for k in range(1, n)]
    place[...] = own[...]
    return copies


def scatter_columns(part, slots, axis, n, sems):
    size = slots.shape[2]
    return [
        send(part.at[:, columns(peer(axis, n, k), size)], slots.at[k - 1], axis, n, k, sems)
        for k in range(1, n)
    ]


def finish(copies):
    for copy in copies:
        copy.wait()


class Payload:

    def __init__(self, n_ctx, rows=None, product=None):
        self.n_ctx = n_ctx
        self.product = product is not None
        self.inputs = list(product) if self.product else [rows]
        last = self.inputs[-1]
        self.rows, self.hidden = last.shape
        self.cut = self.rows // n_ctx
        self.outs = [shape((n_ctx - 1, self.cut, self.hidden), BF)]
        self.scratch = pair_of_sems(n_ctx)
        if self.product:
            self.outs.append(shape((self.cut, self.hidden), BF))
            self.scratch += [
                pltpu.VMEM((self.rows, self.hidden), BF),
                pltpu.VMEM((self.rows, self.hidden), BF),
                DMA,
            ]

    def take(self, ins, outs, scratch):
        self.ins, self.out_refs, self.held = ins, outs, scratch

    def load(self):
        if self.product:
            pltpu.make_async_copy(self.ins[2], self.held[2], self.held[4]).start()

    def copy(self, k):
        to = peer("ctx", self.n_ctx, k)
        source = self.held[3] if self.product else self.ins[0]
        return described(
            source.at[stretch(to, self.cut), :], self.out_refs[0].at[k - 1],
            self.held[0:2], k - 1, {"ctx": to},
        )

    def go(self, first=0, last=4):
        n_ctx, cut = self.n_ctx, self.cut
        if not self.product:
            for j in range(first, last):
                if (j + 2) % n_ctx:
                    self.copy((j + 2) % n_ctx).start()
            return
        left, right, other = self.ins
        if first == 0:
            pltpu.make_async_copy(other, self.held[2], self.held[4]).wait()
        base = lax.axis_index("fsdp") * self.rows

        @pl.loop(first, last)
        def _(j):
            k = lax.rem(j + 2, n_ctx)
            to = peer("ctx", n_ctx, k)
            value = t_mm(left[:, pl.ds(pl.multiple_of(base + to * cut, 128), cut)], right[...])
            value = value + self.held[2][stretch(to, cut), :].astype(F32)
            self.held[3][stretch(to, cut), :] = value.astype(BF)

            @pl.when(j != n_ctx - 2)
            def _():
                self.copy(k).start()

    def wait(self):
        if self.product:
            self.out_refs[1][...] = self.held[3][stretch(lax.axis_index("ctx"), self.cut), :]
        for k in range(1, self.n_ctx):
            self.copy(k).wait()


class RowSums:

    def __init__(self, made, first, count, n_tp):
        self.n_tp, self.first = n_tp, first
        self.shape = (count, made.shape[1] // n_tp)
        self.scratch = [
            pltpu.VMEM((n_tp - 1, *self.shape), BF),
            pltpu.VMEM(self.shape, BF),
            DMA,
        ] + pair_of_sems(n_tp)

    def take(self, made, scratch):
        self.made, self.held = made, scratch

    def rows(self, rank):
        return self.made.at[pl.ds(self.first, self.shape[0]), columns(rank, self.shape[1])]

    def mine(self):
        return pltpu.make_async_copy(
            self.rows(lax.axis_index("tp")), self.held[1], self.held[2]
        )

    def start(self):
        self.mine().start()
        n = self.n_tp
        self.copies = [
            send(self.rows(peer("tp", n, k)), self.held[0].at[k - 1], "tp", n, k, self.held[3:5])
            for k in range(1, n)
        ]

    def total(self):
        self.mine().wait()
        finish(self.copies)
        value = self.held[1][...].astype(F32)
        for k in range(1, self.n_tp):
            value = value + self.held[0][k - 1].astype(F32)
        return value


def quad():
    here = lax.axis_index("ctx")
    return here, here + 1 - 2 * lax.rem(here, 2), lax.rem(here + 2, 4)


def gather_square(own, places, sems, between, local=None):
    cuts = own.shape[1] // 512
    here, beside, across = quad()
    first, second, third = [], [], []
    for i in range(cuts):
        piece = own.at[:, pl.ds(i * 512, 512)]
        first.append(remote(piece, places(here, i), sems, 3 * i, {"ctx": across}))
        second.append(remote(piece, places(here, i), sems, 3 * i + 1, {"ctx": beside}))
        if local is None:
            places(here, i)[...] = piece[...]
        else:
            pltpu.make_async_copy(piece, places(here, i), local.at[i]).start()
    between()
    for i in range(cuts):
        first[i].wait()
        third.append(
            remote(places(across, i), places(across, i), sems, 3 * i + 2, {"ctx": beside})
        )
    finish(second)
    finish(third)
    if local is not None:
        for i in range(cuts):
            piece = own.at[:, pl.ds(i * 512, 512)]
            pltpu.make_async_copy(piece, places(here, i), local.at[i]).wait()


def row_sums(values):
    ones = jnp.ones((8, values.shape[1]), F32)
    return lax.dot_general(
        ones,
        values,
        (((1,), (1,)), ((), ())),
        precision=lax.Precision.HIGHEST,
        preferred_element_type=F32,
    )


def as_column(rows, weight):
    return lax.dot_general(
        rows,
        weight,
        (((0,), (0,)), ((), ())),
        precision=lax.Precision.HIGHEST,
        preferred_element_type=F32,
    )


def eighth():
    return jnp.full((8, 128), 0.125, F32)


def total_over(sums, mine, slots, axis, n, sems):
    mine[...] = sums
    copies = [send(mine, slots.at[k - 1], axis, n, k, sems) for k in range(1, n)]
    finish(copies)
    total = sums
    for k in range(1, n):
        total = total + slots[k - 1]
    return total


def call(kernel, out_shape, inputs, scratch, collective, name, left=()):
    anywhere = pl.BlockSpec(memory_space=pl.ANY)
    outs = out_shape if isinstance(out_shape, tuple) else (out_shape,)
    specs = [anywhere if i - len(outs) in left else VM for i in range(len(outs))]
    return pl.pallas_call(
        kernel,
        out_shape=out_shape,
        in_specs=[anywhere if i in left else VM for i in range(len(inputs))],
        out_specs=tuple(specs) if isinstance(out_shape, tuple) else specs[0],
        scratch_shapes=scratch,
        compiler_params=pltpu.CompilerParams(collective_id=collective, has_side_effects=True),
        cost_estimate=pl.CostEstimate(flops=0, bytes_accessed=0, transcendentals=0),
        name=name,
    )(*inputs)


def shape(dims, dtype):
    return jax.ShapeDtypeStruct(dims, dtype)


def pair_of_sems(n):
    return [DMA((n,)), DMA((n,))]


def gather_tp(value, stacks, n_tp):
    rows, size = value.shape
    many = len(stacks)
    member = stacks[0].shape[1:]

    def kernel(own, *refs):
        stk, full, outs = refs[:many], refs[many], refs[many + 1 : 2 * many + 1]
        held, loads, stores = refs[2 * many + 1 : 2 * many + 4]
        sems = refs[2 * many + 4 :]
        here = lax.axis_index("ctx")
        into = [
            pltpu.make_async_copy(stk[i].at[here], held.at[i], loads.at[i]) for i in range(many)
        ]
        away = [pltpu.make_async_copy(held.at[i], outs[i], stores.at[i]) for i in range(many)]
        for copy in into:
            copy.start()
        greet([("tp", n_tp)])
        copies = gather_columns(own, full, "tp", n_tp, sems)
        for i in range(many):
            into[i].wait()
            away[i].start()
        finish(copies)
        finish(away)

    return call(
        kernel,
        (
            shape((rows, size * n_tp), value.dtype),
            *(shape(member, stack.dtype) for stack in stacks),
        ),
        (value, *stacks),
        [pltpu.VMEM((many, *member), BF), DMA((many,)), DMA((many,))] + pair_of_sems(n_tp),
        1,
        "gather_tp",
        left=tuple(range(1, many + 1)) + tuple(range(-many, 0)),
    )


def first_norm(full, grad, gain, weights, quarter, n_tp, n_ctx):
    rows, width = full.shape
    with_quarter = quarter is not None

    def kernel(*refs):
        hid, grd, gn = refs[:3]
        refs = refs[3:]
        if with_quarter:
            wgts, refs = refs[: len(weights)], refs[len(weights) :]
            qrt, out, scale, grd_full, many_full, last_full, held, local, loads, stores = refs[:10]
            sems = refs[10:]
            half, inner = wgts[0].shape
            last = len(wgts) - 1
            mine = lax.axis_index("fsdp")

            def target(i, first_row, count):
                at = pl.ds(pl.multiple_of(first_row, 16), count)
                if i == last:
                    return last_full.at[at, :]
                return many_full.at[at, pl.ds(i * inner, inner)]

            into = [
                pltpu.make_async_copy(wgts[i], held.at[i], loads.at[i]) for i in range(len(wgts))
            ]
            away = [
                pltpu.make_async_copy(held.at[i], target(i, mine * half, half), stores.at[i])
                for i in range(len(wgts))
            ]
            for copy in into:
                copy.start()
            greet([("tp", n_tp), ("ctx", n_ctx)])
        else:
            out, scale, grd_full = refs[:3]
            sems = refs[3:]
            greet([("tp", n_tp)])
        grads = gather_columns(grd, grd_full, "tp", n_tp, sems[0:2])

        def norm():
            values = hid[...].astype(F32)
            mean = jnp.sum(values * values, axis=-1, keepdims=True) * (1.0 / width)
            factor = lax.rsqrt(mean + EPS)
            scale[...] = jnp.broadcast_to(factor, scale.shape)
            out[...] = (values * factor * gn[0:1, :]).astype(BF)

        if with_quarter:
            count = qrt.shape[0]

            def work():
                for i in range(len(wgts)):
                    into[i].wait()
                    away[i].start()
                norm()

            def places(rank, i):
                return target(i, (1 - mine) * half + rank * count, count)

            gather_square(qrt, places, sems[2:4], work, local)
            finish(away)
        else:
            norm()
        finish(grads)

    outs = [shape((rows, width), BF), shape((rows, 128), F32), shape((rows, width), BF)]
    inputs = [full, grad, gain]
    scratch, left = [], ()
    if with_quarter:
        half, inner = weights[0].shape
        many = len(weights)
        assert inner == 512
        outs.append(shape((2 * half, (many - 1) * inner), BF))
        outs.append(shape((2 * half, inner), BF))
        inputs += [*weights, quarter]
        scratch = [pltpu.VMEM((many, half, inner), BF), DMA((many,)), DMA((many,)), DMA((many,))]
        left = tuple(range(3, 3 + many)) + (-2, -1)
    return call(
        kernel,
        tuple(outs),
        inputs,
        scratch + pair_of_sems(n_tp) + pair_of_sems(12),
        7,
        "first_norm",
        left=left,
    )


def turn(values, cosine, sine):
    return values * cosine + pltpu.roll(values, HD // 2, axis=1) * sine


def softmax_rows(query, key, first_row):
    scores = mm_t(query, key) * (1.0 / math.sqrt(HD))
    rows = first_row + lax.broadcasted_iota(jnp.int32, scores.shape, 0)
    cols = lax.broadcasted_iota(jnp.int32, scores.shape, 1)
    scores = jnp.where(cols <= rows, scores, NEG)
    top = jnp.max(scores, axis=-1, keepdims=True)
    weights = jnp.exp(scores - top)
    return weights / jnp.sum(weights, axis=-1, keepdims=True)


def attention_forward(qkv, cosine, sine, n_ctx):
    rows = qkv.shape[0]
    width = qkv.shape[1] // 3
    heads = width // HD

    def kernel(prj, cs, sn, out, qry, full, own, *sems):
        greet([("ctx", n_ctx)])
        here = lax.axis_index("ctx")

        @pl.loop(0, heads)
        def _(h):
            own[:, columns(h, HD)] = turn(
                prj[:, columns(h + heads, HD)], cs[...], sn[...]
            ).astype(BF)
            own[:, columns(h + heads, HD)] = prj[:, columns(h + 2 * heads, HD)].astype(BF)

        def queries():
            @pl.loop(0, heads)
            def _(h):
                qry[:, columns(h, HD)] = turn(prj[:, columns(h, HD)], cs[...], sn[...]).astype(BF)

        def places(rank, i):
            return full.at[stretch(rank, rows), pl.ds(i * 512, 512)]

        gather_square(own, places, sems, queries)

        @pl.loop(0, heads)
        def _(h):
            probs = softmax_rows(qry[:, columns(h, HD)], full[:, columns(h, HD)], here * rows)
            out[:, columns(h, HD)] = mm(
                probs.astype(BF), full[:, columns(h + heads, HD)]
            ).astype(BF)

    return call(
        kernel,
        (
            shape((rows, width), BF),
            shape((rows, width), BF),
            shape((rows * n_ctx, 2 * width), BF),
        ),
        (qkv, cosine, sine),
        [pltpu.VMEM((rows, 2 * width), BF)] + pair_of_sems(6 * width // 512),
        2,
        "attention_forward",
    )


def second_norm(part, hidden, gain, slabs, picks, router, onehot, names, n_tp, n_ctx):
    rows, size = hidden.shape
    width = size * n_tp
    experts = n_ctx

    def kernel(
        prt, hid, gn, slb, pck, rtr, one, nms,
        resid, scale, out, moved, tokens, slot_gates, gates, mix,
        slots, mine, sums, mine_two, sums_two, low, sent, own_gates, *sems
    ):
        greet([("tp", n_tp), ("ctx", n_ctx)])
        here = lax.axis_index("tp")
        copies = scatter_columns(prt, slots, "tp", n_tp, sems[0:2])
        others = [
            send(
                slb.at[pl.ds(k * CAP, CAP)], moved.at[pl.ds(k * CAP, CAP)],
                "ctx", n_ctx, k, sems[6:8],
            )
            for k in range(1, n_ctx)
        ]
        moved[0:CAP] = slb[0:CAP]
        total = prt[:, columns(here, size)].astype(F32)
        finish(copies)
        for k in range(1, n_tp):
            total = total + slots[k - 1].astype(F32)
        total = hid[...].astype(F32) + total
        resid[...] = total
        square = total_over(row_sums(total * total), mine, sums, "tp", n_tp, sems[2:4])
        factor = lax.rsqrt(as_column(square, eighth()) * (1.0 / width) + EPS)
        scale[...] = factor
        low[...] = (resid[...] * factor[:, 0:1] * gn[0:1, :]).astype(BF)
        partial_logits = mm_t(rtr[...].astype(BF), low[...])
        mine_two[...] = partial_logits
        logit_copies = [
            send(mine_two, sums_two.at[k - 1], "tp", n_tp, k, sems[12:14]) for k in range(1, n_tp)
        ]
        gather_columns(low, out, "tp", n_tp, sems[4:6])

        def route():
            finish(logit_copies)
            logits = partial_logits
            for k in range(1, n_tp):
                logits = logits + sums_two[k - 1]
            named = [jnp.sum(one[j] * logits, axis=0, keepdims=True) for j in range(2)]
            top = jnp.maximum(named[0], named[1])
            powers = [jnp.exp(value - top) for value in named]
            both = powers[0] + powers[1]
            gate = [value / both for value in powers]
            mixed = gate[0] * nms[0] + gate[1] * nms[1]
            mix[...] = mixed
            order = lax.broadcasted_iota(jnp.int32, (8, rows), 0)
            gates[...] = jnp.where(order == 0, gate[0], jnp.where(order == 1, gate[1], 0.0))
            own_gates[...] = jnp.zeros(own_gates.shape, F32)
            for k in range(experts):
                own_gates[k, :, 0:CAP] = lax.dot_general(
                    jnp.broadcast_to(mixed[k : k + 1], (8, rows)),
                    pck[k * CAP : (k + 1) * CAP].astype(F32),
                    (((1,), (1,)), ((), ())),
                    precision=lax.Precision.HIGHEST,
                    preferred_element_type=F32,
                )
            slot_gates[0] = own_gates[0]
            for k in range(1, n_ctx):
                others.append(
                    send(own_gates.at[k], slot_gates.at[k], "ctx", n_ctx, k, sems[10:12])
                )


        def slab(k, step):
            at = columns(peer("tp", n_tp, n_tp - step), size)
            return described(
                sent.at[step, pl.ds(k * CAP, CAP)], tokens.at[pl.ds(k * CAP, CAP), at],
                sems[8:10], step * n_ctx + k, {"ctx": peer("ctx", n_ctx, k)},
            )

        def dispatch(step, block):
            sent[step] = mm(pck[...], block).astype(BF)
            tokens[0:CAP, columns(peer("tp", n_tp, n_tp - step), size)] = sent[step, 0:CAP]
            for k in (2, 3, 1):
                slab(k, step).start()

        route()

        @pl.loop(0, n_tp)
        def _(step):
            @pl.when(step > 0)
            def _():
                described(
                    low, out.at[:, columns(here, size)], sems[4:6], step - 1,
                    {"tp": peer("tp", n_tp, step)},
                ).wait()

            dispatch(step, out[:, columns(peer("tp", n_tp, n_tp - step), size)])

        for step in range(n_tp):
            for k in (2, 3, 1):
                slab(k, step).wait()
        finish(others)

    return call(
        kernel,
        (
            shape((rows, size), F32),
            shape((rows, 128), F32),
            shape((rows, width), BF),
            shape(slabs.shape, BF),
            shape(slabs.shape, BF),
            shape((experts, 8, rows), F32),
            shape((8, rows), F32),
            shape((8, rows), F32),
        ),
        (part, hidden, gain, slabs, picks, router, onehot, names),
        [
            pltpu.VMEM((n_tp - 1, rows, size), BF),
            pltpu.VMEM((8, rows), F32),
            pltpu.VMEM((n_tp - 1, 8, rows), F32),
            pltpu.VMEM((8, rows), F32),
            pltpu.VMEM((n_tp - 1, 8, rows), F32),
            pltpu.VMEM((rows, size), BF),
            pltpu.VMEM((n_tp, experts * CAP, size), BF),
            pltpu.VMEM((experts, 8, rows), F32),
        ]
        + pair_of_sems(n_tp) * 3
        + pair_of_sems(n_ctx)
        + pair_of_sems(n_tp * n_ctx)
        + pair_of_sems(n_ctx)
        + pair_of_sems(n_tp),
        3,
        "second_norm",
    )


def expert_acts(tokens, gate_w, up_w, n_fsdp):
    rows, width = tokens.shape
    hidden = gate_w[0].shape[1]
    count = len(gate_w)
    part = gate_w[0].shape[0]
    chunk = 256
    per = part // chunk
    steps = count * per
    pair = count == 2

    def kernel(tok, *refs):
        wgt = [refs[:count], refs[count : 2 * count]]
        to_gate, to_up, hid, buffer, loads = refs[2 * count :]
        first = lax.axis_index("fsdp") if pair else 0

        def load(step):
            slot = lax.rem(step, 2)
            at = stretch(lax.rem(step, per), chunk)
            for lane in range(2):
                for i in range(count):

                    @pl.when(step // per == i)
                    def _():
                        pltpu.make_async_copy(
                            wgt[lane][i].at[at], buffer.at[slot, lane], loads.at[slot, lane]
                        ).start()

        load(0)
        to_gate[...] = jnp.zeros_like(to_gate)
        to_up[...] = jnp.zeros_like(to_up)

        @pl.loop(0, steps)
        def _(step):
            slot = lax.rem(step, 2)
            for lane in range(2):
                pltpu.make_async_copy(
                    wgt[lane][0].at[pl.ds(0, chunk)], buffer.at[slot, lane], loads.at[slot, lane]
                ).wait()

            @pl.when(step + 1 < steps)
            def _():
                load(step + 1)

            which = lax.rem(first + step // per, count)
            column = which * part + lax.rem(step, per) * chunk
            values = tok[:, pl.ds(pl.multiple_of(column, 128), chunk)]
            to_gate[...] += mm(values, buffer[slot, 0])
            to_up[...] += mm(values, buffer[slot, 1])

        @pl.loop(0, rows // 32)
        def _(i):
            at = stretch(i, 32)
            a, b = to_gate[at, :], to_up[at, :]
            sigma = 1.0 / (1.0 + jnp.exp(-a))
            silu = a * sigma
            hid[at, :] = (silu * b).astype(BF)
            to_up[at, :] = silu
            to_gate[at, :] = b * sigma * (1.0 + a * (1.0 - sigma))

    anywhere = pl.BlockSpec(memory_space=pl.ANY)
    return pl.pallas_call(
        kernel,
        out_shape=(
            shape((rows, hidden), F32),
            shape((rows, hidden), F32),
            shape((rows, hidden), BF),
        ),
        in_specs=[VM] + [anywhere] * (2 * count),
        out_specs=(VM, VM, VM),
        scratch_shapes=[pltpu.VMEM((2, 2, chunk, hidden), BF), DMA((2, 2))],
        cost_estimate=pl.CostEstimate(flops=0, bytes_accessed=0, transcendentals=0),
        name="expert_acts",
    )(tokens, *gate_w, *up_w)


def second_norm_back(
    acts, weights, tokens, dots, picks, gates, onehot, names, router, resid, scale, gain, grad,
    n_tp, n_ctx,
):
    rows, size = resid.shape
    width = size * n_tp
    experts = n_ctx
    hidden = acts[0].shape[1]
    count = len(weights[0])
    part = weights[0][0].shape[0]

    def kernel(*refs):
        dga, dup, hid = refs[:3]
        wgt = [refs[3 + i * count : 3 + (i + 1) * count] for i in range(3)]
        refs = refs[3 + 3 * count :]
        tok, dts, pck, gts, one, nms, rtr, rsd, scl, gn, grd = refs[:11]
        d_resid, low, d_gain, d_logits, out_rows = refs[11:16]
        refs = refs[16:]
        if count == 2:
            up_away, up_held, up_sem = refs[:1] + refs[1:3]
            refs = refs[3:]
        (
            drw, eo, buffer, back, back_dots, parts, slots, mine, sums, mine_two, sums_two, loads,
            out_sem,
        ) = refs[:13]
        sems = refs[13:]
        here = lax.axis_index("tp")
        first = lax.axis_index("fsdp")

        def load(which, rank, slot, lane):
            feature = rank * size
            inside = pl.ds(pl.multiple_of(lax.rem(feature, part), 16), size)
            target = buffer.at[slot, lane]
            if count == 1:
                pltpu.make_async_copy(
                    wgt[which][0].at[inside], target, loads.at[slot, lane]
                ).start()
                return
            own = feature // part == first

            @pl.when(own)
            def _():
                pltpu.make_async_copy(
                    wgt[which][0].at[inside], target, loads.at[slot, lane]
                ).start()

            @pl.when(jnp.logical_not(own))
            def _():
                pltpu.make_async_copy(
                    wgt[which][1].at[inside], target, loads.at[slot, lane]
                ).start()

        def loaded(which, slot, lane):
            pltpu.make_async_copy(
                wgt[which][0].at[pl.ds(0, size)], buffer.at[slot, lane], loads.at[slot, lane]
            ).wait()

        load(0, peer("tp", n_tp, 1), 0, 0)
        load(1, peer("tp", n_tp, 1), 0, 1)
        greet([("tp", n_tp), ("ctx", n_ctx)])
        small = []
        for k in range(1, n_ctx):
            small.append(
                send(dts.at[k], back_dots.at[k - 1], "ctx", n_ctx, n_ctx - k, sems[0:2])
            )

        def slab(k, rank, step):
            at = columns(rank, size)
            return described(
                drw.at[pl.ds(k * CAP, CAP), at], back.at[k - 1, :, at],
                sems[2:4], step * n_ctx + k - 1, {"ctx": peer("ctx", n_ctx, n_ctx - k)},
            )

        @pl.loop(0, n_tp)
        def _(step):
            rank = peer("tp", n_tp, step + 1)
            slot = lax.rem(step, 2)
            loaded(0, slot, 0)
            loaded(1, slot, 1)

            @pl.when(step + 1 < n_tp)
            def _():
                load(0, peer("tp", n_tp, step + 2), 1 - slot, 0)
                load(1, peer("tp", n_tp, step + 2), 1 - slot, 1)

            drw[:, columns(rank, size)] = (
                mm_t(dga[...], buffer[slot, 0]) + mm_t(dup[...], buffer[slot, 1])
            ).astype(BF)
            for k in (2, 3, 1):
                slab(k, rank, step).start()

        def combined(step):
            rank = peer("tp", n_tp, step)
            at = columns(rank, size)
            for k in (2, 3, 1):
                slab(k, rank, step - 1).wait()
            block = t_mm(pck[0:CAP], drw[0:CAP, at])
            for k in range(1, experts):
                block = block + t_mm(pck[k * CAP : (k + 1) * CAP], back[k - 1, :, at])
            return block

        def give(step):
            return described(
                parts.at[step - 1], slots.at[step - 1], sems[6:8], step - 1,
                {"tp": peer("tp", n_tp, step)},
            )

        def pass_on(begin, end):
            @pl.loop(begin, end)
            def _(step):
                parts[step - 1] = combined(step).astype(BF)
                give(step).start()

        load(2, 0, 0, 0)
        finish(small)
        order = lax.broadcasted_iota(jnp.int32, (8, rows), 0)
        own = jnp.zeros((8, rows), F32)
        for k in range(experts):
            by_slot = dts[0] if k == 0 else back_dots[k - 1]
            by_row = lax.dot_general(
                by_slot[:, 0:CAP],
                pck[k * CAP : (k + 1) * CAP].astype(F32),
                (((1,), (0,)), ((), ())),
                precision=lax.Precision.HIGHEST,
                preferred_element_type=F32,
            )
            own = own + jnp.where(order == k, by_row, 0.0)
        mine[...] = own
        shared = [
            send(mine, sums.at[k - 1], "tp", n_tp, k, sems[4:6]) for k in range(1, n_tp)
        ]
        pass_on(1, n_tp - 1)


        @pl.loop(0, n_tp)
        def _(rank):
            slot = lax.rem(rank, 2)
            loaded(2, slot, 0)

            @pl.when(rank + 1 < n_tp)
            def _():
                load(2, rank + 1, 1 - slot, 0)

            eo[:, columns(rank, size)] = mm_t(hid[...], buffer[slot, 0]).astype(BF)

        pltpu.make_async_copy(eo, out_rows, out_sem).start()
        pass_on(n_tp - 1, n_tp)
        if count == 2:

            @pl.loop(0, part // 256)
            def _(i):
                at = pl.ds(pl.multiple_of((1 - first) * part + i * 256, 128), 256)
                up_held[stretch(i, 256), :] = t_mm(tok[:, at], dup[...]).astype(BF)

            pltpu.make_async_copy(up_held, up_away, up_sem).start()
        finish(shared)
        gate_grad = mine[...]
        for k in range(1, n_tp):
            gate_grad = gate_grad + sums[k - 1]
        both = [jnp.sum(nms[j] * gate_grad, axis=0, keepdims=True) for j in range(2)]
        gate = [gts[j : j + 1, :] for j in range(2)]
        mean = gate[0] * both[0] + gate[1] * both[1]
        logits = sum(gate[j] * (both[j] - mean) * one[j] for j in range(2))
        d_logits[...] = logits

        copies = [give(step) for step in range(1, n_tp)]
        total = combined(n_tp)
        total = total + lax.dot_general(
            logits.astype(BF),
            rtr[...].astype(BF),
            (((0,), (0,)), ((), ())),
            preferred_element_type=F32,
        )
        finish(copies)
        for k in range(1, n_tp):
            total = total + slots[k - 1].astype(F32)
        factor = scl[:, 0:1]
        unit = rsd[...] * factor
        d_gain[...] = jnp.broadcast_to(jnp.sum(total * unit, axis=0, keepdims=True), d_gain.shape)
        gained = total * gn[0:1, :]
        d_resid[...] = gained
        dot = total_over(row_sums(unit * gained), mine_two, sums_two, "tp", n_tp, sems[8:10])
        dot = as_column(dot, eighth())[:, 0:1] * (1.0 / width)
        result = grd[...].astype(F32) + factor * (d_resid[...] - rsd[...] * factor * dot)
        d_resid[...] = result
        low[...] = result.astype(BF)
        pltpu.make_async_copy(eo, out_rows, out_sem).wait()
        if count == 2:
            pltpu.make_async_copy(up_held, up_away, up_sem).wait()

    outs = [
        shape((rows, size), F32),
        shape((rows, size), BF),
        shape((8, size), F32),
        shape((8, rows), F32),
        shape((experts * CAP, width), BF),
    ]
    held = []
    if count == 2:
        outs.append(shape((part, hidden), BF))
        held = [pltpu.VMEM((part, hidden), BF), DMA]
    flat = [array for group in weights for array in group]
    return call(
        kernel,
        tuple(outs),
        (*acts, *flat, tokens, dots, picks, gates, onehot, names, router, resid, scale, gain, grad),
        held
        + [
            pltpu.VMEM((experts * CAP, width), BF),
            pltpu.VMEM((experts * CAP, width), BF),
            pltpu.VMEM((2, 2, size, hidden), BF),
            pltpu.VMEM((n_ctx - 1, CAP, width), BF),
            pltpu.VMEM((n_ctx - 1, 8, rows), F32),
            pltpu.VMEM((n_tp - 1, rows, size), BF),
            pltpu.VMEM((n_tp - 1, rows, size), BF),
            pltpu.VMEM((8, rows), F32),
            pltpu.VMEM((n_tp - 1, 8, rows), F32),
            pltpu.VMEM((8, rows), F32),
            pltpu.VMEM((n_tp - 1, 8, rows), F32),
            DMA((2, 2)),
            DMA,
        ]
        + pair_of_sems(n_ctx)
        + pair_of_sems(n_tp * n_ctx)
        + pair_of_sems(n_tp) * 3,
        4,
        "second_norm_back",
        left=tuple(range(3, 3 + 3 * count)) + ((-2, -1) if count == 2 else (-1,)),
    )


def attention_backward(
    low, output_w, query, kv, cosine, sine, sums, payload, n_tp, n_ctx
):
    rows, size = low.shape
    width = size * n_tp
    inner = query.shape[1]
    heads = inner // HD
    scale = 1.0 / math.sqrt(HD)

    half = heads // 2
    sums, sums_input = sums
    lane = 2 * half * HD

    def kernel(*refs):
        lw, wgt, qry, full, cs, sn, made = refs[:7]
        n_in, n_out = 7 + len(payload.inputs), len(payload.outs)
        d_attn, d_qkv, summed = refs[n_in : n_in + 3]
        scratch = refs[n_in + 3 + n_out :]
        dot, dqs, dkv, slots, last, both, total, kept = scratch[:8]
        sems = scratch[8:12]
        sums.take(made, scratch[12 : 12 + len(sums.scratch)])
        payload.take(
            refs[7:n_in], refs[n_in + 3 : n_in + 3 + n_out], scratch[12 + len(sums.scratch) :]
        )
        payload.load()
        greet([("tp", n_tp), ("ctx", n_ctx)])
        here, beside, across = quad()
        beyond = lax.rem(beside + 2, 4)
        copies = gather_columns(lw, d_attn, "tp", n_tp, sems[2:4])
        sums.start()
        payload.go()

        @pl.loop(0, heads)
        def _(h):
            at = columns(h, HD)
            kept[h] = softmax_rows(qry[:, at], full[:, at], here * rows)

        for step in range(n_tp):
            rank = peer("tp", n_tp, n_tp - step)
            weights = wgt[pl.ds(pl.multiple_of(rank * size, 16), size), :]
            if step:
                copies[step - 1].wait()
                total[...] += mm(d_attn[:, columns(rank, size)], weights)
            else:
                total[...] = mm(lw[...], weights)
        dot[...] = total[...].astype(BF)
        first, second, third = [], [], []
        for j in range(2):

            @pl.loop(0, half)
            def _(i):
                h = j * half + i
                at, at_v = columns(h, HD), columns(h + heads, HD)
                key_at = pl.ds(pl.multiple_of(j * lane + i * HD, 128), HD)
                value_at = pl.ds(pl.multiple_of(j * lane + (half + i) * HD, 128), HD)
                probs = kept[h]
                d_probs = mm_t(dot[:, at], full[:, at_v])
                delta = jnp.sum(probs * d_probs, axis=-1, keepdims=True)
                d_scores = (probs * (d_probs - delta)).astype(BF)
                dqs[:, at] = mm(d_scores, full[:, at]) * scale
                dkv[:, key_at] = (t_mm(d_scores, qry[:, at]) * scale).astype(BF)
                dkv[:, value_at] = t_mm(probs.astype(BF), dot[:, at]).astype(BF)

            at = pl.ds(j * lane, lane)
            first.append(
                remote(
                    dkv.at[stretch(beyond, rows), at], slots.at[0, :, at],
                    sems, 3 * j, {"ctx": beside},
                )
            )
            second.append(
                remote(
                    dkv.at[stretch(beside, rows), at], slots.at[1, :, at],
                    sems, 3 * j + 1, {"ctx": beside},
                )
            )
        for j in range(2):
            at = pl.ds(j * lane, lane)
            first[j].wait()
            both[:, at] = (
                dkv[stretch(across, rows), at].astype(F32) + slots[0, :, at].astype(F32)
            ).astype(BF)
            third.append(
                remote(both.at[:, at], last.at[:, at], sems, 3 * j + 2, {"ctx": across})
            )

        @pl.loop(0, heads)
        def _(h):
            d_qkv[:, columns(h, HD)] = turn(dqs[:, columns(h, HD)], cs[...], sn[...]).astype(BF)

        for j in range(2):
            second[j].wait()
            third[j].wait()

            @pl.loop(0, half)
            def _(i):
                h = j * half + i
                key_at = pl.ds(pl.multiple_of(j * lane + i * HD, 128), HD)
                value_at = pl.ds(pl.multiple_of(j * lane + (half + i) * HD, 128), HD)
                mine = stretch(here, rows)
                d_key = dkv[mine, key_at].astype(F32) + slots[1, :, key_at].astype(F32)
                d_key = d_key + last[:, key_at].astype(F32)
                d_qkv[:, columns(h + heads, HD)] = turn(d_key, cs[...], sn[...]).astype(BF)
                d_value = dkv[mine, value_at].astype(F32) + slots[1, :, value_at].astype(F32)
                d_value = d_value + last[:, value_at].astype(F32)
                d_qkv[:, columns(h + 2 * heads, HD)] = d_value.astype(BF)

        summed[...] = sums.total().astype(BF)
        payload.wait()

    return call(
        kernel,
        (
            shape((rows, width), BF),
            shape((rows, 3 * inner), BF),
            shape(sums.shape, BF),
            *payload.outs,
        ),
        (low, output_w, query, kv, cosine, sine, sums_input, *payload.inputs),
        [
            pltpu.VMEM((rows, inner), BF),
            pltpu.VMEM((rows, inner), F32),
            pltpu.VMEM((rows * n_ctx, 2 * inner), BF),
            pltpu.VMEM((2, rows, 2 * inner), BF),
            pltpu.VMEM((rows, 2 * inner), BF),
            pltpu.VMEM((rows, 2 * inner), BF),
            pltpu.VMEM((rows, inner), F32),
            pltpu.VMEM((heads, rows, rows * n_ctx), F32),
        ]
        + pair_of_sems(6)
        + pair_of_sems(n_tp)
        + sums.scratch
        + payload.scratch,
        5,
        "attention_backward",
        left=(6, 6 + len(payload.inputs), -len(payload.outs)),
    )


def first_norm_back(d_qkv, weights, hidden, scale, gain, d_resid, early, payload, n_tp, n_ctx):
    rows, size = hidden.shape
    width = size * n_tp

    def kernel(*refs):
        dpr, wgt, hid, scl, gn, dr, erl = refs[:7]
        n_in, n_out = 7 + len(payload.inputs), len(payload.outs)
        out, d_gain, returned = refs[n_in : n_in + 3]
        scratch = refs[n_in + 3 + n_out :]
        held, parts, slots, mine, sums, loads = scratch[:6]
        sems = scratch[6:10]
        payload.take(refs[7:n_in], refs[n_in + 3 : n_in + 3 + n_out], scratch[12:])

        def block(step):
            rank = peer("tp", n_tp, step)
            return pltpu.make_async_copy(
                wgt.at[stretch(rank, size), :], held.at[step - 1], loads.at[step - 1]
            )

        for step in range(1, n_tp + 1):
            block(step).start()
        payload.load()
        greet([("tp", n_tp), ("ctx", n_ctx)])
        given = [
            send(
                erl.at[pl.ds((k - 2) * CAP, CAP)], returned.at[k - 2],
                "ctx", n_ctx, n_ctx - k, scratch[10:12],
            )
            for k in range(2, n_ctx)
        ]

        def give(step):
            return described(
                parts.at[step - 1], slots.at[step - 1], sems[0:2], step - 1,
                {"tp": peer("tp", n_tp, step)},
            )

        @pl.loop(1, n_tp + 1)
        def _(step):
            block(step).wait()
            out[...] = mm_t(dpr[...], held[step - 1])

            @pl.when(step < n_tp)
            def _():
                parts[step - 1] = out[...].astype(BF)
                give(step).start()

        copies = [give(step) for step in range(1, n_tp)]
        payload.go()
        finish(copies)
        total = out[...]
        for k in range(1, n_tp):
            total = total + slots[k - 1].astype(F32)
        factor = scl[:, 0:1]
        unit = hid[...].astype(F32) * factor
        d_gain[...] = jnp.broadcast_to(jnp.sum(total * unit, axis=0, keepdims=True), d_gain.shape)
        gained = total * gn[0:1, :]
        out[...] = gained
        dot = total_over(row_sums(unit * gained), mine, sums, "tp", n_tp, sems[2:4])
        dot = as_column(dot, eighth())[:, 0:1] * (1.0 / width)
        unit = hid[...].astype(F32) * factor
        out[...] = dr[...] + factor * (out[...] - unit * dot)
        finish(given)
        payload.wait()

    return call(
        kernel,
        (
            shape((rows, size), F32),
            shape((8, size), F32),
            shape((n_ctx - 2, CAP, size), BF),
            *payload.outs,
        ),
        (d_qkv, weights, hidden, scale, gain, d_resid, early, *payload.inputs),
        [
            pltpu.VMEM((n_tp, size, d_qkv.shape[1]), BF),
            pltpu.VMEM((n_tp - 1, rows, size), BF),
            pltpu.VMEM((n_tp - 1, rows, size), BF),
            pltpu.VMEM((8, rows), F32),
            pltpu.VMEM((n_tp - 1, 8, rows), F32),
            DMA((n_tp,)),
        ]
        + pair_of_sems(n_tp) * 2
        + pair_of_sems(n_ctx)
        + payload.scratch,
        6,
        "first_norm_back",
        left=(1, 6 + len(payload.inputs), -len(payload.outs)),
    )


class ExpertsOut:

    def __init__(self, made, returned, picks, mix, resid, n_tp, n_ctx):
        self.n_ctx = n_ctx
        self.left = n_ctx - returned.shape[0]
        self.sums = RowSums(made, 0, self.left * CAP, n_tp)
        self.inputs = [made, returned, picks, mix, resid]
        self.size = resid.shape[1]
        self.out = shape(resid.shape, BF)
        self.scratch = [
            pltpu.VMEM(self.sums.shape, BF),
            pltpu.VMEM((self.left - 1, CAP, self.size), BF),
        ]
        self.scratch += pair_of_sems(n_ctx)
        self.scratch += [pltpu.VMEM((n_ctx, resid.shape[0], 128), F32)] + self.sums.scratch

    def take(self, ins, out, scratch):
        self.ins, self.out_ref, self.held = ins, out, scratch[:5]
        self.sums.take(ins[0], scratch[5:])

    def give_back(self):
        share, back = self.held[:2]
        share[...] = self.sums.total().astype(BF)
        n_ctx = self.n_ctx
        self.copies = [
            send(
                share.at[pl.ds(k * CAP, CAP)], back.at[k - 1],
                "ctx", n_ctx, n_ctx - k, self.held[2:4],
            )
            for k in range(1, self.left)
        ]

    def prepare(self):
        order = lax.broadcasted_iota(jnp.int32, (8, 128), 0)

        @pl.loop(0, self.n_ctx)
        def _(k):
            self.held[4][k] = as_column(self.ins[-2][...], jnp.where(order == k, 1.0, 0.0))

    def mix(self):
        returned, picks, mix, resid = self.ins[1:]
        share, back = self.held[:2]
        finish(self.copies)
        total = resid[...]
        for k in range(self.n_ctx):
            gate = self.held[4][k, :, 0:1]
            if k == 0:
                rows = share[0:CAP]
            elif k < self.left:
                rows = back[k - 1]
            else:
                rows = returned[k - self.left]
            total = total + gate * t_mm(picks[k * CAP : (k + 1) * CAP], rows)
        self.out_ref[...] = total.astype(BF)


def weight_grads(products, groups, small, payload, experts_out, n_tp, n_ctx):
    width = products[0][0].shape[1]
    places = 2 * n_ctx
    cut = width // places
    total_columns = sum(size for _, _, size in groups)
    flat = [array for pair in products for array in pair]
    inputs = [*flat, small, *experts_out.inputs, *payload.inputs]

    def kernel(*refs):
        factors, refs = refs[: len(flat)], refs[len(flat) :]
        sml, refs = refs[0], refs[1:]
        given, refs = refs[: len(experts_out.inputs)], refs[len(experts_out.inputs) :]
        paid, refs = refs[: len(payload.inputs)], refs[len(payload.inputs) :]
        out, small_out, block_out = refs[:3]
        paid_out, refs = refs[3 : 3 + len(payload.outs)], refs[3 + len(payload.outs) :]
        sml_full, sml_slots, refs = refs[0], refs[1], refs[2:]
        scratch, refs = refs[: 6 * len(groups)], refs[6 * len(groups) :]
        experts_out.take(given, block_out, refs[: len(experts_out.scratch)])
        refs = refs[len(experts_out.scratch) :]
        payload.take(paid, paid_out, refs[: len(payload.scratch)])
        sems = refs[len(payload.scratch) :]
        payload.load()
        barrier = pltpu.get_barrier_semaphore()
        here, beside, across = quad()
        beyond = lax.rem(beside + 2, 4)
        mine = lax.axis_index("fsdp")
        other = 1 - mine
        place = mine * n_ctx + here
        others = []
        for i in range(1, places):
            to = lax.rem(place + i, places)
            others.append((to, {"fsdp": to // n_ctx, "ctx": lax.rem(to, n_ctx)}))
        ahead = [{"tp": peer("tp", n_tp, k)} for k in range(1, n_tp)]
        for device in ahead + [device for _, device in others]:
            pl.semaphore_signal(barrier, inc=1, device_id=device, device_id_type=MESH)
        pl.semaphore_wait(barrier, n_tp - 1 + places - 1)
        gathers = gather_columns(sml, sml_full, "tp", n_tp, sems[0:2])
        experts_out.sums.start()
        moves = []

        def near(g):
            which, start, size = groups[g]
            prt, come = scratch[6 * g : 6 * g + 2]
            left, right = factors[2 * which : 2 * which + 2]

            @pl.loop(0, places)
            def _(i):
                prt[i] = t_mm(left[:, columns(i, cut)], right[:, start : start + size]).astype(BF)

            blocks = [(other, beyond), (other, beside), (mine, beyond), (mine, beside)]
            moves.append(
                [
                    remote(
                        prt.at[rank * n_ctx + column], come.at[i],
                        sems[4 + 6 * g : 6 + 6 * g], i, {"ctx": beside},
                    )
                    for i, (rank, column) in enumerate(blocks)
                ]
            )

        def chip(g, i, rank, column):
            prt, come = scratch[6 * g : 6 * g + 2]
            moves[g][i].wait()
            return prt[rank * n_ctx + column].astype(F32) + come[i].astype(F32)

        hops = []

        def hop(g):
            two, far = scratch[6 * g + 2 : 6 * g + 4]
            sent = []
            for i, column in enumerate((across, here)):
                two[i] = chip(g, i, other, column).astype(BF)
                sent.append(
                    remote(
                        two.at[i], far.at[i], sems[6 + 6 * g : 8 + 6 * g], i, {"fsdp": other}
                    )
                )
            hops.append(sent)

        payload.go()
        near(0)
        finish(gathers)
        totals = [
            remote(sml_full.at[:, columns(to, cut)], sml_slots.at[i], sems[2:4], i, device)
            for i, (to, device) in enumerate(others)
        ]
        hop(0)
        for g in range(1, len(groups)):
            near(g)
            hop(g)
        experts_out.prepare()
        lasts = []
        for g in range(len(groups)):
            far, one, last = scratch[6 * g + 3 : 6 * g + 6]
            value = chip(g, 2, mine, across)
            hops[g][0].wait()
            one[...] = (value + far[0].astype(F32)).astype(BF)
            lasts.append(
                remote(one, last, sems[8 + 6 * g : 10 + 6 * g], 0, {"ctx": across})
            )
            if g == 0:
                experts_out.give_back()
        finish(totals)
        sums = sml_full[:, columns(place, cut)]
        for i in range(places - 1):
            sums = sums + sml_slots[i]
        small_out[...] = sums
        start = 0
        for g, (_, _, size) in enumerate(groups):
            far = scratch[6 * g + 3]
            value = chip(g, 3, mine, here)
            hops[g][1].wait()
            value = value + far[1].astype(F32)
            out[:, start : start + size] = value
            start += size
        experts_out.mix()
        payload.wait()
        start = 0
        for g, (_, _, size) in enumerate(groups):
            lasts[g].wait()
            at = pl.ds(start, size)
            out[:, at] = out[:, at] + scratch[6 * g + 5][...].astype(F32)
            start += size

    buffers = [pltpu.VMEM((8, width), F32), pltpu.VMEM((places - 1, 8, cut), F32)]
    sems = pair_of_sems(n_tp) + pair_of_sems(places)
    for _, _, size in groups:
        buffers += [
            pltpu.VMEM((places, cut, size), BF),
            pltpu.VMEM((4, cut, size), BF),
            pltpu.VMEM((2, cut, size), BF),
            pltpu.VMEM((2, cut, size), BF),
            pltpu.VMEM((cut, size), BF),
            pltpu.VMEM((cut, size), BF),
        ]
        sems += pair_of_sems(4) + pair_of_sems(2) + pair_of_sems(1)
    return call(
        kernel,
        (
            shape((cut, total_columns), F32),
            shape((8, cut), F32),
            experts_out.out,
            *payload.outs,
        ),
        inputs,
        buffers + experts_out.scratch + payload.scratch + sems,
        10,
        "weight_grads",
        left=(
            len(flat) + 1,
            len(inputs) - 1,
            -len(payload.outs),
        ),
    )


def experts_back(experts_out, payload, n_tp, n_ctx):
    inputs = [*experts_out.inputs, *payload.inputs]
    given = len(experts_out.inputs)

    def kernel(*refs):
        ins, refs = refs[: len(inputs)], refs[len(inputs) :]
        outs, scratch = refs[: 1 + len(payload.outs)], refs[1 + len(payload.outs) :]
        experts_out.take(ins[:given], outs[0], scratch[: len(experts_out.scratch)])
        payload.take(ins[given:], outs[1:], scratch[len(experts_out.scratch) :])
        greet([("tp", n_tp), ("ctx", n_ctx)])
        experts_out.sums.start()
        payload.go()
        experts_out.prepare()
        experts_out.give_back()
        experts_out.mix()
        payload.wait()

    return call(
        kernel,
        (experts_out.out, *payload.outs),
        inputs,
        experts_out.scratch + payload.scratch,
        9,
        "experts_back",
        left=(0, len(inputs) - 1, -len(payload.outs)),
    )


def write_out(experts_grads, attn_grad, plain, n_ctx):
    _, rows, size = experts_grads[0][0].shape
    steps = max(1, rows // 32)
    tile = rows // steps
    many = len(experts_grads)
    plain = list(plain)
    blocks = []
    if attn_grad is not None:
        block = attn_grad.shape[1] // 4
        blocks = [shape((attn_grad.shape[0], block), F32)] * 4
        plain.append(attn_grad)

    def kernel(*refs):
        here = lax.axis_index("ctx")
        ins, outs = refs[: 2 * many + len(plain)], refs[2 * many + len(plain) :]
        for i in range(many):
            came, mine = ins[2 * i : 2 * i + 2]
            outs[i][here] = mine[...].astype(F32)
            for k in range(1, n_ctx):
                outs[i][lax.rem(here + n_ctx - k, n_ctx)] = came[k - 1].astype(F32)
        for i in range(len(plain) - (1 if blocks else 0)):
            outs[many + i][...] = ins[2 * many + i][...]
        for i in range(len(blocks)):
            outs[i - 4][...] = ins[-1][:, i * block : (i + 1) * block]

    def flat(array):
        return pl.BlockSpec((array.shape[0] // steps, array.shape[1]), lambda i: (i, 0))

    in_specs, out_specs, out_shape = [], [], []
    for _ in experts_grads:
        in_specs.append(pl.BlockSpec((n_ctx - 1, tile, size), lambda i: (0, i, 0)))
        in_specs.append(pl.BlockSpec((tile, size), lambda i: (i, 0)))
        out_specs.append(pl.BlockSpec((n_ctx, tile, size), lambda i: (0, i, 0)))
        out_shape.append(shape((n_ctx, rows, size), F32))
    for array in plain[: len(plain) - (1 if blocks else 0)] + blocks:
        out_specs.append(flat(array))
        out_shape.append(shape(array.shape, array.dtype))
    in_specs += [flat(array) for array in plain]
    inputs = [array for pair in experts_grads for array in pair] + plain
    return pl.pallas_call(
        kernel,
        grid=(steps,),
        in_specs=in_specs,
        out_specs=out_specs,
        out_shape=out_shape,
        cost_estimate=pl.CostEstimate(
            flops=0, bytes_accessed=6 * many * n_ctx * rows * size, transcendentals=0
        ),
        name="write_out",
    )(*inputs)


def after(value, *needed):
    return lax.optimization_barrier((value, *needed))[0]


def shards(
    hidden_in,
    out_grad,
    attn_gain,
    w_query,
    w_key,
    w_value,
    w_output,
    ffn_gain,
    w_router,
    w_gate,
    w_up,
    w_down,
    routes,
):
    rows_here, width_tp = hidden_in.shape
    here_tp = lax.axis_index("tp")
    here_ctx = lax.axis_index("ctx")
    here_fsdp = lax.axis_index("fsdp")
    n_fsdp = lax.axis_size("fsdp")
    n_ctx = lax.axis_size("ctx")
    n_tp = lax.axis_size("tp")
    experts = w_gate.shape[0]
    assert experts == n_ctx == 4
    width = width_tp * n_tp
    part = width // n_fsdp
    pair = n_fsdp == 2
    heads_width = w_query.shape[1]

    def swap_fsdp(value):
        return lax.ppermute(value, "fsdp", [(0, 1), (1, 0)])

    def other_parts(weight):
        if pair:
            return [weight, swap_fsdp(weight)]
        return [lax.all_gather(weight, "fsdp", axis=0, tiled=True)]

    def split(values):
        if pair:
            return [
                lax.dynamic_slice_in_dim(values, here_fsdp * part, part, 1),
                lax.dynamic_slice_in_dim(values, (1 - here_fsdp) * part, part, 1),
            ]
        return [values]

    def join(pieces):
        if pair:
            first = here_fsdp == 0
            return jnp.concatenate(
                [jnp.where(first, pieces[0], pieces[1]), jnp.where(first, pieces[1], pieces[0])],
                axis=1,
            )
        return pieces[0]

    def into(values, weights):
        return sum(mm(x, w) for x, w in zip(split(values), weights))

    def back(values, weights):
        return join([mm_t(values, w) for w in weights])

    def my_features(values):
        return lax.dynamic_slice_in_dim(values, here_tp * width_tp, width_tp, values.ndim - 1)

    attn_w = (w_query, w_key, w_value, w_output)
    small = jnp.concatenate(
        [attn_gain[None], ffn_gain[None], w_router.T, jnp.zeros((2, part), BF)], axis=0
    )
    if pair:
        quarter = part // n_ctx
        own_quarter = jnp.concatenate(
            [lax.dynamic_slice_in_dim(w, here_ctx * quarter, quarter, 0) for w in attn_w], axis=1
        )
        other_quarter = swap_fsdp(own_quarter)
        other_small = swap_fsdp(small)
        small_full = join([small, other_small]).astype(F32)
    else:
        other_quarter = None
        small_full = lax.all_gather(small, "fsdp", axis=1, tiled=True).astype(F32)
    inputs_full, up_mine, down_mine = gather_tp(hidden_in, (w_up, w_down), n_tp)
    gate_w = other_parts(lax.dynamic_index_in_dim(w_gate, here_ctx, 0, False))
    up_w = other_parts(up_mine)
    down_w = other_parts(down_mine)
    small_here = my_features(small_full)
    gain_one_here = jnp.broadcast_to(small_here[0:1], small_here.shape)
    gain_two_here = jnp.broadcast_to(small_here[1:2], small_here.shape)
    nothing = [(0, 8 - experts), (0, 0)]
    router_here = jnp.pad(small_here[2 : 2 + experts], nothing)

    relative = (jnp.arange(experts, dtype=jnp.int32) + here_ctx) % experts
    numbers = jnp.arange(8, dtype=jnp.int32)
    onehot = (routes.T[:, None, :] == numbers[None, :, None]).astype(F32)
    named = (routes.T[:, None, :] == relative[None, :, None]).astype(F32)
    names = jnp.pad(named, [(0, 0)] + nothing)
    chosen = jnp.sum(named, axis=0)
    earlier = jnp.triu(jnp.ones((rows_here, rows_here), BF), 1)
    slot_of = mm(chosen.astype(BF), earlier).astype(jnp.int32)
    slots = jnp.arange(CAP, dtype=jnp.int32)
    picks = (slot_of[:, None, :] == slots[None, :, None]) & (chosen[:, None, :] > 0)
    picks = picks.astype(BF).reshape(experts * CAP, rows_here)

    gathered = first_norm(
        inputs_full, out_grad, small_full, attn_w, other_quarter, n_tp, n_ctx
    )
    normed_one, scale_one, grad_full = gathered[:3]
    if pair:
        qkv_w, output_w = gathered[3:]
    else:
        qkv_w, output_w = (
            lax.all_gather(w, "fsdp", axis=0, tiled=True)
            for w in (jnp.concatenate(attn_w[:3], axis=1), w_output)
        )
    positions = here_ctx * rows_here + jnp.arange(rows_here, dtype=jnp.int32)
    cosine, sine = rotary_tables(positions)
    attended, query, kv = attention_forward(mm(normed_one, qkv_w), cosine, sine, n_ctx)
    resid, scale_two, normed_two, grad_rows, token_rows, slot_gates, gates, mix = second_norm(
        mm_t(attended, output_w).astype(BF),
        hidden_in,
        gain_two_here,
        mm(picks, grad_full).astype(BF),
        picks,
        router_here,
        onehot,
        names,
        n_tp,
        n_ctx,
    )
    gate_rows = slot_gates[:, 0, :CAP].reshape(experts * CAP, 1)

    to_gate, to_up, hidden_act = expert_acts(token_rows, gate_w, up_w, n_fsdp)
    d_result = (gate_rows * grad_rows.astype(F32)).astype(BF)

    def away(left, right):
        value = t_mm(split(left)[1], right).astype(BF)
        return value, swap_fsdp(value)

    def payload_of(left, right, come):
        if pair:
            return Payload(n_ctx, product=(left, right, come))
        return Payload(
            n_ctx,
            rows=lax.psum_scatter(
                t_mm(left, right).astype(BF), "fsdp", scatter_dimension=0, tiled=True
            ),
        )

    def came_and_own(outs, payload):
        if pair:
            return tuple(outs)
        own = lax.dynamic_slice_in_dim(payload.inputs[0], here_ctx * payload.cut, payload.cut, 0)
        return outs[0], own

    down_come = gate_come = up_come = None
    if pair:
        down_away, down_come = away(d_result, hidden_act)
        grad_rows = after(grad_rows, down_away)
    d_hidden = into(grad_rows, down_w)
    gate_dot = jnp.sum(hidden_act.astype(F32) * d_hidden, axis=-1).reshape(experts, CAP)
    gate_dot = jnp.broadcast_to(
        jnp.pad(gate_dot, [(0, 0), (0, rows_here - CAP)])[:, None, :], (experts, 8, rows_here)
    )
    d_hidden = gate_rows * d_hidden
    d_gate_act = (d_hidden * to_gate).astype(BF)
    d_up_act = (d_hidden * to_up).astype(BF)
    if pair:
        gate_away, gate_come = away(token_rows, d_gate_act)

    acts = (d_gate_act, d_up_act, hidden_act)
    if pair:
        acts = lax.optimization_barrier((*acts, gate_away))[:3]
    d_resid, d_attn_here, gain_two_part, d_logits, made, *up_away = second_norm_back(
        acts,
        (gate_w, up_w, down_w),
        token_rows,
        gate_dot,
        picks,
        gates,
        onehot,
        names,
        router_here,
        resid,
        scale_two,
        gain_two_here,
        out_grad,
        n_tp,
        n_ctx,
    )
    if pair:
        up_come = swap_fsdp(up_away[0])

    payload = payload_of(d_result, hidden_act, down_come)
    early = (RowSums(made, 2 * CAP, 2 * CAP, n_tp), made)
    d_attn, d_qkv, made_early, *outs = attention_backward(
        d_attn_here, output_w, query, kv, cosine, -sine, early, payload, n_tp, n_ctx
    )
    grad_down = came_and_own(outs, payload)
    payload = payload_of(token_rows, d_gate_act, gate_come)
    in_grad, gain_one_part, returned, *outs = first_norm_back(
        d_qkv,
        qkv_w,
        hidden_in,
        scale_one,
        gain_one_here,
        d_resid,
        made_early,
        payload,
        n_tp,
        n_ctx,
    )
    grad_gate = came_and_own(outs, payload)
    payload = payload_of(token_rows, d_up_act, up_come)

    small_part = jnp.concatenate(
        [
            gain_one_part[:1],
            gain_two_part[:1],
            mm(d_logits[:experts].astype(BF), my_features(normed_two)),
            jnp.zeros((6 - experts, width_tp), F32),
        ],
        axis=0,
    )
    written = write_out([grad_gate, grad_down], None, (), n_ctx)
    if pair:
        small_part = after(small_part, *written)
    grad_gate, grad_down = written
    experts_out = ExpertsOut(made, returned, picks, mix, resid, n_tp, n_ctx)
    if pair:
        grad_attn, small_grad, block_out, *outs = weight_grads(
            [(d_attn, attended), (normed_one, d_qkv)],
            [(0, 0, heads_width), (1, 0, 2 * heads_width), (1, 2 * heads_width, heads_width)],
            small_part,
            payload,
            experts_out,
            n_tp,
            n_ctx,
        )
    else:
        grad_attn = jnp.concatenate([t_mm(d_attn, attended), t_mm(normed_one, d_qkv)], axis=1)
        scatter = partial(
            lax.psum_scatter, axis_name=("fsdp", "ctx"), scatter_dimension=0, tiled=True
        )
        grad_attn = scatter(grad_attn.astype(BF)).astype(F32)
        small_grad = lax.all_gather(small_part, "tp", axis=1, tiled=True)
        small_grad = scatter(small_grad.T).T
        block_out, *outs = experts_back(experts_out, payload, n_tp, n_ctx)
    grad_up = came_and_own(outs, payload)
    grad_up, block_out, in_grad, grad_output, grad_query, grad_key, grad_value = write_out(
        [grad_up], grad_attn, (block_out, in_grad), n_ctx
    )
    return (
        block_out,
        in_grad,
        small_grad[0],
        grad_query,
        grad_key,
        grad_value,
        grad_output,
        small_grad[1],
        small_grad[2 : 2 + experts].T,
        grad_gate,
        grad_up,
        grad_down,
    )


def solution(mesh):
    rows = ("fsdp", "ctx")
    placed = (
        P(rows, "tp"),
        P(rows, "tp"),
        P("fsdp"),
        P("fsdp", "tp"),
        P("fsdp", "tp"),
        P("fsdp", "tp"),
        P("fsdp", "tp"),
        P("fsdp"),
        P("fsdp", None),
        P(None, "fsdp", "tp"),
        P(None, "fsdp", "tp"),
        P(None, "fsdp", "tp"),
        P(rows, None),
    )
    return jax.shard_map(
        shards,
        mesh=mesh,
        in_specs=placed,
        out_specs=(
            P(rows, "tp"),
            P(rows, "tp"),
            P(rows),
            P(rows, "tp"),
            P(rows, "tp"),
            P(rows, "tp"),
            P(rows, "tp"),
            P(rows),
            P(rows, None),
            P(None, rows, "tp"),
            P(None, rows, "tp"),
            P(None, rows, "tp"),
        ),
        check_vma=False,
    )
```

```python
from functools import partial
import math

import jax
import jax.numpy as jnp
from jax import lax
from jax.experimental import pallas as pl
from jax.experimental.pallas import tpu as pltpu
from jax.sharding import PartitionSpec as P

HD = 128
CAP = 160


EPS = 1e-05
THETA = 10000.0
NEG = -1e30
BF = jnp.bfloat16
F32 = jnp.float32


def mm(left, right):
    return jnp.dot(left, right, preferred_element_type=F32)


def mm_t(left, right):
    return lax.dot_general(left, right, (((1,), (1,)), ((), ())), preferred_element_type=F32)


def t_mm(left, right):
    return lax.dot_general(left, right, (((0,), (0,)), ((), ())), preferred_element_type=F32)


def rotary_tables(positions):
    half_size = HD // 2
    frequency = THETA ** (-(jnp.arange(half_size, dtype=F32) * 2.0 / HD))
    angles = positions.astype(F32)[:, None] * frequency[None, :]
    cosine, sine = jnp.cos(angles), jnp.sin(angles)
    return jnp.concatenate([cosine, cosine], axis=1), jnp.concatenate([-sine, sine], axis=1)


MESH = pl.DeviceIdType.MESH
VM = pl.BlockSpec(memory_space=pltpu.VMEM)
DMA = pltpu.SemaphoreType.DMA


def peer(axis, n, k):
    return lax.rem(lax.axis_index(axis) + k, n)


def greet(groups):
    barrier = pltpu.get_barrier_semaphore()
    for axis, n in groups:
        for k in range(1, n):
            pl.semaphore_signal(
                barrier, inc=1, device_id={axis: peer(axis, n, k)}, device_id_type=MESH
            )
    pl.semaphore_wait(barrier, sum(n - 1 for _, n in groups))


def described(source, target, sems, i, to):
    return pltpu.make_async_remote_copy(
        src_ref=source,
        dst_ref=target,
        send_sem=sems[0].at[i],
        recv_sem=sems[1].at[i],
        device_id=to,
        device_id_type=MESH,
    )


def remote(source, target, sems, i, to):
    copy = described(source, target, sems, i, to)
    copy.start()
    return copy


def send(source, target, axis, n, k, sems):
    return remote(source, target, sems, k - 1, {axis: peer(axis, n, k)})


def columns(n, size):
    return pl.ds(pl.multiple_of(n * size, 128), size)


def stretch(n, size):
    return pl.ds(pl.multiple_of(n * size, 16), size)


def gather_columns(own, full, axis, n, sems):
    size = own.shape[1]
    place = full.at[:, columns(lax.axis_index(axis), size)]
    copies = [send(own, place, axis, n, k, sems) for k in range(1, n)]
    place[...] = own[...]
    return copies


def scatter_columns(part, slots, axis, n, sems):
    size = slots.shape[2]
    return [
        send(part.at[:, columns(peer(axis, n, k), size)], slots.at[k - 1], axis, n, k, sems)
        for k in range(1, n)
    ]


def finish(copies):
    for copy in copies:
        copy.wait()


class Payload:

    def __init__(self, n_ctx, rows=None, product=None):
        self.n_ctx = n_ctx
        self.product = product is not None
        self.inputs = list(product) if self.product else [rows]
        last = self.inputs[-1]
        self.rows, self.hidden = last.shape
        self.cut = self.rows // n_ctx
        self.outs = [shape((n_ctx - 1, self.cut, self.hidden), BF)]
        self.scratch = pair_of_sems(n_ctx)
        if self.product:
            self.outs.append(shape((self.cut, self.hidden), BF))
            self.scratch += [
                pltpu.VMEM((self.rows, self.hidden), BF),
                pltpu.VMEM((self.rows, self.hidden), BF),
                pltpu.VMEM((self.inputs[0].shape[0], self.rows), BF),
                pltpu.VMEM(self.inputs[1].shape, BF),
                DMA((3,)),
            ]

    def take(self, ins, outs, scratch):
        self.ins, self.out_refs, self.held = ins, outs, scratch

    def fetches(self):
        left, right, other = self.ins
        mine = left.at[:, columns(lax.axis_index("fsdp"), self.rows)]
        return [
            pltpu.make_async_copy(source, self.held[i], self.held[6].at[j])
            for j, (source, i) in enumerate([(mine, 4), (right, 5), (other, 2)])
        ]

    def load(self):
        if self.product:
            for copy in self.fetches():
                copy.start()

    def copy(self, k):
        to = peer("ctx", self.n_ctx, k)
        source = self.held[3] if self.product else self.ins[0]
        return described(
            source.at[stretch(to, self.cut), :], self.out_refs[0].at[k - 1],
            self.held[0:2], k - 1, {"ctx": to},
        )

    def go(self, between=lambda j: None):
        n_ctx, cut = self.n_ctx, self.cut
        if not self.product:
            for k in (2, 3, 1):
                self.copy(k).start()
            return
        finish(self.fetches())

        @pl.loop(0, n_ctx)
        def _(j):
            k = lax.rem(j + 2, n_ctx)
            to = peer("ctx", n_ctx, k)
            value = t_mm(self.held[4][:, columns(to, cut)], self.held[5][...])
            value = value + self.held[2][stretch(to, cut), :].astype(F32)
            self.held[3][stretch(to, cut), :] = value.astype(BF)

            @pl.when(j != n_ctx - 2)
            def _():
                self.copy(k).start()

            between(j)

    def wait(self):
        if self.product:
            self.out_refs[1][...] = self.held[3][stretch(lax.axis_index("ctx"), self.cut), :]
        for k in range(1, self.n_ctx):
            self.copy(k).wait()


class RowSums:

    def __init__(self, made, first, count, n_tp):
        self.n_tp, self.first = n_tp, first
        self.shape = (count, made.shape[1] // n_tp)
        self.scratch = [
            pltpu.VMEM((n_tp - 1, *self.shape), BF),
            pltpu.VMEM(self.shape, BF),
            DMA,
        ] + pair_of_sems(n_tp)

    def take(self, made, scratch):
        self.made, self.held = made, scratch

    def rows(self, rank):
        return self.made.at[pl.ds(self.first, self.shape[0]), columns(rank, self.shape[1])]

    def mine(self):
        return pltpu.make_async_copy(
            self.rows(lax.axis_index("tp")), self.held[1], self.held[2]
        )

    def start(self):
        self.mine().start()
        n = self.n_tp
        self.copies = [
            send(self.rows(peer("tp", n, k)), self.held[0].at[k - 1], "tp", n, k, self.held[3:5])
            for k in range(1, n)
        ]

    def total(self):
        self.mine().wait()
        finish(self.copies)
        value = self.held[1][...].astype(F32)
        for k in range(1, self.n_tp):
            value = value + self.held[0][k - 1].astype(F32)
        return value


def quad():
    here = lax.axis_index("ctx")
    return here, here + 1 - 2 * lax.rem(here, 2), lax.rem(here + 2, 4)


def gather_square(own, places, sems, between, local=None):
    cuts = own.shape[1] // 512
    here, beside, across = quad()
    first, second, third = [], [], []
    for i in range(cuts):
        piece = own.at[:, pl.ds(i * 512, 512)]
        first.append(remote(piece, places(here, i), sems, 3 * i, {"ctx": across}))
        second.append(remote(piece, places(here, i), sems, 3 * i + 1, {"ctx": beside}))
        if local is None:
            places(here, i)[...] = piece[...]
        else:
            pltpu.make_async_copy(piece, places(here, i), local.at[i]).start()
    between()
    for i in range(cuts):
        first[i].wait()
        third.append(
            remote(places(across, i), places(across, i), sems, 3 * i + 2, {"ctx": beside})
        )
    finish(second)
    finish(third)
    if local is not None:
        for i in range(cuts):
            piece = own.at[:, pl.ds(i * 512, 512)]
            pltpu.make_async_copy(piece, places(here, i), local.at[i]).wait()


def row_sums(values):
    ones = jnp.ones((8, values.shape[1]), F32)
    return lax.dot_general(
        ones,
        values,
        (((1,), (1,)), ((), ())),
        precision=lax.Precision.HIGHEST,
        preferred_element_type=F32,
    )


def as_column(rows, weight):
    return lax.dot_general(
        rows,
        weight,
        (((0,), (0,)), ((), ())),
        precision=lax.Precision.HIGHEST,
        preferred_element_type=F32,
    )


def eighth():
    return jnp.full((8, 128), 0.125, F32)


def total_over(sums, mine, slots, axis, n, sems):
    mine[...] = sums
    copies = [send(mine, slots.at[k - 1], axis, n, k, sems) for k in range(1, n)]
    finish(copies)
    total = sums
    for k in range(1, n):
        total = total + slots[k - 1]
    return total


def call(kernel, out_shape, inputs, scratch, collective, name, left=()):
    anywhere = pl.BlockSpec(memory_space=pl.ANY)
    outs = out_shape if isinstance(out_shape, tuple) else (out_shape,)
    specs = [anywhere if i - len(outs) in left else VM for i in range(len(outs))]
    return pl.pallas_call(
        kernel,
        out_shape=out_shape,
        in_specs=[anywhere if i in left else VM for i in range(len(inputs))],
        out_specs=tuple(specs) if isinstance(out_shape, tuple) else specs[0],
        scratch_shapes=scratch,
        compiler_params=pltpu.CompilerParams(collective_id=collective, has_side_effects=True),
        cost_estimate=pl.CostEstimate(flops=0, bytes_accessed=0, transcendentals=0),
        name=name,
    )(*inputs)


def shape(dims, dtype):
    return jax.ShapeDtypeStruct(dims, dtype)


def pair_of_sems(n):
    return [DMA((n,)), DMA((n,))]


def gather_tp(value, stacks, n_tp):
    rows, size = value.shape
    many = len(stacks)
    member = stacks[0].shape[1:]

    def kernel(own, *refs):
        stk, full, outs = refs[:many], refs[many], refs[many + 1 : 2 * many + 1]
        held, loads, stores = refs[2 * many + 1 : 2 * many + 4]
        sems = refs[2 * many + 4 :]
        here = lax.axis_index("ctx")
        into = [
            pltpu.make_async_copy(stk[i].at[here], held.at[i], loads.at[i]) for i in range(many)
        ]
        away = [pltpu.make_async_copy(held.at[i], outs[i], stores.at[i]) for i in range(many)]
        for copy in into:
            copy.start()
        greet([("tp", n_tp)])
        copies = gather_columns(own, full, "tp", n_tp, sems)
        for i in range(many):
            into[i].wait()
            away[i].start()
        finish(copies)
        finish(away)

    return call(
        kernel,
        (
            shape((rows, size * n_tp), value.dtype),
            *(shape(member, stack.dtype) for stack in stacks),
        ),
        (value, *stacks),
        [pltpu.VMEM((many, *member), BF), DMA((many,)), DMA((many,))] + pair_of_sems(n_tp),
        1,
        "gather_tp",
        left=tuple(range(1, many + 1)) + tuple(range(-many, 0)),
    )


def first_norm(full, grad, gain, weights, quarter, n_tp, n_ctx):
    rows, width = full.shape
    with_quarter = quarter is not None

    def kernel(*refs):
        hid, grd, gn = refs[:3]
        refs = refs[3:]
        if with_quarter:
            wgts, refs = refs[: len(weights)], refs[len(weights) :]
            qrt, out, scale, grd_full, many_full, last_full, held, local, loads, stores = refs[:10]
            sems = refs[10:]
            half, inner = wgts[0].shape
            last = len(wgts) - 1
            mine = lax.axis_index("fsdp")

            def target(i, first_row, count):
                at = pl.ds(pl.multiple_of(first_row, 16), count)
                if i == last:
                    return last_full.at[at, :]
                return many_full.at[at, pl.ds(i * inner, inner)]

            into = [
                pltpu.make_async_copy(wgts[i], held.at[i], loads.at[i]) for i in range(len(wgts))
            ]
            away = [
                pltpu.make_async_copy(held.at[i], target(i, mine * half, half), stores.at[i])
                for i in range(len(wgts))
            ]
            for copy in into:
                copy.start()
            greet([("tp", n_tp), ("ctx", n_ctx)])
        else:
            out, scale, grd_full = refs[:3]
            sems = refs[3:]
            greet([("tp", n_tp)])
        grads = gather_columns(grd, grd_full, "tp", n_tp, sems[0:2])

        def norm():
            values = hid[...].astype(F32)
            mean = jnp.sum(values * values, axis=-1, keepdims=True) * (1.0 / width)
            factor = lax.rsqrt(mean + EPS)
            scale[...] = jnp.broadcast_to(factor, scale.shape)
            out[...] = (values * factor * gn[0:1, :]).astype(BF)

        if with_quarter:
            count = qrt.shape[0]

            def work():
                for i in range(len(wgts)):
                    into[i].wait()
                    away[i].start()
                norm()

            def places(rank, i):
                return target(i, (1 - mine) * half + rank * count, count)

            gather_square(qrt, places, sems[2:4], work, local)
            finish(away)
        else:
            norm()
        finish(grads)

    outs = [shape((rows, width), BF), shape((rows, 128), F32), shape((rows, width), BF)]
    inputs = [full, grad, gain]
    scratch, left = [], ()
    if with_quarter:
        half, inner = weights[0].shape
        many = len(weights)
        assert inner == 512
        outs.append(shape((2 * half, (many - 1) * inner), BF))
        outs.append(shape((2 * half, inner), BF))
        inputs += [*weights, quarter]
        scratch = [pltpu.VMEM((many, half, inner), BF), DMA((many,)), DMA((many,)), DMA((many,))]
        left = tuple(range(3, 3 + many)) + (-2, -1)
    return call(
        kernel,
        tuple(outs),
        inputs,
        scratch + pair_of_sems(n_tp) + pair_of_sems(12),
        7,
        "first_norm",
        left=left,
    )


def turn(values, cosine, sine):
    return values * cosine + pltpu.roll(values, HD // 2, axis=1) * sine


def softmax_rows(query, key, first_row):
    scores = mm_t(query, key) * (1.0 / math.sqrt(HD))
    rows = first_row + lax.broadcasted_iota(jnp.int32, scores.shape, 0)
    cols = lax.broadcasted_iota(jnp.int32, scores.shape, 1)
    scores = jnp.where(cols <= rows, scores, NEG)
    top = jnp.max(scores, axis=-1, keepdims=True)
    weights = jnp.exp(scores - top)
    return weights / jnp.sum(weights, axis=-1, keepdims=True)


def attention_forward(qkv, cosine, sine, n_ctx):
    rows = qkv.shape[0]
    width = qkv.shape[1] // 3
    heads = width // HD

    def kernel(prj, cs, sn, out, qry, full, own, *sems):
        greet([("ctx", n_ctx)])
        here = lax.axis_index("ctx")

        @pl.loop(0, heads)
        def _(h):
            own[:, columns(h, HD)] = turn(
                prj[:, columns(h + heads, HD)], cs[...], sn[...]
            ).astype(BF)
            own[:, columns(h + heads, HD)] = prj[:, columns(h + 2 * heads, HD)].astype(BF)

        def queries():
            @pl.loop(0, heads)
            def _(h):
                qry[:, columns(h, HD)] = turn(prj[:, columns(h, HD)], cs[...], sn[...]).astype(BF)

        def places(rank, i):
            return full.at[stretch(rank, rows), pl.ds(i * 512, 512)]

        gather_square(own, places, sems, queries)

        @pl.loop(0, heads)
        def _(h):
            probs = softmax_rows(qry[:, columns(h, HD)], full[:, columns(h, HD)], here * rows)
            out[:, columns(h, HD)] = mm(
                probs.astype(BF), full[:, columns(h + heads, HD)]
            ).astype(BF)

    return call(
        kernel,
        (
            shape((rows, width), BF),
            shape((rows, width), BF),
            shape((rows * n_ctx, 2 * width), BF),
        ),
        (qkv, cosine, sine),
        [pltpu.VMEM((rows, 2 * width), BF)] + pair_of_sems(6 * width // 512),
        2,
        "attention_forward",
    )


def second_norm(part, hidden, gain, slabs, picks, router, onehot, names, n_tp, n_ctx):
    rows, size = hidden.shape
    width = size * n_tp
    experts = n_ctx

    def kernel(
        prt, hid, gn, slb, pck, rtr, one, nms,
        resid, scale, out, moved, tokens, slot_gates, gates, mix,
        slots, mine, sums, mine_two, sums_two, low, sent, own_gates, *sems
    ):
        greet([("tp", n_tp), ("ctx", n_ctx)])
        here = lax.axis_index("tp")
        copies = scatter_columns(prt, slots, "tp", n_tp, sems[0:2])
        others = [
            send(
                slb.at[pl.ds(k * CAP, CAP)], moved.at[pl.ds(k * CAP, CAP)],
                "ctx", n_ctx, k, sems[6:8],
            )
            for k in range(1, n_ctx)
        ]
        moved[0:CAP] = slb[0:CAP]
        total = prt[:, columns(here, size)].astype(F32)
        finish(copies)
        for k in range(1, n_tp):
            total = total + slots[k - 1].astype(F32)
        total = hid[...].astype(F32) + total
        resid[...] = total
        square = total_over(row_sums(total * total), mine, sums, "tp", n_tp, sems[2:4])
        factor = lax.rsqrt(as_column(square, eighth()) * (1.0 / width) + EPS)
        scale[...] = factor
        low[...] = (resid[...] * factor[:, 0:1] * gn[0:1, :]).astype(BF)
        partial_logits = mm_t(rtr[...].astype(BF), low[...])
        mine_two[...] = partial_logits
        logit_copies = [
            send(mine_two, sums_two.at[k - 1], "tp", n_tp, k, sems[12:14]) for k in range(1, n_tp)
        ]
        gather_columns(low, out, "tp", n_tp, sems[4:6])

        def route():
            finish(logit_copies)
            logits = partial_logits
            for k in range(1, n_tp):
                logits = logits + sums_two[k - 1]
            named = [jnp.sum(one[j] * logits, axis=0, keepdims=True) for j in range(2)]
            top = jnp.maximum(named[0], named[1])
            powers = [jnp.exp(value - top) for value in named]
            both = powers[0] + powers[1]
            gate = [value / both for value in powers]
            mixed = gate[0] * nms[0] + gate[1] * nms[1]
            mix[...] = mixed
            order = lax.broadcasted_iota(jnp.int32, (8, rows), 0)
            gates[...] = jnp.where(order == 0, gate[0], jnp.where(order == 1, gate[1], 0.0))
            own_gates[...] = jnp.zeros(own_gates.shape, F32)
            for k in range(experts):
                own_gates[k, :, 0:CAP] = lax.dot_general(
                    jnp.broadcast_to(mixed[k : k + 1], (8, rows)),
                    pck[k * CAP : (k + 1) * CAP].astype(F32),
                    (((1,), (1,)), ((), ())),
                    precision=lax.Precision.HIGHEST,
                    preferred_element_type=F32,
                )
            slot_gates[0] = own_gates[0]
            for k in range(1, n_ctx):
                others.append(
                    send(own_gates.at[k], slot_gates.at[k], "ctx", n_ctx, k, sems[10:12])
                )


        def slab(k, step):
            at = columns(peer("tp", n_tp, n_tp - step), size)
            return described(
                sent.at[step, pl.ds(k * CAP, CAP)], tokens.at[pl.ds(k * CAP, CAP), at],
                sems[8:10], step * n_ctx + k, {"ctx": peer("ctx", n_ctx, k)},
            )

        def dispatch(step, block):
            sent[step] = mm(pck[...], block).astype(BF)
            tokens[0:CAP, columns(peer("tp", n_tp, n_tp - step), size)] = sent[step, 0:CAP]
            for k in (2, 3, 1):
                slab(k, step).start()

        route()

        @pl.loop(0, n_tp)
        def _(step):
            @pl.when(step > 0)
            def _():
                described(
                    low, out.at[:, columns(here, size)], sems[4:6], step - 1,
                    {"tp": peer("tp", n_tp, step)},
                ).wait()

            dispatch(step, out[:, columns(peer("tp", n_tp, n_tp - step), size)])

        for step in range(n_tp):
            for k in (2, 3, 1):
                slab(k, step).wait()
        finish(others)

    return call(
        kernel,
        (
            shape((rows, size), F32),
            shape((rows, 128), F32),
            shape((rows, width), BF),
            shape(slabs.shape, BF),
            shape(slabs.shape, BF),
            shape((experts, 8, rows), F32),
            shape((8, rows), F32),
            shape((8, rows), F32),
        ),
        (part, hidden, gain, slabs, picks, router, onehot, names),
        [
            pltpu.VMEM((n_tp - 1, rows, size), BF),
            pltpu.VMEM((8, rows), F32),
            pltpu.VMEM((n_tp - 1, 8, rows), F32),
            pltpu.VMEM((8, rows), F32),
            pltpu.VMEM((n_tp - 1, 8, rows), F32),
            pltpu.VMEM((rows, size), BF),
            pltpu.VMEM((n_tp, experts * CAP, size), BF),
            pltpu.VMEM((experts, 8, rows), F32),
        ]
        + pair_of_sems(n_tp) * 3
        + pair_of_sems(n_ctx)
        + pair_of_sems(n_tp * n_ctx)
        + pair_of_sems(n_ctx)
        + pair_of_sems(n_tp),
        3,
        "second_norm",
    )


def expert_acts(tokens, gate_w, up_w, n_fsdp):
    rows, width = tokens.shape
    hidden = gate_w[0].shape[1]
    count = len(gate_w)
    part = gate_w[0].shape[0]
    chunk = 256
    per = part // chunk
    steps = count * per
    pair = count == 2

    def kernel(tok, *refs):
        wgt = [refs[:count], refs[count : 2 * count]]
        to_gate, to_up, hid, buffer, loads = refs[2 * count :]
        first = lax.axis_index("fsdp") if pair else 0

        def load(step):
            slot = lax.rem(step, 2)
            at = stretch(lax.rem(step, per), chunk)
            for lane in range(2):
                for i in range(count):

                    @pl.when(step // per == i)
                    def _():
                        pltpu.make_async_copy(
                            wgt[lane][i].at[at], buffer.at[slot, lane], loads.at[slot, lane]
                        ).start()

        load(0)
        to_gate[...] = jnp.zeros_like(to_gate)
        to_up[...] = jnp.zeros_like(to_up)

        @pl.loop(0, steps)
        def _(step):
            slot = lax.rem(step, 2)
            for lane in range(2):
                pltpu.make_async_copy(
                    wgt[lane][0].at[pl.ds(0, chunk)], buffer.at[slot, lane], loads.at[slot, lane]
                ).wait()

            @pl.when(step + 1 < steps)
            def _():
                load(step + 1)

            which = lax.rem(first + step // per, count)
            column = which * part + lax.rem(step, per) * chunk
            values = tok[:, pl.ds(pl.multiple_of(column, 128), chunk)]
            to_gate[...] += mm(values, buffer[slot, 0])
            to_up[...] += mm(values, buffer[slot, 1])

        @pl.loop(0, rows // 32)
        def _(i):
            at = stretch(i, 32)
            a, b = to_gate[at, :], to_up[at, :]
            sigma = 1.0 / (1.0 + jnp.exp(-a))
            silu = a * sigma
            hid[at, :] = (silu * b).astype(BF)
            to_up[at, :] = silu
            to_gate[at, :] = b * sigma * (1.0 + a * (1.0 - sigma))

    anywhere = pl.BlockSpec(memory_space=pl.ANY)
    return pl.pallas_call(
        kernel,
        out_shape=(
            shape((rows, hidden), F32),
            shape((rows, hidden), F32),
            shape((rows, hidden), BF),
        ),
        in_specs=[VM] + [anywhere] * (2 * count),
        out_specs=(VM, VM, VM),
        scratch_shapes=[pltpu.VMEM((2, 2, chunk, hidden), BF), DMA((2, 2))],
        cost_estimate=pl.CostEstimate(flops=0, bytes_accessed=0, transcendentals=0),
        name="expert_acts",
    )(tokens, *gate_w, *up_w)


def second_norm_back(
    acts, weights, tokens, dots, picks, gates, onehot, names, router, resid, scale, gain, grad,
    n_tp, n_ctx,
):
    rows, size = resid.shape
    width = size * n_tp
    experts = n_ctx
    hidden = acts[0].shape[1]
    count = len(weights[0])
    part = weights[0][0].shape[0]

    def kernel(*refs):
        dga, dup, hid_far = refs[:3]
        wgt = [refs[3 + i * count : 3 + (i + 1) * count] for i in range(3)]
        refs = refs[3 + 3 * count :]
        tok_far, dts, pck, gts, one, nms, rtr, rsd, scl, gn, grd = refs[:11]
        d_resid, low, d_gain, d_logits, out_rows = refs[11:16]
        refs = refs[16:]
        if count == 2:
            up_away, up_held, up_sem = refs[:1] + refs[1:3]
            refs = refs[3:]
        (
            drw, eo, buffer, back, back_dots, parts, slots, mine, sums, mine_two, sums_two, loads,
            out_sem, hid, tok, late,
        ) = refs[:16]
        sems = refs[16:]
        fetches = [
            pltpu.make_async_copy(hid_far, hid, late.at[0]),
            pltpu.make_async_copy(tok_far, tok, late.at[1]),
        ]
        here = lax.axis_index("tp")
        first = lax.axis_index("fsdp")

        def load(which, rank, slot, lane):
            feature = rank * size
            inside = pl.ds(pl.multiple_of(lax.rem(feature, part), 16), size)
            target = buffer.at[slot, lane]
            if count == 1:
                pltpu.make_async_copy(
                    wgt[which][0].at[inside], target, loads.at[slot, lane]
                ).start()
                return
            own = feature // part == first

            @pl.when(own)
            def _():
                pltpu.make_async_copy(
                    wgt[which][0].at[inside], target, loads.at[slot, lane]
                ).start()

            @pl.when(jnp.logical_not(own))
            def _():
                pltpu.make_async_copy(
                    wgt[which][1].at[inside], target, loads.at[slot, lane]
                ).start()

        def loaded(which, slot, lane):
            pltpu.make_async_copy(
                wgt[which][0].at[pl.ds(0, size)], buffer.at[slot, lane], loads.at[slot, lane]
            ).wait()

        load(0, peer("tp", n_tp, 1), 0, 0)
        load(1, peer("tp", n_tp, 1), 0, 1)
        for copy in fetches:
            copy.start()
        greet([("tp", n_tp), ("ctx", n_ctx)])
        small = []
        for k in range(1, n_ctx):
            small.append(
                send(dts.at[k], back_dots.at[k - 1], "ctx", n_ctx, n_ctx - k, sems[0:2])
            )

        def slab(k, rank, step):
            at = columns(rank, size)
            return described(
                drw.at[pl.ds(k * CAP, CAP), at], back.at[k - 1, :, at],
                sems[2:4], step * n_ctx + k - 1, {"ctx": peer("ctx", n_ctx, n_ctx - k)},
            )

        @pl.loop(0, n_tp)
        def _(step):
            rank = peer("tp", n_tp, step + 1)
            slot = lax.rem(step, 2)
            loaded(0, slot, 0)
            loaded(1, slot, 1)

            @pl.when(step + 1 < n_tp)
            def _():
                load(0, peer("tp", n_tp, step + 2), 1 - slot, 0)
                load(1, peer("tp", n_tp, step + 2), 1 - slot, 1)

            drw[:, columns(rank, size)] = (
                mm_t(dga[...], buffer[slot, 0]) + mm_t(dup[...], buffer[slot, 1])
            ).astype(BF)
            for k in (2, 3, 1):
                slab(k, rank, step).start()

        def combined(step):
            rank = peer("tp", n_tp, step)
            at = columns(rank, size)
            for k in (2, 3, 1):
                slab(k, rank, step - 1).wait()
            block = t_mm(pck[0:CAP], drw[0:CAP, at])
            for k in range(1, experts):
                block = block + t_mm(pck[k * CAP : (k + 1) * CAP], back[k - 1, :, at])
            return block

        def give(step):
            return described(
                parts.at[step - 1], slots.at[step - 1], sems[6:8], step - 1,
                {"tp": peer("tp", n_tp, step)},
            )

        def pass_on(begin, end):
            @pl.loop(begin, end)
            def _(step):
                parts[step - 1] = combined(step).astype(BF)
                give(step).start()

        load(2, 0, 0, 0)
        finish(small)
        order = lax.broadcasted_iota(jnp.int32, (8, rows), 0)
        own = jnp.zeros((8, rows), F32)
        for k in range(experts):
            by_slot = dts[0] if k == 0 else back_dots[k - 1]
            by_row = lax.dot_general(
                by_slot[:, 0:CAP],
                pck[k * CAP : (k + 1) * CAP].astype(F32),
                (((1,), (0,)), ((), ())),
                precision=lax.Precision.HIGHEST,
                preferred_element_type=F32,
            )
            own = own + jnp.where(order == k, by_row, 0.0)
        mine[...] = own
        shared = [
            send(mine, sums.at[k - 1], "tp", n_tp, k, sems[4:6]) for k in range(1, n_tp)
        ]
        pass_on(1, n_tp - 1)

        finish(fetches)

        @pl.loop(0, n_tp)
        def _(rank):
            slot = lax.rem(rank, 2)
            loaded(2, slot, 0)

            @pl.when(rank + 1 < n_tp)
            def _():
                load(2, rank + 1, 1 - slot, 0)

            eo[:, columns(rank, size)] = mm_t(hid[...], buffer[slot, 0]).astype(BF)

        pltpu.make_async_copy(eo, out_rows, out_sem).start()
        pass_on(n_tp - 1, n_tp)
        if count == 2:

            @pl.loop(0, part // 256)
            def _(i):
                at = pl.ds(pl.multiple_of((1 - first) * part + i * 256, 128), 256)
                up_held[stretch(i, 256), :] = t_mm(tok[:, at], dup[...]).astype(BF)

            pltpu.make_async_copy(up_held, up_away, up_sem).start()
        finish(shared)
        gate_grad = mine[...]
        for k in range(1, n_tp):
            gate_grad = gate_grad + sums[k - 1]
        both = [jnp.sum(nms[j] * gate_grad, axis=0, keepdims=True) for j in range(2)]
        gate = [gts[j : j + 1, :] for j in range(2)]
        mean = gate[0] * both[0] + gate[1] * both[1]
        logits = sum(gate[j] * (both[j] - mean) * one[j] for j in range(2))
        d_logits[...] = logits

        copies = [give(step) for step in range(1, n_tp)]
        total = combined(n_tp)
        total = total + lax.dot_general(
            logits.astype(BF),
            rtr[...].astype(BF),
            (((0,), (0,)), ((), ())),
            preferred_element_type=F32,
        )
        finish(copies)
        for k in range(1, n_tp):
            total = total + slots[k - 1].astype(F32)
        factor = scl[:, 0:1]
        unit = rsd[...] * factor
        d_gain[...] = jnp.broadcast_to(jnp.sum(total * unit, axis=0, keepdims=True), d_gain.shape)
        gained = total * gn[0:1, :]
        d_resid[...] = gained
        dot = total_over(row_sums(unit * gained), mine_two, sums_two, "tp", n_tp, sems[8:10])
        dot = as_column(dot, eighth())[:, 0:1] * (1.0 / width)
        result = grd[...].astype(F32) + factor * (d_resid[...] - rsd[...] * factor * dot)
        d_resid[...] = result
        low[...] = result.astype(BF)
        pltpu.make_async_copy(eo, out_rows, out_sem).wait()
        if count == 2:
            pltpu.make_async_copy(up_held, up_away, up_sem).wait()

    outs = [
        shape((rows, size), F32),
        shape((rows, size), BF),
        shape((8, size), F32),
        shape((8, rows), F32),
        shape((experts * CAP, width), BF),
    ]
    held = []
    if count == 2:
        outs.append(shape((part, hidden), BF))
        held = [pltpu.VMEM((part, hidden), BF), DMA]
    flat = [array for group in weights for array in group]
    return call(
        kernel,
        tuple(outs),
        (*acts, *flat, tokens, dots, picks, gates, onehot, names, router, resid, scale, gain, grad),
        held
        + [
            pltpu.VMEM((experts * CAP, width), BF),
            pltpu.VMEM((experts * CAP, width), BF),
            pltpu.VMEM((2, 2, size, hidden), BF),
            pltpu.VMEM((n_ctx - 1, CAP, width), BF),
            pltpu.VMEM((n_ctx - 1, 8, rows), F32),
            pltpu.VMEM((n_tp - 1, rows, size), BF),
            pltpu.VMEM((n_tp - 1, rows, size), BF),
            pltpu.VMEM((8, rows), F32),
            pltpu.VMEM((n_tp - 1, 8, rows), F32),
            pltpu.VMEM((8, rows), F32),
            pltpu.VMEM((n_tp - 1, 8, rows), F32),
            DMA((2, 2)),
            DMA,
            pltpu.VMEM((experts * CAP, hidden), BF),
            pltpu.VMEM((experts * CAP, width), BF),
            DMA((2,)),
        ]
        + pair_of_sems(n_ctx)
        + pair_of_sems(n_tp * n_ctx)
        + pair_of_sems(n_tp) * 3,
        4,
        "second_norm_back",
        left=tuple(range(2, 4 + 3 * count)) + ((-2, -1) if count == 2 else (-1,)),
    )


def attention_backward(
    low, output_w, query, kv, cosine, sine, sums, payload, n_tp, n_ctx
):
    rows, size = low.shape
    width = size * n_tp
    inner = query.shape[1]
    heads = inner // HD
    scale = 1.0 / math.sqrt(HD)

    half = heads // 2
    sums, sums_input = sums
    lane = 2 * half * HD

    def kernel(*refs):
        lw, wgt_far, qry_far, full_far, cs, sn, made = refs[:7]
        n_in, n_out = 7 + len(payload.inputs), len(payload.outs)
        d_attn, d_qkv, summed = refs[n_in : n_in + 3]
        scratch = refs[n_in + 3 + n_out :]
        dot, dqs, dkv, slots, last, both, total, kept = scratch[:8]
        sems = scratch[8:12]
        wgt, qry, full, late = scratch[12:16]
        sums.take(made, scratch[16 : 16 + len(sums.scratch)])
        payload.take(
            refs[7:n_in], refs[n_in + 3 : n_in + 3 + n_out], scratch[16 + len(sums.scratch) :]
        )
        payload.load()
        fetches = [
            pltpu.make_async_copy(far, near, late.at[i])
            for i, (far, near) in enumerate([(qry_far, qry), (full_far, full), (wgt_far, wgt)])
        ]
        for copy in fetches:
            copy.start()
        greet([("tp", n_tp), ("ctx", n_ctx)])
        here, beside, across = quad()
        beyond = lax.rem(beside + 2, 4)
        copies = gather_columns(lw, d_attn, "tp", n_tp, sems[2:4])
        sums.start()
        payload.go()
        finish(fetches)

        @pl.loop(0, heads)
        def _(h):
            at = columns(h, HD)
            kept[h] = softmax_rows(qry[:, at], full[:, at], here * rows)

        for step in range(n_tp):
            rank = peer("tp", n_tp, n_tp - step)
            weights = wgt[pl.ds(pl.multiple_of(rank * size, 16), size), :]
            if step:
                copies[step - 1].wait()
                total[...] += mm(d_attn[:, columns(rank, size)], weights)
            else:
                total[...] = mm(lw[...], weights)
        dot[...] = total[...].astype(BF)
        first, second, third = [], [], []
        for j in range(2):

            @pl.loop(0, half)
            def _(i):
                h = j * half + i
                at, at_v = columns(h, HD), columns(h + heads, HD)
                key_at = pl.ds(pl.multiple_of(j * lane + i * HD, 128), HD)
                value_at = pl.ds(pl.multiple_of(j * lane + (half + i) * HD, 128), HD)
                probs = kept[h]
                d_probs = mm_t(dot[:, at], full[:, at_v])
                delta = jnp.sum(probs * d_probs, axis=-1, keepdims=True)
                d_scores = (probs * (d_probs - delta)).astype(BF)
                dqs[:, at] = mm(d_scores, full[:, at]) * scale
                dkv[:, key_at] = (t_mm(d_scores, qry[:, at]) * scale).astype(BF)
                dkv[:, value_at] = t_mm(probs.astype(BF), dot[:, at]).astype(BF)

            at = pl.ds(j * lane, lane)
            first.append(
                remote(
                    dkv.at[stretch(beyond, rows), at], slots.at[0, :, at],
                    sems, 3 * j, {"ctx": beside},
                )
            )
            second.append(
                remote(
                    dkv.at[stretch(beside, rows), at], slots.at[1, :, at],
                    sems, 3 * j + 1, {"ctx": beside},
                )
            )
        for j in range(2):
            at = pl.ds(j * lane, lane)
            first[j].wait()
            both[:, at] = (
                dkv[stretch(across, rows), at].astype(F32) + slots[0, :, at].astype(F32)
            ).astype(BF)
            third.append(
                remote(both.at[:, at], last.at[:, at], sems, 3 * j + 2, {"ctx": across})
            )

        @pl.loop(0, heads)
        def _(h):
            d_qkv[:, columns(h, HD)] = turn(dqs[:, columns(h, HD)], cs[...], sn[...]).astype(BF)

        for j in range(2):
            second[j].wait()
            third[j].wait()

            @pl.loop(0, half)
            def _(i):
                h = j * half + i
                key_at = pl.ds(pl.multiple_of(j * lane + i * HD, 128), HD)
                value_at = pl.ds(pl.multiple_of(j * lane + (half + i) * HD, 128), HD)
                mine = stretch(here, rows)
                d_key = dkv[mine, key_at].astype(F32) + slots[1, :, key_at].astype(F32)
                d_key = d_key + last[:, key_at].astype(F32)
                d_qkv[:, columns(h + heads, HD)] = turn(d_key, cs[...], sn[...]).astype(BF)
                d_value = dkv[mine, value_at].astype(F32) + slots[1, :, value_at].astype(F32)
                d_value = d_value + last[:, value_at].astype(F32)
                d_qkv[:, columns(h + 2 * heads, HD)] = d_value.astype(BF)

        summed[...] = sums.total().astype(BF)
        payload.wait()

    return call(
        kernel,
        (
            shape((rows, width), BF),
            shape((rows, 3 * inner), BF),
            shape(sums.shape, BF),
            *payload.outs,
        ),
        (low, output_w, query, kv, cosine, sine, sums_input, *payload.inputs),
        [
            pltpu.VMEM((rows, inner), BF),
            pltpu.VMEM((rows, inner), F32),
            pltpu.VMEM((rows * n_ctx, 2 * inner), BF),
            pltpu.VMEM((2, rows, 2 * inner), BF),
            pltpu.VMEM((rows, 2 * inner), BF),
            pltpu.VMEM((rows, 2 * inner), BF),
            pltpu.VMEM((rows, inner), F32),
            pltpu.VMEM((heads, rows, rows * n_ctx), F32),
        ]
        + pair_of_sems(6)
        + pair_of_sems(n_tp)
        + [
            pltpu.VMEM(array.shape, BF) for array in (output_w, query, kv)
        ]
        + [DMA((3,))]
        + sums.scratch
        + payload.scratch,
        5,
        "attention_backward",
        left=(1, 2, 3, *range(6, 7 + len(payload.inputs)), -len(payload.outs)),
    )


def first_norm_back(d_qkv, weights, hidden, scale, gain, d_resid, early, payload, n_tp, n_ctx):
    rows, size = hidden.shape
    width = size * n_tp

    def kernel(*refs):
        dpr, wgt, hid, scl, gn, dr, erl = refs[:7]
        n_in, n_out = 7 + len(payload.inputs), len(payload.outs)
        out, d_gain, returned = refs[n_in : n_in + 3]
        scratch = refs[n_in + 3 + n_out :]
        held, parts, slots, mine, sums, loads = scratch[:6]
        sems = scratch[6:10]
        payload.take(refs[7:n_in], refs[n_in + 3 : n_in + 3 + n_out], scratch[12:])

        def block(step):
            rank = peer("tp", n_tp, step)
            return pltpu.make_async_copy(
                wgt.at[stretch(rank, size), :], held.at[step - 1], loads.at[step - 1]
            )

        for step in range(1, n_tp + 1):
            block(step).start()
        payload.load()
        greet([("tp", n_tp), ("ctx", n_ctx)])
        given = [
            send(
                erl.at[pl.ds((k - 2) * CAP, CAP)], returned.at[k - 2],
                "ctx", n_ctx, n_ctx - k, scratch[10:12],
            )
            for k in range(2, n_ctx)
        ]

        def give(step):
            return described(
                parts.at[step - 1], slots.at[step - 1], sems[0:2], step - 1,
                {"tp": peer("tp", n_tp, step)},
            )

        @pl.loop(1, n_tp + 1)
        def _(step):
            block(step).wait()
            out[...] = mm_t(dpr[...], held[step - 1])

            @pl.when(step < n_tp)
            def _():
                parts[step - 1] = out[...].astype(BF)
                give(step).start()

        copies = [give(step) for step in range(1, n_tp)]
        payload.go()
        finish(copies)
        total = out[...]
        for k in range(1, n_tp):
            total = total + slots[k - 1].astype(F32)
        factor = scl[:, 0:1]
        unit = hid[...].astype(F32) * factor
        d_gain[...] = jnp.broadcast_to(jnp.sum(total * unit, axis=0, keepdims=True), d_gain.shape)
        gained = total * gn[0:1, :]
        out[...] = gained
        dot = total_over(row_sums(unit * gained), mine, sums, "tp", n_tp, sems[2:4])
        dot = as_column(dot, eighth())[:, 0:1] * (1.0 / width)
        unit = hid[...].astype(F32) * factor
        out[...] = dr[...] + factor * (out[...] - unit * dot)
        finish(given)
        payload.wait()

    return call(
        kernel,
        (
            shape((rows, size), F32),
            shape((8, size), F32),
            shape((n_ctx - 2, CAP, size), BF),
            *payload.outs,
        ),
        (d_qkv, weights, hidden, scale, gain, d_resid, early, *payload.inputs),
        [
            pltpu.VMEM((n_tp, size, d_qkv.shape[1]), BF),
            pltpu.VMEM((n_tp - 1, rows, size), BF),
            pltpu.VMEM((n_tp - 1, rows, size), BF),
            pltpu.VMEM((8, rows), F32),
            pltpu.VMEM((n_tp - 1, 8, rows), F32),
            DMA((n_tp,)),
        ]
        + pair_of_sems(n_tp) * 2
        + pair_of_sems(n_ctx)
        + payload.scratch,
        6,
        "first_norm_back",
        left=(1, *range(7, 7 + len(payload.inputs)), -len(payload.outs)),
    )


class ExpertsOut:

    def __init__(self, made, returned, picks, mix, resid, n_tp, n_ctx):
        self.n_ctx = n_ctx
        self.left = n_ctx - returned.shape[0]
        self.sums = RowSums(made, 0, self.left * CAP, n_tp)
        self.inputs = [made, returned, picks, mix, resid]
        self.size = resid.shape[1]
        self.out = shape(resid.shape, BF)
        self.scratch = [
            pltpu.VMEM(self.sums.shape, BF),
            pltpu.VMEM((self.left - 1, CAP, self.size), BF),
        ]
        self.scratch += pair_of_sems(n_ctx)
        self.scratch += [pltpu.VMEM((n_ctx, resid.shape[0], 128), F32)] + self.sums.scratch

    def take(self, ins, out, scratch):
        self.ins, self.out_ref, self.held = ins, out, scratch[:5]
        self.sums.take(ins[0], scratch[5:])

    def give_back(self):
        share, back = self.held[:2]
        share[...] = self.sums.total().astype(BF)
        n_ctx = self.n_ctx
        self.copies = [
            send(
                share.at[pl.ds(k * CAP, CAP)], back.at[k - 1],
                "ctx", n_ctx, n_ctx - k, self.held[2:4],
            )
            for k in range(1, self.left)
        ]

    def prepare(self):
        order = lax.broadcasted_iota(jnp.int32, (8, 128), 0)

        @pl.loop(0, self.n_ctx)
        def _(k):
            self.held[4][k] = as_column(self.ins[-2][...], jnp.where(order == k, 1.0, 0.0))

    def mix(self):
        returned, picks, mix, resid = self.ins[1:]
        share, back = self.held[:2]
        finish(self.copies)
        total = resid[...]
        for k in range(self.n_ctx):
            gate = self.held[4][k, :, 0:1]
            if k == 0:
                rows = share[0:CAP]
            elif k < self.left:
                rows = back[k - 1]
            else:
                rows = returned[k - self.left]
            total = total + gate * t_mm(picks[k * CAP : (k + 1) * CAP], rows)
        self.out_ref[...] = total.astype(BF)


def weight_grads(ready, products, groups, small, payload, experts_out, n_tp, n_ctx):
    width = products[0][0].shape[1]
    places = 2 * n_ctx
    cut = width // places
    total_columns = sum(size for _, _, size in groups)
    flat = [array for pair in products for array in pair]
    ready = ready.reshape(places, cut, -1)
    inputs = [ready, *flat, small, *experts_out.inputs, *payload.inputs]

    def kernel(*refs):
        made_ready, factors, refs = refs[0], refs[1 : 1 + len(flat)], refs[1 + len(flat) :]
        sml, refs = refs[0], refs[1:]
        given, refs = refs[: len(experts_out.inputs)], refs[len(experts_out.inputs) :]
        paid, refs = refs[: len(payload.inputs)], refs[len(payload.inputs) :]
        out, small_out, block_out = refs[:3]
        paid_out, refs = refs[3 : 3 + len(payload.outs)], refs[3 + len(payload.outs) :]
        sml_full, sml_slots, refs = refs[0], refs[1], refs[2:]
        scratch, refs = refs[: 6 * len(groups)], refs[6 * len(groups) :]
        experts_out.take(given, block_out, refs[: len(experts_out.scratch)])
        refs = refs[len(experts_out.scratch) :]
        payload.take(paid, paid_out, refs[: len(payload.scratch)])
        sems = refs[len(payload.scratch) : -1]
        fetch = pltpu.make_async_copy(made_ready, scratch[0], refs[-1])
        fetch.start()
        payload.load()
        barrier = pltpu.get_barrier_semaphore()
        here, beside, across = quad()
        beyond = lax.rem(beside + 2, 4)
        mine = lax.axis_index("fsdp")
        other = 1 - mine
        place = mine * n_ctx + here
        others = []
        for i in range(1, places):
            to = lax.rem(place + i, places)
            others.append((to, {"fsdp": to // n_ctx, "ctx": lax.rem(to, n_ctx)}))
        ahead = [{"tp": peer("tp", n_tp, k)} for k in range(1, n_tp)]
        for device in ahead + [device for _, device in others]:
            pl.semaphore_signal(barrier, inc=1, device_id=device, device_id_type=MESH)
        pl.semaphore_wait(barrier, n_tp - 1 + places - 1)
        gathers = gather_columns(sml, sml_full, "tp", n_tp, sems[0:2])
        experts_out.sums.start()
        blocks = [(other, beyond), (other, beside), (mine, beyond), (mine, beside)]

        def near_copy(g, i):
            prt, come = scratch[6 * g : 6 * g + 2]
            rank, column = blocks[i]
            return described(
                prt.at[rank * n_ctx + column], come.at[i],
                sems[4 + 6 * g : 6 + 6 * g], i, {"ctx": beside},
            )

        def near(g):
            which, start, size = groups[g]
            prt = scratch[6 * g]
            if which is None:
                fetch.wait()
            else:
                left, right = factors[2 * which : 2 * which + 2]

                @pl.loop(0, places)
                def _(i):
                    prt[i] = t_mm(
                        left[:, columns(i, cut)], right[:, start : start + size]
                    ).astype(BF)

            for i in range(4):
                near_copy(g, i).start()

        def chip(g, i, rank, column):
            prt, come = scratch[6 * g : 6 * g + 2]
            near_copy(g, i).wait()
            return prt[rank * n_ctx + column].astype(F32) + come[i].astype(F32)

        def hop_copy(g, i):
            two, far = scratch[6 * g + 2 : 6 * g + 4]
            return described(
                two.at[i], far.at[i], sems[6 + 6 * g : 8 + 6 * g], i, {"fsdp": other}
            )

        def hop(g):
            for i, column in enumerate((across, here)):
                scratch[6 * g + 2][i] = chip(g, i, other, column).astype(BF)
                hop_copy(g, i).start()

        def between(j):
            for turn_of, act in enumerate(
                (lambda: hop(0), lambda: near(1), lambda: hop(1), lambda: near(2))
            ):
                pl.when(j == turn_of)(act)

        near(0)
        payload.go(between)
        hop(2)
        finish(gathers)
        totals = [
            remote(sml_full.at[:, columns(to, cut)], sml_slots.at[i], sems[2:4], i, device)
            for i, (to, device) in enumerate(others)
        ]
        experts_out.prepare()
        lasts = []
        for g in range(len(groups)):
            far, one, last = scratch[6 * g + 3 : 6 * g + 6]
            value = chip(g, 2, mine, across)
            hop_copy(g, 0).wait()
            one[...] = (value + far[0].astype(F32)).astype(BF)
            lasts.append(
                remote(one, last, sems[8 + 6 * g : 10 + 6 * g], 0, {"ctx": across})
            )
            if g == 1:
                experts_out.give_back()
        finish(totals)
        sums = sml_full[:, columns(place, cut)]
        for i in range(places - 1):
            sums = sums + sml_slots[i]
        small_out[...] = sums
        start = 0
        for g, (_, _, size) in enumerate(groups):
            far = scratch[6 * g + 3]
            value = chip(g, 3, mine, here)
            hop_copy(g, 1).wait()
            value = value + far[1].astype(F32)
            out[:, start : start + size] = value
            start += size
        experts_out.mix()
        payload.wait()
        start = 0
        for g, (_, _, size) in enumerate(groups):
            lasts[g].wait()
            at = pl.ds(start, size)
            out[:, at] = out[:, at] + scratch[6 * g + 5][...].astype(F32)
            start += size

    buffers = [pltpu.VMEM((8, width), F32), pltpu.VMEM((places - 1, 8, cut), F32)]
    sems = pair_of_sems(n_tp) + pair_of_sems(places)
    for _, _, size in groups:
        buffers += [
            pltpu.VMEM((places, cut, size), BF),
            pltpu.VMEM((4, cut, size), BF),
            pltpu.VMEM((2, cut, size), BF),
            pltpu.VMEM((2, cut, size), BF),
            pltpu.VMEM((cut, size), BF),
            pltpu.VMEM((cut, size), BF),
        ]
        sems += pair_of_sems(4) + pair_of_sems(2) + pair_of_sems(1)
    return call(
        kernel,
        (
            shape((cut, total_columns), F32),
            shape((8, cut), F32),
            experts_out.out,
            *payload.outs,
        ),
        inputs,
        buffers + experts_out.scratch + payload.scratch + sems + [DMA],
        10,
        "weight_grads",
        left=(
            0,
            len(flat) + 2,
            *range(len(inputs) - len(payload.inputs), len(inputs)),
            -len(payload.outs),
        ),
    )


def experts_back(experts_out, payload, n_tp, n_ctx):
    inputs = [*experts_out.inputs, *payload.inputs]
    given = len(experts_out.inputs)

    def kernel(*refs):
        ins, refs = refs[: len(inputs)], refs[len(inputs) :]
        outs, scratch = refs[: 1 + len(payload.outs)], refs[1 + len(payload.outs) :]
        experts_out.take(ins[:given], outs[0], scratch[: len(experts_out.scratch)])
        payload.take(ins[given:], outs[1:], scratch[len(experts_out.scratch) :])
        greet([("tp", n_tp), ("ctx", n_ctx)])
        experts_out.sums.start()
        payload.go()
        experts_out.prepare()
        experts_out.give_back()
        experts_out.mix()
        payload.wait()

    return call(
        kernel,
        (experts_out.out, *payload.outs),
        inputs,
        experts_out.scratch + payload.scratch,
        9,
        "experts_back",
        left=(0, *range(given, len(inputs)), -len(payload.outs)),
    )


def write_out(experts_grads, attn_grad, plain, n_ctx):
    _, rows, size = experts_grads[0][0].shape
    steps = max(1, rows // 128)
    tile = rows // steps
    many = len(experts_grads)
    plain = list(plain)
    blocks = []
    if attn_grad is not None:
        block = attn_grad.shape[1] // 4
        blocks = [shape((attn_grad.shape[0], block), F32)] * 4
        plain.append(attn_grad)

    def kernel(*refs):
        here = lax.axis_index("ctx")
        ins, outs = refs[: 2 * many + len(plain)], refs[2 * many + len(plain) :]
        for i in range(many):
            came, mine = ins[2 * i : 2 * i + 2]
            outs[i][here] = mine[...].astype(F32)
            for k in range(1, n_ctx):
                outs[i][lax.rem(here + n_ctx - k, n_ctx)] = came[k - 1].astype(F32)
        for i in range(len(plain) - (1 if blocks else 0)):
            outs[many + i][...] = ins[2 * many + i][...]
        for i in range(len(blocks)):
            outs[i - 4][...] = ins[-1][:, i * block : (i + 1) * block]

    def flat(array):
        return pl.BlockSpec((array.shape[0] // steps, array.shape[1]), lambda i: (i, 0))

    in_specs, out_specs, out_shape = [], [], []
    for _ in experts_grads:
        in_specs.append(pl.BlockSpec((n_ctx - 1, tile, size), lambda i: (0, i, 0)))
        in_specs.append(pl.BlockSpec((tile, size), lambda i: (i, 0)))
        out_specs.append(pl.BlockSpec((n_ctx, tile, size), lambda i: (0, i, 0)))
        out_shape.append(shape((n_ctx, rows, size), F32))
    for array in plain[: len(plain) - (1 if blocks else 0)] + blocks:
        out_specs.append(flat(array))
        out_shape.append(shape(array.shape, array.dtype))
    in_specs += [flat(array) for array in plain]
    inputs = [array for pair in experts_grads for array in pair] + plain
    return pl.pallas_call(
        kernel,
        grid=(steps,),
        in_specs=in_specs,
        out_specs=out_specs,
        out_shape=out_shape,
        cost_estimate=pl.CostEstimate(
            flops=0, bytes_accessed=6 * many * n_ctx * rows * size, transcendentals=0
        ),
        name="write_out",
    )(*inputs)


def after(value, *needed):
    return lax.optimization_barrier((value, *needed))[0]


def shards(
    hidden_in,
    out_grad,
    attn_gain,
    w_query,
    w_key,
    w_value,
    w_output,
    ffn_gain,
    w_router,
    w_gate,
    w_up,
    w_down,
    routes,
):
    rows_here, width_tp = hidden_in.shape
    here_tp = lax.axis_index("tp")
    here_ctx = lax.axis_index("ctx")
    here_fsdp = lax.axis_index("fsdp")
    n_fsdp = lax.axis_size("fsdp")
    n_ctx = lax.axis_size("ctx")
    n_tp = lax.axis_size("tp")
    experts = w_gate.shape[0]
    assert experts == n_ctx == 4
    width = width_tp * n_tp
    part = width // n_fsdp
    pair = n_fsdp == 2
    heads_width = w_query.shape[1]

    def swap_fsdp(value):
        return lax.ppermute(value, "fsdp", [(0, 1), (1, 0)])

    def other_parts(weight):
        if pair:
            return [weight, swap_fsdp(weight)]
        return [lax.all_gather(weight, "fsdp", axis=0, tiled=True)]

    def split(values):
        if pair:
            return [
                lax.dynamic_slice_in_dim(values, here_fsdp * part, part, 1),
                lax.dynamic_slice_in_dim(values, (1 - here_fsdp) * part, part, 1),
            ]
        return [values]

    def join(pieces):
        if pair:
            first = here_fsdp == 0
            return jnp.concatenate(
                [jnp.where(first, pieces[0], pieces[1]), jnp.where(first, pieces[1], pieces[0])],
                axis=1,
            )
        return pieces[0]

    def into(values, weights):
        return sum(mm(x, w) for x, w in zip(split(values), weights))

    def back(values, weights):
        return join([mm_t(values, w) for w in weights])

    def my_features(values):
        return lax.dynamic_slice_in_dim(values, here_tp * width_tp, width_tp, values.ndim - 1)

    attn_w = (w_query, w_key, w_value, w_output)
    small = jnp.concatenate(
        [attn_gain[None], ffn_gain[None], w_router.T, jnp.zeros((2, part), BF)], axis=0
    )
    if pair:
        quarter = part // n_ctx
        own_quarter = jnp.concatenate(
            [lax.dynamic_slice_in_dim(w, here_ctx * quarter, quarter, 0) for w in attn_w], axis=1
        )
        other_quarter = swap_fsdp(own_quarter)
        other_small = swap_fsdp(small)
        small_full = join([small, other_small]).astype(F32)
    else:
        other_quarter = None
        small_full = lax.all_gather(small, "fsdp", axis=1, tiled=True).astype(F32)
    inputs_full, up_mine, down_mine = gather_tp(hidden_in, (w_up, w_down), n_tp)
    gate_w = other_parts(lax.dynamic_index_in_dim(w_gate, here_ctx, 0, False))
    up_w = other_parts(up_mine)
    down_w = other_parts(down_mine)
    small_here = my_features(small_full)
    gain_one_here = jnp.broadcast_to(small_here[0:1], small_here.shape)
    gain_two_here = jnp.broadcast_to(small_here[1:2], small_here.shape)
    nothing = [(0, 8 - experts), (0, 0)]
    router_here = jnp.pad(small_here[2 : 2 + experts], nothing)

    relative = (jnp.arange(experts, dtype=jnp.int32) + here_ctx) % experts
    numbers = jnp.arange(8, dtype=jnp.int32)
    onehot = (routes.T[:, None, :] == numbers[None, :, None]).astype(F32)
    named = (routes.T[:, None, :] == relative[None, :, None]).astype(F32)
    names = jnp.pad(named, [(0, 0)] + nothing)
    chosen = jnp.sum(named, axis=0)
    earlier = jnp.triu(jnp.ones((rows_here, rows_here), BF), 1)
    slot_of = mm(chosen.astype(BF), earlier).astype(jnp.int32)
    slots = jnp.arange(CAP, dtype=jnp.int32)
    picks = (slot_of[:, None, :] == slots[None, :, None]) & (chosen[:, None, :] > 0)
    picks = picks.astype(BF).reshape(experts * CAP, rows_here)

    gathered = first_norm(
        inputs_full, out_grad, small_full, attn_w, other_quarter, n_tp, n_ctx
    )
    normed_one, scale_one, grad_full = gathered[:3]
    if pair:
        qkv_w, output_w = gathered[3:]
    else:
        qkv_w, output_w = (
            lax.all_gather(w, "fsdp", axis=0, tiled=True)
            for w in (jnp.concatenate(attn_w[:3], axis=1), w_output)
        )
    positions = here_ctx * rows_here + jnp.arange(rows_here, dtype=jnp.int32)
    cosine, sine = rotary_tables(positions)
    attended, query, kv = attention_forward(mm(normed_one, qkv_w), cosine, sine, n_ctx)
    resid, scale_two, normed_two, grad_rows, token_rows, slot_gates, gates, mix = second_norm(
        mm_t(attended, output_w).astype(BF),
        hidden_in,
        gain_two_here,
        mm(picks, grad_full).astype(BF),
        picks,
        router_here,
        onehot,
        names,
        n_tp,
        n_ctx,
    )
    gate_rows = slot_gates[:, 0, :CAP].reshape(experts * CAP, 1)

    to_gate, to_up, hidden_act = expert_acts(token_rows, gate_w, up_w, n_fsdp)
    d_result = (gate_rows * grad_rows.astype(F32)).astype(BF)

    def away(left, right):
        value = t_mm(split(left)[1], right).astype(BF)
        return value, swap_fsdp(value)

    def payload_of(left, right, come):
        if pair:
            return Payload(n_ctx, product=(left, right, come))
        return Payload(
            n_ctx,
            rows=lax.psum_scatter(
                t_mm(left, right).astype(BF), "fsdp", scatter_dimension=0, tiled=True
            ),
        )

    def came_and_own(outs, payload):
        if pair:
            return tuple(outs)
        own = lax.dynamic_slice_in_dim(payload.inputs[0], here_ctx * payload.cut, payload.cut, 0)
        return outs[0], own

    down_come = gate_come = up_come = None
    if pair:
        down_away, down_come = away(d_result, hidden_act)
        grad_rows = after(grad_rows, down_away)
    d_hidden = into(grad_rows, down_w)
    gate_dot = jnp.sum(hidden_act.astype(F32) * d_hidden, axis=-1).reshape(experts, CAP)
    gate_dot = jnp.broadcast_to(
        jnp.pad(gate_dot, [(0, 0), (0, rows_here - CAP)])[:, None, :], (experts, 8, rows_here)
    )
    d_hidden = gate_rows * d_hidden
    d_gate_act = (d_hidden * to_gate).astype(BF)
    d_up_act = (d_hidden * to_up).astype(BF)
    if pair:
        gate_away, gate_come = away(token_rows, d_gate_act)

    acts = (d_gate_act, d_up_act, hidden_act)
    if pair:
        acts = lax.optimization_barrier((*acts, gate_away))[:3]
    d_resid, d_attn_here, gain_two_part, d_logits, made, *up_away = second_norm_back(
        acts,
        (gate_w, up_w, down_w),
        token_rows,
        gate_dot,
        picks,
        gates,
        onehot,
        names,
        router_here,
        resid,
        scale_two,
        gain_two_here,
        out_grad,
        n_tp,
        n_ctx,
    )
    if pair:
        up_come = swap_fsdp(up_away[0])

    payload = payload_of(d_result, hidden_act, down_come)
    early = (RowSums(made, 2 * CAP, 2 * CAP, n_tp), made)
    d_attn, d_qkv, made_early, *outs = attention_backward(
        d_attn_here, output_w, query, kv, cosine, -sine, early, payload, n_tp, n_ctx
    )
    grad_down = came_and_own(outs, payload)
    payload = payload_of(token_rows, d_gate_act, gate_come)
    in_grad, gain_one_part, returned, *outs = first_norm_back(
        d_qkv,
        qkv_w,
        hidden_in,
        scale_one,
        gain_one_here,
        d_resid,
        made_early,
        payload,
        n_tp,
        n_ctx,
    )
    grad_gate = came_and_own(outs, payload)
    payload = payload_of(token_rows, d_up_act, up_come)

    small_part = jnp.concatenate(
        [
            gain_one_part[:1],
            gain_two_part[:1],
            mm(d_logits[:experts].astype(BF), my_features(normed_two)),
            jnp.zeros((6 - experts, width_tp), F32),
        ],
        axis=0,
    )
    written = write_out([grad_gate, grad_down], None, (), n_ctx)
    if pair:
        small_part = after(small_part, *written)
    grad_gate, grad_down = written
    experts_out = ExpertsOut(made, returned, picks, mix, resid, n_tp, n_ctx)
    if pair:
        grad_attn, small_grad, block_out, *outs = weight_grads(
            t_mm(d_attn, attended).astype(BF),
            [(normed_one, d_qkv)],
            [(None, 0, heads_width), (0, 0, 2 * heads_width), (0, 2 * heads_width, heads_width)],
            small_part,
            payload,
            experts_out,
            n_tp,
            n_ctx,
        )
    else:
        grad_attn = jnp.concatenate([t_mm(d_attn, attended), t_mm(normed_one, d_qkv)], axis=1)
        scatter = partial(
            lax.psum_scatter, axis_name=("fsdp", "ctx"), scatter_dimension=0, tiled=True
        )
        grad_attn = scatter(grad_attn.astype(BF)).astype(F32)
        small_grad = lax.all_gather(small_part, "tp", axis=1, tiled=True)
        small_grad = scatter(small_grad.T).T
        block_out, *outs = experts_back(experts_out, payload, n_tp, n_ctx)
    grad_up = came_and_own(outs, payload)
    grad_up, block_out, in_grad, grad_output, grad_query, grad_key, grad_value = write_out(
        [grad_up], grad_attn, (block_out, in_grad), n_ctx
    )
    return (
        block_out,
        in_grad,
        small_grad[0],
        grad_query,
        grad_key,
        grad_value,
        grad_output,
        small_grad[1],
        small_grad[2 : 2 + experts].T,
        grad_gate,
        grad_up,
        grad_down,
    )


def solution(mesh):
    rows = ("fsdp", "ctx")
    placed = (
        P(rows, "tp"),
        P(rows, "tp"),
        P("fsdp"),
        P("fsdp", "tp"),
        P("fsdp", "tp"),
        P("fsdp", "tp"),
        P("fsdp", "tp"),
        P("fsdp"),
        P("fsdp", None),
        P(None, "fsdp", "tp"),
        P(None, "fsdp", "tp"),
        P(None, "fsdp", "tp"),
        P(rows, None),
    )
    return jax.shard_map(
        shards,
        mesh=mesh,
        in_specs=placed,
        out_specs=(
            P(rows, "tp"),
            P(rows, "tp"),
            P(rows),
            P(rows, "tp"),
            P(rows, "tp"),
            P(rows, "tp"),
            P(rows, "tp"),
            P(rows),
            P(rows, None),
            P(None, rows, "tp"),
            P(None, rows, "tp"),
            P(None, rows, "tp"),
        ),
        check_vma=False,
    )
```

```python
from functools import partial
import math

import jax
import jax.numpy as jnp
from jax import lax
from jax.experimental import pallas as pl
from jax.experimental.pallas import tpu as pltpu
from jax.sharding import PartitionSpec as P

HD = 128
CAP = 160


EPS = 1e-05
THETA = 10000.0
NEG = -1e30
BF = jnp.bfloat16
F32 = jnp.float32


def mm(left, right):
    return jnp.dot(left, right, preferred_element_type=F32)


def mm_t(left, right):
    return lax.dot_general(left, right, (((1,), (1,)), ((), ())), preferred_element_type=F32)


def t_mm(left, right):
    return lax.dot_general(left, right, (((0,), (0,)), ((), ())), preferred_element_type=F32)


def rotary_tables(positions):
    half_size = HD // 2
    frequency = THETA ** (-(jnp.arange(half_size, dtype=F32) * 2.0 / HD))
    angles = positions.astype(F32)[:, None] * frequency[None, :]
    cosine, sine = jnp.cos(angles), jnp.sin(angles)
    return jnp.concatenate([cosine, cosine], axis=1), jnp.concatenate([-sine, sine], axis=1)


MESH = pl.DeviceIdType.MESH
VM = pl.BlockSpec(memory_space=pltpu.VMEM)
DMA = pltpu.SemaphoreType.DMA


def peer(axis, n, k):
    return lax.rem(lax.axis_index(axis) + k, n)


def greet(groups):
    barrier = pltpu.get_barrier_semaphore()
    for axis, n in groups:
        for k in range(1, n):
            pl.semaphore_signal(
                barrier, inc=1, device_id={axis: peer(axis, n, k)}, device_id_type=MESH
            )
    pl.semaphore_wait(barrier, sum(n - 1 for _, n in groups))


def described(source, target, sems, i, to):
    return pltpu.make_async_remote_copy(
        src_ref=source,
        dst_ref=target,
        send_sem=sems[0].at[i],
        recv_sem=sems[1].at[i],
        device_id=to,
        device_id_type=MESH,
    )


def remote(source, target, sems, i, to):
    copy = described(source, target, sems, i, to)
    copy.start()
    return copy


def send(source, target, axis, n, k, sems):
    return remote(source, target, sems, k - 1, {axis: peer(axis, n, k)})


def columns(n, size):
    return pl.ds(pl.multiple_of(n * size, 128), size)


def stretch(n, size):
    return pl.ds(pl.multiple_of(n * size, 16), size)


def gather_columns(own, full, axis, n, sems):
    size = own.shape[1]
    place = full.at[:, columns(lax.axis_index(axis), size)]
    copies = [send(own, place, axis, n, k, sems) for k in range(1, n)]
    place[...] = own[...]
    return copies


def scatter_columns(part, slots, axis, n, sems):
    size = slots.shape[2]
    return [
        send(part.at[:, columns(peer(axis, n, k), size)], slots.at[k - 1], axis, n, k, sems)
        for k in range(1, n)
    ]


def finish(copies):
    for copy in copies:
        copy.wait()


class Payload:

    def __init__(self, n_ctx, rows=None, product=None):
        self.n_ctx = n_ctx
        self.product = product is not None
        self.inputs = list(product) if self.product else [rows]
        last = self.inputs[-1]
        self.rows, self.hidden = last.shape
        self.cut = self.rows // n_ctx
        self.outs = [shape((n_ctx - 1, self.cut, self.hidden), BF)]
        self.scratch = pair_of_sems(n_ctx)
        if self.product:
            self.outs.append(shape((self.cut, self.hidden), BF))
            self.scratch += [
                pltpu.VMEM((self.rows, self.hidden), BF),
                pltpu.VMEM((self.rows, self.hidden), BF),
                pltpu.VMEM((self.inputs[0].shape[0], self.rows), BF),
                pltpu.VMEM(self.inputs[1].shape, BF),
                DMA((3,)),
            ]

    def take(self, ins, outs, scratch):
        self.ins, self.out_refs, self.held = ins, outs, scratch

    def fetches(self):
        left, right, other = self.ins
        mine = left.at[:, columns(lax.axis_index("fsdp"), self.rows)]
        return [
            pltpu.make_async_copy(source, self.held[i], self.held[6].at[j])
            for j, (source, i) in enumerate([(mine, 4), (right, 5), (other, 2)])
        ]

    def load(self):
        if self.product:
            for copy in self.fetches():
                copy.start()

    def copy(self, k):
        to = peer("ctx", self.n_ctx, k)
        source = self.held[3] if self.product else self.ins[0]
        return described(
            source.at[stretch(to, self.cut), :], self.out_refs[0].at[k - 1],
            self.held[0:2], k - 1, {"ctx": to},
        )

    def go(self, between=lambda j: None):
        n_ctx, cut = self.n_ctx, self.cut
        if not self.product:
            for k in (2, 3, 1):
                self.copy(k).start()
            return
        finish(self.fetches())

        @pl.loop(0, n_ctx)
        def _(j):
            k = lax.rem(j + 2, n_ctx)
            to = peer("ctx", n_ctx, k)
            value = t_mm(self.held[4][:, columns(to, cut)], self.held[5][...])
            value = value + self.held[2][stretch(to, cut), :].astype(F32)
            self.held[3][stretch(to, cut), :] = value.astype(BF)

            @pl.when(j != n_ctx - 2)
            def _():
                self.copy(k).start()

            between(j)

    def wait(self):
        if self.product:
            self.out_refs[1][...] = self.held[3][stretch(lax.axis_index("ctx"), self.cut), :]
        for k in range(1, self.n_ctx):
            self.copy(k).wait()


class RowSums:

    def __init__(self, made, first, count, n_tp):
        self.n_tp, self.first = n_tp, first
        self.shape = (count, made.shape[1] // n_tp)
        self.scratch = [
            pltpu.VMEM((n_tp - 1, *self.shape), BF),
            pltpu.VMEM(self.shape, BF),
            DMA,
        ] + pair_of_sems(n_tp)

    def take(self, made, scratch):
        self.made, self.held = made, scratch

    def rows(self, rank):
        return self.made.at[pl.ds(self.first, self.shape[0]), columns(rank, self.shape[1])]

    def mine(self):
        return pltpu.make_async_copy(
            self.rows(lax.axis_index("tp")), self.held[1], self.held[2]
        )

    def start(self):
        self.mine().start()
        n = self.n_tp
        self.copies = [
            send(self.rows(peer("tp", n, k)), self.held[0].at[k - 1], "tp", n, k, self.held[3:5])
            for k in range(1, n)
        ]

    def total(self):
        self.mine().wait()
        finish(self.copies)
        value = self.held[1][...].astype(F32)
        for k in range(1, self.n_tp):
            value = value + self.held[0][k - 1].astype(F32)
        return value


def quad():
    here = lax.axis_index("ctx")
    return here, here + 1 - 2 * lax.rem(here, 2), lax.rem(here + 2, 4)


def gather_square(own, places, sems, between, local=None):
    cuts = own.shape[1] // 512
    here, beside, across = quad()
    first, second, third = [], [], []
    for i in range(cuts):
        piece = own.at[:, pl.ds(i * 512, 512)]
        first.append(remote(piece, places(here, i), sems, 3 * i, {"ctx": across}))
        second.append(remote(piece, places(here, i), sems, 3 * i + 1, {"ctx": beside}))
        if local is None:
            places(here, i)[...] = piece[...]
        else:
            pltpu.make_async_copy(piece, places(here, i), local.at[i]).start()
    between()
    for i in range(cuts):
        first[i].wait()
        third.append(
            remote(places(across, i), places(across, i), sems, 3 * i + 2, {"ctx": beside})
        )
    finish(second)
    finish(third)
    if local is not None:
        for i in range(cuts):
            piece = own.at[:, pl.ds(i * 512, 512)]
            pltpu.make_async_copy(piece, places(here, i), local.at[i]).wait()


def row_sums(values):
    ones = jnp.ones((8, values.shape[1]), F32)
    return lax.dot_general(
        ones,
        values,
        (((1,), (1,)), ((), ())),
        precision=lax.Precision.HIGHEST,
        preferred_element_type=F32,
    )


def as_column(rows, weight):
    return lax.dot_general(
        rows,
        weight,
        (((0,), (0,)), ((), ())),
        precision=lax.Precision.HIGHEST,
        preferred_element_type=F32,
    )


def eighth():
    return jnp.full((8, 128), 0.125, F32)


def total_over(sums, mine, slots, axis, n, sems):
    mine[...] = sums
    copies = [send(mine, slots.at[k - 1], axis, n, k, sems) for k in range(1, n)]
    finish(copies)
    total = sums
    for k in range(1, n):
        total = total + slots[k - 1]
    return total


def call(kernel, out_shape, inputs, scratch, collective, name, left=()):
    anywhere = pl.BlockSpec(memory_space=pl.ANY)
    outs = out_shape if isinstance(out_shape, tuple) else (out_shape,)
    specs = [anywhere if i - len(outs) in left else VM for i in range(len(outs))]
    return pl.pallas_call(
        kernel,
        out_shape=out_shape,
        in_specs=[anywhere if i in left else VM for i in range(len(inputs))],
        out_specs=tuple(specs) if isinstance(out_shape, tuple) else specs[0],
        scratch_shapes=scratch,
        compiler_params=pltpu.CompilerParams(collective_id=collective, has_side_effects=True),
        cost_estimate=pl.CostEstimate(flops=0, bytes_accessed=0, transcendentals=0),
        name=name,
    )(*inputs)


def shape(dims, dtype):
    return jax.ShapeDtypeStruct(dims, dtype)


def pair_of_sems(n):
    return [DMA((n,)), DMA((n,))]


def gather_tp(value, stacks, n_tp):
    rows, size = value.shape
    many = len(stacks)
    member = stacks[0].shape[1:]

    def kernel(own, *refs):
        stk, full, outs = refs[:many], refs[many], refs[many + 1 : 2 * many + 1]
        held, loads, stores = refs[2 * many + 1 : 2 * many + 4]
        sems = refs[2 * many + 4 :]
        here = lax.axis_index("ctx")
        into = [
            pltpu.make_async_copy(stk[i].at[here], held.at[i], loads.at[i]) for i in range(many)
        ]
        away = [pltpu.make_async_copy(held.at[i], outs[i], stores.at[i]) for i in range(many)]
        for copy in into:
            copy.start()
        greet([("tp", n_tp)])
        copies = gather_columns(own, full, "tp", n_tp, sems)
        for i in range(many):
            into[i].wait()
            away[i].start()
        finish(copies)
        finish(away)

    return call(
        kernel,
        (
            shape((rows, size * n_tp), value.dtype),
            *(shape(member, stack.dtype) for stack in stacks),
        ),
        (value, *stacks),
        [pltpu.VMEM((many, *member), BF), DMA((many,)), DMA((many,))] + pair_of_sems(n_tp),
        1,
        "gather_tp",
        left=tuple(range(1, many + 1)) + tuple(range(-many, 0)),
    )


def first_norm(full, grad, gain, weights, quarter, n_tp, n_ctx):
    rows, width = full.shape
    with_quarter = quarter is not None

    def kernel(*refs):
        hid, grd, gn = refs[:3]
        refs = refs[3:]
        if with_quarter:
            wgts, refs = refs[: len(weights)], refs[len(weights) :]
            qrt, out, scale, grd_full, many_full, last_full, held, local, loads, stores = refs[:10]
            sems = refs[10:]
            half, inner = wgts[0].shape
            last = len(wgts) - 1
            mine = lax.axis_index("fsdp")

            def target(i, first_row, count):
                at = pl.ds(pl.multiple_of(first_row, 16), count)
                if i == last:
                    return last_full.at[at, :]
                return many_full.at[at, pl.ds(i * inner, inner)]

            into = [
                pltpu.make_async_copy(wgts[i], held.at[i], loads.at[i]) for i in range(len(wgts))
            ]
            away = [
                pltpu.make_async_copy(held.at[i], target(i, mine * half, half), stores.at[i])
                for i in range(len(wgts))
            ]
            for copy in into:
                copy.start()
            greet([("tp", n_tp), ("ctx", n_ctx)])
        else:
            out, scale, grd_full = refs[:3]
            sems = refs[3:]
            greet([("tp", n_tp)])
        grads = gather_columns(grd, grd_full, "tp", n_tp, sems[0:2])

        def norm():
            values = hid[...].astype(F32)
            mean = jnp.sum(values * values, axis=-1, keepdims=True) * (1.0 / width)
            factor = lax.rsqrt(mean + EPS)
            scale[...] = jnp.broadcast_to(factor, scale.shape)
            out[...] = (values * factor * gn[0:1, :]).astype(BF)

        if with_quarter:
            count = qrt.shape[0]

            def work():
                for i in range(len(wgts)):
                    into[i].wait()
                    away[i].start()
                norm()

            def places(rank, i):
                return target(i, (1 - mine) * half + rank * count, count)

            gather_square(qrt, places, sems[2:4], work, local)
            finish(away)
        else:
            norm()
        finish(grads)

    outs = [shape((rows, width), BF), shape((rows, 128), F32), shape((rows, width), BF)]
    inputs = [full, grad, gain]
    scratch, left = [], ()
    if with_quarter:
        half, inner = weights[0].shape
        many = len(weights)
        assert inner == 512
        outs.append(shape((2 * half, (many - 1) * inner), BF))
        outs.append(shape((2 * half, inner), BF))
        inputs += [*weights, quarter]
        scratch = [pltpu.VMEM((many, half, inner), BF), DMA((many,)), DMA((many,)), DMA((many,))]
        left = tuple(range(3, 3 + many)) + (-2, -1)
    return call(
        kernel,
        tuple(outs),
        inputs,
        scratch + pair_of_sems(n_tp) + pair_of_sems(12),
        7,
        "first_norm",
        left=left,
    )


def turn(values, cosine, sine):
    return values * cosine + pltpu.roll(values, HD // 2, axis=1) * sine


def softmax_rows(query, key, first_row):
    scores = mm_t(query, key) * (1.0 / math.sqrt(HD))
    rows = first_row + lax.broadcasted_iota(jnp.int32, scores.shape, 0)
    cols = lax.broadcasted_iota(jnp.int32, scores.shape, 1)
    scores = jnp.where(cols <= rows, scores, NEG)
    top = jnp.max(scores, axis=-1, keepdims=True)
    weights = jnp.exp(scores - top)
    return weights / jnp.sum(weights, axis=-1, keepdims=True)


def attention_forward(qkv, cosine, sine, n_ctx):
    rows = qkv.shape[0]
    width = qkv.shape[1] // 3
    heads = width // HD

    def kernel(prj, cs, sn, out, qry, full, own, *sems):
        greet([("ctx", n_ctx)])
        here = lax.axis_index("ctx")

        @pl.loop(0, heads)
        def _(h):
            own[:, columns(h, HD)] = turn(
                prj[:, columns(h + heads, HD)], cs[...], sn[...]
            ).astype(BF)
            own[:, columns(h + heads, HD)] = prj[:, columns(h + 2 * heads, HD)].astype(BF)

        def queries():
            @pl.loop(0, heads)
            def _(h):
                qry[:, columns(h, HD)] = turn(prj[:, columns(h, HD)], cs[...], sn[...]).astype(BF)

        def places(rank, i):
            return full.at[stretch(rank, rows), pl.ds(i * 512, 512)]

        gather_square(own, places, sems, queries)

        @pl.loop(0, heads)
        def _(h):
            probs = softmax_rows(qry[:, columns(h, HD)], full[:, columns(h, HD)], here * rows)
            out[:, columns(h, HD)] = mm(
                probs.astype(BF), full[:, columns(h + heads, HD)]
            ).astype(BF)

    return call(
        kernel,
        (
            shape((rows, width), BF),
            shape((rows, width), BF),
            shape((rows * n_ctx, 2 * width), BF),
        ),
        (qkv, cosine, sine),
        [pltpu.VMEM((rows, 2 * width), BF)] + pair_of_sems(6 * width // 512),
        2,
        "attention_forward",
    )


def second_norm(part, hidden, gain, slabs, picks, router, onehot, names, n_tp, n_ctx):
    rows, size = hidden.shape
    width = size * n_tp
    experts = n_ctx

    def kernel(
        prt, hid, gn, slb, pck, rtr, one, nms,
        resid, scale, out, moved, tokens, slot_gates, gates, mix,
        slots, mine, sums, mine_two, sums_two, low, sent, own_gates, *sems
    ):
        greet([("tp", n_tp), ("ctx", n_ctx)])
        here = lax.axis_index("tp")
        copies = scatter_columns(prt, slots, "tp", n_tp, sems[0:2])
        others = [
            send(
                slb.at[pl.ds(k * CAP, CAP)], moved.at[pl.ds(k * CAP, CAP)],
                "ctx", n_ctx, k, sems[6:8],
            )
            for k in range(1, n_ctx)
        ]
        moved[0:CAP] = slb[0:CAP]
        total = prt[:, columns(here, size)].astype(F32)
        finish(copies)
        for k in range(1, n_tp):
            total = total + slots[k - 1].astype(F32)
        total = hid[...].astype(F32) + total
        resid[...] = total
        square = total_over(row_sums(total * total), mine, sums, "tp", n_tp, sems[2:4])
        factor = lax.rsqrt(as_column(square, eighth()) * (1.0 / width) + EPS)
        scale[...] = factor
        low[...] = (resid[...] * factor[:, 0:1] * gn[0:1, :]).astype(BF)
        partial_logits = mm_t(rtr[...].astype(BF), low[...])
        mine_two[...] = partial_logits
        logit_copies = [
            send(mine_two, sums_two.at[k - 1], "tp", n_tp, k, sems[12:14]) for k in range(1, n_tp)
        ]
        gather_columns(low, out, "tp", n_tp, sems[4:6])

        def route():
            finish(logit_copies)
            logits = partial_logits
            for k in range(1, n_tp):
                logits = logits + sums_two[k - 1]
            named = [jnp.sum(one[j] * logits, axis=0, keepdims=True) for j in range(2)]
            top = jnp.maximum(named[0], named[1])
            powers = [jnp.exp(value - top) for value in named]
            both = powers[0] + powers[1]
            gate = [value / both for value in powers]
            mixed = gate[0] * nms[0] + gate[1] * nms[1]
            mix[...] = mixed
            order = lax.broadcasted_iota(jnp.int32, (8, rows), 0)
            gates[...] = jnp.where(order == 0, gate[0], jnp.where(order == 1, gate[1], 0.0))
            own_gates[...] = jnp.zeros(own_gates.shape, F32)
            for k in range(experts):
                own_gates[k, :, 0:CAP] = lax.dot_general(
                    jnp.broadcast_to(mixed[k : k + 1], (8, rows)),
                    pck[k * CAP : (k + 1) * CAP].astype(F32),
                    (((1,), (1,)), ((), ())),
                    precision=lax.Precision.HIGHEST,
                    preferred_element_type=F32,
                )
            slot_gates[0] = own_gates[0]
            for k in range(1, n_ctx):
                others.append(
                    send(own_gates.at[k], slot_gates.at[k], "ctx", n_ctx, k, sems[10:12])
                )


        def slab(k, step):
            at = columns(peer("tp", n_tp, n_tp - step), size)
            return described(
                sent.at[step, pl.ds(k * CAP, CAP)], tokens.at[pl.ds(k * CAP, CAP), at],
                sems[8:10], step * n_ctx + k, {"ctx": peer("ctx", n_ctx, k)},
            )

        def dispatch(step, block):
            sent[step] = mm(pck[...], block).astype(BF)
            tokens[0:CAP, columns(peer("tp", n_tp, n_tp - step), size)] = sent[step, 0:CAP]
            for k in (2, 3, 1):
                slab(k, step).start()

        route()

        @pl.loop(0, n_tp)
        def _(step):
            @pl.when(step > 0)
            def _():
                described(
                    low, out.at[:, columns(here, size)], sems[4:6], step - 1,
                    {"tp": peer("tp", n_tp, step)},
                ).wait()

            dispatch(step, out[:, columns(peer("tp", n_tp, n_tp - step), size)])

        for step in range(n_tp):
            for k in (2, 3, 1):
                slab(k, step).wait()
        finish(others)

    return call(
        kernel,
        (
            shape((rows, size), F32),
            shape((rows, 128), F32),
            shape((rows, width), BF),
            shape(slabs.shape, BF),
            shape(slabs.shape, BF),
            shape((experts, 8, rows), F32),
            shape((8, rows), F32),
            shape((8, rows), F32),
        ),
        (part, hidden, gain, slabs, picks, router, onehot, names),
        [
            pltpu.VMEM((n_tp - 1, rows, size), BF),
            pltpu.VMEM((8, rows), F32),
            pltpu.VMEM((n_tp - 1, 8, rows), F32),
            pltpu.VMEM((8, rows), F32),
            pltpu.VMEM((n_tp - 1, 8, rows), F32),
            pltpu.VMEM((rows, size), BF),
            pltpu.VMEM((n_tp, experts * CAP, size), BF),
            pltpu.VMEM((experts, 8, rows), F32),
        ]
        + pair_of_sems(n_tp) * 3
        + pair_of_sems(n_ctx)
        + pair_of_sems(n_tp * n_ctx)
        + pair_of_sems(n_ctx)
        + pair_of_sems(n_tp),
        3,
        "second_norm",
    )


def expert_acts(tokens, gate_w, up_w, n_fsdp):
    rows, width = tokens.shape
    hidden = gate_w[0].shape[1]
    count = len(gate_w)
    part = gate_w[0].shape[0]
    chunk = 256
    per = part // chunk
    steps = count * per
    pair = count == 2

    def kernel(tok, *refs):
        wgt = [refs[:count], refs[count : 2 * count]]
        to_gate, to_up, hid, buffer, loads = refs[2 * count :]
        first = lax.axis_index("fsdp") if pair else 0

        def load(step):
            slot = lax.rem(step, 2)
            at = stretch(lax.rem(step, per), chunk)
            for lane in range(2):
                for i in range(count):

                    @pl.when(step // per == i)
                    def _():
                        pltpu.make_async_copy(
                            wgt[lane][i].at[at], buffer.at[slot, lane], loads.at[slot, lane]
                        ).start()

        load(0)
        to_gate[...] = jnp.zeros_like(to_gate)
        to_up[...] = jnp.zeros_like(to_up)

        @pl.loop(0, steps)
        def _(step):
            slot = lax.rem(step, 2)
            for lane in range(2):
                pltpu.make_async_copy(
                    wgt[lane][0].at[pl.ds(0, chunk)], buffer.at[slot, lane], loads.at[slot, lane]
                ).wait()

            @pl.when(step + 1 < steps)
            def _():
                load(step + 1)

            which = lax.rem(first + step // per, count)
            column = which * part + lax.rem(step, per) * chunk
            values = tok[:, pl.ds(pl.multiple_of(column, 128), chunk)]
            to_gate[...] += mm(values, buffer[slot, 0])
            to_up[...] += mm(values, buffer[slot, 1])

        @pl.loop(0, rows // 32)
        def _(i):
            at = stretch(i, 32)
            a, b = to_gate[at, :], to_up[at, :]
            sigma = 1.0 / (1.0 + jnp.exp(-a))
            silu = a * sigma
            hid[at, :] = (silu * b).astype(BF)
            to_up[at, :] = silu
            to_gate[at, :] = b * sigma * (1.0 + a * (1.0 - sigma))

    anywhere = pl.BlockSpec(memory_space=pl.ANY)
    return pl.pallas_call(
        kernel,
        out_shape=(
            shape((rows, hidden), F32),
            shape((rows, hidden), F32),
            shape((rows, hidden), BF),
        ),
        in_specs=[VM] + [anywhere] * (2 * count),
        out_specs=(VM, VM, VM),
        scratch_shapes=[pltpu.VMEM((2, 2, chunk, hidden), BF), DMA((2, 2))],
        cost_estimate=pl.CostEstimate(flops=0, bytes_accessed=0, transcendentals=0),
        name="expert_acts",
    )(tokens, *gate_w, *up_w)


def second_norm_back(
    acts, weights, tokens, dots, picks, gates, onehot, names, router, resid, scale, gain, grad,
    n_tp, n_ctx,
):
    rows, size = resid.shape
    width = size * n_tp
    experts = n_ctx
    hidden = acts[0].shape[1]
    count = len(weights[0])
    part = weights[0][0].shape[0]

    def kernel(*refs):
        dga, dup, hid_far = refs[:3]
        wgt = [refs[3 + i * count : 3 + (i + 1) * count] for i in range(3)]
        refs = refs[3 + 3 * count :]
        tok_far, dts, pck, gts, one, nms, rtr, rsd, scl, gn, grd = refs[:11]
        d_resid, low, d_gain, d_logits, out_rows = refs[11:16]
        refs = refs[16:]
        if count == 2:
            up_away, up_held, up_sem = refs[:1] + refs[1:3]
            refs = refs[3:]
        (
            drw, eo, buffer, back, back_dots, parts, slots, mine, sums, mine_two, sums_two, loads,
            out_sem, hid, tok, late,
        ) = refs[:16]
        sems = refs[16:]
        fetches = [
            pltpu.make_async_copy(hid_far, hid, late.at[0]),
            pltpu.make_async_copy(tok_far, tok, late.at[1]),
        ]
        here = lax.axis_index("tp")
        first = lax.axis_index("fsdp")

        def load(which, rank, slot, lane):
            feature = rank * size
            inside = pl.ds(pl.multiple_of(lax.rem(feature, part), 16), size)
            target = buffer.at[slot, lane]
            if count == 1:
                pltpu.make_async_copy(
                    wgt[which][0].at[inside], target, loads.at[slot, lane]
                ).start()
                return
            own = feature // part == first

            @pl.when(own)
            def _():
                pltpu.make_async_copy(
                    wgt[which][0].at[inside], target, loads.at[slot, lane]
                ).start()

            @pl.when(jnp.logical_not(own))
            def _():
                pltpu.make_async_copy(
                    wgt[which][1].at[inside], target, loads.at[slot, lane]
                ).start()

        def loaded(which, slot, lane):
            pltpu.make_async_copy(
                wgt[which][0].at[pl.ds(0, size)], buffer.at[slot, lane], loads.at[slot, lane]
            ).wait()

        load(0, peer("tp", n_tp, 1), 0, 0)
        load(1, peer("tp", n_tp, 1), 0, 1)
        for copy in fetches:
            copy.start()
        greet([("tp", n_tp), ("ctx", n_ctx)])
        small = []
        for k in range(1, n_ctx):
            small.append(
                send(dts.at[k], back_dots.at[k - 1], "ctx", n_ctx, n_ctx - k, sems[0:2])
            )

        def slab(k, rank, step):
            at = columns(rank, size)
            return described(
                drw.at[pl.ds(k * CAP, CAP), at], back.at[k - 1, :, at],
                sems[2:4], step * n_ctx + k - 1, {"ctx": peer("ctx", n_ctx, n_ctx - k)},
            )

        @pl.loop(0, n_tp)
        def _(step):
            rank = peer("tp", n_tp, step + 1)
            slot = lax.rem(step, 2)
            loaded(0, slot, 0)
            loaded(1, slot, 1)

            @pl.when(step + 1 < n_tp)
            def _():
                load(0, peer("tp", n_tp, step + 2), 1 - slot, 0)
                load(1, peer("tp", n_tp, step + 2), 1 - slot, 1)

            drw[:, columns(rank, size)] = (
                mm_t(dga[...], buffer[slot, 0]) + mm_t(dup[...], buffer[slot, 1])
            ).astype(BF)
            for k in (2, 3, 1):
                slab(k, rank, step).start()

        def combined(step):
            rank = peer("tp", n_tp, step)
            at = columns(rank, size)
            for k in (2, 3, 1):
                slab(k, rank, step - 1).wait()
            block = t_mm(pck[0:CAP], drw[0:CAP, at])
            for k in range(1, experts):
                block = block + t_mm(pck[k * CAP : (k + 1) * CAP], back[k - 1, :, at])
            return block

        def give(step):
            return described(
                parts.at[step - 1], slots.at[step - 1], sems[6:8], step - 1,
                {"tp": peer("tp", n_tp, step)},
            )

        def pass_on(begin, end):
            @pl.loop(begin, end)
            def _(step):
                parts[step - 1] = combined(step).astype(BF)
                give(step).start()

        load(2, 0, 0, 0)
        finish(small)
        order = lax.broadcasted_iota(jnp.int32, (8, rows), 0)
        own = jnp.zeros((8, rows), F32)
        for k in range(experts):
            by_slot = dts[0] if k == 0 else back_dots[k - 1]
            by_row = lax.dot_general(
                by_slot[:, 0:CAP],
                pck[k * CAP : (k + 1) * CAP].astype(F32),
                (((1,), (0,)), ((), ())),
                precision=lax.Precision.HIGHEST,
                preferred_element_type=F32,
            )
            own = own + jnp.where(order == k, by_row, 0.0)
        mine[...] = own
        shared = [
            send(mine, sums.at[k - 1], "tp", n_tp, k, sems[4:6]) for k in range(1, n_tp)
        ]
        pass_on(1, n_tp - 1)

        finish(fetches)

        @pl.loop(0, n_tp)
        def _(rank):
            slot = lax.rem(rank, 2)
            loaded(2, slot, 0)

            @pl.when(rank + 1 < n_tp)
            def _():
                load(2, rank + 1, 1 - slot, 0)

            eo[:, columns(rank, size)] = mm_t(hid[...], buffer[slot, 0]).astype(BF)

        pltpu.make_async_copy(eo, out_rows, out_sem).start()
        pass_on(n_tp - 1, n_tp)
        if count == 2:

            @pl.loop(0, part // 256)
            def _(i):
                at = pl.ds(pl.multiple_of((1 - first) * part + i * 256, 128), 256)
                up_held[stretch(i, 256), :] = t_mm(tok[:, at], dup[...]).astype(BF)

            pltpu.make_async_copy(up_held, up_away, up_sem).start()
        finish(shared)
        gate_grad = mine[...]
        for k in range(1, n_tp):
            gate_grad = gate_grad + sums[k - 1]
        both = [jnp.sum(nms[j] * gate_grad, axis=0, keepdims=True) for j in range(2)]
        gate = [gts[j : j + 1, :] for j in range(2)]
        mean = gate[0] * both[0] + gate[1] * both[1]
        logits = sum(gate[j] * (both[j] - mean) * one[j] for j in range(2))
        d_logits[...] = logits

        copies = [give(step) for step in range(1, n_tp)]
        total = combined(n_tp)
        total = total + lax.dot_general(
            logits.astype(BF),
            rtr[...].astype(BF),
            (((0,), (0,)), ((), ())),
            preferred_element_type=F32,
        )
        finish(copies)
        for k in range(1, n_tp):
            total = total + slots[k - 1].astype(F32)
        factor = scl[:, 0:1]
        unit = rsd[...] * factor
        d_gain[...] = jnp.broadcast_to(jnp.sum(total * unit, axis=0, keepdims=True), d_gain.shape)
        gained = total * gn[0:1, :]
        d_resid[...] = gained
        dot = total_over(row_sums(unit * gained), mine_two, sums_two, "tp", n_tp, sems[8:10])
        dot = as_column(dot, eighth())[:, 0:1] * (1.0 / width)
        result = grd[...].astype(F32) + factor * (d_resid[...] - rsd[...] * factor * dot)
        d_resid[...] = result
        low[...] = result.astype(BF)
        pltpu.make_async_copy(eo, out_rows, out_sem).wait()
        if count == 2:
            pltpu.make_async_copy(up_held, up_away, up_sem).wait()

    outs = [
        shape((rows, size), F32),
        shape((rows, size), BF),
        shape((8, size), F32),
        shape((8, rows), F32),
        shape((experts * CAP, width), BF),
    ]
    held = []
    if count == 2:
        outs.append(shape((part, hidden), BF))
        held = [pltpu.VMEM((part, hidden), BF), DMA]
    flat = [array for group in weights for array in group]
    return call(
        kernel,
        tuple(outs),
        (*acts, *flat, tokens, dots, picks, gates, onehot, names, router, resid, scale, gain, grad),
        held
        + [
            pltpu.VMEM((experts * CAP, width), BF),
            pltpu.VMEM((experts * CAP, width), BF),
            pltpu.VMEM((2, 2, size, hidden), BF),
            pltpu.VMEM((n_ctx - 1, CAP, width), BF),
            pltpu.VMEM((n_ctx - 1, 8, rows), F32),
            pltpu.VMEM((n_tp - 1, rows, size), BF),
            pltpu.VMEM((n_tp - 1, rows, size), BF),
            pltpu.VMEM((8, rows), F32),
            pltpu.VMEM((n_tp - 1, 8, rows), F32),
            pltpu.VMEM((8, rows), F32),
            pltpu.VMEM((n_tp - 1, 8, rows), F32),
            DMA((2, 2)),
            DMA,
            pltpu.VMEM((experts * CAP, hidden), BF),
            pltpu.VMEM((experts * CAP, width), BF),
            DMA((2,)),
        ]
        + pair_of_sems(n_ctx)
        + pair_of_sems(n_tp * n_ctx)
        + pair_of_sems(n_tp) * 3,
        4,
        "second_norm_back",
        left=tuple(range(2, 4 + 3 * count)) + ((-2, -1) if count == 2 else (-1,)),
    )


def attention_backward(
    low, output_w, query, kv, cosine, sine, sums, payload, n_tp, n_ctx
):
    rows, size = low.shape
    width = size * n_tp
    inner = query.shape[1]
    heads = inner // HD
    scale = 1.0 / math.sqrt(HD)

    half = heads // 2
    sums, sums_input = sums
    lane = 2 * half * HD

    def kernel(*refs):
        lw, wgt_far, qry_far, full_far, cs, sn, made = refs[:7]
        n_in, n_out = 7 + len(payload.inputs), len(payload.outs)
        d_attn, d_qkv, summed = refs[n_in : n_in + 3]
        scratch = refs[n_in + 3 + n_out :]
        dot, dqs, dkv, slots, last, both, total, kept = scratch[:8]
        sems = scratch[8:12]
        wgt, qry, full, late = scratch[12:16]
        sums.take(made, scratch[16 : 16 + len(sums.scratch)])
        payload.take(
            refs[7:n_in], refs[n_in + 3 : n_in + 3 + n_out], scratch[16 + len(sums.scratch) :]
        )
        payload.load()
        fetches = [
            pltpu.make_async_copy(far, near, late.at[i])
            for i, (far, near) in enumerate([(qry_far, qry), (full_far, full), (wgt_far, wgt)])
        ]
        for copy in fetches:
            copy.start()
        greet([("tp", n_tp), ("ctx", n_ctx)])
        here, beside, across = quad()
        beyond = lax.rem(beside + 2, 4)
        copies = gather_columns(lw, d_attn, "tp", n_tp, sems[2:4])
        sums.start()
        payload.go()
        finish(fetches)

        @pl.loop(0, heads)
        def _(h):
            at = columns(h, HD)
            kept[h] = softmax_rows(qry[:, at], full[:, at], here * rows)

        for step in range(n_tp):
            rank = peer("tp", n_tp, n_tp - step)
            weights = wgt[pl.ds(pl.multiple_of(rank * size, 16), size), :]
            if step:
                copies[step - 1].wait()
                total[...] += mm(d_attn[:, columns(rank, size)], weights)
            else:
                total[...] = mm(lw[...], weights)
        dot[...] = total[...].astype(BF)
        first, second, third = [], [], []
        for j in range(2):

            @pl.loop(0, half)
            def _(i):
                h = j * half + i
                at, at_v = columns(h, HD), columns(h + heads, HD)
                key_at = pl.ds(pl.multiple_of(j * lane + i * HD, 128), HD)
                value_at = pl.ds(pl.multiple_of(j * lane + (half + i) * HD, 128), HD)
                probs = kept[h]
                d_probs = mm_t(dot[:, at], full[:, at_v])
                delta = jnp.sum(probs * d_probs, axis=-1, keepdims=True)
                d_scores = (probs * (d_probs - delta)).astype(BF)
                dqs[:, at] = mm(d_scores, full[:, at]) * scale
                dkv[:, key_at] = (t_mm(d_scores, qry[:, at]) * scale).astype(BF)
                dkv[:, value_at] = t_mm(probs.astype(BF), dot[:, at]).astype(BF)

            at = pl.ds(j * lane, lane)
            first.append(
                remote(
                    dkv.at[stretch(beyond, rows), at], slots.at[0, :, at],
                    sems, 3 * j, {"ctx": beside},
                )
            )
            second.append(
                remote(
                    dkv.at[stretch(beside, rows), at], slots.at[1, :, at],
                    sems, 3 * j + 1, {"ctx": beside},
                )
            )
        for j in range(2):
            at = pl.ds(j * lane, lane)
            first[j].wait()
            both[:, at] = (
                dkv[stretch(across, rows), at].astype(F32) + slots[0, :, at].astype(F32)
            ).astype(BF)
            third.append(
                remote(both.at[:, at], last.at[:, at], sems, 3 * j + 2, {"ctx": across})
            )

        @pl.loop(0, heads)
        def _(h):
            d_qkv[:, columns(h, HD)] = turn(dqs[:, columns(h, HD)], cs[...], sn[...]).astype(BF)

        for j in range(2):
            second[j].wait()
            third[j].wait()

            @pl.loop(0, half)
            def _(i):
                h = j * half + i
                key_at = pl.ds(pl.multiple_of(j * lane + i * HD, 128), HD)
                value_at = pl.ds(pl.multiple_of(j * lane + (half + i) * HD, 128), HD)
                mine = stretch(here, rows)
                d_key = dkv[mine, key_at].astype(F32) + slots[1, :, key_at].astype(F32)
                d_key = d_key + last[:, key_at].astype(F32)
                d_qkv[:, columns(h + heads, HD)] = turn(d_key, cs[...], sn[...]).astype(BF)
                d_value = dkv[mine, value_at].astype(F32) + slots[1, :, value_at].astype(F32)
                d_value = d_value + last[:, value_at].astype(F32)
                d_qkv[:, columns(h + 2 * heads, HD)] = d_value.astype(BF)

        summed[...] = sums.total().astype(BF)
        payload.wait()

    return call(
        kernel,
        (
            shape((rows, width), BF),
            shape((rows, 3 * inner), BF),
            shape(sums.shape, BF),
            *payload.outs,
        ),
        (low, output_w, query, kv, cosine, sine, sums_input, *payload.inputs),
        [
            pltpu.VMEM((rows, inner), BF),
            pltpu.VMEM((rows, inner), F32),
            pltpu.VMEM((rows * n_ctx, 2 * inner), BF),
            pltpu.VMEM((2, rows, 2 * inner), BF),
            pltpu.VMEM((rows, 2 * inner), BF),
            pltpu.VMEM((rows, 2 * inner), BF),
            pltpu.VMEM((rows, inner), F32),
            pltpu.VMEM((heads, rows, rows * n_ctx), F32),
        ]
        + pair_of_sems(6)
        + pair_of_sems(n_tp)
        + [
            pltpu.VMEM(array.shape, BF) for array in (output_w, query, kv)
        ]
        + [DMA((3,))]
        + sums.scratch
        + payload.scratch,
        5,
        "attention_backward",
        left=(1, 2, 3, *range(6, 7 + len(payload.inputs)), -len(payload.outs)),
    )


def first_norm_back(d_qkv, weights, hidden, scale, gain, d_resid, early, later, square, payload, n_tp, n_ctx):
    n_square = len(square.inputs) if square else 0
    more, more_input = later
    rows, size = hidden.shape
    width = size * n_tp

    def kernel(*refs):
        dpr, wgt, hid, scl, gn, dr, erl, made = refs[:8]
        refs = refs[:7] + refs[8:]
        squared, refs = refs[7 : 7 + n_square], refs[:7] + refs[7 + n_square :]
        n_in, n_out = 7 + len(payload.inputs), len(payload.outs)
        out, d_gain, returned, summed = refs[n_in : n_in + 4]
        refs = refs[: n_in + 3] + refs[n_in + 4 :]
        squared_out = refs[n_in + 3 : n_in + 3 + 2 * n_square]
        refs = refs[: n_in + 3] + refs[n_in + 3 + 2 * n_square :]
        scratch = refs[n_in + 3 + n_out :]
        held, parts, slots, mine, sums, loads = scratch[:6]
        sems = scratch[6:10]
        begin = 12 + len(more.scratch)
        more.take(made, scratch[12:begin])
        first = begin + (len(square.scratch) if square else 0)
        payload.take(refs[7:n_in], refs[n_in + 3 : n_in + 3 + n_out], scratch[first:])
        if square:
            square.take(squared, squared_out, scratch[begin:first])

        def block(step):
            rank = peer("tp", n_tp, step)
            return pltpu.make_async_copy(
                wgt.at[stretch(rank, size), :], held.at[step - 1], loads.at[step - 1]
            )

        for step in range(1, n_tp + 1):
            block(step).start()
        payload.load()
        greet([("tp", n_tp), ("ctx", n_ctx)])
        given = [
            send(erl, returned, "ctx", n_ctx, n_ctx - 2, scratch[10:12])
        ]
        if square:
            square.start()

        def give(step):
            return described(
                parts.at[step - 1], slots.at[step - 1], sems[0:2], step - 1,
                {"tp": peer("tp", n_tp, step)},
            )

        @pl.loop(1, n_tp + 1)
        def _(step):
            block(step).wait()
            out[...] = mm_t(dpr[...], held[step - 1])

            @pl.when(step < n_tp)
            def _():
                parts[step - 1] = out[...].astype(BF)
                give(step).start()

        copies = [give(step) for step in range(1, n_tp)]
        payload.go()
        if square:
            square.cross()
        finish(copies)
        total = out[...]
        for k in range(1, n_tp):
            total = total + slots[k - 1].astype(F32)
        factor = scl[:, 0:1]
        unit = hid[...].astype(F32) * factor
        d_gain[...] = jnp.broadcast_to(jnp.sum(total * unit, axis=0, keepdims=True), d_gain.shape)
        gained = total * gn[0:1, :]
        out[...] = gained
        dot = total_over(row_sums(unit * gained), mine, sums, "tp", n_tp, sems[2:4])
        dot = as_column(dot, eighth())[:, 0:1] * (1.0 / width)
        more.start()
        unit = hid[...].astype(F32) * factor
        out[...] = dr[...] + factor * (out[...] - unit * dot)
        finish(given)
        summed[...] = more.total().astype(BF)
        if square:
            square.end()
        payload.wait()

    return call(
        kernel,
        (
            shape((rows, size), F32),
            shape((8, size), F32),
            shape((CAP, size), BF),
            shape(more.shape, BF),
            *(square.outs if square else []),
            *payload.outs,
        ),
        (
            *(d_qkv, weights, hidden, scale, gain, d_resid, early, more_input),
            *(square.inputs if square else []),
            *payload.inputs,
        ),
        [
            pltpu.VMEM((n_tp, size, d_qkv.shape[1]), BF),
            pltpu.VMEM((n_tp - 1, rows, size), BF),
            pltpu.VMEM((n_tp - 1, rows, size), BF),
            pltpu.VMEM((8, rows), F32),
            pltpu.VMEM((n_tp - 1, 8, rows), F32),
            DMA((n_tp,)),
        ]
        + pair_of_sems(n_tp) * 2
        + pair_of_sems(n_ctx)
        + more.scratch
        + (square.scratch if square else [])
        + payload.scratch,
        6,
        "first_norm_back",
        left=(1, *range(7, 8 + n_square + len(payload.inputs)), -len(payload.outs)),
    )


class SquareSum:

    def __init__(self, ready, n_ctx):
        self.n_ctx = n_ctx
        _, rows, size = ready.shape
        self.inputs = [ready]
        self.outs = [shape((rows, size), BF), shape((rows, size), F32)]
        self.scratch = [
            pltpu.VMEM((4, rows, size), BF),
            pltpu.VMEM((4, rows, size), BF),
            pltpu.VMEM((2, rows, size), BF),
            pltpu.VMEM((2, rows, size), BF),
            DMA((4,)),
        ]
        self.scratch += pair_of_sems(4) + pair_of_sems(2)

    def take(self, ins, outs, scratch):
        self.ready, self.out_refs, self.held = ins[0], outs, scratch

    def start(self):
        here, beside, across = quad()
        beyond = lax.rem(beside + 2, 4)
        mine = lax.axis_index("fsdp")
        other = 1 - mine

        def block(rank, column):
            return self.ready.at[rank * self.n_ctx + column]

        self.fetches, self.near = [], []
        for i, (rank, theirs, ours) in enumerate(
            [(other, beyond, across), (mine, beyond, across),
             (other, beside, here), (mine, beside, here)]
        ):
            self.near.append(
                remote(
                    block(rank, theirs), self.held[1].at[i], self.held[5:7], i, {"ctx": beside}
                )
            )
            copy = pltpu.make_async_copy(
                block(rank, ours), self.held[0].at[i], self.held[4].at[i]
            )
            copy.start()
            self.fetches.append(copy)

    def chip(self, i):
        self.fetches[i].wait()
        self.near[i].wait()
        return self.held[0][i].astype(F32) + self.held[1][i].astype(F32)

    def cross(self):
        across = quad()[2]
        two, far = self.held[2:4]
        self.far = []
        for i in range(2):
            two[i] = self.chip(i).astype(BF)
            self.far.append(
                remote(two.at[i], far.at[i], self.held[7:9], i, {"ctx": across})
            )

    def end(self):
        for i in range(2):
            value = self.chip(2 + i)
            self.far[i].wait()
            value = value + self.held[3][i].astype(F32)
            self.out_refs[i][...] = value.astype(BF) if i == 0 else value


class ExpertsOut:

    def __init__(self, made, returned, last, picks, mix, resid, n_tp, n_ctx):
        self.n_ctx = n_ctx
        self.sums = RowSums(made, 0, 2 * CAP, n_tp)
        self.inputs = [made, returned, last, picks, mix, resid]
        self.size = resid.shape[1]
        self.out = shape(resid.shape, BF)
        self.scratch = [
            pltpu.VMEM(self.sums.shape, BF),
            pltpu.VMEM((2, CAP, self.size), BF),
        ]
        self.scratch += pair_of_sems(n_ctx)
        self.scratch += [pltpu.VMEM((n_ctx, resid.shape[0], 128), F32)] + self.sums.scratch

    def take(self, ins, out, scratch):
        self.ins, self.out_ref, self.held = ins, out, scratch[:5]
        self.sums.take(ins[0], scratch[5:])

    def give_back(self):
        share, back = self.held[:2]
        share[...] = self.sums.total().astype(BF)
        n_ctx = self.n_ctx
        self.copies = [
            send(share.at[pl.ds(CAP, CAP)], back.at[0], "ctx", n_ctx, n_ctx - 1, self.held[2:4]),
            send(self.ins[2], back.at[1], "ctx", n_ctx, 1, self.held[2:4]),
        ]

    def prepare(self):
        order = lax.broadcasted_iota(jnp.int32, (8, 128), 0)

        @pl.loop(0, self.n_ctx)
        def _(k):
            self.held[4][k] = as_column(self.ins[-2][...], jnp.where(order == k, 1.0, 0.0))

    def mix(self):
        returned, _, picks, mix, resid = self.ins[1:]
        share, back = self.held[:2]
        finish(self.copies)
        total = resid[...]
        for k in range(self.n_ctx):
            gate = self.held[4][k, :, 0:1]
            rows = (share[0:CAP], back[0], returned[...], back[1])[k]
            total = total + gate * t_mm(picks[k * CAP : (k + 1) * CAP], rows)
        self.out_ref[...] = total.astype(BF)


def weight_grads(squared, products, groups, small, payload, experts_out, n_tp, n_ctx):
    width = products[0][0].shape[1]
    places = 2 * n_ctx
    cut = width // places
    total_columns = squared[0].shape[1] + sum(size for _, _, size in groups)
    flat = [array for pair in products for array in pair]
    done = squared[0].shape[1]
    inputs = [*squared, *flat, small, *experts_out.inputs, *payload.inputs]

    def kernel(*refs):
        theirs, ours, refs = refs[0], refs[1], refs[2:]
        factors, refs = refs[: len(flat)], refs[len(flat) :]
        sml, refs = refs[0], refs[1:]
        given, refs = refs[: len(experts_out.inputs)], refs[len(experts_out.inputs) :]
        paid, refs = refs[: len(payload.inputs)], refs[len(payload.inputs) :]
        out, small_out, block_out = refs[:3]
        paid_out, refs = refs[3 : 3 + len(payload.outs)], refs[3 + len(payload.outs) :]
        sml_full, sml_slots, refs = refs[0], refs[1], refs[2:]
        scratch, refs = refs[: 6 * len(groups)], refs[6 * len(groups) :]
        experts_out.take(given, block_out, refs[: len(experts_out.scratch)])
        refs = refs[len(experts_out.scratch) :]
        payload.take(paid, paid_out, refs[: len(payload.scratch)])
        refs = refs[len(payload.scratch) :]
        come, come_sems, sems = refs[0], refs[1:3], refs[3:]
        payload.load()
        barrier = pltpu.get_barrier_semaphore()
        here, beside, across = quad()
        beyond = lax.rem(beside + 2, 4)
        mine = lax.axis_index("fsdp")
        other = 1 - mine
        place = mine * n_ctx + here
        others = []
        for i in range(1, places):
            to = lax.rem(place + i, places)
            others.append((to, {"fsdp": to // n_ctx, "ctx": lax.rem(to, n_ctx)}))
        ahead = [{"tp": peer("tp", n_tp, k)} for k in range(1, n_tp)]
        for device in ahead + [device for _, device in others]:
            pl.semaphore_signal(barrier, inc=1, device_id=device, device_id_type=MESH)
        pl.semaphore_wait(barrier, n_tp - 1 + places - 1)
        gathers = gather_columns(sml, sml_full, "tp", n_tp, sems[0:2])
        early = remote(theirs, come, come_sems, 0, {"fsdp": other})
        experts_out.sums.start()
        blocks = [(other, beyond), (other, beside), (mine, beyond), (mine, beside)]

        def near_copy(g, i):
            prt, come = scratch[6 * g : 6 * g + 2]
            rank, column = blocks[i]
            return described(
                prt.at[rank * n_ctx + column], come.at[i],
                sems[4 + 6 * g : 6 + 6 * g], i, {"ctx": beside},
            )

        def near(g):
            which, start, size = groups[g]
            prt = scratch[6 * g]
            left, right = factors[2 * which : 2 * which + 2]

            @pl.loop(0, places)
            def _(i):
                prt[i] = t_mm(left[:, columns(i, cut)], right[:, start : start + size]).astype(BF)

            for i in range(4):
                near_copy(g, i).start()

        def chip(g, i, rank, column):
            prt, come = scratch[6 * g : 6 * g + 2]
            near_copy(g, i).wait()
            return prt[rank * n_ctx + column].astype(F32) + come[i].astype(F32)

        def hop_copy(g, i):
            two, far = scratch[6 * g + 2 : 6 * g + 4]
            return described(
                two.at[i], far.at[i], sems[6 + 6 * g : 8 + 6 * g], i, {"fsdp": other}
            )

        def hop(g):
            for i, column in enumerate((across, here)):
                scratch[6 * g + 2][i] = chip(g, i, other, column).astype(BF)
                hop_copy(g, i).start()

        def between(j):
            for turn_of, act in enumerate(
                (lambda: near(0), lambda: hop(0), lambda: near(1), lambda: hop(1))
            ):
                pl.when(j == turn_of)(act)

        payload.go(between)
        finish(gathers)
        totals = [
            remote(sml_full.at[:, columns(to, cut)], sml_slots.at[i], sems[2:4], i, device)
            for i, (to, device) in enumerate(others)
        ]
        experts_out.prepare()
        lasts = []
        for g in range(len(groups)):
            far, one, last = scratch[6 * g + 3 : 6 * g + 6]
            value = chip(g, 2, mine, across)
            hop_copy(g, 0).wait()
            one[...] = (value + far[0].astype(F32)).astype(BF)
            lasts.append(
                remote(one, last, sems[8 + 6 * g : 10 + 6 * g], 0, {"ctx": across})
            )
            if g == 0:
                experts_out.give_back()
        finish(totals)
        sums = sml_full[:, columns(place, cut)]
        for i in range(places - 1):
            sums = sums + sml_slots[i]
        small_out[...] = sums
        start = done
        for g, (_, _, size) in enumerate(groups):
            far = scratch[6 * g + 3]
            value = chip(g, 3, mine, here)
            hop_copy(g, 1).wait()
            value = value + far[1].astype(F32)
            out[:, start : start + size] = value
            start += size
        early.wait()
        out[:, 0:done] = ours[...] + come[...].astype(F32)
        experts_out.mix()
        payload.wait()
        start = done
        for g, (_, _, size) in enumerate(groups):
            lasts[g].wait()
            at = pl.ds(start, size)
            out[:, at] = out[:, at] + scratch[6 * g + 5][...].astype(F32)
            start += size

    buffers = [pltpu.VMEM((8, width), F32), pltpu.VMEM((places - 1, 8, cut), F32)]
    sems = pair_of_sems(n_tp) + pair_of_sems(places)
    for _, _, size in groups:
        buffers += [
            pltpu.VMEM((places, cut, size), BF),
            pltpu.VMEM((4, cut, size), BF),
            pltpu.VMEM((2, cut, size), BF),
            pltpu.VMEM((2, cut, size), BF),
            pltpu.VMEM((cut, size), BF),
            pltpu.VMEM((cut, size), BF),
        ]
        sems += pair_of_sems(4) + pair_of_sems(2) + pair_of_sems(1)
    return call(
        kernel,
        (
            shape((cut, total_columns), F32),
            shape((8, cut), F32),
            experts_out.out,
            *payload.outs,
        ),
        inputs,
        buffers
        + experts_out.scratch
        + payload.scratch
        + [pltpu.VMEM(squared[0].shape, BF)]
        + pair_of_sems(1)
        + sems,
        10,
        "weight_grads",
        left=(
            len(flat) + 3,
            *range(len(inputs) - len(payload.inputs), len(inputs)),
            -len(payload.outs),
        ),
    )


def experts_back(experts_out, payload, n_tp, n_ctx):
    inputs = [*experts_out.inputs, *payload.inputs]
    given = len(experts_out.inputs)

    def kernel(*refs):
        ins, refs = refs[: len(inputs)], refs[len(inputs) :]
        outs, scratch = refs[: 1 + len(payload.outs)], refs[1 + len(payload.outs) :]
        experts_out.take(ins[:given], outs[0], scratch[: len(experts_out.scratch)])
        payload.take(ins[given:], outs[1:], scratch[len(experts_out.scratch) :])
        greet([("tp", n_tp), ("ctx", n_ctx)])
        experts_out.sums.start()
        payload.go()
        experts_out.prepare()
        experts_out.give_back()
        experts_out.mix()
        payload.wait()

    return call(
        kernel,
        (experts_out.out, *payload.outs),
        inputs,
        experts_out.scratch + payload.scratch,
        9,
        "experts_back",
        left=(0, *range(given, len(inputs)), -len(payload.outs)),
    )


def write_out(experts_grads, attn_grad, plain, n_ctx):
    _, rows, size = experts_grads[0][0].shape
    steps = max(1, rows // 128)
    tile = rows // steps
    many = len(experts_grads)
    plain = list(plain)
    blocks = []
    if attn_grad is not None:
        block = attn_grad.shape[1] // 4
        blocks = [shape((attn_grad.shape[0], block), F32)] * 4
        plain.append(attn_grad)

    def kernel(*refs):
        here = lax.axis_index("ctx")
        ins, outs = refs[: 2 * many + len(plain)], refs[2 * many + len(plain) :]
        for i in range(many):
            came, mine = ins[2 * i : 2 * i + 2]
            outs[i][here] = mine[...].astype(F32)
            for k in range(1, n_ctx):
                outs[i][lax.rem(here + n_ctx - k, n_ctx)] = came[k - 1].astype(F32)
        for i in range(len(plain) - (1 if blocks else 0)):
            outs[many + i][...] = ins[2 * many + i][...]
        for i in range(len(blocks)):
            outs[i - 4][...] = ins[-1][:, i * block : (i + 1) * block]

    def flat(array):
        return pl.BlockSpec((array.shape[0] // steps, array.shape[1]), lambda i: (i, 0))

    in_specs, out_specs, out_shape = [], [], []
    for _ in experts_grads:
        in_specs.append(pl.BlockSpec((n_ctx - 1, tile, size), lambda i: (0, i, 0)))
        in_specs.append(pl.BlockSpec((tile, size), lambda i: (i, 0)))
        out_specs.append(pl.BlockSpec((n_ctx, tile, size), lambda i: (0, i, 0)))
        out_shape.append(shape((n_ctx, rows, size), F32))
    for array in plain[: len(plain) - (1 if blocks else 0)] + blocks:
        out_specs.append(flat(array))
        out_shape.append(shape(array.shape, array.dtype))
    in_specs += [flat(array) for array in plain]
    inputs = [array for pair in experts_grads for array in pair] + plain
    return pl.pallas_call(
        kernel,
        grid=(steps,),
        in_specs=in_specs,
        out_specs=out_specs,
        out_shape=out_shape,
        cost_estimate=pl.CostEstimate(
            flops=0, bytes_accessed=6 * many * n_ctx * rows * size, transcendentals=0
        ),
        name="write_out",
    )(*inputs)


def after(value, *needed):
    return lax.optimization_barrier((value, *needed))[0]


def shards(
    hidden_in,
    out_grad,
    attn_gain,
    w_query,
    w_key,
    w_value,
    w_output,
    ffn_gain,
    w_router,
    w_gate,
    w_up,
    w_down,
    routes,
):
    rows_here, width_tp = hidden_in.shape
    here_tp = lax.axis_index("tp")
    here_ctx = lax.axis_index("ctx")
    here_fsdp = lax.axis_index("fsdp")
    n_fsdp = lax.axis_size("fsdp")
    n_ctx = lax.axis_size("ctx")
    n_tp = lax.axis_size("tp")
    experts = w_gate.shape[0]
    assert experts == n_ctx == 4
    width = width_tp * n_tp
    part = width // n_fsdp
    pair = n_fsdp == 2
    heads_width = w_query.shape[1]

    def swap_fsdp(value):
        return lax.ppermute(value, "fsdp", [(0, 1), (1, 0)])

    def other_parts(weight):
        if pair:
            return [weight, swap_fsdp(weight)]
        return [lax.all_gather(weight, "fsdp", axis=0, tiled=True)]

    def split(values):
        if pair:
            return [
                lax.dynamic_slice_in_dim(values, here_fsdp * part, part, 1),
                lax.dynamic_slice_in_dim(values, (1 - here_fsdp) * part, part, 1),
            ]
        return [values]

    def join(pieces):
        if pair:
            first = here_fsdp == 0
            return jnp.concatenate(
                [jnp.where(first, pieces[0], pieces[1]), jnp.where(first, pieces[1], pieces[0])],
                axis=1,
            )
        return pieces[0]

    def into(values, weights):
        return sum(mm(x, w) for x, w in zip(split(values), weights))

    def back(values, weights):
        return join([mm_t(values, w) for w in weights])

    def my_features(values):
        return lax.dynamic_slice_in_dim(values, here_tp * width_tp, width_tp, values.ndim - 1)

    attn_w = (w_query, w_key, w_value, w_output)
    small = jnp.concatenate(
        [attn_gain[None], ffn_gain[None], w_router.T, jnp.zeros((2, part), BF)], axis=0
    )
    if pair:
        quarter = part // n_ctx
        own_quarter = jnp.concatenate(
            [lax.dynamic_slice_in_dim(w, here_ctx * quarter, quarter, 0) for w in attn_w], axis=1
        )
        other_quarter = swap_fsdp(own_quarter)
        other_small = swap_fsdp(small)
        small_full = join([small, other_small]).astype(F32)
    else:
        other_quarter = None
        small_full = lax.all_gather(small, "fsdp", axis=1, tiled=True).astype(F32)
    inputs_full, up_mine, down_mine = gather_tp(hidden_in, (w_up, w_down), n_tp)
    gate_w = other_parts(lax.dynamic_index_in_dim(w_gate, here_ctx, 0, False))
    up_w = other_parts(up_mine)
    down_w = other_parts(down_mine)
    small_here = my_features(small_full)
    gain_one_here = jnp.broadcast_to(small_here[0:1], small_here.shape)
    gain_two_here = jnp.broadcast_to(small_here[1:2], small_here.shape)
    nothing = [(0, 8 - experts), (0, 0)]
    router_here = jnp.pad(small_here[2 : 2 + experts], nothing)

    relative = (jnp.arange(experts, dtype=jnp.int32) + here_ctx) % experts
    numbers = jnp.arange(8, dtype=jnp.int32)
    onehot = (routes.T[:, None, :] == numbers[None, :, None]).astype(F32)
    named = (routes.T[:, None, :] == relative[None, :, None]).astype(F32)
    names = jnp.pad(named, [(0, 0)] + nothing)
    chosen = jnp.sum(named, axis=0)
    earlier = jnp.triu(jnp.ones((rows_here, rows_here), BF), 1)
    slot_of = mm(chosen.astype(BF), earlier).astype(jnp.int32)
    slots = jnp.arange(CAP, dtype=jnp.int32)
    picks = (slot_of[:, None, :] == slots[None, :, None]) & (chosen[:, None, :] > 0)
    picks = picks.astype(BF).reshape(experts * CAP, rows_here)

    gathered = first_norm(
        inputs_full, out_grad, small_full, attn_w, other_quarter, n_tp, n_ctx
    )
    normed_one, scale_one, grad_full = gathered[:3]
    if pair:
        qkv_w, output_w = gathered[3:]
    else:
        qkv_w, output_w = (
            lax.all_gather(w, "fsdp", axis=0, tiled=True)
            for w in (jnp.concatenate(attn_w[:3], axis=1), w_output)
        )
    positions = here_ctx * rows_here + jnp.arange(rows_here, dtype=jnp.int32)
    cosine, sine = rotary_tables(positions)
    attended, query, kv = attention_forward(mm(normed_one, qkv_w), cosine, sine, n_ctx)
    resid, scale_two, normed_two, grad_rows, token_rows, slot_gates, gates, mix = second_norm(
        mm_t(attended, output_w).astype(BF),
        hidden_in,
        gain_two_here,
        mm(picks, grad_full).astype(BF),
        picks,
        router_here,
        onehot,
        names,
        n_tp,
        n_ctx,
    )
    gate_rows = slot_gates[:, 0, :CAP].reshape(experts * CAP, 1)

    to_gate, to_up, hidden_act = expert_acts(token_rows, gate_w, up_w, n_fsdp)
    d_result = (gate_rows * grad_rows.astype(F32)).astype(BF)

    def away(left, right):
        value = t_mm(split(left)[1], right).astype(BF)
        return value, swap_fsdp(value)

    def payload_of(left, right, come):
        if pair:
            return Payload(n_ctx, product=(left, right, come))
        return Payload(
            n_ctx,
            rows=lax.psum_scatter(
                t_mm(left, right).astype(BF), "fsdp", scatter_dimension=0, tiled=True
            ),
        )

    def came_and_own(outs, payload):
        if pair:
            return tuple(outs)
        own = lax.dynamic_slice_in_dim(payload.inputs[0], here_ctx * payload.cut, payload.cut, 0)
        return outs[0], own

    down_come = gate_come = up_come = None
    if pair:
        down_away, down_come = away(d_result, hidden_act)
        grad_rows = after(grad_rows, down_away)
    d_hidden = into(grad_rows, down_w)
    gate_dot = jnp.sum(hidden_act.astype(F32) * d_hidden, axis=-1).reshape(experts, CAP)
    gate_dot = jnp.broadcast_to(
        jnp.pad(gate_dot, [(0, 0), (0, rows_here - CAP)])[:, None, :], (experts, 8, rows_here)
    )
    d_hidden = gate_rows * d_hidden
    d_gate_act = (d_hidden * to_gate).astype(BF)
    d_up_act = (d_hidden * to_up).astype(BF)
    if pair:
        gate_away, gate_come = away(token_rows, d_gate_act)

    acts = (d_gate_act, d_up_act, hidden_act)
    if pair:
        acts = lax.optimization_barrier((*acts, gate_away))[:3]
    d_resid, d_attn_here, gain_two_part, d_logits, made, *up_away = second_norm_back(
        acts,
        (gate_w, up_w, down_w),
        token_rows,
        gate_dot,
        picks,
        gates,
        onehot,
        names,
        router_here,
        resid,
        scale_two,
        gain_two_here,
        out_grad,
        n_tp,
        n_ctx,
    )
    if pair:
        up_come = swap_fsdp(up_away[0])

    payload = payload_of(d_result, hidden_act, down_come)
    early = (RowSums(made, 2 * CAP, CAP, n_tp), made)
    d_attn, d_qkv, made_early, *outs = attention_backward(
        d_attn_here, output_w, query, kv, cosine, -sine, early, payload, n_tp, n_ctx
    )
    grad_down = came_and_own(outs, payload)
    payload = payload_of(token_rows, d_gate_act, gate_come)
    square = None
    if pair:
        share = t_mm(d_attn, attended).astype(BF)
        square = SquareSum(share.reshape(n_fsdp * n_ctx, quarter, heads_width), n_ctx)
    later = (RowSums(made, 3 * CAP, CAP, n_tp), made)
    in_grad, gain_one_part, returned, made_later, *outs = first_norm_back(
        d_qkv,
        qkv_w,
        hidden_in,
        scale_one,
        gain_one_here,
        d_resid,
        made_early,
        later,
        square,
        payload,
        n_tp,
        n_ctx,
    )
    if pair:
        squared, outs = outs[:2], outs[2:]
    grad_gate = came_and_own(outs, payload)
    payload = payload_of(token_rows, d_up_act, up_come)

    small_part = jnp.concatenate(
        [
            gain_one_part[:1],
            gain_two_part[:1],
            mm(d_logits[:experts].astype(BF), my_features(normed_two)),
            jnp.zeros((6 - experts, width_tp), F32),
        ],
        axis=0,
    )
    written = write_out([grad_gate, grad_down], None, (), n_ctx)
    if pair:
        small_part = after(small_part, *written)
    grad_gate, grad_down = written
    experts_out = ExpertsOut(made, returned, made_later, picks, mix, resid, n_tp, n_ctx)
    if pair:
        grad_attn, small_grad, block_out, *outs = weight_grads(
            squared,
            [(normed_one, d_qkv)],
            [(0, 0, 2 * heads_width), (0, 2 * heads_width, heads_width)],
            small_part,
            payload,
            experts_out,
            n_tp,
            n_ctx,
        )
    else:
        grad_attn = jnp.concatenate([t_mm(d_attn, attended), t_mm(normed_one, d_qkv)], axis=1)
        scatter = partial(
            lax.psum_scatter, axis_name=("fsdp", "ctx"), scatter_dimension=0, tiled=True
        )
        grad_attn = scatter(grad_attn.astype(BF)).astype(F32)
        small_grad = lax.all_gather(small_part, "tp", axis=1, tiled=True)
        small_grad = scatter(small_grad.T).T
        block_out, *outs = experts_back(experts_out, payload, n_tp, n_ctx)
    grad_up = came_and_own(outs, payload)
    grad_up, block_out, in_grad, grad_output, grad_query, grad_key, grad_value = write_out(
        [grad_up], grad_attn, (block_out, in_grad), n_ctx
    )
    return (
        block_out,
        in_grad,
        small_grad[0],
        grad_query,
        grad_key,
        grad_value,
        grad_output,
        small_grad[1],
        small_grad[2 : 2 + experts].T,
        grad_gate,
        grad_up,
        grad_down,
    )


def solution(mesh):
    rows = ("fsdp", "ctx")
    placed = (
        P(rows, "tp"),
        P(rows, "tp"),
        P("fsdp"),
        P("fsdp", "tp"),
        P("fsdp", "tp"),
        P("fsdp", "tp"),
        P("fsdp", "tp"),
        P("fsdp"),
        P("fsdp", None),
        P(None, "fsdp", "tp"),
        P(None, "fsdp", "tp"),
        P(None, "fsdp", "tp"),
        P(rows, None),
    )
    return jax.shard_map(
        shards,
        mesh=mesh,
        in_specs=placed,
        out_specs=(
            P(rows, "tp"),
            P(rows, "tp"),
            P(rows),
            P(rows, "tp"),
            P(rows, "tp"),
            P(rows, "tp"),
            P(rows, "tp"),
            P(rows),
            P(rows, None),
            P(None, rows, "tp"),
            P(None, rows, "tp"),
            P(None, rows, "tp"),
        ),
        check_vma=False,
    )
```

```python
from functools import partial
import math

import jax
import jax.numpy as jnp
from jax import lax
from jax.experimental import pallas as pl
from jax.experimental.pallas import tpu as pltpu
from jax.sharding import PartitionSpec as P

HD = 128
CAP = 160


EPS = 1e-05
THETA = 10000.0
NEG = -1e30
BF = jnp.bfloat16
F32 = jnp.float32


def mm(left, right):
    return jnp.dot(left, right, preferred_element_type=F32)


def mm_t(left, right):
    return lax.dot_general(left, right, (((1,), (1,)), ((), ())), preferred_element_type=F32)


def t_mm(left, right):
    return lax.dot_general(left, right, (((0,), (0,)), ((), ())), preferred_element_type=F32)


def rotary_tables(positions):
    half_size = HD // 2
    frequency = THETA ** (-(jnp.arange(half_size, dtype=F32) * 2.0 / HD))
    angles = positions.astype(F32)[:, None] * frequency[None, :]
    cosine, sine = jnp.cos(angles), jnp.sin(angles)
    return jnp.concatenate([cosine, cosine], axis=1), jnp.concatenate([-sine, sine], axis=1)


MESH = pl.DeviceIdType.MESH
VM = pl.BlockSpec(memory_space=pltpu.VMEM)
DMA = pltpu.SemaphoreType.DMA


def peer(axis, n, k):
    return lax.rem(lax.axis_index(axis) + k, n)


def greet(groups):
    barrier = pltpu.get_barrier_semaphore()
    for axis, n in groups:
        for k in range(1, n):
            pl.semaphore_signal(
                barrier, inc=1, device_id={axis: peer(axis, n, k)}, device_id_type=MESH
            )
    pl.semaphore_wait(barrier, sum(n - 1 for _, n in groups))


def described(source, target, sems, i, to):
    return pltpu.make_async_remote_copy(
        src_ref=source,
        dst_ref=target,
        send_sem=sems[0].at[i],
        recv_sem=sems[1].at[i],
        device_id=to,
        device_id_type=MESH,
    )


def remote(source, target, sems, i, to):
    copy = described(source, target, sems, i, to)
    copy.start()
    return copy


def send(source, target, axis, n, k, sems):
    return remote(source, target, sems, k - 1, {axis: peer(axis, n, k)})


def columns(n, size):
    return pl.ds(pl.multiple_of(n * size, 128), size)


def stretch(n, size):
    return pl.ds(pl.multiple_of(n * size, 16), size)


def gather_columns(own, full, axis, n, sems):
    size = own.shape[1]
    place = full.at[:, columns(lax.axis_index(axis), size)]
    copies = [send(own, place, axis, n, k, sems) for k in range(1, n)]
    place[...] = own[...]
    return copies


def scatter_columns(part, slots, axis, n, sems):
    size = slots.shape[2]
    return [
        send(part.at[:, columns(peer(axis, n, k), size)], slots.at[k - 1], axis, n, k, sems)
        for k in range(1, n)
    ]


def finish(copies):
    for copy in copies:
        copy.wait()


class Payload:

    def __init__(self, n_ctx, rows=None, product=None):
        self.n_ctx = n_ctx
        self.product = product is not None
        self.inputs = list(product) if self.product else [rows]
        last = self.inputs[-1]
        self.rows, self.hidden = last.shape
        self.cut = self.rows // n_ctx
        self.outs = [shape((n_ctx - 1, self.cut, self.hidden), BF)]
        self.scratch = pair_of_sems(n_ctx)
        if self.product:
            self.outs.append(shape((self.cut, self.hidden), BF))
            self.scratch += [
                pltpu.VMEM((self.rows, self.hidden), BF),
                pltpu.VMEM((self.rows, self.hidden), BF),
                pltpu.VMEM((self.inputs[0].shape[0], self.rows), BF),
                pltpu.VMEM(self.inputs[1].shape, BF),
                DMA((3,)),
            ]

    def take(self, ins, outs, scratch):
        self.ins, self.out_refs, self.held = ins, outs, scratch

    def fetches(self):
        left, right, other = self.ins
        mine = left.at[:, columns(lax.axis_index("fsdp"), self.rows)]
        return [
            pltpu.make_async_copy(source, self.held[i], self.held[6].at[j])
            for j, (source, i) in enumerate([(mine, 4), (right, 5), (other, 2)])
        ]

    def load(self):
        if self.product:
            for copy in self.fetches():
                copy.start()

    def copy(self, k):
        to = peer("ctx", self.n_ctx, k)
        source = self.held[3] if self.product else self.ins[0]
        return described(
            source.at[stretch(to, self.cut), :], self.out_refs[0].at[k - 1],
            self.held[0:2], k - 1, {"ctx": to},
        )

    def go(self, between=lambda j: None):
        n_ctx, cut = self.n_ctx, self.cut
        if not self.product:
            for k in (2, 3, 1):
                self.copy(k).start()
            return
        finish(self.fetches())

        @pl.loop(0, n_ctx)
        def _(j):
            k = lax.rem(j + 2, n_ctx)
            to = peer("ctx", n_ctx, k)
            value = t_mm(self.held[4][:, columns(to, cut)], self.held[5][...])
            value = value + self.held[2][stretch(to, cut), :].astype(F32)
            self.held[3][stretch(to, cut), :] = value.astype(BF)

            @pl.when(j != n_ctx - 2)
            def _():
                self.copy(k).start()

            between(j)

    def wait(self):
        if self.product:
            self.out_refs[1][...] = self.held[3][stretch(lax.axis_index("ctx"), self.cut), :]
        for k in range(1, self.n_ctx):
            self.copy(k).wait()


class RowSums:

    def __init__(self, made, first, count, n_tp):
        self.n_tp, self.first = n_tp, first
        self.shape = (count, made.shape[1] // n_tp)
        self.scratch = [
            pltpu.VMEM((n_tp - 1, *self.shape), BF),
            pltpu.VMEM(self.shape, BF),
            DMA,
        ] + pair_of_sems(n_tp)

    def take(self, made, scratch):
        self.made, self.held = made, scratch

    def rows(self, rank):
        return self.made.at[pl.ds(self.first, self.shape[0]), columns(rank, self.shape[1])]

    def mine(self):
        return pltpu.make_async_copy(
            self.rows(lax.axis_index("tp")), self.held[1], self.held[2]
        )

    def start(self):
        self.mine().start()
        n = self.n_tp
        self.copies = [
            send(self.rows(peer("tp", n, k)), self.held[0].at[k - 1], "tp", n, k, self.held[3:5])
            for k in range(1, n)
        ]

    def total(self):
        self.mine().wait()
        finish(self.copies)
        value = self.held[1][...].astype(F32)
        for k in range(1, self.n_tp):
            value = value + self.held[0][k - 1].astype(F32)
        return value


def quad():
    here = lax.axis_index("ctx")
    return here, here + 1 - 2 * lax.rem(here, 2), lax.rem(here + 2, 4)


def gather_square(own, places, sems, between, local=None):
    cuts = own.shape[1] // 512
    here, beside, across = quad()
    first, second, third = [], [], []
    for i in range(cuts):
        piece = own.at[:, pl.ds(i * 512, 512)]
        first.append(remote(piece, places(here, i), sems, 3 * i, {"ctx": across}))
        second.append(remote(piece, places(here, i), sems, 3 * i + 1, {"ctx": beside}))
        if local is None:
            places(here, i)[...] = piece[...]
        else:
            pltpu.make_async_copy(piece, places(here, i), local.at[i]).start()
    between()
    for i in range(cuts):
        first[i].wait()
        third.append(
            remote(places(across, i), places(across, i), sems, 3 * i + 2, {"ctx": beside})
        )
    finish(second)
    finish(third)
    if local is not None:
        for i in range(cuts):
            piece = own.at[:, pl.ds(i * 512, 512)]
            pltpu.make_async_copy(piece, places(here, i), local.at[i]).wait()


def row_sums(values):
    ones = jnp.ones((8, values.shape[1]), F32)
    return lax.dot_general(
        ones,
        values,
        (((1,), (1,)), ((), ())),
        precision=lax.Precision.HIGHEST,
        preferred_element_type=F32,
    )


def as_column(rows, weight):
    return lax.dot_general(
        rows,
        weight,
        (((0,), (0,)), ((), ())),
        precision=lax.Precision.HIGHEST,
        preferred_element_type=F32,
    )


def eighth():
    return jnp.full((8, 128), 0.125, F32)


def total_over(sums, mine, slots, axis, n, sems):
    mine[...] = sums
    copies = [send(mine, slots.at[k - 1], axis, n, k, sems) for k in range(1, n)]
    finish(copies)
    total = sums
    for k in range(1, n):
        total = total + slots[k - 1]
    return total


def call(kernel, out_shape, inputs, scratch, collective, name, left=()):
    anywhere = pl.BlockSpec(memory_space=pl.ANY)
    outs = out_shape if isinstance(out_shape, tuple) else (out_shape,)
    specs = [anywhere if i - len(outs) in left else VM for i in range(len(outs))]
    return pl.pallas_call(
        kernel,
        out_shape=out_shape,
        in_specs=[anywhere if i in left else VM for i in range(len(inputs))],
        out_specs=tuple(specs) if isinstance(out_shape, tuple) else specs[0],
        scratch_shapes=scratch,
        compiler_params=pltpu.CompilerParams(collective_id=collective, has_side_effects=True),
        cost_estimate=pl.CostEstimate(flops=0, bytes_accessed=0, transcendentals=0),
        name=name,
    )(*inputs)


def shape(dims, dtype):
    return jax.ShapeDtypeStruct(dims, dtype)


def pair_of_sems(n):
    return [DMA((n,)), DMA((n,))]


def gather_tp(value, stacks, n_tp):
    rows, size = value.shape
    many = len(stacks)
    member = stacks[0].shape[1:]

    def kernel(own, *refs):
        stk, full, outs = refs[:many], refs[many], refs[many + 1 : 2 * many + 1]
        held, loads, stores = refs[2 * many + 1 : 2 * many + 4]
        sems = refs[2 * many + 4 :]
        here = lax.axis_index("ctx")
        into = [
            pltpu.make_async_copy(stk[i].at[here], held.at[i], loads.at[i]) for i in range(many)
        ]
        away = [pltpu.make_async_copy(held.at[i], outs[i], stores.at[i]) for i in range(many)]
        for copy in into:
            copy.start()
        greet([("tp", n_tp)])
        copies = gather_columns(own, full, "tp", n_tp, sems)
        for i in range(many):
            into[i].wait()
            away[i].start()
        finish(copies)
        finish(away)

    return call(
        kernel,
        (
            shape((rows, size * n_tp), value.dtype),
            *(shape(member, stack.dtype) for stack in stacks),
        ),
        (value, *stacks),
        [pltpu.VMEM((many, *member), BF), DMA((many,)), DMA((many,))] + pair_of_sems(n_tp),
        1,
        "gather_tp",
        left=tuple(range(1, many + 1)) + tuple(range(-many, 0)),
    )


def first_norm(full, grad, gain, weights, quarter, n_tp, n_ctx):
    rows, width = full.shape
    with_quarter = quarter is not None

    def kernel(*refs):
        hid, grd, gn = refs[:3]
        refs = refs[3:]
        if with_quarter:
            wgts, refs = refs[: len(weights)], refs[len(weights) :]
            qrt, out, scale, grd_full, many_full, last_full, held, local, loads, stores = refs[:10]
            sems = refs[10:]
            half, inner = wgts[0].shape
            last = len(wgts) - 1
            mine = lax.axis_index("fsdp")

            def target(i, first_row, count):
                at = pl.ds(pl.multiple_of(first_row, 16), count)
                if i == last:
                    return last_full.at[at, :]
                return many_full.at[at, pl.ds(i * inner, inner)]

            into = [
                pltpu.make_async_copy(wgts[i], held.at[i], loads.at[i]) for i in range(len(wgts))
            ]
            away = [
                pltpu.make_async_copy(held.at[i], target(i, mine * half, half), stores.at[i])
                for i in range(len(wgts))
            ]
            for copy in into:
                copy.start()
            greet([("tp", n_tp), ("ctx", n_ctx)])
        else:
            out, scale, grd_full = refs[:3]
            sems = refs[3:]
            greet([("tp", n_tp)])
        grads = gather_columns(grd, grd_full, "tp", n_tp, sems[0:2])

        def norm():
            values = hid[...].astype(F32)
            mean = jnp.sum(values * values, axis=-1, keepdims=True) * (1.0 / width)
            factor = lax.rsqrt(mean + EPS)
            scale[...] = jnp.broadcast_to(factor, scale.shape)
            out[...] = (values * factor * gn[0:1, :]).astype(BF)

        if with_quarter:
            count = qrt.shape[0]

            def work():
                for i in range(len(wgts)):
                    into[i].wait()
                    away[i].start()
                norm()

            def places(rank, i):
                return target(i, (1 - mine) * half + rank * count, count)

            gather_square(qrt, places, sems[2:4], work, local)
            finish(away)
        else:
            norm()
        finish(grads)

    outs = [shape((rows, width), BF), shape((rows, 128), F32), shape((rows, width), BF)]
    inputs = [full, grad, gain]
    scratch, left = [], ()
    if with_quarter:
        half, inner = weights[0].shape
        many = len(weights)
        assert inner == 512
        outs.append(shape((2 * half, (many - 1) * inner), BF))
        outs.append(shape((2 * half, inner), BF))
        inputs += [*weights, quarter]
        scratch = [pltpu.VMEM((many, half, inner), BF), DMA((many,)), DMA((many,)), DMA((many,))]
        left = tuple(range(3, 3 + many)) + (-2, -1)
    return call(
        kernel,
        tuple(outs),
        inputs,
        scratch + pair_of_sems(n_tp) + pair_of_sems(12),
        7,
        "first_norm",
        left=left,
    )


def turn(values, cosine, sine):
    return values * cosine + pltpu.roll(values, HD // 2, axis=1) * sine


def softmax_rows(query, key, first_row):
    scores = mm_t(query, key) * (1.0 / math.sqrt(HD))
    rows = first_row + lax.broadcasted_iota(jnp.int32, scores.shape, 0)
    cols = lax.broadcasted_iota(jnp.int32, scores.shape, 1)
    scores = jnp.where(cols <= rows, scores, NEG)
    top = jnp.max(scores, axis=-1, keepdims=True)
    weights = jnp.exp(scores - top)
    return weights / jnp.sum(weights, axis=-1, keepdims=True)


def attention_forward(qkv, cosine, sine, n_ctx):
    rows = qkv.shape[0]
    width = qkv.shape[1] // 3
    heads = width // HD

    def kernel(prj, cs, sn, out, qry, full, own, *sems):
        greet([("ctx", n_ctx)])
        here = lax.axis_index("ctx")

        @pl.loop(0, heads)
        def _(h):
            own[:, columns(h, HD)] = turn(
                prj[:, columns(h + heads, HD)], cs[...], sn[...]
            ).astype(BF)
            own[:, columns(h + heads, HD)] = prj[:, columns(h + 2 * heads, HD)].astype(BF)

        def queries():
            @pl.loop(0, heads)
            def _(h):
                qry[:, columns(h, HD)] = turn(prj[:, columns(h, HD)], cs[...], sn[...]).astype(BF)

        def places(rank, i):
            return full.at[stretch(rank, rows), pl.ds(i * 512, 512)]

        gather_square(own, places, sems, queries)

        @pl.loop(0, heads)
        def _(h):
            probs = softmax_rows(qry[:, columns(h, HD)], full[:, columns(h, HD)], here * rows)
            out[:, columns(h, HD)] = mm(
                probs.astype(BF), full[:, columns(h + heads, HD)]
            ).astype(BF)

    return call(
        kernel,
        (
            shape((rows, width), BF),
            shape((rows, width), BF),
            shape((rows * n_ctx, 2 * width), BF),
        ),
        (qkv, cosine, sine),
        [pltpu.VMEM((rows, 2 * width), BF)] + pair_of_sems(6 * width // 512),
        2,
        "attention_forward",
    )


def second_norm(part, hidden, gain, slabs, picks, router, onehot, names, n_tp, n_ctx):
    rows, size = hidden.shape
    width = size * n_tp
    experts = n_ctx

    def kernel(
        prt, hid, gn, slb, pck, rtr, one, nms,
        resid, scale, out, moved, tokens, slot_gates, gates, mix,
        slots, mine, sums, mine_two, sums_two, low, sent, own_gates, *sems
    ):
        greet([("tp", n_tp), ("ctx", n_ctx)])
        here = lax.axis_index("tp")
        copies = scatter_columns(prt, slots, "tp", n_tp, sems[0:2])
        others = [
            send(
                slb.at[pl.ds(k * CAP, CAP)], moved.at[pl.ds(k * CAP, CAP)],
                "ctx", n_ctx, k, sems[6:8],
            )
            for k in range(1, n_ctx)
        ]
        moved[0:CAP] = slb[0:CAP]
        total = prt[:, columns(here, size)].astype(F32)
        finish(copies)
        for k in range(1, n_tp):
            total = total + slots[k - 1].astype(F32)
        total = hid[...].astype(F32) + total
        resid[...] = total
        square = total_over(row_sums(total * total), mine, sums, "tp", n_tp, sems[2:4])
        factor = lax.rsqrt(as_column(square, eighth()) * (1.0 / width) + EPS)
        scale[...] = factor
        low[...] = (resid[...] * factor[:, 0:1] * gn[0:1, :]).astype(BF)
        partial_logits = mm_t(rtr[...].astype(BF), low[...])
        mine_two[...] = partial_logits
        logit_copies = [
            send(mine_two, sums_two.at[k - 1], "tp", n_tp, k, sems[12:14]) for k in range(1, n_tp)
        ]
        gather_columns(low, out, "tp", n_tp, sems[4:6])

        def route():
            finish(logit_copies)
            logits = partial_logits
            for k in range(1, n_tp):
                logits = logits + sums_two[k - 1]
            named = [jnp.sum(one[j] * logits, axis=0, keepdims=True) for j in range(2)]
            top = jnp.maximum(named[0], named[1])
            powers = [jnp.exp(value - top) for value in named]
            both = powers[0] + powers[1]
            gate = [value / both for value in powers]
            mixed = gate[0] * nms[0] + gate[1] * nms[1]
            mix[...] = mixed
            order = lax.broadcasted_iota(jnp.int32, (8, rows), 0)
            gates[...] = jnp.where(order == 0, gate[0], jnp.where(order == 1, gate[1], 0.0))
            own_gates[...] = jnp.zeros(own_gates.shape, F32)
            for k in range(experts):
                own_gates[k, :, 0:CAP] = lax.dot_general(
                    jnp.broadcast_to(mixed[k : k + 1], (8, rows)),
                    pck[k * CAP : (k + 1) * CAP].astype(F32),
                    (((1,), (1,)), ((), ())),
                    precision=lax.Precision.HIGHEST,
                    preferred_element_type=F32,
                )
            slot_gates[0] = own_gates[0]
            for k in range(1, n_ctx):
                others.append(
                    send(own_gates.at[k], slot_gates.at[k], "ctx", n_ctx, k, sems[10:12])
                )


        def slab(k, step):
            at = columns(peer("tp", n_tp, n_tp - step), size)
            return described(
                sent.at[step, pl.ds(k * CAP, CAP)], tokens.at[pl.ds(k * CAP, CAP), at],
                sems[8:10], step * n_ctx + k, {"ctx": peer("ctx", n_ctx, k)},
            )

        def dispatch(step, block):
            sent[step] = mm(pck[...], block).astype(BF)
            tokens[0:CAP, columns(peer("tp", n_tp, n_tp - step), size)] = sent[step, 0:CAP]
            for k in (2, 3, 1):
                slab(k, step).start()

        route()

        @pl.loop(0, n_tp)
        def _(step):
            @pl.when(step > 0)
            def _():
                described(
                    low, out.at[:, columns(here, size)], sems[4:6], step - 1,
                    {"tp": peer("tp", n_tp, step)},
                ).wait()

            dispatch(step, out[:, columns(peer("tp", n_tp, n_tp - step), size)])

        for step in range(n_tp):
            for k in (2, 3, 1):
                slab(k, step).wait()
        finish(others)

    return call(
        kernel,
        (
            shape((rows, size), F32),
            shape((rows, 128), F32),
            shape((rows, width), BF),
            shape(slabs.shape, BF),
            shape(slabs.shape, BF),
            shape((experts, 8, rows), F32),
            shape((8, rows), F32),
            shape((8, rows), F32),
        ),
        (part, hidden, gain, slabs, picks, router, onehot, names),
        [
            pltpu.VMEM((n_tp - 1, rows, size), BF),
            pltpu.VMEM((8, rows), F32),
            pltpu.VMEM((n_tp - 1, 8, rows), F32),
            pltpu.VMEM((8, rows), F32),
            pltpu.VMEM((n_tp - 1, 8, rows), F32),
            pltpu.VMEM((rows, size), BF),
            pltpu.VMEM((n_tp, experts * CAP, size), BF),
            pltpu.VMEM((experts, 8, rows), F32),
        ]
        + pair_of_sems(n_tp) * 3
        + pair_of_sems(n_ctx)
        + pair_of_sems(n_tp * n_ctx)
        + pair_of_sems(n_ctx)
        + pair_of_sems(n_tp),
        3,
        "second_norm",
    )


def expert_acts(tokens, gate_w, up_w, n_fsdp):
    rows, width = tokens.shape
    hidden = gate_w[0].shape[1]
    count = len(gate_w)
    part = gate_w[0].shape[0]
    chunk = 256
    per = part // chunk
    steps = count * per
    pair = count == 2

    def kernel(tok, *refs):
        wgt = [refs[:count], refs[count : 2 * count]]
        to_gate, to_up, hid, buffer, loads = refs[2 * count :]
        first = lax.axis_index("fsdp") if pair else 0

        def load(step):
            slot = lax.rem(step, 2)
            at = stretch(lax.rem(step, per), chunk)
            for lane in range(2):
                for i in range(count):

                    @pl.when(step // per == i)
                    def _():
                        pltpu.make_async_copy(
                            wgt[lane][i].at[at], buffer.at[slot, lane], loads.at[slot, lane]
                        ).start()

        load(0)
        to_gate[...] = jnp.zeros_like(to_gate)
        to_up[...] = jnp.zeros_like(to_up)

        @pl.loop(0, steps)
        def _(step):
            slot = lax.rem(step, 2)
            for lane in range(2):
                pltpu.make_async_copy(
                    wgt[lane][0].at[pl.ds(0, chunk)], buffer.at[slot, lane], loads.at[slot, lane]
                ).wait()

            @pl.when(step + 1 < steps)
            def _():
                load(step + 1)

            which = lax.rem(first + step // per, count)
            column = which * part + lax.rem(step, per) * chunk
            values = tok[:, pl.ds(pl.multiple_of(column, 128), chunk)]
            to_gate[...] += mm(values, buffer[slot, 0])
            to_up[...] += mm(values, buffer[slot, 1])

        @pl.loop(0, rows // 32)
        def _(i):
            at = stretch(i, 32)
            a, b = to_gate[at, :], to_up[at, :]
            sigma = 1.0 / (1.0 + jnp.exp(-a))
            silu = a * sigma
            hid[at, :] = (silu * b).astype(BF)
            to_up[at, :] = silu
            to_gate[at, :] = b * sigma * (1.0 + a * (1.0 - sigma))

    anywhere = pl.BlockSpec(memory_space=pl.ANY)
    return pl.pallas_call(
        kernel,
        out_shape=(
            shape((rows, hidden), F32),
            shape((rows, hidden), F32),
            shape((rows, hidden), BF),
        ),
        in_specs=[VM] + [anywhere] * (2 * count),
        out_specs=(VM, VM, VM),
        scratch_shapes=[pltpu.VMEM((2, 2, chunk, hidden), BF), DMA((2, 2))],
        cost_estimate=pl.CostEstimate(flops=0, bytes_accessed=0, transcendentals=0),
        name="expert_acts",
    )(tokens, *gate_w, *up_w)


def second_norm_back(
    acts, weights, tokens, dots, picks, gates, onehot, names, router, resid, scale, gain, grad,
    n_tp, n_ctx,
):
    rows, size = resid.shape
    width = size * n_tp
    experts = n_ctx
    hidden = acts[0].shape[1]
    count = len(weights[0])
    part = weights[0][0].shape[0]

    def kernel(*refs):
        dga, dup, hid_far = refs[:3]
        wgt = [refs[3 + i * count : 3 + (i + 1) * count] for i in range(3)]
        refs = refs[3 + 3 * count :]
        tok_far, dts, pck, gts, one, nms, rtr, rsd, scl, gn, grd = refs[:11]
        d_resid, low, d_gain, d_logits, out_rows = refs[11:16]
        refs = refs[16:]
        if count == 2:
            up_away, up_held, up_sem = refs[:1] + refs[1:3]
            refs = refs[3:]
        (
            drw, eo, buffer, back, back_dots, parts, slots, mine, sums, mine_two, sums_two, loads,
            out_sem, hid, tok, late,
        ) = refs[:16]
        sems = refs[16:]
        fetches = [
            pltpu.make_async_copy(hid_far, hid, late.at[0]),
            pltpu.make_async_copy(tok_far, tok, late.at[1]),
        ]
        here = lax.axis_index("tp")
        first = lax.axis_index("fsdp")

        def load(which, rank, slot, lane):
            feature = rank * size
            inside = pl.ds(pl.multiple_of(lax.rem(feature, part), 16), size)
            target = buffer.at[slot, lane]
            if count == 1:
                pltpu.make_async_copy(
                    wgt[which][0].at[inside], target, loads.at[slot, lane]
                ).start()
                return
            own = feature // part == first

            @pl.when(own)
            def _():
                pltpu.make_async_copy(
                    wgt[which][0].at[inside], target, loads.at[slot, lane]
                ).start()

            @pl.when(jnp.logical_not(own))
            def _():
                pltpu.make_async_copy(
                    wgt[which][1].at[inside], target, loads.at[slot, lane]
                ).start()

        def loaded(which, slot, lane):
            pltpu.make_async_copy(
                wgt[which][0].at[pl.ds(0, size)], buffer.at[slot, lane], loads.at[slot, lane]
            ).wait()

        load(0, peer("tp", n_tp, 1), 0, 0)
        load(1, peer("tp", n_tp, 1), 0, 1)
        for copy in fetches:
            copy.start()
        greet([("tp", n_tp), ("ctx", n_ctx)])
        small = []
        for k in range(1, n_ctx):
            small.append(
                send(dts.at[k], back_dots.at[k - 1], "ctx", n_ctx, n_ctx - k, sems[0:2])
            )

        def slab(k, rank, step):
            at = columns(rank, size)
            return described(
                drw.at[pl.ds(k * CAP, CAP), at], back.at[k - 1, :, at],
                sems[2:4], step * n_ctx + k - 1, {"ctx": peer("ctx", n_ctx, n_ctx - k)},
            )

        @pl.loop(0, n_tp)
        def _(step):
            rank = peer("tp", n_tp, step + 1)
            slot = lax.rem(step, 2)
            loaded(0, slot, 0)
            loaded(1, slot, 1)

            @pl.when(step + 1 < n_tp)
            def _():
                load(0, peer("tp", n_tp, step + 2), 1 - slot, 0)
                load(1, peer("tp", n_tp, step + 2), 1 - slot, 1)

            drw[:, columns(rank, size)] = (
                mm_t(dga[...], buffer[slot, 0]) + mm_t(dup[...], buffer[slot, 1])
            ).astype(BF)
            for k in (2, 3, 1):
                slab(k, rank, step).start()

        def combined(step):
            rank = peer("tp", n_tp, step)
            at = columns(rank, size)
            for k in (2, 3, 1):
                slab(k, rank, step - 1).wait()
            block = t_mm(pck[0:CAP], drw[0:CAP, at])
            for k in range(1, experts):
                block = block + t_mm(pck[k * CAP : (k + 1) * CAP], back[k - 1, :, at])
            return block

        def give(step):
            return described(
                parts.at[step - 1], slots.at[step - 1], sems[6:8], step - 1,
                {"tp": peer("tp", n_tp, step)},
            )

        def pass_on(begin, end):
            @pl.loop(begin, end)
            def _(step):
                parts[step - 1] = combined(step).astype(BF)
                give(step).start()

        load(2, 0, 0, 0)
        finish(small)
        order = lax.broadcasted_iota(jnp.int32, (8, rows), 0)
        own = jnp.zeros((8, rows), F32)
        for k in range(experts):
            by_slot = dts[0] if k == 0 else back_dots[k - 1]
            by_row = lax.dot_general(
                by_slot[:, 0:CAP],
                pck[k * CAP : (k + 1) * CAP].astype(F32),
                (((1,), (0,)), ((), ())),
                precision=lax.Precision.HIGHEST,
                preferred_element_type=F32,
            )
            own = own + jnp.where(order == k, by_row, 0.0)
        mine[...] = own
        shared = [
            send(mine, sums.at[k - 1], "tp", n_tp, k, sems[4:6]) for k in range(1, n_tp)
        ]
        pass_on(1, n_tp - 1)

        finish(fetches)

        @pl.loop(0, n_tp)
        def _(rank):
            slot = lax.rem(rank, 2)
            loaded(2, slot, 0)

            @pl.when(rank + 1 < n_tp)
            def _():
                load(2, rank + 1, 1 - slot, 0)

            eo[:, columns(rank, size)] = mm_t(hid[...], buffer[slot, 0]).astype(BF)

        pltpu.make_async_copy(eo, out_rows, out_sem).start()
        pass_on(n_tp - 1, n_tp)
        if count == 2:

            @pl.loop(0, part // 256)
            def _(i):
                at = pl.ds(pl.multiple_of((1 - first) * part + i * 256, 128), 256)
                up_held[stretch(i, 256), :] = t_mm(tok[:, at], dup[...]).astype(BF)

            pltpu.make_async_copy(up_held, up_away, up_sem).start()
        finish(shared)
        gate_grad = mine[...]
        for k in range(1, n_tp):
            gate_grad = gate_grad + sums[k - 1]
        both = [jnp.sum(nms[j] * gate_grad, axis=0, keepdims=True) for j in range(2)]
        gate = [gts[j : j + 1, :] for j in range(2)]
        mean = gate[0] * both[0] + gate[1] * both[1]
        logits = sum(gate[j] * (both[j] - mean) * one[j] for j in range(2))
        d_logits[...] = logits

        copies = [give(step) for step in range(1, n_tp)]
        total = combined(n_tp)
        total = total + lax.dot_general(
            logits.astype(BF),
            rtr[...].astype(BF),
            (((0,), (0,)), ((), ())),
            preferred_element_type=F32,
        )
        finish(copies)
        for k in range(1, n_tp):
            total = total + slots[k - 1].astype(F32)
        factor = scl[:, 0:1]
        unit = rsd[...] * factor
        d_gain[...] = jnp.broadcast_to(jnp.sum(total * unit, axis=0, keepdims=True), d_gain.shape)
        gained = total * gn[0:1, :]
        d_resid[...] = gained
        dot = total_over(row_sums(unit * gained), mine_two, sums_two, "tp", n_tp, sems[8:10])
        dot = as_column(dot, eighth())[:, 0:1] * (1.0 / width)
        result = grd[...].astype(F32) + factor * (d_resid[...] - rsd[...] * factor * dot)
        d_resid[...] = result
        low[...] = result.astype(BF)
        pltpu.make_async_copy(eo, out_rows, out_sem).wait()
        if count == 2:
            pltpu.make_async_copy(up_held, up_away, up_sem).wait()

    outs = [
        shape((rows, size), F32),
        shape((rows, size), BF),
        shape((8, size), F32),
        shape((8, rows), F32),
        shape((experts * CAP, width), BF),
    ]
    held = []
    if count == 2:
        outs.append(shape((part, hidden), BF))
        held = [pltpu.VMEM((part, hidden), BF), DMA]
    flat = [array for group in weights for array in group]
    return call(
        kernel,
        tuple(outs),
        (*acts, *flat, tokens, dots, picks, gates, onehot, names, router, resid, scale, gain, grad),
        held
        + [
            pltpu.VMEM((experts * CAP, width), BF),
            pltpu.VMEM((experts * CAP, width), BF),
            pltpu.VMEM((2, 2, size, hidden), BF),
            pltpu.VMEM((n_ctx - 1, CAP, width), BF),
            pltpu.VMEM((n_ctx - 1, 8, rows), F32),
            pltpu.VMEM((n_tp - 1, rows, size), BF),
            pltpu.VMEM((n_tp - 1, rows, size), BF),
            pltpu.VMEM((8, rows), F32),
            pltpu.VMEM((n_tp - 1, 8, rows), F32),
            pltpu.VMEM((8, rows), F32),
            pltpu.VMEM((n_tp - 1, 8, rows), F32),
            DMA((2, 2)),
            DMA,
            pltpu.VMEM((experts * CAP, hidden), BF),
            pltpu.VMEM((experts * CAP, width), BF),
            DMA((2,)),
        ]
        + pair_of_sems(n_ctx)
        + pair_of_sems(n_tp * n_ctx)
        + pair_of_sems(n_tp) * 3,
        4,
        "second_norm_back",
        left=tuple(range(2, 4 + 3 * count)) + ((-2, -1) if count == 2 else (-1,)),
    )


def attention_backward(
    low, output_w, query, kv, cosine, sine, sums, payload, n_tp, n_ctx
):
    rows, size = low.shape
    width = size * n_tp
    inner = query.shape[1]
    heads = inner // HD
    scale = 1.0 / math.sqrt(HD)

    half = heads // 2
    sums, sums_input = sums
    lane = 2 * half * HD

    def kernel(*refs):
        lw, wgt_far, qry_far, full_far, cs, sn, made = refs[:7]
        n_in, n_out = 7 + len(payload.inputs), len(payload.outs)
        d_attn, d_qkv, summed = refs[n_in : n_in + 3]
        scratch = refs[n_in + 3 + n_out :]
        dot, dqs, dkv, slots, last, both, total, kept = scratch[:8]
        sems = scratch[8:12]
        wgt, qry, full, late = scratch[12:16]
        sums.take(made, scratch[16 : 16 + len(sums.scratch)])
        payload.take(
            refs[7:n_in], refs[n_in + 3 : n_in + 3 + n_out], scratch[16 + len(sums.scratch) :]
        )
        payload.load()
        fetches = [
            pltpu.make_async_copy(far, near, late.at[i])
            for i, (far, near) in enumerate([(qry_far, qry), (full_far, full), (wgt_far, wgt)])
        ]
        for copy in fetches:
            copy.start()
        greet([("tp", n_tp), ("ctx", n_ctx)])
        here, beside, across = quad()
        beyond = lax.rem(beside + 2, 4)
        copies = gather_columns(lw, d_attn, "tp", n_tp, sems[2:4])
        sums.start()
        payload.go()
        finish(fetches)

        @pl.loop(0, heads)
        def _(h):
            at = columns(h, HD)
            kept[h] = softmax_rows(qry[:, at], full[:, at], here * rows)

        for step in range(n_tp):
            rank = peer("tp", n_tp, n_tp - step)
            weights = wgt[pl.ds(pl.multiple_of(rank * size, 16), size), :]
            if step:
                copies[step - 1].wait()
                total[...] += mm(d_attn[:, columns(rank, size)], weights)
            else:
                total[...] = mm(lw[...], weights)
        dot[...] = total[...].astype(BF)
        first, second, third = [], [], []
        for j in range(2):

            @pl.loop(0, half)
            def _(i):
                h = j * half + i
                at, at_v = columns(h, HD), columns(h + heads, HD)
                key_at = pl.ds(pl.multiple_of(j * lane + i * HD, 128), HD)
                value_at = pl.ds(pl.multiple_of(j * lane + (half + i) * HD, 128), HD)
                probs = kept[h]
                d_probs = mm_t(dot[:, at], full[:, at_v])
                delta = jnp.sum(probs * d_probs, axis=-1, keepdims=True)
                d_scores = (probs * (d_probs - delta)).astype(BF)
                dqs[:, at] = mm(d_scores, full[:, at]) * scale
                dkv[:, key_at] = (t_mm(d_scores, qry[:, at]) * scale).astype(BF)
                dkv[:, value_at] = t_mm(probs.astype(BF), dot[:, at]).astype(BF)

            at = pl.ds(j * lane, lane)
            first.append(
                remote(
                    dkv.at[stretch(beyond, rows), at], slots.at[0, :, at],
                    sems, 3 * j, {"ctx": beside},
                )
            )
            second.append(
                remote(
                    dkv.at[stretch(beside, rows), at], slots.at[1, :, at],
                    sems, 3 * j + 1, {"ctx": beside},
                )
            )
        for j in range(2):
            at = pl.ds(j * lane, lane)
            first[j].wait()
            both[:, at] = (
                dkv[stretch(across, rows), at].astype(F32) + slots[0, :, at].astype(F32)
            ).astype(BF)
            third.append(
                remote(both.at[:, at], last.at[:, at], sems, 3 * j + 2, {"ctx": across})
            )

        @pl.loop(0, heads)
        def _(h):
            d_qkv[:, columns(h, HD)] = turn(dqs[:, columns(h, HD)], cs[...], sn[...]).astype(BF)

        for j in range(2):
            second[j].wait()
            third[j].wait()

            @pl.loop(0, half)
            def _(i):
                h = j * half + i
                key_at = pl.ds(pl.multiple_of(j * lane + i * HD, 128), HD)
                value_at = pl.ds(pl.multiple_of(j * lane + (half + i) * HD, 128), HD)
                mine = stretch(here, rows)
                d_key = dkv[mine, key_at].astype(F32) + slots[1, :, key_at].astype(F32)
                d_key = d_key + last[:, key_at].astype(F32)
                d_qkv[:, columns(h + heads, HD)] = turn(d_key, cs[...], sn[...]).astype(BF)
                d_value = dkv[mine, value_at].astype(F32) + slots[1, :, value_at].astype(F32)
                d_value = d_value + last[:, value_at].astype(F32)
                d_qkv[:, columns(h + 2 * heads, HD)] = d_value.astype(BF)

        summed[...] = sums.total().astype(BF)
        payload.wait()

    return call(
        kernel,
        (
            shape((rows, width), BF),
            shape((rows, 3 * inner), BF),
            shape(sums.shape, BF),
            *payload.outs,
        ),
        (low, output_w, query, kv, cosine, sine, sums_input, *payload.inputs),
        [
            pltpu.VMEM((rows, inner), BF),
            pltpu.VMEM((rows, inner), F32),
            pltpu.VMEM((rows * n_ctx, 2 * inner), BF),
            pltpu.VMEM((2, rows, 2 * inner), BF),
            pltpu.VMEM((rows, 2 * inner), BF),
            pltpu.VMEM((rows, 2 * inner), BF),
            pltpu.VMEM((rows, inner), F32),
            pltpu.VMEM((heads, rows, rows * n_ctx), F32),
        ]
        + pair_of_sems(6)
        + pair_of_sems(n_tp)
        + [
            pltpu.VMEM(array.shape, BF) for array in (output_w, query, kv)
        ]
        + [DMA((3,))]
        + sums.scratch
        + payload.scratch,
        5,
        "attention_backward",
        left=(1, 2, 3, *range(6, 7 + len(payload.inputs)), -len(payload.outs)),
    )


def first_norm_back(d_qkv, weights, hidden, scale, gain, d_resid, early, later, square, payload, n_tp, n_ctx):
    n_square = len(square.inputs) if square else 0
    more, more_input = later
    rows, size = hidden.shape
    width = size * n_tp

    def kernel(*refs):
        dpr, wgt, hid, scl, gn, dr, erl, made = refs[:8]
        refs = refs[:7] + refs[8:]
        squared, refs = refs[7 : 7 + n_square], refs[:7] + refs[7 + n_square :]
        n_in, n_out = 7 + len(payload.inputs), len(payload.outs)
        out, d_gain, returned, summed = refs[n_in : n_in + 4]
        refs = refs[: n_in + 3] + refs[n_in + 4 :]
        squared_out = refs[n_in + 3 : n_in + 3 + 2 * n_square]
        refs = refs[: n_in + 3] + refs[n_in + 3 + 2 * n_square :]
        scratch = refs[n_in + 3 + n_out :]
        held, parts, slots, mine, sums, loads = scratch[:6]
        sems = scratch[6:10]
        begin = 12 + len(more.scratch)
        more.take(made, scratch[12:begin])
        first = begin + (len(square.scratch) if square else 0)
        payload.take(refs[7:n_in], refs[n_in + 3 : n_in + 3 + n_out], scratch[first:])
        if square:
            square.take(squared, squared_out, scratch[begin:first])

        def block(step):
            rank = peer("tp", n_tp, step)
            return pltpu.make_async_copy(
                wgt.at[stretch(rank, size), :], held.at[step - 1], loads.at[step - 1]
            )

        for step in range(1, n_tp + 1):
            block(step).start()
        payload.load()
        greet([("tp", n_tp), ("ctx", n_ctx)])
        given = [
            send(erl, returned, "ctx", n_ctx, n_ctx - 2, scratch[10:12])
        ]
        if square:
            square.start()

        def give(step):
            return described(
                parts.at[step - 1], slots.at[step - 1], sems[0:2], step - 1,
                {"tp": peer("tp", n_tp, step)},
            )

        @pl.loop(1, n_tp + 1)
        def _(step):
            block(step).wait()
            out[...] = mm_t(dpr[...], held[step - 1])

            @pl.when(step < n_tp)
            def _():
                parts[step - 1] = out[...].astype(BF)
                give(step).start()

        copies = [give(step) for step in range(1, n_tp)]
        payload.go()
        if square:
            square.cross()
        finish(copies)
        total = out[...]
        for k in range(1, n_tp):
            total = total + slots[k - 1].astype(F32)
        factor = scl[:, 0:1]
        unit = hid[...].astype(F32) * factor
        d_gain[...] = jnp.broadcast_to(jnp.sum(total * unit, axis=0, keepdims=True), d_gain.shape)
        gained = total * gn[0:1, :]
        out[...] = gained
        dot = total_over(row_sums(unit * gained), mine, sums, "tp", n_tp, sems[2:4])
        dot = as_column(dot, eighth())[:, 0:1] * (1.0 / width)
        more.start()
        unit = hid[...].astype(F32) * factor
        out[...] = dr[...] + factor * (out[...] - unit * dot)
        finish(given)
        summed[...] = more.total().astype(BF)
        if square:
            square.end()
        payload.wait()

    return call(
        kernel,
        (
            shape((rows, size), F32),
            shape((8, size), F32),
            shape((CAP, size), BF),
            shape(more.shape, BF),
            *(square.outs if square else []),
            *payload.outs,
        ),
        (
            *(d_qkv, weights, hidden, scale, gain, d_resid, early, more_input),
            *(square.inputs if square else []),
            *payload.inputs,
        ),
        [
            pltpu.VMEM((n_tp, size, d_qkv.shape[1]), BF),
            pltpu.VMEM((n_tp - 1, rows, size), BF),
            pltpu.VMEM((n_tp - 1, rows, size), BF),
            pltpu.VMEM((8, rows), F32),
            pltpu.VMEM((n_tp - 1, 8, rows), F32),
            DMA((n_tp,)),
        ]
        + pair_of_sems(n_tp) * 2
        + pair_of_sems(n_ctx)
        + more.scratch
        + (square.scratch if square else [])
        + payload.scratch,
        6,
        "first_norm_back",
        left=(1, *range(7, 8 + n_square + len(payload.inputs)), -len(payload.outs)),
    )


class SquareSum:

    def __init__(self, ready, n_ctx):
        self.n_ctx = n_ctx
        _, rows, size = ready.shape
        self.inputs = [ready]
        self.outs = [shape((rows, size), BF), shape((rows, size), F32)]
        self.scratch = [
            pltpu.VMEM((4, rows, size), BF),
            pltpu.VMEM((4, rows, size), BF),
            pltpu.VMEM((2, rows, size), BF),
            pltpu.VMEM((2, rows, size), BF),
            DMA((4,)),
        ]
        self.scratch += pair_of_sems(4) + pair_of_sems(2)

    def take(self, ins, outs, scratch):
        self.ready, self.out_refs, self.held = ins[0], outs, scratch

    def start(self):
        here, beside, across = quad()
        beyond = lax.rem(beside + 2, 4)
        mine = lax.axis_index("fsdp")
        other = 1 - mine

        def block(rank, column):
            return self.ready.at[rank * self.n_ctx + column]

        self.fetches, self.near = [], []
        for i, (rank, theirs, ours) in enumerate(
            [(other, beyond, across), (mine, beyond, across),
             (other, beside, here), (mine, beside, here)]
        ):
            self.near.append(
                remote(
                    block(rank, theirs), self.held[1].at[i], self.held[5:7], i, {"ctx": beside}
                )
            )
            copy = pltpu.make_async_copy(
                block(rank, ours), self.held[0].at[i], self.held[4].at[i]
            )
            copy.start()
            self.fetches.append(copy)

    def chip(self, i):
        self.fetches[i].wait()
        self.near[i].wait()
        return self.held[0][i].astype(F32) + self.held[1][i].astype(F32)

    def cross(self):
        across = quad()[2]
        two, far = self.held[2:4]
        self.far = []
        for i in range(2):
            two[i] = self.chip(i).astype(BF)
            self.far.append(
                remote(two.at[i], far.at[i], self.held[7:9], i, {"ctx": across})
            )

    def end(self):
        for i in range(2):
            value = self.chip(2 + i)
            self.far[i].wait()
            value = value + self.held[3][i].astype(F32)
            self.out_refs[i][...] = value.astype(BF) if i == 0 else value


class ExpertsOut:

    def __init__(self, made, returned, last, picks, mix, resid, n_tp, n_ctx):
        self.n_ctx = n_ctx
        self.sums = RowSums(made, 0, 2 * CAP, n_tp)
        self.inputs = [made, returned, last, picks, mix, resid]
        self.size = resid.shape[1]
        self.out = shape(resid.shape, BF)
        self.scratch = [
            pltpu.VMEM(self.sums.shape, BF),
            pltpu.VMEM((2, CAP, self.size), BF),
        ]
        self.scratch += pair_of_sems(n_ctx)
        self.scratch += [pltpu.VMEM((n_ctx, resid.shape[0], 128), F32)] + self.sums.scratch

    def take(self, ins, out, scratch):
        self.ins, self.out_ref, self.held = ins, out, scratch[:5]
        self.sums.take(ins[0], scratch[5:])

    def give_back(self):
        share, back = self.held[:2]
        share[...] = self.sums.total().astype(BF)
        n_ctx = self.n_ctx
        self.copies = [
            send(share.at[pl.ds(CAP, CAP)], back.at[0], "ctx", n_ctx, n_ctx - 1, self.held[2:4]),
            send(self.ins[2], back.at[1], "ctx", n_ctx, 1, self.held[2:4]),
        ]

    def prepare(self):
        order = lax.broadcasted_iota(jnp.int32, (8, 128), 0)

        @pl.loop(0, self.n_ctx)
        def _(k):
            self.held[4][k] = as_column(self.ins[-2][...], jnp.where(order == k, 1.0, 0.0))

    def mix(self):
        returned, _, picks, mix, resid = self.ins[1:]
        share, back = self.held[:2]
        finish(self.copies)
        total = resid[...]
        for k in range(self.n_ctx):
            gate = self.held[4][k, :, 0:1]
            rows = (share[0:CAP], back[0], returned[...], back[1])[k]
            total = total + gate * t_mm(picks[k * CAP : (k + 1) * CAP], rows)
        self.out_ref[...] = total.astype(BF)


def weight_grads(squared, products, groups, small, payload, experts_out, n_tp, n_ctx):
    width = products[0][0].shape[1]
    places = 2 * n_ctx
    cut = width // places
    total_columns = squared[0].shape[1] + sum(size for _, _, size in groups)
    flat = [array for pair in products for array in pair]
    done = squared[0].shape[1]
    inputs = [*squared, *flat, small, *experts_out.inputs, *payload.inputs]

    def kernel(*refs):
        theirs, ours, refs = refs[0], refs[1], refs[2:]
        factors, refs = refs[: len(flat)], refs[len(flat) :]
        sml, refs = refs[0], refs[1:]
        given, refs = refs[: len(experts_out.inputs)], refs[len(experts_out.inputs) :]
        paid, refs = refs[: len(payload.inputs)], refs[len(payload.inputs) :]
        out, small_out, block_out = refs[:3]
        paid_out, refs = refs[3 : 3 + len(payload.outs)], refs[3 + len(payload.outs) :]
        sml_full, sml_slots, refs = refs[0], refs[1], refs[2:]
        scratch, refs = refs[: 6 * len(groups)], refs[6 * len(groups) :]
        experts_out.take(given, block_out, refs[: len(experts_out.scratch)])
        refs = refs[len(experts_out.scratch) :]
        payload.take(paid, paid_out, refs[: len(payload.scratch)])
        refs = refs[len(payload.scratch) :]
        come, come_sems, sems = refs[0], refs[1:3], refs[3:]
        payload.load()
        barrier = pltpu.get_barrier_semaphore()
        here, beside, across = quad()
        beyond = lax.rem(beside + 2, 4)
        mine = lax.axis_index("fsdp")
        other = 1 - mine
        place = mine * n_ctx + here
        others = []
        for i in range(1, places):
            to = lax.rem(place + i, places)
            others.append((to, {"fsdp": to // n_ctx, "ctx": lax.rem(to, n_ctx)}))
        ahead = [{"tp": peer("tp", n_tp, k)} for k in range(1, n_tp)]
        for device in ahead + [device for _, device in others]:
            pl.semaphore_signal(barrier, inc=1, device_id=device, device_id_type=MESH)
        pl.semaphore_wait(barrier, n_tp - 1 + places - 1)
        gathers = gather_columns(sml, sml_full, "tp", n_tp, sems[0:2])
        early = remote(theirs, come, come_sems, 0, {"fsdp": other})
        experts_out.sums.start()
        blocks = [(other, beyond), (other, beside), (mine, beyond), (mine, beside)]

        def near_copy(g, i):
            prt, come = scratch[6 * g : 6 * g + 2]
            rank, column = blocks[i]
            return described(
                prt.at[rank * n_ctx + column], come.at[i],
                sems[4 + 6 * g : 6 + 6 * g], i, {"ctx": beside},
            )

        def near(g):
            which, start, size = groups[g]
            prt = scratch[6 * g]
            left, right = factors[2 * which : 2 * which + 2]

            @pl.loop(0, places)
            def _(i):
                prt[i] = t_mm(left[:, columns(i, cut)], right[:, start : start + size]).astype(BF)

            for i in range(4):
                near_copy(g, i).start()

        def chip(g, i, rank, column):
            prt, come = scratch[6 * g : 6 * g + 2]
            near_copy(g, i).wait()
            return prt[rank * n_ctx + column].astype(F32) + come[i].astype(F32)

        def hop_copy(g, i):
            two, far = scratch[6 * g + 2 : 6 * g + 4]
            return described(
                two.at[i], far.at[i], sems[6 + 6 * g : 8 + 6 * g], i, {"fsdp": other}
            )

        def hop(g):
            for i, column in enumerate((across, here)):
                scratch[6 * g + 2][i] = chip(g, i, other, column).astype(BF)
                hop_copy(g, i).start()

        def between(j):
            for turn_of, act in enumerate(
                (lambda: near(0), lambda: hop(0), lambda: near(1), lambda: hop(1))
            ):
                pl.when(j == turn_of)(act)

        payload.go(between)
        finish(gathers)
        totals = [
            remote(sml_full.at[:, columns(to, cut)], sml_slots.at[i], sems[2:4], i, device)
            for i, (to, device) in enumerate(others)
        ]
        experts_out.prepare()
        lasts = []
        for g in range(len(groups)):
            far, one, last = scratch[6 * g + 3 : 6 * g + 6]
            value = chip(g, 2, mine, across)
            hop_copy(g, 0).wait()
            one[...] = (value + far[0].astype(F32)).astype(BF)
            lasts.append(
                remote(one, last, sems[8 + 6 * g : 10 + 6 * g], 0, {"ctx": across})
            )
            if g == 0:
                experts_out.give_back()
        finish(totals)
        sums = sml_full[:, columns(place, cut)]
        for i in range(places - 1):
            sums = sums + sml_slots[i]
        small_out[...] = sums
        start = done
        for g, (_, _, size) in enumerate(groups):
            far = scratch[6 * g + 3]
            value = chip(g, 3, mine, here)
            hop_copy(g, 1).wait()
            value = value + far[1].astype(F32)
            out[:, start : start + size] = value
            start += size
        early.wait()
        out[:, 0:done] = ours[...] + come[...].astype(F32)
        experts_out.mix()
        payload.wait()
        start = done
        for g, (_, _, size) in enumerate(groups):
            lasts[g].wait()
            at = pl.ds(start, size)
            out[:, at] = out[:, at] + scratch[6 * g + 5][...].astype(F32)
            start += size

    buffers = [pltpu.VMEM((8, width), F32), pltpu.VMEM((places - 1, 8, cut), F32)]
    sems = pair_of_sems(n_tp) + pair_of_sems(places)
    for _, _, size in groups:
        buffers += [
            pltpu.VMEM((places, cut, size), BF),
            pltpu.VMEM((4, cut, size), BF),
            pltpu.VMEM((2, cut, size), BF),
            pltpu.VMEM((2, cut, size), BF),
            pltpu.VMEM((cut, size), BF),
            pltpu.VMEM((cut, size), BF),
        ]
        sems += pair_of_sems(4) + pair_of_sems(2) + pair_of_sems(1)
    return call(
        kernel,
        (
            shape((cut, total_columns), F32),
            shape((8, cut), F32),
            experts_out.out,
            *payload.outs,
        ),
        inputs,
        buffers
        + experts_out.scratch
        + payload.scratch
        + [pltpu.VMEM(squared[0].shape, BF)]
        + pair_of_sems(1)
        + sems,
        10,
        "weight_grads",
        left=(
            len(flat) + 3,
            *range(len(inputs) - len(payload.inputs), len(inputs)),
            -len(payload.outs),
        ),
    )


def experts_back(experts_out, payload, n_tp, n_ctx):
    inputs = [*experts_out.inputs, *payload.inputs]
    given = len(experts_out.inputs)

    def kernel(*refs):
        ins, refs = refs[: len(inputs)], refs[len(inputs) :]
        outs, scratch = refs[: 1 + len(payload.outs)], refs[1 + len(payload.outs) :]
        experts_out.take(ins[:given], outs[0], scratch[: len(experts_out.scratch)])
        payload.take(ins[given:], outs[1:], scratch[len(experts_out.scratch) :])
        greet([("tp", n_tp), ("ctx", n_ctx)])
        experts_out.sums.start()
        payload.go()
        experts_out.prepare()
        experts_out.give_back()
        experts_out.mix()
        payload.wait()

    return call(
        kernel,
        (experts_out.out, *payload.outs),
        inputs,
        experts_out.scratch + payload.scratch,
        9,
        "experts_back",
        left=(0, *range(given, len(inputs)), -len(payload.outs)),
    )


def write_out(experts_grads, attn_grad, plain, n_ctx, gains=None):
    _, rows, size = experts_grads[0][0].shape
    steps = max(1, rows // 128)
    tile = rows // steps
    many = len(experts_grads)
    plain = list(plain)
    blocks = []
    if attn_grad is not None:
        block = attn_grad.shape[1] // 4
        blocks = [shape((attn_grad.shape[0], block), F32)] * 4
        plain.append(attn_grad)

    def kernel(*refs):
        here = lax.axis_index("ctx")
        if gains is not None:
            rows_in, refs, rows_out = refs[0], refs[1:-2], refs[-2:]
            for i in range(2):
                rows_out[i][...] = rows_in[i : i + 1, :]
        ins, outs = refs[: 2 * many + len(plain)], refs[2 * many + len(plain) :]
        for i in range(many):
            came, mine = ins[2 * i : 2 * i + 2]
            outs[i][here] = mine[...].astype(F32)
            for k in range(1, n_ctx):
                outs[i][lax.rem(here + n_ctx - k, n_ctx)] = came[k - 1].astype(F32)
        for i in range(len(plain) - (1 if blocks else 0)):
            outs[many + i][...] = ins[2 * many + i][...]
        for i in range(len(blocks)):
            outs[i - 4][...] = ins[-1][:, i * block : (i + 1) * block]

    def flat(array):
        return pl.BlockSpec((array.shape[0] // steps, array.shape[1]), lambda i: (i, 0))

    in_specs, out_specs, out_shape = [], [], []
    for _ in experts_grads:
        in_specs.append(pl.BlockSpec((n_ctx - 1, tile, size), lambda i: (0, i, 0)))
        in_specs.append(pl.BlockSpec((tile, size), lambda i: (i, 0)))
        out_specs.append(pl.BlockSpec((n_ctx, tile, size), lambda i: (0, i, 0)))
        out_shape.append(shape((n_ctx, rows, size), F32))
    for array in plain[: len(plain) - (1 if blocks else 0)] + blocks:
        out_specs.append(flat(array))
        out_shape.append(shape(array.shape, array.dtype))
    in_specs += [flat(array) for array in plain]
    inputs = [array for pair in experts_grads for array in pair] + plain
    if gains is not None:
        inputs = [gains] + inputs
        in_specs = [pl.BlockSpec(gains.shape, lambda i: (0, 0))] + in_specs
        for _ in range(2):
            out_specs.append(pl.BlockSpec((1, gains.shape[1]), lambda i: (0, 0)))
            out_shape.append(shape((1, gains.shape[1]), F32))
    return pl.pallas_call(
        kernel,
        grid=(steps,),
        in_specs=in_specs,
        out_specs=out_specs,
        out_shape=out_shape,
        cost_estimate=pl.CostEstimate(
            flops=0, bytes_accessed=6 * many * n_ctx * rows * size, transcendentals=0
        ),
        name="write_out",
    )(*inputs)


def after(value, *needed):
    return lax.optimization_barrier((value, *needed))[0]


def shards(
    hidden_in,
    out_grad,
    attn_gain,
    w_query,
    w_key,
    w_value,
    w_output,
    ffn_gain,
    w_router,
    w_gate,
    w_up,
    w_down,
    routes,
):
    rows_here, width_tp = hidden_in.shape
    here_tp = lax.axis_index("tp")
    here_ctx = lax.axis_index("ctx")
    here_fsdp = lax.axis_index("fsdp")
    n_fsdp = lax.axis_size("fsdp")
    n_ctx = lax.axis_size("ctx")
    n_tp = lax.axis_size("tp")
    experts = w_gate.shape[0]
    assert experts == n_ctx == 4
    width = width_tp * n_tp
    part = width // n_fsdp
    pair = n_fsdp == 2
    heads_width = w_query.shape[1]

    def swap_fsdp(value):
        return lax.ppermute(value, "fsdp", [(0, 1), (1, 0)])

    def other_parts(weight):
        if pair:
            return [weight, swap_fsdp(weight)]
        return [lax.all_gather(weight, "fsdp", axis=0, tiled=True)]

    def split(values):
        if pair:
            return [
                lax.dynamic_slice_in_dim(values, here_fsdp * part, part, 1),
                lax.dynamic_slice_in_dim(values, (1 - here_fsdp) * part, part, 1),
            ]
        return [values]

    def join(pieces):
        if pair:
            first = here_fsdp == 0
            return jnp.concatenate(
                [jnp.where(first, pieces[0], pieces[1]), jnp.where(first, pieces[1], pieces[0])],
                axis=1,
            )
        return pieces[0]

    def into(values, weights):
        return sum(mm(x, w) for x, w in zip(split(values), weights))

    def back(values, weights):
        return join([mm_t(values, w) for w in weights])

    def my_features(values):
        return lax.dynamic_slice_in_dim(values, here_tp * width_tp, width_tp, values.ndim - 1)

    attn_w = (w_query, w_key, w_value, w_output)
    small = jnp.concatenate(
        [attn_gain[None], ffn_gain[None], w_router.T, jnp.zeros((2, part), BF)], axis=0
    )
    if pair:
        quarter = part // n_ctx
        own_quarter = jnp.concatenate(
            [lax.dynamic_slice_in_dim(w, here_ctx * quarter, quarter, 0) for w in attn_w], axis=1
        )
        other_quarter = swap_fsdp(own_quarter)
        other_small = swap_fsdp(small)
        small_full = join([small, other_small]).astype(F32)
    else:
        other_quarter = None
        small_full = lax.all_gather(small, "fsdp", axis=1, tiled=True).astype(F32)
    inputs_full, up_mine, down_mine = gather_tp(hidden_in, (w_up, w_down), n_tp)
    gate_w = other_parts(lax.dynamic_index_in_dim(w_gate, here_ctx, 0, False))
    up_w = other_parts(up_mine)
    down_w = other_parts(down_mine)
    small_here = my_features(small_full)
    gain_one_here = jnp.broadcast_to(small_here[0:1], small_here.shape)
    gain_two_here = jnp.broadcast_to(small_here[1:2], small_here.shape)
    nothing = [(0, 8 - experts), (0, 0)]
    router_here = jnp.pad(small_here[2 : 2 + experts], nothing)

    relative = (jnp.arange(experts, dtype=jnp.int32) + here_ctx) % experts
    numbers = jnp.arange(8, dtype=jnp.int32)
    onehot = (routes.T[:, None, :] == numbers[None, :, None]).astype(F32)
    named = (routes.T[:, None, :] == relative[None, :, None]).astype(F32)
    names = jnp.pad(named, [(0, 0)] + nothing)
    chosen = jnp.sum(named, axis=0)
    earlier = jnp.triu(jnp.ones((rows_here, rows_here), BF), 1)
    slot_of = mm(chosen.astype(BF), earlier).astype(jnp.int32)
    slots = jnp.arange(CAP, dtype=jnp.int32)
    picks = (slot_of[:, None, :] == slots[None, :, None]) & (chosen[:, None, :] > 0)
    picks = picks.astype(BF).reshape(experts * CAP, rows_here)

    gathered = first_norm(
        inputs_full, out_grad, small_full, attn_w, other_quarter, n_tp, n_ctx
    )
    normed_one, scale_one, grad_full = gathered[:3]
    if pair:
        qkv_w, output_w = gathered[3:]
    else:
        qkv_w, output_w = (
            lax.all_gather(w, "fsdp", axis=0, tiled=True)
            for w in (jnp.concatenate(attn_w[:3], axis=1), w_output)
        )
    positions = here_ctx * rows_here + jnp.arange(rows_here, dtype=jnp.int32)
    cosine, sine = rotary_tables(positions)
    attended, query, kv = attention_forward(mm(normed_one, qkv_w), cosine, sine, n_ctx)
    resid, scale_two, normed_two, grad_rows, token_rows, slot_gates, gates, mix = second_norm(
        mm_t(attended, output_w).astype(BF),
        hidden_in,
        gain_two_here,
        mm(picks, grad_full).astype(BF),
        picks,
        router_here,
        onehot,
        names,
        n_tp,
        n_ctx,
    )
    gate_rows = slot_gates[:, 0, :CAP].reshape(experts * CAP, 1)

    to_gate, to_up, hidden_act = expert_acts(token_rows, gate_w, up_w, n_fsdp)
    d_result = (gate_rows * grad_rows.astype(F32)).astype(BF)

    def away(left, right):
        value = t_mm(split(left)[1], right).astype(BF)
        return value, swap_fsdp(value)

    def payload_of(left, right, come):
        if pair:
            return Payload(n_ctx, product=(left, right, come))
        return Payload(
            n_ctx,
            rows=lax.psum_scatter(
                t_mm(left, right).astype(BF), "fsdp", scatter_dimension=0, tiled=True
            ),
        )

    def came_and_own(outs, payload):
        if pair:
            return tuple(outs)
        own = lax.dynamic_slice_in_dim(payload.inputs[0], here_ctx * payload.cut, payload.cut, 0)
        return outs[0], own

    down_come = gate_come = up_come = None
    if pair:
        down_away, down_come = away(d_result, hidden_act)
        grad_rows = after(grad_rows, down_away)
    d_hidden = into(grad_rows, down_w)
    gate_dot = jnp.sum(hidden_act.astype(F32) * d_hidden, axis=-1).reshape(experts, CAP)
    gate_dot = jnp.broadcast_to(
        jnp.pad(gate_dot, [(0, 0), (0, rows_here - CAP)])[:, None, :], (experts, 8, rows_here)
    )
    d_hidden = gate_rows * d_hidden
    d_gate_act = (d_hidden * to_gate).astype(BF)
    d_up_act = (d_hidden * to_up).astype(BF)
    if pair:
        gate_away, gate_come = away(token_rows, d_gate_act)

    acts = (d_gate_act, d_up_act, hidden_act)
    if pair:
        acts = lax.optimization_barrier((*acts, gate_away))[:3]
    d_resid, d_attn_here, gain_two_part, d_logits, made, *up_away = second_norm_back(
        acts,
        (gate_w, up_w, down_w),
        token_rows,
        gate_dot,
        picks,
        gates,
        onehot,
        names,
        router_here,
        resid,
        scale_two,
        gain_two_here,
        out_grad,
        n_tp,
        n_ctx,
    )
    if pair:
        up_come = swap_fsdp(up_away[0])

    payload = payload_of(d_result, hidden_act, down_come)
    early = (RowSums(made, 2 * CAP, CAP, n_tp), made)
    d_attn, d_qkv, made_early, *outs = attention_backward(
        d_attn_here, output_w, query, kv, cosine, -sine, early, payload, n_tp, n_ctx
    )
    grad_down = came_and_own(outs, payload)
    payload = payload_of(token_rows, d_gate_act, gate_come)
    square = None
    if pair:
        share = t_mm(d_attn, attended).astype(BF)
        square = SquareSum(share.reshape(n_fsdp * n_ctx, quarter, heads_width), n_ctx)
    later = (RowSums(made, 3 * CAP, CAP, n_tp), made)
    in_grad, gain_one_part, returned, made_later, *outs = first_norm_back(
        d_qkv,
        qkv_w,
        hidden_in,
        scale_one,
        gain_one_here,
        d_resid,
        made_early,
        later,
        square,
        payload,
        n_tp,
        n_ctx,
    )
    if pair:
        squared, outs = outs[:2], outs[2:]
    grad_gate = came_and_own(outs, payload)
    payload = payload_of(token_rows, d_up_act, up_come)

    small_part = jnp.concatenate(
        [
            gain_one_part[:1],
            gain_two_part[:1],
            mm(d_logits[:experts].astype(BF), my_features(normed_two)),
            jnp.zeros((6 - experts, width_tp), F32),
        ],
        axis=0,
    )
    written = write_out([grad_gate, grad_down], None, (), n_ctx)
    if pair:
        small_part = after(small_part, *written)
    grad_gate, grad_down = written
    experts_out = ExpertsOut(made, returned, made_later, picks, mix, resid, n_tp, n_ctx)
    if pair:
        grad_attn, small_grad, block_out, *outs = weight_grads(
            squared,
            [(normed_one, d_qkv)],
            [(0, 0, 2 * heads_width), (0, 2 * heads_width, heads_width)],
            small_part,
            payload,
            experts_out,
            n_tp,
            n_ctx,
        )
    else:
        grad_attn = jnp.concatenate([t_mm(d_attn, attended), t_mm(normed_one, d_qkv)], axis=1)
        scatter = partial(
            lax.psum_scatter, axis_name=("fsdp", "ctx"), scatter_dimension=0, tiled=True
        )
        grad_attn = scatter(grad_attn.astype(BF)).astype(F32)
        small_grad = lax.all_gather(small_part, "tp", axis=1, tiled=True)
        small_grad = scatter(small_grad.T).T
        block_out, *outs = experts_back(experts_out, payload, n_tp, n_ctx)
    grad_up = came_and_own(outs, payload)
    (
        grad_up, block_out, in_grad, grad_output, grad_query, grad_key, grad_value,
        gain_one_grad, gain_two_grad,
    ) = write_out(
        [grad_up], grad_attn, (block_out, in_grad), n_ctx, small_grad
    )
    return (
        block_out,
        in_grad,
        gain_one_grad.reshape(-1),
        grad_query,
        grad_key,
        grad_value,
        grad_output,
        gain_two_grad.reshape(-1),
        small_grad[2 : 2 + experts].T,
        grad_gate,
        grad_up,
        grad_down,
    )


def solution(mesh):
    rows = ("fsdp", "ctx")
    placed = (
        P(rows, "tp"),
        P(rows, "tp"),
        P("fsdp"),
        P("fsdp", "tp"),
        P("fsdp", "tp"),
        P("fsdp", "tp"),
        P("fsdp", "tp"),
        P("fsdp"),
        P("fsdp", None),
        P(None, "fsdp", "tp"),
        P(None, "fsdp", "tp"),
        P(None, "fsdp", "tp"),
        P(rows, None),
    )
    return jax.shard_map(
        shards,
        mesh=mesh,
        in_specs=placed,
        out_specs=(
            P(rows, "tp"),
            P(rows, "tp"),
            P(rows),
            P(rows, "tp"),
            P(rows, "tp"),
            P(rows, "tp"),
            P(rows, "tp"),
            P(rows),
            P(rows, None),
            P(None, rows, "tp"),
            P(None, rows, "tp"),
            P(None, rows, "tp"),
        ),
        check_vma=False,
    )
```

```python
from functools import partial
import math

import jax
import jax.numpy as jnp
from jax import lax
from jax.experimental import pallas as pl
from jax.experimental.pallas import tpu as pltpu
from jax.sharding import PartitionSpec as P

HD = 128
CAP = 160


EPS = 1e-05
THETA = 10000.0
NEG = -1e30
BF = jnp.bfloat16
F32 = jnp.float32


def mm(left, right):
    return jnp.dot(left, right, preferred_element_type=F32)


def mm_t(left, right):
    return lax.dot_general(left, right, (((1,), (1,)), ((), ())), preferred_element_type=F32)


def t_mm(left, right):
    return lax.dot_general(left, right, (((0,), (0,)), ((), ())), preferred_element_type=F32)


def rotary_tables(positions):
    half_size = HD // 2
    frequency = THETA ** (-(jnp.arange(half_size, dtype=F32) * 2.0 / HD))
    angles = positions.astype(F32)[:, None] * frequency[None, :]
    cosine, sine = jnp.cos(angles), jnp.sin(angles)
    return jnp.concatenate([cosine, cosine], axis=1), jnp.concatenate([-sine, sine], axis=1)


MESH = pl.DeviceIdType.MESH
VM = pl.BlockSpec(memory_space=pltpu.VMEM)
DMA = pltpu.SemaphoreType.DMA


def peer(axis, n, k):
    return lax.rem(lax.axis_index(axis) + k, n)


def greet(groups):
    barrier = pltpu.get_barrier_semaphore()
    for axis, n in groups:
        for k in range(1, n):
            pl.semaphore_signal(
                barrier, inc=1, device_id={axis: peer(axis, n, k)}, device_id_type=MESH
            )
    pl.semaphore_wait(barrier, sum(n - 1 for _, n in groups))


def described(source, target, sems, i, to):
    return pltpu.make_async_remote_copy(
        src_ref=source,
        dst_ref=target,
        send_sem=sems[0].at[i],
        recv_sem=sems[1].at[i],
        device_id=to,
        device_id_type=MESH,
    )


def remote(source, target, sems, i, to):
    copy = described(source, target, sems, i, to)
    copy.start()
    return copy


def send(source, target, axis, n, k, sems):
    return remote(source, target, sems, k - 1, {axis: peer(axis, n, k)})


def columns(n, size):
    return pl.ds(pl.multiple_of(n * size, 128), size)


def stretch(n, size):
    return pl.ds(pl.multiple_of(n * size, 16), size)


def gather_columns(own, full, axis, n, sems):
    size = own.shape[1]
    place = full.at[:, columns(lax.axis_index(axis), size)]
    copies = [send(own, place, axis, n, k, sems) for k in range(1, n)]
    place[...] = own[...]
    return copies


def scatter_columns(part, slots, axis, n, sems):
    size = slots.shape[2]
    return [
        send(part.at[:, columns(peer(axis, n, k), size)], slots.at[k - 1], axis, n, k, sems)
        for k in range(1, n)
    ]


def finish(copies):
    for copy in copies:
        copy.wait()


class Payload:

    def __init__(self, n_ctx, rows=None, product=None):
        self.n_ctx = n_ctx
        self.product = product is not None
        self.inputs = list(product) if self.product else [rows]
        last = self.inputs[-1]
        self.rows, self.hidden = last.shape
        self.cut = self.rows // n_ctx
        self.outs = [shape((n_ctx - 1, self.cut, self.hidden), BF)]
        self.scratch = pair_of_sems(n_ctx)
        if self.product:
            self.outs.append(shape((self.cut, self.hidden), BF))
            self.scratch += [
                pltpu.VMEM((self.rows, self.hidden), BF),
                pltpu.VMEM((self.rows, self.hidden), BF),
                pltpu.VMEM((self.inputs[0].shape[0], self.rows), BF),
                pltpu.VMEM(self.inputs[1].shape, BF),
                DMA((3,)),
            ]

    def take(self, ins, outs, scratch):
        self.ins, self.out_refs, self.held = ins, outs, scratch

    def fetches(self):
        left, right, other = self.ins
        mine = left.at[:, columns(lax.axis_index("fsdp"), self.rows)]
        return [
            pltpu.make_async_copy(source, self.held[i], self.held[6].at[j])
            for j, (source, i) in enumerate([(mine, 4), (right, 5), (other, 2)])
        ]

    def load(self):
        if self.product:
            for copy in self.fetches():
                copy.start()

    def copy(self, k):
        to = peer("ctx", self.n_ctx, k)
        source = self.held[3] if self.product else self.ins[0]
        return described(
            source.at[stretch(to, self.cut), :], self.out_refs[0].at[k - 1],
            self.held[0:2], k - 1, {"ctx": to},
        )

    def go(self, between=lambda j: None):
        n_ctx, cut = self.n_ctx, self.cut
        if not self.product:
            for k in (2, 3, 1):
                self.copy(k).start()
            return
        finish(self.fetches())

        @pl.loop(0, n_ctx)
        def _(j):
            k = lax.rem(j + 2, n_ctx)
            to = peer("ctx", n_ctx, k)
            value = t_mm(self.held[4][:, columns(to, cut)], self.held[5][...])
            value = value + self.held[2][stretch(to, cut), :].astype(F32)
            self.held[3][stretch(to, cut), :] = value.astype(BF)

            @pl.when(j != n_ctx - 2)
            def _():
                self.copy(k).start()

            between(j)

    def wait(self):
        if self.product:
            self.out_refs[1][...] = self.held[3][stretch(lax.axis_index("ctx"), self.cut), :]
        for k in range(1, self.n_ctx):
            self.copy(k).wait()


class RowSums:

    def __init__(self, made, first, count, n_tp):
        self.n_tp, self.first = n_tp, first
        self.shape = (count, made.shape[1] // n_tp)
        self.scratch = [
            pltpu.VMEM((n_tp - 1, *self.shape), BF),
            pltpu.VMEM(self.shape, BF),
            DMA,
        ] + pair_of_sems(n_tp)

    def take(self, made, scratch):
        self.made, self.held = made, scratch

    def rows(self, rank):
        return self.made.at[pl.ds(self.first, self.shape[0]), columns(rank, self.shape[1])]

    def mine(self):
        return pltpu.make_async_copy(
            self.rows(lax.axis_index("tp")), self.held[1], self.held[2]
        )

    def start(self):
        self.mine().start()
        n = self.n_tp
        self.copies = [
            send(self.rows(peer("tp", n, k)), self.held[0].at[k - 1], "tp", n, k, self.held[3:5])
            for k in range(1, n)
        ]

    def total(self):
        self.mine().wait()
        finish(self.copies)
        value = self.held[1][...].astype(F32)
        for k in range(1, self.n_tp):
            value = value + self.held[0][k - 1].astype(F32)
        return value


def quad():
    here = lax.axis_index("ctx")
    return here, here + 1 - 2 * lax.rem(here, 2), lax.rem(here + 2, 4)


def gather_square(own, places, sems, between, local=None):
    cuts = own.shape[1] // 512
    here, beside, across = quad()
    first, second, third = [], [], []
    for i in range(cuts):
        piece = own.at[:, pl.ds(i * 512, 512)]
        first.append(remote(piece, places(here, i), sems, 3 * i, {"ctx": across}))
        second.append(remote(piece, places(here, i), sems, 3 * i + 1, {"ctx": beside}))
        if local is None:
            places(here, i)[...] = piece[...]
        else:
            pltpu.make_async_copy(piece, places(here, i), local.at[i]).start()
    between()
    for i in range(cuts):
        first[i].wait()
        third.append(
            remote(places(across, i), places(across, i), sems, 3 * i + 2, {"ctx": beside})
        )
    finish(second)
    finish(third)
    if local is not None:
        for i in range(cuts):
            piece = own.at[:, pl.ds(i * 512, 512)]
            pltpu.make_async_copy(piece, places(here, i), local.at[i]).wait()


def row_sums(values):
    ones = jnp.ones((8, values.shape[1]), F32)
    return lax.dot_general(
        ones,
        values,
        (((1,), (1,)), ((), ())),
        precision=lax.Precision.HIGHEST,
        preferred_element_type=F32,
    )


def as_column(rows, weight):
    return lax.dot_general(
        rows,
        weight,
        (((0,), (0,)), ((), ())),
        precision=lax.Precision.HIGHEST,
        preferred_element_type=F32,
    )


def eighth():
    return jnp.full((8, 128), 0.125, F32)


def total_over(sums, mine, slots, axis, n, sems):
    mine[...] = sums
    copies = [send(mine, slots.at[k - 1], axis, n, k, sems) for k in range(1, n)]
    finish(copies)
    total = sums
    for k in range(1, n):
        total = total + slots[k - 1]
    return total


def call(kernel, out_shape, inputs, scratch, collective, name, left=()):
    anywhere = pl.BlockSpec(memory_space=pl.ANY)
    outs = out_shape if isinstance(out_shape, tuple) else (out_shape,)
    specs = [anywhere if i - len(outs) in left else VM for i in range(len(outs))]
    return pl.pallas_call(
        kernel,
        out_shape=out_shape,
        in_specs=[anywhere if i in left else VM for i in range(len(inputs))],
        out_specs=tuple(specs) if isinstance(out_shape, tuple) else specs[0],
        scratch_shapes=scratch,
        compiler_params=pltpu.CompilerParams(collective_id=collective, has_side_effects=True),
        cost_estimate=pl.CostEstimate(flops=0, bytes_accessed=0, transcendentals=0),
        name=name,
    )(*inputs)


def shape(dims, dtype):
    return jax.ShapeDtypeStruct(dims, dtype)


def pair_of_sems(n):
    return [DMA((n,)), DMA((n,))]


def gather_tp(value, stacks, n_tp):
    rows, size = value.shape
    many = len(stacks)
    member = stacks[0].shape[1:]

    def kernel(own, *refs):
        stk, full, outs = refs[:many], refs[many], refs[many + 1 : 2 * many + 1]
        held, loads, stores = refs[2 * many + 1 : 2 * many + 4]
        sems = refs[2 * many + 4 :]
        here = lax.axis_index("ctx")
        into = [
            pltpu.make_async_copy(stk[i].at[here], held.at[i], loads.at[i]) for i in range(many)
        ]
        away = [pltpu.make_async_copy(held.at[i], outs[i], stores.at[i]) for i in range(many)]
        for copy in into:
            copy.start()
        greet([("tp", n_tp)])
        copies = gather_columns(own, full, "tp", n_tp, sems)
        for i in range(many):
            into[i].wait()
            away[i].start()
        finish(copies)
        finish(away)

    return call(
        kernel,
        (
            shape((rows, size * n_tp), value.dtype),
            *(shape(member, stack.dtype) for stack in stacks),
        ),
        (value, *stacks),
        [pltpu.VMEM((many, *member), BF), DMA((many,)), DMA((many,))] + pair_of_sems(n_tp),
        1,
        "gather_tp",
        left=tuple(range(1, many + 1)) + tuple(range(-many, 0)),
    )


def first_norm(full, grad, gain, weights, quarter, n_tp, n_ctx):
    rows, width = full.shape
    with_quarter = quarter is not None

    def kernel(*refs):
        hid, grd, gn = refs[:3]
        refs = refs[3:]
        if with_quarter:
            wgts, refs = refs[: len(weights)], refs[len(weights) :]
            qrt, out, scale, grd_full, many_full, last_full, held, local, loads, stores = refs[:10]
            sems = refs[10:]
            half, inner = wgts[0].shape
            last = len(wgts) - 1
            mine = lax.axis_index("fsdp")

            def target(i, first_row, count):
                at = pl.ds(pl.multiple_of(first_row, 16), count)
                if i == last:
                    return last_full.at[at, :]
                return many_full.at[at, pl.ds(i * inner, inner)]

            into = [
                pltpu.make_async_copy(wgts[i], held.at[i], loads.at[i]) for i in range(len(wgts))
            ]
            away = [
                pltpu.make_async_copy(held.at[i], target(i, mine * half, half), stores.at[i])
                for i in range(len(wgts))
            ]
            for copy in into:
                copy.start()
            greet([("tp", n_tp), ("ctx", n_ctx)])
        else:
            out, scale, grd_full = refs[:3]
            sems = refs[3:]
            greet([("tp", n_tp)])
        grads = gather_columns(grd, grd_full, "tp", n_tp, sems[0:2])

        def norm():
            values = hid[...].astype(F32)
            mean = jnp.sum(values * values, axis=-1, keepdims=True) * (1.0 / width)
            factor = lax.rsqrt(mean + EPS)
            scale[...] = jnp.broadcast_to(factor, scale.shape)
            out[...] = (values * factor * gn[0:1, :]).astype(BF)

        if with_quarter:
            count = qrt.shape[0]

            def work():
                for i in range(len(wgts)):
                    into[i].wait()
                    away[i].start()
                norm()

            def places(rank, i):
                return target(i, (1 - mine) * half + rank * count, count)

            gather_square(qrt, places, sems[2:4], work, local)
            finish(away)
        else:
            norm()
        finish(grads)

    outs = [shape((rows, width), BF), shape((rows, 128), F32), shape((rows, width), BF)]
    inputs = [full, grad, gain]
    scratch, left = [], ()
    if with_quarter:
        half, inner = weights[0].shape
        many = len(weights)
        assert inner == 512
        outs.append(shape((2 * half, (many - 1) * inner), BF))
        outs.append(shape((2 * half, inner), BF))
        inputs += [*weights, quarter]
        scratch = [pltpu.VMEM((many, half, inner), BF), DMA((many,)), DMA((many,)), DMA((many,))]
        left = tuple(range(3, 3 + many)) + (-2, -1)
    return call(
        kernel,
        tuple(outs),
        inputs,
        scratch + pair_of_sems(n_tp) + pair_of_sems(12),
        7,
        "first_norm",
        left=left,
    )


def turn(values, cosine, sine):
    return values * cosine + pltpu.roll(values, HD // 2, axis=1) * sine


def softmax_rows(query, key, first_row):
    scores = mm_t(query, key) * (1.0 / math.sqrt(HD))
    rows = first_row + lax.broadcasted_iota(jnp.int32, scores.shape, 0)
    cols = lax.broadcasted_iota(jnp.int32, scores.shape, 1)
    scores = jnp.where(cols <= rows, scores, NEG)
    top = jnp.max(scores, axis=-1, keepdims=True)
    weights = jnp.exp(scores - top)
    return weights / jnp.sum(weights, axis=-1, keepdims=True)


def attention_forward(qkv, cosine, sine, n_ctx):
    rows = qkv.shape[0]
    width = qkv.shape[1] // 3
    heads = width // HD

    def kernel(prj, cs, sn, out, qry, full, own, *sems):
        greet([("ctx", n_ctx)])
        here = lax.axis_index("ctx")

        @pl.loop(0, heads)
        def _(h):
            own[:, columns(h, HD)] = turn(
                prj[:, columns(h + heads, HD)], cs[...], sn[...]
            ).astype(BF)
            own[:, columns(h + heads, HD)] = prj[:, columns(h + 2 * heads, HD)].astype(BF)

        def queries():
            @pl.loop(0, heads)
            def _(h):
                qry[:, columns(h, HD)] = turn(prj[:, columns(h, HD)], cs[...], sn[...]).astype(BF)

        def places(rank, i):
            return full.at[stretch(rank, rows), pl.ds(i * 512, 512)]

        gather_square(own, places, sems, queries)

        @pl.loop(0, heads)
        def _(h):
            probs = softmax_rows(qry[:, columns(h, HD)], full[:, columns(h, HD)], here * rows)
            out[:, columns(h, HD)] = mm(
                probs.astype(BF), full[:, columns(h + heads, HD)]
            ).astype(BF)

    return call(
        kernel,
        (
            shape((rows, width), BF),
            shape((rows, width), BF),
            shape((rows * n_ctx, 2 * width), BF),
        ),
        (qkv, cosine, sine),
        [pltpu.VMEM((rows, 2 * width), BF)] + pair_of_sems(6 * width // 512),
        2,
        "attention_forward",
    )


def second_norm(part, hidden, gain, slabs, picks, router, onehot, names, n_tp, n_ctx):
    rows, size = hidden.shape
    width = size * n_tp
    experts = n_ctx

    def kernel(
        prt, hid, gn, slb, pck, rtr, one, nms,
        resid, scale, out, moved, tokens, slot_gates, gates, mix,
        slots, mine, sums, mine_two, sums_two, low, sent, own_gates, *sems
    ):
        greet([("tp", n_tp), ("ctx", n_ctx)])
        here = lax.axis_index("tp")
        copies = scatter_columns(prt, slots, "tp", n_tp, sems[0:2])
        others = [
            send(
                slb.at[pl.ds(k * CAP, CAP)], moved.at[pl.ds(k * CAP, CAP)],
                "ctx", n_ctx, k, sems[6:8],
            )
            for k in range(1, n_ctx)
        ]
        moved[0:CAP] = slb[0:CAP]
        total = prt[:, columns(here, size)].astype(F32)
        finish(copies)
        for k in range(1, n_tp):
            total = total + slots[k - 1].astype(F32)
        total = hid[...].astype(F32) + total
        resid[...] = total
        square = total_over(row_sums(total * total), mine, sums, "tp", n_tp, sems[2:4])
        factor = lax.rsqrt(as_column(square, eighth()) * (1.0 / width) + EPS)
        scale[...] = factor
        low[...] = (resid[...] * factor[:, 0:1] * gn[0:1, :]).astype(BF)
        partial_logits = mm_t(rtr[...].astype(BF), low[...])
        mine_two[...] = partial_logits
        logit_copies = [
            send(mine_two, sums_two.at[k - 1], "tp", n_tp, k, sems[12:14]) for k in range(1, n_tp)
        ]
        gather_columns(low, out, "tp", n_tp, sems[4:6])

        def route():
            finish(logit_copies)
            logits = partial_logits
            for k in range(1, n_tp):
                logits = logits + sums_two[k - 1]
            named = [jnp.sum(one[j] * logits, axis=0, keepdims=True) for j in range(2)]
            top = jnp.maximum(named[0], named[1])
            powers = [jnp.exp(value - top) for value in named]
            both = powers[0] + powers[1]
            gate = [value / both for value in powers]
            mixed = gate[0] * nms[0] + gate[1] * nms[1]
            mix[...] = mixed
            order = lax.broadcasted_iota(jnp.int32, (8, rows), 0)
            gates[...] = jnp.where(order == 0, gate[0], jnp.where(order == 1, gate[1], 0.0))
            own_gates[...] = jnp.zeros(own_gates.shape, F32)
            for k in range(experts):
                own_gates[k, :, 0:CAP] = lax.dot_general(
                    jnp.broadcast_to(mixed[k : k + 1], (8, rows)),
                    pck[k * CAP : (k + 1) * CAP].astype(F32),
                    (((1,), (1,)), ((), ())),
                    precision=lax.Precision.HIGHEST,
                    preferred_element_type=F32,
                )
            slot_gates[0] = own_gates[0]
            for k in range(1, n_ctx):
                others.append(
                    send(own_gates.at[k], slot_gates.at[k], "ctx", n_ctx, k, sems[10:12])
                )


        def slab(k, step):
            at = columns(peer("tp", n_tp, n_tp - step), size)
            return described(
                sent.at[step, pl.ds(k * CAP, CAP)], tokens.at[pl.ds(k * CAP, CAP), at],
                sems[8:10], step * n_ctx + k, {"ctx": peer("ctx", n_ctx, k)},
            )

        def dispatch(step, block):
            sent[step] = mm(pck[...], block).astype(BF)
            tokens[0:CAP, columns(peer("tp", n_tp, n_tp - step), size)] = sent[step, 0:CAP]
            for k in (2, 3, 1):
                slab(k, step).start()

        route()

        @pl.loop(0, n_tp)
        def _(step):
            @pl.when(step > 0)
            def _():
                described(
                    low, out.at[:, columns(here, size)], sems[4:6], step - 1,
                    {"tp": peer("tp", n_tp, step)},
                ).wait()

            dispatch(step, out[:, columns(peer("tp", n_tp, n_tp - step), size)])

        for step in range(n_tp):
            for k in (2, 3, 1):
                slab(k, step).wait()
        finish(others)

    return call(
        kernel,
        (
            shape((rows, size), F32),
            shape((rows, 128), F32),
            shape((rows, width), BF),
            shape(slabs.shape, BF),
            shape(slabs.shape, BF),
            shape((experts, 8, rows), F32),
            shape((8, rows), F32),
            shape((8, rows), F32),
        ),
        (part, hidden, gain, slabs, picks, router, onehot, names),
        [
            pltpu.VMEM((n_tp - 1, rows, size), BF),
            pltpu.VMEM((8, rows), F32),
            pltpu.VMEM((n_tp - 1, 8, rows), F32),
            pltpu.VMEM((8, rows), F32),
            pltpu.VMEM((n_tp - 1, 8, rows), F32),
            pltpu.VMEM((rows, size), BF),
            pltpu.VMEM((n_tp, experts * CAP, size), BF),
            pltpu.VMEM((experts, 8, rows), F32),
        ]
        + pair_of_sems(n_tp) * 3
        + pair_of_sems(n_ctx)
        + pair_of_sems(n_tp * n_ctx)
        + pair_of_sems(n_ctx)
        + pair_of_sems(n_tp),
        3,
        "second_norm",
    )


def expert_acts(tokens, gate_w, up_w, n_fsdp):
    rows, width = tokens.shape
    hidden = gate_w[0].shape[1]
    count = len(gate_w)
    part = gate_w[0].shape[0]
    chunk = 256
    per = part // chunk
    steps = count * per
    pair = count == 2

    def kernel(tok, *refs):
        wgt = [refs[:count], refs[count : 2 * count]]
        to_gate, to_up, hid, buffer, loads = refs[2 * count :]
        first = lax.axis_index("fsdp") if pair else 0

        def load(step):
            slot = lax.rem(step, 2)
            at = stretch(lax.rem(step, per), chunk)
            for lane in range(2):
                for i in range(count):

                    @pl.when(step // per == i)
                    def _():
                        pltpu.make_async_copy(
                            wgt[lane][i].at[at], buffer.at[slot, lane], loads.at[slot, lane]
                        ).start()

        load(0)
        to_gate[...] = jnp.zeros_like(to_gate)
        to_up[...] = jnp.zeros_like(to_up)

        @pl.loop(0, steps)
        def _(step):
            slot = lax.rem(step, 2)
            for lane in range(2):
                pltpu.make_async_copy(
                    wgt[lane][0].at[pl.ds(0, chunk)], buffer.at[slot, lane], loads.at[slot, lane]
                ).wait()

            @pl.when(step + 1 < steps)
            def _():
                load(step + 1)

            which = lax.rem(first + step // per, count)
            column = which * part + lax.rem(step, per) * chunk
            values = tok[:, pl.ds(pl.multiple_of(column, 128), chunk)]
            to_gate[...] += mm(values, buffer[slot, 0])
            to_up[...] += mm(values, buffer[slot, 1])

        @pl.loop(0, rows // 32)
        def _(i):
            at = stretch(i, 32)
            a, b = to_gate[at, :], to_up[at, :]
            sigma = 1.0 / (1.0 + jnp.exp(-a))
            silu = a * sigma
            hid[at, :] = (silu * b).astype(BF)
            to_up[at, :] = silu
            to_gate[at, :] = b * sigma * (1.0 + a * (1.0 - sigma))

    anywhere = pl.BlockSpec(memory_space=pl.ANY)
    return pl.pallas_call(
        kernel,
        out_shape=(
            shape((rows, hidden), F32),
            shape((rows, hidden), F32),
            shape((rows, hidden), BF),
        ),
        in_specs=[VM] + [anywhere] * (2 * count),
        out_specs=(VM, VM, VM),
        scratch_shapes=[pltpu.VMEM((2, 2, chunk, hidden), BF), DMA((2, 2))],
        cost_estimate=pl.CostEstimate(flops=0, bytes_accessed=0, transcendentals=0),
        name="expert_acts",
    )(tokens, *gate_w, *up_w)


def second_norm_back(
    acts, weights, tokens, dots, picks, gates, onehot, names, router, resid, scale, gain, grad,
    n_tp, n_ctx,
):
    rows, size = resid.shape
    width = size * n_tp
    experts = n_ctx
    hidden = acts[0].shape[1]
    count = len(weights[0])
    part = weights[0][0].shape[0]

    def kernel(*refs):
        dga, dup, hid_far = refs[:3]
        wgt = [refs[3 + i * count : 3 + (i + 1) * count] for i in range(3)]
        refs = refs[3 + 3 * count :]
        tok_far, dts, pck, gts, one, nms, rtr, rsd, scl, gn, grd = refs[:11]
        d_resid, low, d_gain, d_logits, out_rows = refs[11:16]
        refs = refs[16:]
        if count == 2:
            up_away, up_held, up_sem = refs[:1] + refs[1:3]
            refs = refs[3:]
        (
            drw, eo, buffer, back, back_dots, parts, slots, mine, sums, mine_two, sums_two, loads,
            out_sem, hid, tok, late,
        ) = refs[:16]
        sems = refs[16:]
        fetches = [
            pltpu.make_async_copy(hid_far, hid, late.at[0]),
            pltpu.make_async_copy(tok_far, tok, late.at[1]),
        ]
        here = lax.axis_index("tp")
        first = lax.axis_index("fsdp")

        def load(which, rank, slot, lane):
            feature = rank * size
            inside = pl.ds(pl.multiple_of(lax.rem(feature, part), 16), size)
            target = buffer.at[slot, lane]
            if count == 1:
                pltpu.make_async_copy(
                    wgt[which][0].at[inside], target, loads.at[slot, lane]
                ).start()
                return
            own = feature // part == first

            @pl.when(own)
            def _():
                pltpu.make_async_copy(
                    wgt[which][0].at[inside], target, loads.at[slot, lane]
                ).start()

            @pl.when(jnp.logical_not(own))
            def _():
                pltpu.make_async_copy(
                    wgt[which][1].at[inside], target, loads.at[slot, lane]
                ).start()

        def loaded(which, slot, lane):
            pltpu.make_async_copy(
                wgt[which][0].at[pl.ds(0, size)], buffer.at[slot, lane], loads.at[slot, lane]
            ).wait()

        load(0, peer("tp", n_tp, 1), 0, 0)
        load(1, peer("tp", n_tp, 1), 0, 1)
        for copy in fetches:
            copy.start()
        greet([("tp", n_tp), ("ctx", n_ctx)])
        small = []
        for k in range(1, n_ctx):
            small.append(
                send(dts.at[k], back_dots.at[k - 1], "ctx", n_ctx, n_ctx - k, sems[0:2])
            )

        def slab(k, rank, step):
            at = columns(rank, size)
            return described(
                drw.at[pl.ds(k * CAP, CAP), at], back.at[k - 1, :, at],
                sems[2:4], step * n_ctx + k - 1, {"ctx": peer("ctx", n_ctx, n_ctx - k)},
            )

        @pl.loop(0, n_tp)
        def _(step):
            rank = peer("tp", n_tp, step + 1)
            slot = lax.rem(step, 2)
            loaded(0, slot, 0)
            loaded(1, slot, 1)

            @pl.when(step + 1 < n_tp)
            def _():
                load(0, peer("tp", n_tp, step + 2), 1 - slot, 0)
                load(1, peer("tp", n_tp, step + 2), 1 - slot, 1)

            drw[:, columns(rank, size)] = (
                mm_t(dga[...], buffer[slot, 0]) + mm_t(dup[...], buffer[slot, 1])
            ).astype(BF)
            for k in (2, 3, 1):
                slab(k, rank, step).start()

        def combined(step):
            rank = peer("tp", n_tp, step)
            at = columns(rank, size)
            for k in (2, 3, 1):
                slab(k, rank, step - 1).wait()
            block = t_mm(pck[0:CAP], drw[0:CAP, at])
            for k in range(1, experts):
                block = block + t_mm(pck[k * CAP : (k + 1) * CAP], back[k - 1, :, at])
            return block

        def give(step):
            return described(
                parts.at[step - 1], slots.at[step - 1], sems[6:8], step - 1,
                {"tp": peer("tp", n_tp, step)},
            )

        def pass_on(begin, end):
            @pl.loop(begin, end)
            def _(step):
                parts[step - 1] = combined(step).astype(BF)
                give(step).start()

        load(2, 0, 0, 0)
        finish(small)
        order = lax.broadcasted_iota(jnp.int32, (8, rows), 0)
        own = jnp.zeros((8, rows), F32)
        for k in range(experts):
            by_slot = dts[0] if k == 0 else back_dots[k - 1]
            by_row = lax.dot_general(
                by_slot[:, 0:CAP],
                pck[k * CAP : (k + 1) * CAP].astype(F32),
                (((1,), (0,)), ((), ())),
                precision=lax.Precision.HIGHEST,
                preferred_element_type=F32,
            )
            own = own + jnp.where(order == k, by_row, 0.0)
        mine[...] = own
        shared = [
            send(mine, sums.at[k - 1], "tp", n_tp, k, sems[4:6]) for k in range(1, n_tp)
        ]
        pass_on(1, n_tp - 1)

        finish(fetches)

        @pl.loop(0, n_tp)
        def _(rank):
            slot = lax.rem(rank, 2)
            loaded(2, slot, 0)

            @pl.when(rank + 1 < n_tp)
            def _():
                load(2, rank + 1, 1 - slot, 0)

            eo[:, columns(rank, size)] = mm_t(hid[...], buffer[slot, 0]).astype(BF)

        pltpu.make_async_copy(eo, out_rows, out_sem).start()
        pass_on(n_tp - 1, n_tp)
        if count == 2:

            @pl.loop(0, part // 256)
            def _(i):
                at = pl.ds(pl.multiple_of((1 - first) * part + i * 256, 128), 256)
                up_held[stretch(i, 256), :] = t_mm(tok[:, at], dup[...]).astype(BF)

            pltpu.make_async_copy(up_held, up_away, up_sem).start()
        finish(shared)
        gate_grad = mine[...]
        for k in range(1, n_tp):
            gate_grad = gate_grad + sums[k - 1]
        both = [jnp.sum(nms[j] * gate_grad, axis=0, keepdims=True) for j in range(2)]
        gate = [gts[j : j + 1, :] for j in range(2)]
        mean = gate[0] * both[0] + gate[1] * both[1]
        logits = sum(gate[j] * (both[j] - mean) * one[j] for j in range(2))
        d_logits[...] = logits

        copies = [give(step) for step in range(1, n_tp)]
        total = combined(n_tp)
        total = total + lax.dot_general(
            logits.astype(BF),
            rtr[...].astype(BF),
            (((0,), (0,)), ((), ())),
            preferred_element_type=F32,
        )
        finish(copies)
        for k in range(1, n_tp):
            total = total + slots[k - 1].astype(F32)
        factor = scl[:, 0:1]
        unit = rsd[...] * factor
        d_gain[...] = jnp.broadcast_to(jnp.sum(total * unit, axis=0, keepdims=True), d_gain.shape)
        gained = total * gn[0:1, :]
        d_resid[...] = gained
        dot = total_over(row_sums(unit * gained), mine_two, sums_two, "tp", n_tp, sems[8:10])
        dot = as_column(dot, eighth())[:, 0:1] * (1.0 / width)
        result = grd[...].astype(F32) + factor * (d_resid[...] - rsd[...] * factor * dot)
        d_resid[...] = result
        low[...] = result.astype(BF)
        pltpu.make_async_copy(eo, out_rows, out_sem).wait()
        if count == 2:
            pltpu.make_async_copy(up_held, up_away, up_sem).wait()

    outs = [
        shape((rows, size), F32),
        shape((rows, size), BF),
        shape((8, size), F32),
        shape((8, rows), F32),
        shape((experts * CAP, width), BF),
    ]
    held = []
    if count == 2:
        outs.append(shape((part, hidden), BF))
        held = [pltpu.VMEM((part, hidden), BF), DMA]
    flat = [array for group in weights for array in group]
    return call(
        kernel,
        tuple(outs),
        (*acts, *flat, tokens, dots, picks, gates, onehot, names, router, resid, scale, gain, grad),
        held
        + [
            pltpu.VMEM((experts * CAP, width), BF),
            pltpu.VMEM((experts * CAP, width), BF),
            pltpu.VMEM((2, 2, size, hidden), BF),
            pltpu.VMEM((n_ctx - 1, CAP, width), BF),
            pltpu.VMEM((n_ctx - 1, 8, rows), F32),
            pltpu.VMEM((n_tp - 1, rows, size), BF),
            pltpu.VMEM((n_tp - 1, rows, size), BF),
            pltpu.VMEM((8, rows), F32),
            pltpu.VMEM((n_tp - 1, 8, rows), F32),
            pltpu.VMEM((8, rows), F32),
            pltpu.VMEM((n_tp - 1, 8, rows), F32),
            DMA((2, 2)),
            DMA,
            pltpu.VMEM((experts * CAP, hidden), BF),
            pltpu.VMEM((experts * CAP, width), BF),
            DMA((2,)),
        ]
        + pair_of_sems(n_ctx)
        + pair_of_sems(n_tp * n_ctx)
        + pair_of_sems(n_tp) * 3,
        4,
        "second_norm_back",
        left=tuple(range(2, 4 + 3 * count)) + ((-2, -1) if count == 2 else (-1,)),
    )


def attention_backward(
    low, output_w, query, kv, cosine, sine, sums, payload, n_tp, n_ctx
):
    rows, size = low.shape
    width = size * n_tp
    inner = query.shape[1]
    heads = inner // HD
    scale = 1.0 / math.sqrt(HD)

    half = heads // 2
    sums, sums_input = sums
    lane = 2 * half * HD

    def kernel(*refs):
        lw, wgt_far, qry_far, full_far, cs, sn, made = refs[:7]
        n_in, n_out = 7 + len(payload.inputs), len(payload.outs)
        d_attn, d_qkv, summed = refs[n_in : n_in + 3]
        scratch = refs[n_in + 3 + n_out :]
        dot, dqs, dkv, slots, last, both, total, kept = scratch[:8]
        sems = scratch[8:12]
        wgt, qry, full, late = scratch[12:16]
        sums.take(made, scratch[16 : 16 + len(sums.scratch)])
        payload.take(
            refs[7:n_in], refs[n_in + 3 : n_in + 3 + n_out], scratch[16 + len(sums.scratch) :]
        )
        payload.load()
        fetches = [
            pltpu.make_async_copy(far, near, late.at[i])
            for i, (far, near) in enumerate([(qry_far, qry), (full_far, full), (wgt_far, wgt)])
        ]
        for copy in fetches:
            copy.start()
        greet([("tp", n_tp), ("ctx", n_ctx)])
        here, beside, across = quad()
        beyond = lax.rem(beside + 2, 4)
        copies = gather_columns(lw, d_attn, "tp", n_tp, sems[2:4])
        sums.start()
        payload.go()
        finish(fetches)

        @pl.loop(0, heads)
        def _(h):
            at = columns(h, HD)
            kept[h] = softmax_rows(qry[:, at], full[:, at], here * rows)

        for step in range(n_tp):
            rank = peer("tp", n_tp, n_tp - step)
            weights = wgt[pl.ds(pl.multiple_of(rank * size, 16), size), :]
            if step:
                copies[step - 1].wait()
                total[...] += mm(d_attn[:, columns(rank, size)], weights)
            else:
                total[...] = mm(lw[...], weights)
        dot[...] = total[...].astype(BF)
        first, second, third = [], [], []
        for j in range(2):

            @pl.loop(0, half)
            def _(i):
                h = j * half + i
                at, at_v = columns(h, HD), columns(h + heads, HD)
                key_at = pl.ds(pl.multiple_of(j * lane + i * HD, 128), HD)
                value_at = pl.ds(pl.multiple_of(j * lane + (half + i) * HD, 128), HD)
                probs = kept[h]
                d_probs = mm_t(dot[:, at], full[:, at_v])
                delta = jnp.sum(probs * d_probs, axis=-1, keepdims=True)
                d_scores = (probs * (d_probs - delta)).astype(BF)
                dqs[:, at] = mm(d_scores, full[:, at]) * scale
                dkv[:, key_at] = (t_mm(d_scores, qry[:, at]) * scale).astype(BF)
                dkv[:, value_at] = t_mm(probs.astype(BF), dot[:, at]).astype(BF)

            at = pl.ds(j * lane, lane)
            first.append(
                remote(
                    dkv.at[stretch(beyond, rows), at], slots.at[0, :, at],
                    sems, 3 * j, {"ctx": beside},
                )
            )
            second.append(
                remote(
                    dkv.at[stretch(beside, rows), at], slots.at[1, :, at],
                    sems, 3 * j + 1, {"ctx": beside},
                )
            )
        for j in range(2):
            at = pl.ds(j * lane, lane)
            first[j].wait()
            both[:, at] = (
                dkv[stretch(across, rows), at].astype(F32) + slots[0, :, at].astype(F32)
            ).astype(BF)
            third.append(
                remote(both.at[:, at], last.at[:, at], sems, 3 * j + 2, {"ctx": across})
            )

        @pl.loop(0, heads)
        def _(h):
            d_qkv[:, columns(h, HD)] = turn(dqs[:, columns(h, HD)], cs[...], sn[...]).astype(BF)

        for j in range(2):
            second[j].wait()
            third[j].wait()

            @pl.loop(0, half)
            def _(i):
                h = j * half + i
                key_at = pl.ds(pl.multiple_of(j * lane + i * HD, 128), HD)
                value_at = pl.ds(pl.multiple_of(j * lane + (half + i) * HD, 128), HD)
                mine = stretch(here, rows)
                d_key = dkv[mine, key_at].astype(F32) + slots[1, :, key_at].astype(F32)
                d_key = d_key + last[:, key_at].astype(F32)
                d_qkv[:, columns(h + heads, HD)] = turn(d_key, cs[...], sn[...]).astype(BF)
                d_value = dkv[mine, value_at].astype(F32) + slots[1, :, value_at].astype(F32)
                d_value = d_value + last[:, value_at].astype(F32)
                d_qkv[:, columns(h + 2 * heads, HD)] = d_value.astype(BF)

        summed[...] = sums.total().astype(BF)
        payload.wait()

    return call(
        kernel,
        (
            shape((rows, width), BF),
            shape((rows, 3 * inner), BF),
            shape(sums.shape, BF),
            *payload.outs,
        ),
        (low, output_w, query, kv, cosine, sine, sums_input, *payload.inputs),
        [
            pltpu.VMEM((rows, inner), BF),
            pltpu.VMEM((rows, inner), F32),
            pltpu.VMEM((rows * n_ctx, 2 * inner), BF),
            pltpu.VMEM((2, rows, 2 * inner), BF),
            pltpu.VMEM((rows, 2 * inner), BF),
            pltpu.VMEM((rows, 2 * inner), BF),
            pltpu.VMEM((rows, inner), F32),
            pltpu.VMEM((heads, rows, rows * n_ctx), F32),
        ]
        + pair_of_sems(6)
        + pair_of_sems(n_tp)
        + [
            pltpu.VMEM(array.shape, BF) for array in (output_w, query, kv)
        ]
        + [DMA((3,))]
        + sums.scratch
        + payload.scratch,
        5,
        "attention_backward",
        left=(1, 2, 3, *range(6, 7 + len(payload.inputs)), -len(payload.outs)),
    )


def first_norm_back(d_qkv, weights, hidden, scale, gain, d_resid, early, later, square, payload, n_tp, n_ctx):
    n_square = len(square.inputs) if square else 0
    more, more_input = later
    rows, size = hidden.shape
    width = size * n_tp

    def kernel(*refs):
        dpr, wgt, hid, scl, gn, dr, erl, made = refs[:8]
        refs = refs[:7] + refs[8:]
        squared, refs = refs[7 : 7 + n_square], refs[:7] + refs[7 + n_square :]
        n_in, n_out = 7 + len(payload.inputs), len(payload.outs)
        out, d_gain, returned, summed = refs[n_in : n_in + 4]
        refs = refs[: n_in + 3] + refs[n_in + 4 :]
        squared_out = refs[n_in + 3 : n_in + 3 + 2 * n_square]
        refs = refs[: n_in + 3] + refs[n_in + 3 + 2 * n_square :]
        scratch = refs[n_in + 3 + n_out :]
        held, parts, slots, mine, sums, loads = scratch[:6]
        sems = scratch[6:10]
        begin = 12 + len(more.scratch)
        more.take(made, scratch[12:begin])
        first = begin + (len(square.scratch) if square else 0)
        payload.take(refs[7:n_in], refs[n_in + 3 : n_in + 3 + n_out], scratch[first:])
        if square:
            square.take(squared, squared_out, scratch[begin:first])

        def block(step):
            rank = peer("tp", n_tp, step)
            return pltpu.make_async_copy(
                wgt.at[stretch(rank, size), :], held.at[step - 1], loads.at[step - 1]
            )

        for step in range(1, n_tp + 1):
            block(step).start()
        payload.load()
        greet([("tp", n_tp), ("ctx", n_ctx)])
        given = [
            send(erl, returned, "ctx", n_ctx, n_ctx - 2, scratch[10:12])
        ]
        if square:
            square.start()

        def give(step):
            return described(
                parts.at[step - 1], slots.at[step - 1], sems[0:2], step - 1,
                {"tp": peer("tp", n_tp, step)},
            )

        @pl.loop(1, n_tp + 1)
        def _(step):
            block(step).wait()
            out[...] = mm_t(dpr[...], held[step - 1])

            @pl.when(step < n_tp)
            def _():
                parts[step - 1] = out[...].astype(BF)
                give(step).start()

        copies = [give(step) for step in range(1, n_tp)]
        payload.go()
        if square:
            square.cross()
        finish(copies)
        total = out[...]
        for k in range(1, n_tp):
            total = total + slots[k - 1].astype(F32)
        factor = scl[:, 0:1]
        unit = hid[...].astype(F32) * factor
        d_gain[...] = jnp.broadcast_to(jnp.sum(total * unit, axis=0, keepdims=True), d_gain.shape)
        gained = total * gn[0:1, :]
        out[...] = gained
        dot = total_over(row_sums(unit * gained), mine, sums, "tp", n_tp, sems[2:4])
        dot = as_column(dot, eighth())[:, 0:1] * (1.0 / width)
        more.start()
        unit = hid[...].astype(F32) * factor
        out[...] = dr[...] + factor * (out[...] - unit * dot)
        finish(given)
        summed[...] = more.total().astype(BF)
        if square:
            square.end()
        payload.wait()

    return call(
        kernel,
        (
            shape((rows, size), F32),
            shape((8, size), F32),
            shape((CAP, size), BF),
            shape(more.shape, BF),
            *(square.outs if square else []),
            *payload.outs,
        ),
        (
            *(d_qkv, weights, hidden, scale, gain, d_resid, early, more_input),
            *(square.inputs if square else []),
            *payload.inputs,
        ),
        [
            pltpu.VMEM((n_tp, size, d_qkv.shape[1]), BF),
            pltpu.VMEM((n_tp - 1, rows, size), BF),
            pltpu.VMEM((n_tp - 1, rows, size), BF),
            pltpu.VMEM((8, rows), F32),
            pltpu.VMEM((n_tp - 1, 8, rows), F32),
            DMA((n_tp,)),
        ]
        + pair_of_sems(n_tp) * 2
        + pair_of_sems(n_ctx)
        + more.scratch
        + (square.scratch if square else [])
        + payload.scratch,
        6,
        "first_norm_back",
        left=(1, *range(7, 8 + n_square + len(payload.inputs)), -len(payload.outs)),
    )


class SquareSum:

    def __init__(self, ready, n_ctx):
        self.n_ctx = n_ctx
        _, rows, size = ready.shape
        self.inputs = [ready]
        self.outs = [shape((rows, size), BF), shape((rows, size), F32)]
        self.scratch = [
            pltpu.VMEM((4, rows, size), BF),
            pltpu.VMEM((4, rows, size), BF),
            pltpu.VMEM((2, rows, size), BF),
            pltpu.VMEM((2, rows, size), BF),
            DMA((4,)),
        ]
        self.scratch += pair_of_sems(4) + pair_of_sems(2)

    def take(self, ins, outs, scratch):
        self.ready, self.out_refs, self.held = ins[0], outs, scratch

    def start(self):
        here, beside, across = quad()
        beyond = lax.rem(beside + 2, 4)
        mine = lax.axis_index("fsdp")
        other = 1 - mine

        def block(rank, column):
            return self.ready.at[rank * self.n_ctx + column]

        self.fetches, self.near = [], []
        for i, (rank, theirs, ours) in enumerate(
            [(other, beyond, across), (mine, beyond, across),
             (other, beside, here), (mine, beside, here)]
        ):
            self.near.append(
                remote(
                    block(rank, theirs), self.held[1].at[i], self.held[5:7], i, {"ctx": beside}
                )
            )
            copy = pltpu.make_async_copy(
                block(rank, ours), self.held[0].at[i], self.held[4].at[i]
            )
            copy.start()
            self.fetches.append(copy)

    def chip(self, i):
        self.fetches[i].wait()
        self.near[i].wait()
        return self.held[0][i].astype(F32) + self.held[1][i].astype(F32)

    def cross(self):
        across = quad()[2]
        two, far = self.held[2:4]
        self.far = []
        for i in range(2):
            two[i] = self.chip(i).astype(BF)
            self.far.append(
                remote(two.at[i], far.at[i], self.held[7:9], i, {"ctx": across})
            )

    def end(self):
        for i in range(2):
            value = self.chip(2 + i)
            self.far[i].wait()
            value = value + self.held[3][i].astype(F32)
            self.out_refs[i][...] = value.astype(BF) if i == 0 else value


class ExpertsOut:

    def __init__(self, made, returned, last, picks, mix, resid, n_tp, n_ctx):
        self.n_ctx = n_ctx
        self.sums = RowSums(made, 0, 2 * CAP, n_tp)
        self.inputs = [made, returned, last, picks, mix, resid]
        self.size = resid.shape[1]
        self.out = shape(resid.shape, BF)
        self.scratch = [
            pltpu.VMEM(self.sums.shape, BF),
            pltpu.VMEM((2, CAP, self.size), BF),
        ]
        self.scratch += pair_of_sems(n_ctx)
        self.scratch += [pltpu.VMEM((n_ctx, resid.shape[0], 128), F32)] + self.sums.scratch

    def take(self, ins, out, scratch):
        self.ins, self.out_ref, self.held = ins, out, scratch[:5]
        self.sums.take(ins[0], scratch[5:])

    def give_back(self):
        share, back = self.held[:2]
        share[...] = self.sums.total().astype(BF)
        n_ctx = self.n_ctx
        self.copies = [
            send(share.at[pl.ds(CAP, CAP)], back.at[0], "ctx", n_ctx, n_ctx - 1, self.held[2:4]),
            send(self.ins[2], back.at[1], "ctx", n_ctx, 1, self.held[2:4]),
        ]

    def prepare(self):
        order = lax.broadcasted_iota(jnp.int32, (8, 128), 0)

        @pl.loop(0, self.n_ctx)
        def _(k):
            self.held[4][k] = as_column(self.ins[-2][...], jnp.where(order == k, 1.0, 0.0))

    def mix(self):
        returned, _, picks, mix, resid = self.ins[1:]
        share, back = self.held[:2]
        finish(self.copies)
        total = resid[...]
        for k in range(self.n_ctx):
            gate = self.held[4][k, :, 0:1]
            rows = (share[0:CAP], back[0], returned[...], back[1])[k]
            total = total + gate * t_mm(picks[k * CAP : (k + 1) * CAP], rows)
        self.out_ref[...] = total.astype(BF)


def weight_grads(squared, products, groups, small, payload, experts_out, n_tp, n_ctx):
    width = products[0][0].shape[1]
    places = 2 * n_ctx
    cut = width // places
    total_columns = squared[0].shape[1] + sum(size for _, _, size in groups)
    flat = [array for pair in products for array in pair]
    done = squared[0].shape[1]
    inputs = [*squared, *flat, small, *experts_out.inputs, *payload.inputs]

    def kernel(*refs):
        theirs, ours, refs = refs[0], refs[1], refs[2:]
        factors, refs = refs[: len(flat)], refs[len(flat) :]
        sml, refs = refs[0], refs[1:]
        given, refs = refs[: len(experts_out.inputs)], refs[len(experts_out.inputs) :]
        paid, refs = refs[: len(payload.inputs)], refs[len(payload.inputs) :]
        out, small_out, block_out = refs[:3]
        paid_out, refs = refs[3 : 3 + len(payload.outs)], refs[3 + len(payload.outs) :]
        sml_full, sml_slots, refs = refs[0], refs[1], refs[2:]
        scratch, refs = refs[: 6 * len(groups)], refs[6 * len(groups) :]
        experts_out.take(given, block_out, refs[: len(experts_out.scratch)])
        refs = refs[len(experts_out.scratch) :]
        payload.take(paid, paid_out, refs[: len(payload.scratch)])
        refs = refs[len(payload.scratch) :]
        come, come_sems, sems = refs[0], refs[1:3], refs[3:]
        payload.load()
        barrier = pltpu.get_barrier_semaphore()
        here, beside, across = quad()
        beyond = lax.rem(beside + 2, 4)
        mine = lax.axis_index("fsdp")
        other = 1 - mine
        place = mine * n_ctx + here
        others = []
        for i in range(1, places):
            to = lax.rem(place + i, places)
            others.append((to, {"fsdp": to // n_ctx, "ctx": lax.rem(to, n_ctx)}))
        ahead = [{"tp": peer("tp", n_tp, k)} for k in range(1, n_tp)]
        for device in ahead + [device for _, device in others]:
            pl.semaphore_signal(barrier, inc=1, device_id=device, device_id_type=MESH)
        pl.semaphore_wait(barrier, n_tp - 1 + places - 1)
        gathers = gather_columns(sml, sml_full, "tp", n_tp, sems[0:2])
        early = remote(theirs, come, come_sems, 0, {"fsdp": other})
        experts_out.sums.start()
        blocks = [(other, beyond), (other, beside), (mine, beyond), (mine, beside)]

        def near_copy(g, i):
            prt, come = scratch[6 * g : 6 * g + 2]
            rank, column = blocks[i]
            return described(
                prt.at[rank * n_ctx + column], come.at[i],
                sems[4 + 6 * g : 6 + 6 * g], i, {"ctx": beside},
            )

        def near(g):
            which, start, size = groups[g]
            prt = scratch[6 * g]
            left, right = factors[2 * which : 2 * which + 2]

            @pl.loop(0, places)
            def _(i):
                prt[i] = t_mm(left[:, columns(i, cut)], right[:, start : start + size]).astype(BF)

            for i in range(4):
                near_copy(g, i).start()

        def chip(g, i, rank, column):
            prt, come = scratch[6 * g : 6 * g + 2]
            near_copy(g, i).wait()
            return prt[rank * n_ctx + column].astype(F32) + come[i].astype(F32)

        def hop_copy(g, i):
            two, far = scratch[6 * g + 2 : 6 * g + 4]
            return described(
                two.at[i], far.at[i], sems[6 + 6 * g : 8 + 6 * g], i, {"fsdp": other}
            )

        def hop(g):
            for i, column in enumerate((across, here)):
                scratch[6 * g + 2][i] = chip(g, i, other, column).astype(BF)
                hop_copy(g, i).start()

        def between(j):
            for turn_of, act in enumerate(
                (lambda: near(0), lambda: hop(0), lambda: near(1), lambda: hop(1))
            ):
                pl.when(j == turn_of)(act)

        payload.go(between)
        finish(gathers)
        totals = [
            remote(sml_full.at[:, columns(to, cut)], sml_slots.at[i], sems[2:4], i, device)
            for i, (to, device) in enumerate(others)
        ]
        experts_out.prepare()
        lasts = []
        for g in range(len(groups)):
            far, one, last = scratch[6 * g + 3 : 6 * g + 6]
            value = chip(g, 2, mine, across)
            hop_copy(g, 0).wait()
            one[...] = (value + far[0].astype(F32)).astype(BF)
            lasts.append(
                remote(one, last, sems[8 + 6 * g : 10 + 6 * g], 0, {"ctx": across})
            )
            if g == 1:
                experts_out.give_back()
        finish(totals)
        sums = sml_full[:, columns(place, cut)]
        for i in range(places - 1):
            sums = sums + sml_slots[i]
        small_out[...] = sums
        start = done
        for g, (_, _, size) in enumerate(groups):
            far = scratch[6 * g + 3]
            value = chip(g, 3, mine, here)
            hop_copy(g, 1).wait()
            value = value + far[1].astype(F32)
            out[:, start : start + size] = value
            start += size
        early.wait()
        out[:, 0:done] = ours[...] + come[...].astype(F32)
        experts_out.mix()
        payload.wait()
        start = done
        for g, (_, _, size) in enumerate(groups):
            lasts[g].wait()
            at = pl.ds(start, size)
            out[:, at] = out[:, at] + scratch[6 * g + 5][...].astype(F32)
            start += size

    buffers = [pltpu.VMEM((8, width), F32), pltpu.VMEM((places - 1, 8, cut), F32)]
    sems = pair_of_sems(n_tp) + pair_of_sems(places)
    for _, _, size in groups:
        buffers += [
            pltpu.VMEM((places, cut, size), BF),
            pltpu.VMEM((4, cut, size), BF),
            pltpu.VMEM((2, cut, size), BF),
            pltpu.VMEM((2, cut, size), BF),
            pltpu.VMEM((cut, size), BF),
            pltpu.VMEM((cut, size), BF),
        ]
        sems += pair_of_sems(4) + pair_of_sems(2) + pair_of_sems(1)
    return call(
        kernel,
        (
            shape((cut, total_columns), F32),
            shape((8, cut), F32),
            experts_out.out,
            *payload.outs,
        ),
        inputs,
        buffers
        + experts_out.scratch
        + payload.scratch
        + [pltpu.VMEM(squared[0].shape, BF)]
        + pair_of_sems(1)
        + sems,
        10,
        "weight_grads",
        left=(
            len(flat) + 3,
            *range(len(inputs) - len(payload.inputs), len(inputs)),
            -len(payload.outs),
        ),
    )


def experts_back(experts_out, payload, n_tp, n_ctx):
    inputs = [*experts_out.inputs, *payload.inputs]
    given = len(experts_out.inputs)

    def kernel(*refs):
        ins, refs = refs[: len(inputs)], refs[len(inputs) :]
        outs, scratch = refs[: 1 + len(payload.outs)], refs[1 + len(payload.outs) :]
        experts_out.take(ins[:given], outs[0], scratch[: len(experts_out.scratch)])
        payload.take(ins[given:], outs[1:], scratch[len(experts_out.scratch) :])
        greet([("tp", n_tp), ("ctx", n_ctx)])
        experts_out.sums.start()
        payload.go()
        experts_out.prepare()
        experts_out.give_back()
        experts_out.mix()
        payload.wait()

    return call(
        kernel,
        (experts_out.out, *payload.outs),
        inputs,
        experts_out.scratch + payload.scratch,
        9,
        "experts_back",
        left=(0, *range(given, len(inputs)), -len(payload.outs)),
    )


def write_out(experts_grads, attn_grad, plain, n_ctx, gains=None):
    _, rows, size = experts_grads[0][0].shape
    steps = max(1, rows // 128)
    tile = rows // steps
    many = len(experts_grads)
    plain = list(plain)
    blocks = []
    if attn_grad is not None:
        block = attn_grad.shape[1] // 4
        blocks = [shape((attn_grad.shape[0], block), F32)] * 4
        plain.append(attn_grad)

    def kernel(*refs):
        here = lax.axis_index("ctx")
        if gains is not None:
            rows_in, refs, rows_out = refs[0], refs[1:-2], refs[-2:]
            for i in range(2):
                rows_out[i][...] = rows_in[i : i + 1, :]
        ins, outs = refs[: 2 * many + len(plain)], refs[2 * many + len(plain) :]
        for i in range(many):
            came, mine = ins[2 * i : 2 * i + 2]
            outs[i][here] = mine[...].astype(F32)
            for k in range(1, n_ctx):
                outs[i][lax.rem(here + n_ctx - k, n_ctx)] = came[k - 1].astype(F32)
        for i in range(len(plain) - (1 if blocks else 0)):
            outs[many + i][...] = ins[2 * many + i][...]
        for i in range(len(blocks)):
            outs[i - 4][...] = ins[-1][:, i * block : (i + 1) * block]

    def flat(array):
        return pl.BlockSpec((array.shape[0] // steps, array.shape[1]), lambda i: (i, 0))

    in_specs, out_specs, out_shape = [], [], []
    for _ in experts_grads:
        in_specs.append(pl.BlockSpec((n_ctx - 1, tile, size), lambda i: (0, i, 0)))
        in_specs.append(pl.BlockSpec((tile, size), lambda i: (i, 0)))
        out_specs.append(pl.BlockSpec((n_ctx, tile, size), lambda i: (0, i, 0)))
        out_shape.append(shape((n_ctx, rows, size), F32))
    for array in plain[: len(plain) - (1 if blocks else 0)] + blocks:
        out_specs.append(flat(array))
        out_shape.append(shape(array.shape, array.dtype))
    in_specs += [flat(array) for array in plain]
    inputs = [array for pair in experts_grads for array in pair] + plain
    if gains is not None:
        inputs = [gains] + inputs
        in_specs = [pl.BlockSpec(gains.shape, lambda i: (0, 0))] + in_specs
        for _ in range(2):
            out_specs.append(pl.BlockSpec((1, gains.shape[1]), lambda i: (0, 0)))
            out_shape.append(shape((1, gains.shape[1]), F32))
    return pl.pallas_call(
        kernel,
        grid=(steps,),
        in_specs=in_specs,
        out_specs=out_specs,
        out_shape=out_shape,
        cost_estimate=pl.CostEstimate(
            flops=0, bytes_accessed=6 * many * n_ctx * rows * size, transcendentals=0
        ),
        name="write_out",
    )(*inputs)


def after(value, *needed):
    return lax.optimization_barrier((value, *needed))[0]


def shards(
    hidden_in,
    out_grad,
    attn_gain,
    w_query,
    w_key,
    w_value,
    w_output,
    ffn_gain,
    w_router,
    w_gate,
    w_up,
    w_down,
    routes,
):
    rows_here, width_tp = hidden_in.shape
    here_tp = lax.axis_index("tp")
    here_ctx = lax.axis_index("ctx")
    here_fsdp = lax.axis_index("fsdp")
    n_fsdp = lax.axis_size("fsdp")
    n_ctx = lax.axis_size("ctx")
    n_tp = lax.axis_size("tp")
    experts = w_gate.shape[0]
    assert experts == n_ctx == 4
    width = width_tp * n_tp
    part = width // n_fsdp
    pair = n_fsdp == 2
    heads_width = w_query.shape[1]

    def swap_fsdp(value):
        return lax.ppermute(value, "fsdp", [(0, 1), (1, 0)])

    def other_parts(weight):
        if pair:
            return [weight, swap_fsdp(weight)]
        return [lax.all_gather(weight, "fsdp", axis=0, tiled=True)]

    def split(values):
        if pair:
            return [
                lax.dynamic_slice_in_dim(values, here_fsdp * part, part, 1),
                lax.dynamic_slice_in_dim(values, (1 - here_fsdp) * part, part, 1),
            ]
        return [values]

    def join(pieces):
        if pair:
            first = here_fsdp == 0
            return jnp.concatenate(
                [jnp.where(first, pieces[0], pieces[1]), jnp.where(first, pieces[1], pieces[0])],
                axis=1,
            )
        return pieces[0]

    def into(values, weights):
        return sum(mm(x, w) for x, w in zip(split(values), weights))

    def back(values, weights):
        return join([mm_t(values, w) for w in weights])

    def my_features(values):
        return lax.dynamic_slice_in_dim(values, here_tp * width_tp, width_tp, values.ndim - 1)

    attn_w = (w_query, w_key, w_value, w_output)
    small = jnp.concatenate(
        [attn_gain[None], ffn_gain[None], w_router.T, jnp.zeros((2, part), BF)], axis=0
    )
    if pair:
        quarter = part // n_ctx
        own_quarter = jnp.concatenate(
            [lax.dynamic_slice_in_dim(w, here_ctx * quarter, quarter, 0) for w in attn_w], axis=1
        )
        other_quarter = swap_fsdp(own_quarter)
        other_small = swap_fsdp(small)
        small_full = join([small, other_small]).astype(F32)
    else:
        other_quarter = None
        small_full = lax.all_gather(small, "fsdp", axis=1, tiled=True).astype(F32)
    inputs_full, up_mine, down_mine = gather_tp(hidden_in, (w_up, w_down), n_tp)
    gate_w = other_parts(lax.dynamic_index_in_dim(w_gate, here_ctx, 0, False))
    up_w = other_parts(up_mine)
    down_w = other_parts(down_mine)
    small_here = my_features(small_full)
    gain_one_here = jnp.broadcast_to(small_here[0:1], small_here.shape)
    gain_two_here = jnp.broadcast_to(small_here[1:2], small_here.shape)
    nothing = [(0, 8 - experts), (0, 0)]
    router_here = jnp.pad(small_here[2 : 2 + experts], nothing)

    relative = (jnp.arange(experts, dtype=jnp.int32) + here_ctx) % experts
    numbers = jnp.arange(8, dtype=jnp.int32)
    onehot = (routes.T[:, None, :] == numbers[None, :, None]).astype(F32)
    named = (routes.T[:, None, :] == relative[None, :, None]).astype(F32)
    names = jnp.pad(named, [(0, 0)] + nothing)
    chosen = jnp.sum(named, axis=0)
    earlier = jnp.triu(jnp.ones((rows_here, rows_here), BF), 1)
    slot_of = mm(chosen.astype(BF), earlier).astype(jnp.int32)
    slots = jnp.arange(CAP, dtype=jnp.int32)
    picks = (slot_of[:, None, :] == slots[None, :, None]) & (chosen[:, None, :] > 0)
    picks = picks.astype(BF).reshape(experts * CAP, rows_here)

    gathered = first_norm(
        inputs_full, out_grad, small_full, attn_w, other_quarter, n_tp, n_ctx
    )
    normed_one, scale_one, grad_full = gathered[:3]
    if pair:
        qkv_w, output_w = gathered[3:]
    else:
        qkv_w, output_w = (
            lax.all_gather(w, "fsdp", axis=0, tiled=True)
            for w in (jnp.concatenate(attn_w[:3], axis=1), w_output)
        )
    positions = here_ctx * rows_here + jnp.arange(rows_here, dtype=jnp.int32)
    cosine, sine = rotary_tables(positions)
    attended, query, kv = attention_forward(mm(normed_one, qkv_w), cosine, sine, n_ctx)
    resid, scale_two, normed_two, grad_rows, token_rows, slot_gates, gates, mix = second_norm(
        mm_t(attended, output_w).astype(BF),
        hidden_in,
        gain_two_here,
        mm(picks, grad_full).astype(BF),
        picks,
        router_here,
        onehot,
        names,
        n_tp,
        n_ctx,
    )
    gate_rows = slot_gates[:, 0, :CAP].reshape(experts * CAP, 1)

    to_gate, to_up, hidden_act = expert_acts(token_rows, gate_w, up_w, n_fsdp)
    d_result = (gate_rows * grad_rows.astype(F32)).astype(BF)

    def away(left, right):
        value = t_mm(split(left)[1], right).astype(BF)
        return value, swap_fsdp(value)

    def payload_of(left, right, come):
        if pair:
            return Payload(n_ctx, product=(left, right, come))
        return Payload(
            n_ctx,
            rows=lax.psum_scatter(
                t_mm(left, right).astype(BF), "fsdp", scatter_dimension=0, tiled=True
            ),
        )

    def came_and_own(outs, payload):
        if pair:
            return tuple(outs)
        own = lax.dynamic_slice_in_dim(payload.inputs[0], here_ctx * payload.cut, payload.cut, 0)
        return outs[0], own

    down_come = gate_come = up_come = None
    if pair:
        down_away, down_come = away(d_result, hidden_act)
        grad_rows = after(grad_rows, down_away)
    d_hidden = into(grad_rows, down_w)
    gate_dot = jnp.sum(hidden_act.astype(F32) * d_hidden, axis=-1).reshape(experts, CAP)
    gate_dot = jnp.broadcast_to(
        jnp.pad(gate_dot, [(0, 0), (0, rows_here - CAP)])[:, None, :], (experts, 8, rows_here)
    )
    d_hidden = gate_rows * d_hidden
    d_gate_act = (d_hidden * to_gate).astype(BF)
    d_up_act = (d_hidden * to_up).astype(BF)
    if pair:
        gate_away, gate_come = away(token_rows, d_gate_act)

    acts = (d_gate_act, d_up_act, hidden_act)
    if pair:
        acts = lax.optimization_barrier((*acts, gate_away))[:3]
    d_resid, d_attn_here, gain_two_part, d_logits, made, *up_away = second_norm_back(
        acts,
        (gate_w, up_w, down_w),
        token_rows,
        gate_dot,
        picks,
        gates,
        onehot,
        names,
        router_here,
        resid,
        scale_two,
        gain_two_here,
        out_grad,
        n_tp,
        n_ctx,
    )
    if pair:
        up_come = swap_fsdp(up_away[0])

    payload = payload_of(d_result, hidden_act, down_come)
    early = (RowSums(made, 2 * CAP, CAP, n_tp), made)
    d_attn, d_qkv, made_early, *outs = attention_backward(
        d_attn_here, output_w, query, kv, cosine, -sine, early, payload, n_tp, n_ctx
    )
    grad_down = came_and_own(outs, payload)
    payload = payload_of(token_rows, d_gate_act, gate_come)
    square = None
    if pair:
        share = t_mm(d_attn, attended).astype(BF)
        square = SquareSum(share.reshape(n_fsdp * n_ctx, quarter, heads_width), n_ctx)
    later = (RowSums(made, 3 * CAP, CAP, n_tp), made)
    in_grad, gain_one_part, returned, made_later, *outs = first_norm_back(
        d_qkv,
        qkv_w,
        hidden_in,
        scale_one,
        gain_one_here,
        d_resid,
        made_early,
        later,
        square,
        payload,
        n_tp,
        n_ctx,
    )
    if pair:
        squared, outs = outs[:2], outs[2:]
    grad_gate = came_and_own(outs, payload)
    payload = payload_of(token_rows, d_up_act, up_come)

    small_part = jnp.concatenate(
        [
            gain_one_part[:1],
            gain_two_part[:1],
            mm(d_logits[:experts].astype(BF), my_features(normed_two)),
            jnp.zeros((6 - experts, width_tp), F32),
        ],
        axis=0,
    )
    written = write_out([grad_gate, grad_down], None, (), n_ctx)
    if pair:
        small_part = after(small_part, *written)
    grad_gate, grad_down = written
    experts_out = ExpertsOut(made, returned, made_later, picks, mix, resid, n_tp, n_ctx)
    if pair:
        grad_attn, small_grad, block_out, *outs = weight_grads(
            squared,
            [(normed_one, d_qkv)],
            [(0, 0, 2 * heads_width), (0, 2 * heads_width, heads_width)],
            small_part,
            payload,
            experts_out,
            n_tp,
            n_ctx,
        )
    else:
        grad_attn = jnp.concatenate([t_mm(d_attn, attended), t_mm(normed_one, d_qkv)], axis=1)
        scatter = partial(
            lax.psum_scatter, axis_name=("fsdp", "ctx"), scatter_dimension=0, tiled=True
        )
        grad_attn = scatter(grad_attn.astype(BF)).astype(F32)
        small_grad = lax.all_gather(small_part, "tp", axis=1, tiled=True)
        small_grad = scatter(small_grad.T).T
        block_out, *outs = experts_back(experts_out, payload, n_tp, n_ctx)
    grad_up = came_and_own(outs, payload)
    (
        grad_up, block_out, in_grad, grad_output, grad_query, grad_key, grad_value,
        gain_one_grad, gain_two_grad,
    ) = write_out(
        [grad_up], grad_attn, (block_out, in_grad), n_ctx, small_grad
    )
    return (
        block_out,
        in_grad,
        gain_one_grad.reshape(-1),
        grad_query,
        grad_key,
        grad_value,
        grad_output,
        gain_two_grad.reshape(-1),
        small_grad[2 : 2 + experts].T,
        grad_gate,
        grad_up,
        grad_down,
    )


def solution(mesh):
    rows = ("fsdp", "ctx")
    placed = (
        P(rows, "tp"),
        P(rows, "tp"),
        P("fsdp"),
        P("fsdp", "tp"),
        P("fsdp", "tp"),
        P("fsdp", "tp"),
        P("fsdp", "tp"),
        P("fsdp"),
        P("fsdp", None),
        P(None, "fsdp", "tp"),
        P(None, "fsdp", "tp"),
        P(None, "fsdp", "tp"),
        P(rows, None),
    )
    return jax.shard_map(
        shards,
        mesh=mesh,
        in_specs=placed,
        out_specs=(
            P(rows, "tp"),
            P(rows, "tp"),
            P(rows),
            P(rows, "tp"),
            P(rows, "tp"),
            P(rows, "tp"),
            P(rows, "tp"),
            P(rows),
            P(rows, None),
            P(None, rows, "tp"),
            P(None, rows, "tp"),
            P(None, rows, "tp"),
        ),
        check_vma=False,
    )
```
